32 devices in a mesh: section: 2 (over x), dp: 8 (over z, y), tensor: 2 (over core).
Axes of the slice: x: 2, y: 2, z: 4, core: 2. Of those that a mesh axis runs over, the one named last changes fastest.
Arguments:
- tokens: bfloat16 [2, 4096, 384], P(None, 'dp'), may hold values from -6 to 6
- image_counts: int32 [2], replicated, may hold values from 15 to 20, as said below
- cotangent: bfloat16 [2, 4096, 384], P(None, 'dp'), may hold values from -6 to 6
- norm_gains: bfloat16 [2, 2, 384], P('section', None, 'dp'), may hold values from 0.5 to 1.5
- row_biases: bfloat16 [2, 4, 384], P('section', None, 'dp'), may hold values from -3 to 3
- qkv_weight: bfloat16 [2, 384, 3, 384], P('section', 'dp', None, 'tensor'), may hold values from -0.3125 to 0.3125
- qv_bias: bfloat16 [2, 2, 384], P('section', None, 'tensor'), may hold values from -3 to 3
- out_weight: bfloat16 [2, 384, 384], P('section', 'tensor', 'dp'), may hold values from -1.25 to 1.25
- up_weight: bfloat16 [2, 384, 1536], P('section', 'dp', 'tensor'), may hold values from -0.3125 to 0.3125
- up_bias: bfloat16 [2, 1536], P('section', 'tensor'), may hold values from -3 to 3
- down_weight: bfloat16 [2, 1536, 384], P('section', 'tensor', 'dp'), may hold values from -0.21875 to 0.21875
Outputs:
- layer_outputs: bfloat16 [2, 2, 4096, 384], P('section', None, 'dp')
- input_grads: float32 [2, 2, 4096, 384], P('section', None, 'dp')
- grad_norm_gains: float32 [2, 2, 384], P('section', None, 'dp')
- grad_row_biases: float32 [2, 4, 384], P('section', None, 'dp')
- grad_qkv: float32 [2, 384, 3, 384], P('section', 'dp', None, 'tensor')
- grad_qv_bias: float32 [2, 2, 384], P('section', None, 'tensor')
- grad_out: float32 [2, 384, 384], P('section', 'tensor', 'dp')
- grad_up: float32 [2, 384, 1536], P('section', 'dp', 'tensor')
- grad_up_bias: float32 [2, 1536], P('section', 'tensor')
- grad_down: float32 [2, 1536, 384], P('section', 'tensor', 'dp')
The draws below stay inside these ranges and needn't reach their ends.
Inputs may be any that keep to these rules, and one draw needn't show every extreme that they name: `image_counts`: number of images in each micro-batch; image i fills rows i * 197 to (i + 1) * 197 - 1 of its micro-batch, later rows are padding; some micro-batch holds 20 images.
All inputs are finite; a program needn't handle non-finite values.
Results may differ from the reference program's by a relative error of at most 0.019.
Values may be sent and summed in bfloat16 or wider, within the bound.
No kernel may reach another device: no remote copies, remote signals or barrier semaphores. Data moves between devices by JAX's collectives and lax.ppermute only.
A program may use at most 128 MiB of HBM per device.

```python
import math
import jax
import jax.numpy as jnp
from jax import lax

D = 384
HEADS = 6
HD = 64
FF = 1536
IMG_LEN = 197
MICRO = 2
ROWS = 4096
CAP = 20


def draw_image_counts(key, part):
    cut_key, pick_key = jax.random.split(jax.random.fold_in(key, 11))
    removed = jax.random.randint(cut_key, (MICRO,), 0, CAP // 4 + 1)
    chosen = jax.random.randint(pick_key, (), 0, MICRO)
    counts_drawn = CAP - removed
    return jnp.where(jnp.arange(MICRO) == chosen, CAP, counts_drawn).astype(jnp.int32)


def with_spikes(result, rng, source, target, parts, factor):
    def block_of(axis_at):
        return (jnp.arange(result.shape[axis_at]) // (result.shape[axis_at] // parts)).reshape((-1,) + (1,) * (result.ndim - 1 - axis_at))

    near = jax.random.permutation(rng, parts)[block_of(target)]
    far = (block_of(target) + parts // 2) % parts
    return jnp.where((block_of(source) == near) | (block_of(source) == far), factor * result, result)


def block_scale(stream_key, extent, pieces, least, largest):
    gain, own = 1.0, jax.random.fold_in(stream_key, 6)
    for position, parts in pieces:
        heights = jnp.exp(jax.random.uniform(jax.random.fold_in(own, position), (parts,), jnp.float32, least / len(pieces), largest / len(pieces)))
        gain = gain * jnp.repeat(heights, extent[position] // parts).reshape([-1 if axis == position else 1 for axis in range(len(extent))])
    return gain


def bell_draw(own_key, extent, scale, most, shards=(), kind=jnp.bfloat16):
    drawn = scale * jax.random.normal(own_key, extent, jnp.float32)
    if shards:
        drawn = drawn * block_scale(own_key, extent, shards, -0.22, 0.18)
    return jnp.clip(drawn, -most, most).astype(kind)


def bell_draw_with(key, extent, scale, bound, pieces, heavy, kind=jnp.bfloat16):
    drawn = scale * jax.random.normal(key, extent, jnp.float32)
    if pieces:
        drawn = drawn * block_scale(key, extent, pieces, -0.22, 0.18)
    return jnp.clip(with_spikes(drawn, jax.random.fold_in(key, 3), *heavy), -bound, bound).astype(kind)


def setup_inputs(seed: int = 0) -> dict:
    keys = jax.random.split(jax.random.key(seed), 12)
    tokens = bell_draw(keys[0], (MICRO, ROWS, D), 1.0, 6.0, ((1, 8),))
    image_counts = draw_image_counts(jax.random.fold_in(keys[11], 71), 0)
    cotangent = bell_draw_with(keys[2], (MICRO, ROWS, D), 1.0, 6.0, ((1, 8),), (1, 2, 8, 2.0))
    norm_gains = jnp.clip(1.0 + 0.1 * jax.random.normal(keys[3], (2, 2, D), jnp.float32), 0.5, 1.5).astype(jnp.bfloat16)
    row_biases = bell_draw(keys[4], (2, 4, D), 0.3, 3.0, ((0, 2), (2, 8)))
    qkv_weight = bell_draw(keys[5], (2, D, 3, HEADS * HD), D ** -0.5, 0.3125, ((0, 2), (1, 8), (3, 2)))
    qv_bias = bell_draw(keys[6], (2, 2, HEADS * HD), 0.3, 3.0, ((0, 2), (2, 2)))
    out_weight = bell_draw(keys[7], (2, HEADS * HD, D), (HEADS * HD // 16) ** -0.5, 1.25, ((0, 2), (1, 2), (2, 8)))
    up_weight = bell_draw(keys[8], (2, D, FF), D ** -0.5, 0.3125, ((0, 2), (1, 8), (2, 2)))
    up_bias = bell_draw(keys[9], (2, FF), 0.3, 3.0, ((0, 2), (1, 2)))
    down_weight = bell_draw(keys[10], (2, FF, D), (FF // 2) ** -0.5, 0.21875, ((0, 2), (1, 2), (2, 8)))
    return dict(tokens=tokens, image_counts=image_counts, cotangent=cotangent, norm_gains=norm_gains, row_biases=row_biases, qkv_weight=qkv_weight, qv_bias=qv_bias, out_weight=out_weight, up_weight=up_weight, up_bias=up_bias, down_weight=down_weight)


HIGHEST = lax.Precision.HIGHEST
EPSILON = 1e-06

@jax.custom_vjp
def low(v):
    return lax.optimization_barrier(v.astype(jnp.bfloat16)).astype(jnp.float32)

@jax.custom_vjp
def low_back(v):
    return v

def low_keep(v):
    return (low(v), None)

def low_pass(kept, grad):
    return (grad,)

def back_keep(v):
    return (v, None)

def back_low(kept, grad):
    return (low(grad),)
low.defvjp(low_keep, low_pass)
low_back.defvjp(back_keep, back_low)

def round_both(values_in):
    return low_back(low(values_in))

def norm_rows(inputs, gain_row, shift_row):
    centred = inputs - lax.optimization_barrier(jnp.mean(inputs, -1, keepdims=True))
    spread = lax.optimization_barrier(jnp.mean(centred * centred, -1, keepdims=True))
    return centred * lax.rsqrt(spread + EPSILON) * gain_row + shift_row

def attend_images(query_rows, key_rows, value_rows):
    total_rows = query_rows.shape[0]
    groups = -(-total_rows // IMG_LEN)
    padding = groups * IMG_LEN - total_rows

    def by_image(matrix):
        return jnp.pad(matrix, ((0, padding), (0, 0))).reshape(groups, IMG_LEN, HEADS, HD)
    scores = jnp.einsum('gqhd,gkhd->ghqk', by_image(query_rows), by_image(key_rows), precision=HIGHEST)
    scores = low_back(scores * (1.0 / math.sqrt(HD)))
    highest = lax.optimization_barrier(jnp.max(scores, -1, keepdims=True))
    raised = jnp.exp(scores - highest)
    attention = raised / lax.optimization_barrier(jnp.sum(raised, -1, keepdims=True))
    mixed_heads = jnp.einsum('ghqk,gkhd->gqhd', low(attention), by_image(value_rows), precision=HIGHEST)
    return round_both(mixed_heads.reshape(groups * IMG_LEN, HEADS * HD)[:total_rows])

def layer_apply(inputs, params, valid_rows):
    gain_rows, shift_rows, qkv_matrix, qv_shift, out_matrix, up_matrix, up_shift, down_matrix = params
    attn_in = low(norm_rows(inputs, gain_rows[0], shift_rows[0]))
    projected = jnp.einsum('rd,dch->rch', attn_in, qkv_matrix, precision=HIGHEST)
    query_rows = round_both(projected[:, 0] + qv_shift[0])
    key_rows = round_both(projected[:, 1])
    value_rows = round_both(projected[:, 2] + qv_shift[1])
    mixed_heads = attend_images(query_rows, key_rows, value_rows)
    residual = inputs + (low_back(jnp.dot(mixed_heads, out_matrix, precision=HIGHEST)) + shift_rows[1])
    mlp_in = low(norm_rows(residual, gain_rows[1], shift_rows[2]))
    up_value = low_back(jnp.dot(mlp_in, up_matrix, precision=HIGHEST) + up_shift)
    hidden = low(jax.nn.gelu(up_value, approximate=False))
    down_value = low_back(jnp.dot(hidden, down_matrix, precision=HIGHEST))
    return (residual + (down_value + shift_rows[3])) * valid_rows[:, None]

def reference(tokens, image_counts, cotangent, norm_gains, row_biases, qkv_weight, qv_bias, out_weight, up_weight, up_bias, down_weight):
    arrays = (norm_gains, row_biases, qkv_weight, qv_bias, out_weight, up_weight, up_bias, down_weight)
    first_params = tuple((item[0].astype(jnp.float32) for item in arrays))
    second_params = tuple((item[1].astype(jnp.float32) for item in arrays))
    row_index = jnp.arange(ROWS, dtype=jnp.int32)
    valid_all = (row_index[None, :] // IMG_LEN < image_counts.astype(jnp.int32)[:, None]).astype(jnp.float32)

    def forward_pass(inputs, offsets, params_one, params_two):
        first_list = []
        second_list = []
        for batch_number in range(MICRO):
            first_out = layer_apply(inputs[batch_number], params_one, valid_all[batch_number])
            second_in = low(first_out) + offsets[batch_number]
            second_out = layer_apply(second_in, params_two, valid_all[batch_number])
            first_list.append(first_out)
            second_list.append(second_out)
        return (jnp.stack(first_list), jnp.stack(second_list))
    token_values = tokens.astype(jnp.float32)
    offsets = jnp.zeros(token_values.shape, jnp.float32)
    results, backward = jax.vjp(forward_pass, token_values, offsets, first_params, second_params)
    grad_tokens, grad_offsets, grads_one, grads_two = backward((jnp.zeros_like(results[0]), cotangent.astype(jnp.float32)))
    layer_outputs = jnp.stack([results[0], results[1]]).astype(jnp.bfloat16)
    input_grads = jnp.stack([grad_tokens, grad_offsets])
    stacked = [jnp.stack([grads_one[number], grads_two[number]]) for number in range(8)]
    return (layer_outputs, input_grads, stacked[0], stacked[1], stacked[2], stacked[3], stacked[4], stacked[5], stacked[6], stacked[7])
```

```python
import math

import jax
import jax.numpy as jnp
from jax import lax
from jax.sharding import PartitionSpec as P

IMG_LEN = 197
IMG_PAD = 208
HD = 64
EPSILON = 1e-06
NEGATIVE = -1e30
MISC = 128
F32 = jnp.float32
BF16 = jnp.bfloat16


def mm(a, b, dims):
    return lax.dot_general(a, b, (dims, ((), ())), preferred_element_type=F32)


def nn(a, b):
    return mm(a, b, ((1,), (0,)))


def nt(a, b):
    return mm(a, b, ((1,), (1,)))


def tn(a, b):
    return mm(a, b, ((0,), (0,)))


def normed(x):
    centred = x - jnp.mean(x, -1, keepdims=True)
    inverse = lax.rsqrt(jnp.mean(centred * centred, -1, keepdims=True) + EPSILON)
    return centred * inverse, inverse


def norm_back(grad, xhat, inverse, gain):
    t = grad * gain
    return inverse * (
        t - jnp.mean(t, -1, keepdims=True) - xhat * jnp.mean(t * xhat, -1, keepdims=True)
    )


def gelu_parts(u):
    cdf = 0.5 * (1.0 + lax.erf(u * math.sqrt(0.5)))
    pdf = jnp.exp(-0.5 * u * u) * (1.0 / math.sqrt(2.0 * math.pi))
    return u * cdf, cdf + u * pdf


def layer_fwd(x, w, rows):
    wq, wk, wv, wo, wu, wd = w
    gain1, gain2, bias0, bias1, bias2, bias3, qb, vb, ub = rows
    total, width = x.shape
    xhat1, inv1 = normed(x)
    attn_in = (xhat1 * gain1 + bias0).astype(BF16)
    q = ((nn(attn_in, wq) + qb) * (1.0 / math.sqrt(HD))).astype(BF16)
    k = nn(attn_in, wk).astype(BF16)
    v = (nn(attn_in, wv) + vb).astype(BF16)
    low = lax.broadcasted_iota(jnp.int32, (1, 128), 1) < HD
    real = lax.broadcasted_iota(jnp.int32, (1, IMG_PAD), 1) < IMG_LEN
    probs = []
    mixed_rows = []
    for n in range(total // IMG_PAD):
        r = slice(n * IMG_PAD, (n + 1) * IMG_PAD)
        cols = []
        for b in range(width // 128):
            c = slice(b * 128, (b + 1) * 128)
            qq, kk, vv = q[r, c], k[r, c], v[r, c]
            outs = []
            for side in (low, ~low):
                s = jnp.where(real, nt(jnp.where(side, qq, 0), kk), NEGATIVE)
                e = jnp.exp(s - jnp.max(s, -1, keepdims=True))
                p = (e / jnp.sum(e, -1, keepdims=True)).astype(BF16)
                probs.append(p)
                outs.append(nn(p, vv))
            cols.append(jnp.where(low, outs[0], outs[1]))
        mixed_rows.append(jnp.concatenate(cols, 1))
    mixed = jnp.concatenate(mixed_rows, 0).astype(BF16)
    residual = x + (nt(mixed, wo) + bias1)
    xhat2, inv2 = normed(residual)
    mlp_in = (xhat2 * gain2 + bias2).astype(BF16)
    hidden, slope = gelu_parts(nn(mlp_in, wu) + ub)
    hidden = hidden.astype(BF16)
    out = residual + (nt(hidden, wd) + bias3)
    kept = (xhat1, inv1, attn_in, q, k, v, probs, mixed, xhat2, inv2, mlp_in, slope.astype(BF16), hidden)
    return out, kept


def layer_bwd(masked, w, rows, kept):
    wq, wk, wv, wo, wu, wd = w
    gain1, gain2 = rows[0], rows[1]
    xhat1, inv1, attn_in, q, k, v, probs, mixed, xhat2, inv2, mlp_in, slope, hidden = kept
    total, width = masked.shape

    def rsum(a):
        return jnp.sum(a.astype(F32), 0, keepdims=True)

    dg = masked.astype(BF16)
    g_down = tn(dg, hidden)
    up_grad = (nn(dg, wd) * slope).astype(BF16)
    g_up = tn(mlp_in, up_grad)
    mg = nt(up_grad, wu)
    res = masked + norm_back(mg, xhat2, inv2, gain2)
    ag = res.astype(BF16)
    g_out = tn(ag, mixed)
    xg = nn(ag, wo).astype(BF16)
    low = lax.broadcasted_iota(jnp.int32, (1, 128), 1) < HD
    out_rows = []
    at = 0
    for n in range(total // IMG_PAD):
        r = slice(n * IMG_PAD, (n + 1) * IMG_PAD)
        qs, ks, vs = [], [], []
        for b in range(width // 128):
            c = slice(b * 128, (b + 1) * 128)
            qq, kk, vv, gg = q[r, c], k[r, c], v[r, c], xg[r, c]
            dq, dk, dv = [], [], []
            for side in (low, ~low):
                p = probs[at].astype(F32)
                dp = nt(jnp.where(side, gg, 0), vv)
                ds = (p * (dp - jnp.sum(p * dp, -1, keepdims=True))).astype(BF16)
                dv.append(tn(probs[at], gg))
                dq.append(nn(ds, kk) * (1.0 / math.sqrt(HD)))
                dk.append(tn(ds, qq))
                at += 1
            qs.append(jnp.where(low, *dq))
            ks.append(jnp.where(low, *dk))
            vs.append(jnp.where(low, *dv))
        out_rows.append([jnp.concatenate(a, 1).astype(BF16) for a in (qs, ks, vs)])
    dq, dk, dv = [jnp.concatenate([o[i] for o in out_rows], 0) for i in range(3)]
    g_q, g_k, g_v = tn(attn_in, dq), tn(attn_in, dk), tn(attn_in, dv)
    ig = nt(dq, wq) + nt(dk, wk) + nt(dv, wv)
    inp = res + norm_back(ig, xhat1, inv1, gain1)
    row_grads = (
        rsum(ig * xhat1), rsum(mg * xhat2), rsum(ig), rsum(res), rsum(mg), rsum(masked),
        rsum(dq), rsum(dv), rsum(up_grad),
    )
    return inp, (g_q, g_k, g_v, g_out, g_up, g_down), row_grads


def shards(tokens, image_counts, cotangent, norm_gains, row_biases, qkv_weight, qv_bias, out_weight,
           up_weight, up_bias, down_weight):
    sec = lax.axis_index("section")
    dp = lax.axis_index("dp")
    ten = lax.axis_index("tensor")
    n_dp = lax.axis_size("dp")
    m = n_dp // 2
    zi, yi = dp // 2, dp % 2
    local_rows, width = tokens.shape[1:]
    images = local_rows * n_dp // IMG_LEN
    piece = width // n_dp
    heads = qkv_weight.shape[3]
    ff = up_weight.shape[2]
    cols = 4 * heads + 2 * ff
    full = cols + MISC

    def pt(a):
        return lax.ppermute(a, "tensor", [(0, 1), (1, 0)])

    def px(a):
        return lax.ppermute(a, "section", [(0, 1), (1, 0)])

    def py(a):
        return lax.ppermute(a, "dp", [(i, i ^ 1) for i in range(n_dp)])

    def pz(a, k):
        return lax.ppermute(a, "dp", [(2 * z + y, 2 * ((z + k) % m) + y) for z in range(m) for y in range(2)])

    batch_tokens = lax.dynamic_index_in_dim(tokens, sec, 0, keepdims=False)
    batch_cot = lax.dynamic_index_in_dim(cotangent, sec, 0, keepdims=False)
    count = lax.dynamic_index_in_dim(image_counts, sec, 0, keepdims=False)
    first = jnp.minimum((dp * local_rows + IMG_LEN - 1) // IMG_LEN, images)
    last = jnp.minimum(((dp + 1) * local_rows + IMG_LEN - 1) // IMG_LEN, images)
    held = last - first
    slots = -(-(-(-local_rows // IMG_LEN)) // 2)
    lower = held // 2
    own_first = jnp.where(ten == 0, first, first + lower)
    own_count = jnp.where(ten == 0, lower, held - lower)
    total = slots * IMG_PAD
    row = lax.broadcasted_iota(jnp.int32, (total, 1), 0)
    slot, inside = row // IMG_PAD, row % IMG_PAD
    exists = (inside < IMG_LEN) & (slot < own_count)
    valid = (exists & (own_first + slot < count)).astype(F32)
    target = (own_first + slot) * IMG_LEN + inside - dp * local_rows
    canvas_rows = local_rows + IMG_PAD
    select = ((lax.broadcasted_iota(jnp.int32, (total, canvas_rows), 1) == target) & exists).astype(BF16)

    both = jnp.stack([batch_tokens, batch_cot])
    halo = lax.ppermute(both[:, :IMG_PAD], "dp", [(i + 1, i) for i in range(n_dp - 1)])
    both = jnp.concatenate([both, halo], 1)
    x0 = nn(select, both[0])
    cot = nn(select, both[1])

    extra = jnp.concatenate([qv_bias[0].reshape(-1), up_bias[0]])
    extra = extra.reshape(-1, width)
    extra = lax.dynamic_slice_in_dim(extra, dp * piece, piece, 1)
    misc = jnp.concatenate([norm_gains[0], row_biases[0], extra], 0)
    misc = jnp.pad(misc, ((0, MISC - misc.shape[0]), (0, 0))).T
    own = jnp.concatenate(
        [qkv_weight[0].reshape(piece, 3 * heads), out_weight[0].T, up_weight[0], down_weight[0].T, misc], 1
    )
    ring = jnp.stack([own] + [pz(own, k) for k in range(1, m)])
    ring = ring[::-1]
    quad = lax.dynamic_slice_in_dim(jnp.concatenate([ring, ring]), m - 1 - zi, m, 0)
    half = full // 256 * 128
    qx, qy = px(quad), py(quad)
    qd = jnp.concatenate([px(qy[..., :half]), py(qx[..., half:])], -1)

    def order(flag, a, b, axis):
        return jnp.where(flag == 0, jnp.stack([a, b], axis), jnp.stack([b, a], axis))

    mine = order(yi, quad, qy, 1)
    other = order(yi, qx, qd, 1)
    layers = order(sec, mine, other, 0)
    theirs = pt(layers)
    layers = order(ten, layers, theirs, 1).reshape(2, 2, width, full)

    def unpack(l):
        a = layers[l]

        def part(lo, size):
            return jnp.concatenate([a[0, :, lo:lo + size], a[1, :, lo:lo + size]], 1)

        w = [part(i * heads, heads) for i in range(4)] + [part(4 * heads, ff), part(4 * heads + ff, ff)]
        ext = a[:, :, cols:].swapaxes(1, 2).astype(F32)
        rows = [ext[0, i:i + 1] for i in range(6)]
        n_ext = (2 * heads + ff) // width
        tail = ext[:, 6:6 + n_ext].reshape(2, -1)
        rows.append(tail[:, :heads].reshape(1, -1))
        rows.append(tail[:, heads:2 * heads].reshape(1, -1))
        rows.append(tail[:, 2 * heads:].reshape(1, -1))
        return w, rows

    w0, r0 = unpack(0)
    w1, r1 = unpack(1)
    out0, kept0 = layer_fwd(x0, w0, r0)
    low0 = (out0 * valid).astype(BF16)
    out1, kept1 = layer_fwd(low0.astype(F32), w1, r1)
    low1 = (out1 * valid).astype(BF16)
    in1, g1, rg1 = layer_bwd(cot * valid, w1, r1, kept1)
    in0, g0, rg0 = layer_bwd(in1 * valid, w0, r0, kept0)

    def pack(g, rg):
        by_core = []
        small = jnp.concatenate(rg[:6], 0)
        small = jnp.pad(small, ((0, MISC - 6), (0, 0))).T
        for t in range(2):
            parts = [a[:, t * heads:(t + 1) * heads] for a in g[:4]]
            parts += [a[:, t * ff:(t + 1) * ff] for a in g[4:]]
            by_core.append(jnp.concatenate(parts + [small], 1).astype(BF16))
        return jnp.stack(by_core)

    def pack_rows(rg):
        return jnp.stack([
            jnp.concatenate([rg[6][0, t * heads:(t + 1) * heads], rg[7][0, t * heads:(t + 1) * heads],
                             rg[8][0, t * ff:(t + 1) * ff]]) for t in range(2)])

    def pick(a, i, axis):
        return lax.dynamic_index_in_dim(a, i, axis, keepdims=False)

    def plus(a, b):
        return (a.astype(F32) + b.astype(F32)).astype(BF16)

    grads = jnp.stack([pack(g0, rg0), pack(g1, rg1)]).reshape(2, 2, m, 2, piece, full)
    grads = plus(pick(grads, ten, 1), pt(pick(grads, 1 - ten, 1)))
    near, far = pick(grads, sec, 0), pick(grads, 1 - sec, 0)
    g_own, g_y = pick(near, yi, 1), pick(near, 1 - yi, 1)
    g_x, g_d = pick(far, yi, 1), pick(far, 1 - yi, 1)
    via_x, via_y = px(g_d[..., :half]), py(g_d[..., half:])
    g_y = jnp.concatenate([plus(g_y[..., :half], via_x), g_y[..., half:]], -1)
    g_x = jnp.concatenate([g_x[..., :half], plus(g_x[..., half:], via_y)], -1)
    g_own = g_own.astype(F32) + px(g_x).astype(F32) + py(g_y).astype(F32)
    g_low = g_own.astype(BF16)
    final = pick(g_own, zi, 0)
    for k in range(1, m):
        final = final + pz(pick(g_low, (zi + k) % m, 0), k).astype(F32)

    small = jnp.stack([pack_rows(rg0), pack_rows(rg1)])
    small = pick(small, ten, 1) + pt(pick(small, 1 - ten, 1))
    small = pick(small, sec, 0) + px(pick(small, 1 - sec, 0))
    small = small + py(small)
    small = sum([pz(small, k) for k in range(1, m)], small)

    def settle(a):
        canvas = tn(select, a.astype(BF16)).astype(BF16)
        return canvas

    def gathered(a):
        a = a + pt(a)
        spill = lax.ppermute(a[..., local_rows:, :], "dp", [(i, i + 1) for i in range(n_dp - 1)])
        return jnp.concatenate([a[..., :IMG_PAD, :] + spill, a[..., IMG_PAD:local_rows, :]], -2)

    def exchange(a0, a1):
        keep = jnp.where(sec == 0, a0, a1)
        got = px(jnp.where(sec == 0, a1, a0))
        return jnp.where(sec == 0, jnp.stack([keep, got]), jnp.stack([got, keep]))

    block = gathered(jnp.stack([settle(low0), settle(low1), settle(in0), settle(in1)]))
    moved = exchange(block[0::2], block[1::2])
    layer_outputs = moved[:, 0][None]
    input_grads = moved[:, 1].astype(F32)[None]

    g_gain = final[:, cols:cols + 2].T[None]
    g_bias = final[:, cols + 2:cols + 6].T[None]
    return (
        layer_outputs,
        input_grads,
        g_gain,
        g_bias,
        final[:, :3 * heads].reshape(1, piece, 3, heads),
        small[:2 * heads].reshape(1, 2, heads),
        final[:, 3 * heads:4 * heads].T[None],
        final[:, 4 * heads:4 * heads + ff][None],
        small[2 * heads:][None],
        final[:, 4 * heads + ff:cols].T[None],
    )


def solution(mesh):
    in_specs = (
        P(None, "dp", None),
        P(),
        P(None, "dp", None),
        P("section", None, "dp"),
        P("section", None, "dp"),
        P("section", "dp", None, "tensor"),
        P("section", None, "tensor"),
        P("section", "tensor", "dp"),
        P("section", "dp", "tensor"),
        P("section", "tensor"),
        P("section", "tensor", "dp"),
    )
    out_specs = (
        P("section", None, "dp", None),
        P("section", None, "dp", None),
        P("section", None, "dp"),
        P("section", None, "dp"),
        P("section", "dp", None, "tensor"),
        P("section", None, "tensor"),
        P("section", "tensor", "dp"),
        P("section", "dp", "tensor"),
        P("section", "tensor"),
        P("section", "tensor", "dp"),
    )
    return jax.shard_map(shards, mesh=mesh, in_specs=in_specs, out_specs=out_specs, check_vma=False)
```

```python
import math

import jax
import jax.numpy as jnp
from jax import lax
from jax.experimental import pallas as pl
from jax.experimental.pallas import tpu as pltpu
from jax.sharding import PartitionSpec as P

IMG_LEN = 197
IMG_PAD = 208
HD = 64
EPSILON = 1e-06
NEGATIVE = -1e30
F32 = jnp.float32
BF16 = jnp.bfloat16
BLOCK = 128
HALF = 1280
SCALE = 1.0 / math.sqrt(HD)


def mm(a, b, dims):
    return lax.dot_general(a, b, (dims, ((), ())), preferred_element_type=F32)


def nn(a, b):
    return mm(a, b, ((1,), (0,)))


def nt(a, b):
    return mm(a, b, ((1,), (1,)))


def tn(a, b):
    return mm(a, b, ((0,), (0,)))


def normed(x):
    centred = x - jnp.mean(x, -1, keepdims=True)
    inverse = lax.rsqrt(jnp.mean(centred * centred, -1, keepdims=True) + EPSILON)
    return centred * inverse, inverse


def norm_back(grad, xhat, inverse, gain):
    t = grad * gain
    return inverse * (
        t - jnp.mean(t, -1, keepdims=True) - xhat * jnp.mean(t * xhat, -1, keepdims=True)
    )


def gelu_parts(u):
    cdf = 0.5 * (1.0 + lax.erf(u * math.sqrt(0.5)))
    pdf = jnp.exp(-0.5 * u * u) * (1.0 / math.sqrt(2.0 * math.pi))
    return u * cdf, cdf + u * pdf


ATT = 640
OUT = 512
MISC = 768
UP0 = 896
DOWN = 384
ROWSB = 1152
CHUNK = 384


def up_at(w, t, j):
    return w[t, 0, :, UP0:] if j == 0 else w[t, 1, :, :CHUNK]


def down_at(w, t, j):
    return w[t, 1, :, DOWN + j * CHUNK:DOWN + (j + 1) * CHUNK]


def low_lanes():
    return lax.broadcasted_iota(jnp.int32, (1, BLOCK), 1) < HD


def turn(a):
    return jnp.concatenate([a[:, HD:], a[:, :HD]], 1)


def valid_rows(sc, n):
    row = lax.broadcasted_iota(jnp.int32, (IMG_PAD, 1), 0)
    return jnp.where((row < IMG_LEN) & (n < sc[0]), 1.0, 0.0)


def image_rows(n):
    return pl.ds(pl.multiple_of(n * IMG_PAD, 16), IMG_PAD)


def forward_image(n, sc, x_ref, w, vec, brow, out_ref, kept):
    r = image_rows(n)
    x = x_ref[r, :].astype(F32)
    xhat, inv = normed(x)
    attn_in = (xhat * vec[0:1, :] + vec[2:3, :]).astype(BF16)
    kept["xh1"][r, :] = xhat
    kept["inv1"][r, :] = jnp.broadcast_to(inv, (IMG_PAD, BLOCK))
    kept["ain"][r, :] = attn_in
    residual = x + vec[3:4, :]
    low = low_lanes()
    lane = lax.broadcasted_iota(jnp.int32, (1, ATT), 1)
    factor = jnp.where(lane < 192, SCALE, jnp.where(lane < 576, 1.0, 0.0))
    real = lax.broadcasted_iota(jnp.int32, (1, IMG_PAD), 1) < IMG_LEN
    for t in range(2):
        bias = jnp.concatenate([brow[t, i:i + 1, :] for i in range(5)], 1)
        p = ((nn(attn_in, w[t, 0, :, :ATT]) + bias) * factor).astype(BF16)
        kept["qkv"][t, r, :] = p
        q, qk, k, v, vx = [p[:, i * BLOCK:(i + 1) * BLOCK] for i in range(5)]
        kq, xv = turn(qk), turn(vx)
        outs = []
        for i, (qq, kk, vv) in enumerate(
                [(jnp.where(low, q, 0), k, v), (jnp.where(low, 0, q), k, v), (jnp.where(low, qk, 0), kq, xv)]):
            s = jnp.where(real, nt(qq, kk), NEGATIVE)
            e = jnp.exp(s - jnp.max(s, -1, keepdims=True))
            pr = (e * (1.0 / jnp.sum(e, -1, keepdims=True))).astype(BF16)
            kept["pr"][n * 6 + t * 3 + i] = pr
            outs.append(nn(pr, vv))
        mixed = jnp.concatenate([outs[2], jnp.where(low, outs[0], outs[1])], 1).astype(BF16)
        kept["mx"][t, r, :] = mixed
        residual = residual + nt(mixed, w[t, 0, :, OUT:MISC])
    xhat, inv = normed(residual)
    mlp_in = (xhat * vec[1:2, :] + vec[4:5, :]).astype(BF16)
    kept["xh2"][r, :] = xhat
    kept["inv2"][r, :] = jnp.broadcast_to(inv, (IMG_PAD, BLOCK))
    kept["min"][r, :] = mlp_in
    out = residual + vec[5:6, :]
    for t in range(2):
        for j in range(2):
            bias = jnp.concatenate([brow[t, 5 + j * 3 + i:6 + j * 3 + i, :] for i in range(3)], 1)
            hidden, slope = gelu_parts(nn(mlp_in, up_at(w, t, j)) + bias)
            c = slice((t * 2 + j) * CHUNK, (t * 2 + j + 1) * CHUNK)
            hidden = hidden.astype(BF16)
            kept["hd"][r, c] = hidden
            kept["sl"][r, c] = slope.astype(BF16)
            out = out + nt(hidden, down_at(w, t, j))
    out_ref[r, :] = (out * valid_rows(sc, n)).astype(BF16)


def backward_image(n, sc, u_ref, w, vec, in_ref, kept, grad, sums, bsum):
    r = image_rows(n)

    def rsum(a):
        return jnp.sum(a, 0, keepdims=True)

    masked = u_ref[r, :].astype(F32) * valid_rows(sc, n)
    sums[5:6, :] += rsum(masked)
    dg = masked.astype(BF16)
    grad["dg"][r, :] = dg
    mg = jnp.zeros(masked.shape, F32)
    for t in range(2):
        for j in range(2):
            c = slice((t * 2 + j) * CHUNK, (t * 2 + j + 1) * CHUNK)
            up = nn(dg, down_at(w, t, j)) * kept["sl"][r, c].astype(F32)
            up = up.astype(BF16)
            grad["up"][r, c] = up
            total = rsum(up.astype(F32))
            for i in range(3):
                bsum[t, 5 + j * 3 + i:6 + j * 3 + i, :] += total[:, i * BLOCK:(i + 1) * BLOCK]
            mg = mg + nt(up, up_at(w, t, j))
    xhat = kept["xh2"][r, :]
    sums[4:5, :] += rsum(mg)
    sums[1:2, :] += rsum(mg * xhat)
    res = masked + norm_back(mg, xhat, kept["inv2"][r, :1], vec[1:2, :])
    sums[3:4, :] += rsum(res)
    ag = res.astype(BF16)
    grad["ag"][r, :] = ag
    low = low_lanes()
    ig = jnp.zeros(masked.shape, F32)
    for t in range(2):
        xg = nn(ag, w[t, 0, :, OUT:MISC]).astype(BF16)
        gx = jnp.where(low, 0, xg[:, :BLOCK])
        g = xg[:, BLOCK:]
        p = kept["qkv"][t, r, :]
        q, qk, k, v, vx = [p[:, i * BLOCK:(i + 1) * BLOCK] for i in range(5)]
        kq, xv = turn(qk), turn(vx)
        dq, dk, dv = [], [], []
        for i, (qq, kk, vv, gm, gg) in enumerate(
                [(q, k, v, jnp.where(low, g, 0), g), (q, k, v, jnp.where(low, 0, g), g), (qk, kq, xv, gx, turn(gx))]):
            pb = kept["pr"][n * 6 + t * 3 + i]
            pf = pb.astype(F32)
            dp = nt(gm, vv)
            ds = (pf * (dp - jnp.sum(pf * dp, -1, keepdims=True))).astype(BF16)
            dv.append(tn(pb, gg))
            dq.append(nn(ds, kk) * SCALE)
            dk.append(tn(ds, kq if i == 2 else qq))
        blocks = [
            jnp.where(low, dq[0], dq[1]), jnp.where(low, dq[2], dk[2]), jnp.where(low, dk[0], dk[1]),
            jnp.where(low, dv[0], dv[1]), dv[2],
        ]
        d = jnp.concatenate(blocks, 1).astype(BF16)
        grad["qkv"][t, r, :] = d
        total = rsum(d.astype(F32))
        for i in range(5):
            bsum[t, i:i + 1, :] += total[:, i * BLOCK:(i + 1) * BLOCK]
        ig = ig + nt(d, w[t, 0, :, :ATT])
    xhat = kept["xh1"][r, :]
    sums[2:3, :] += rsum(ig)
    sums[0:1, :] += rsum(ig * xhat)
    in_ref[r, :] = res + norm_back(ig, xhat, kept["inv1"][r, :1], vec[0:1, :])


def weight_grads(t, piece, kept, grad, small, bsum, g):
    width = small.shape[0]
    ag, dg = grad["ag"][...], grad["dg"][...]
    ain, mlp_in = kept["ain"][...], kept["min"][...]
    high = jnp.where(low_lanes(), 0.0, 1.0)
    d = grad["qkv"][t]
    g[t, 0, :, :OUT] = tn(ain, d[:, :OUT]).astype(BF16)
    out = tn(ag, kept["mx"][t])
    g[t, 0, :, OUT:ATT] = (tn(ain, d[:, OUT:]) + out[:, :BLOCK] * high).astype(BF16)
    g[t, 0, :, ATT:MISC] = out[:, BLOCK:].astype(BF16)
    g[t, 0, :, MISC:UP0] = small
    for j in range(2):
        c = pl.ds(pl.multiple_of((t * 2 + j) * CHUNK, BLOCK), CHUNK)
        up = tn(mlp_in, grad["up"][:, c]).astype(BF16)
        if j == 0:
            g[t, 0, :, UP0:] = up
        else:
            g[t, 1, :, :CHUNK] = up
        g[t, 1, :, DOWN + j * CHUNK:DOWN + (j + 1) * CHUNK] = tn(dg, kept["hd"][:, c]).astype(BF16)
    if piece % 16 == 0:
        rows = jnp.concatenate([bsum[t], jnp.zeros((piece - 16, BLOCK), F32)], 0).astype(BF16)
        for i in range(width // piece):
            g[t, 1, i * piece:(i + 1) * piece, ROWSB:] = rows


KEPT = ("xh1", "inv1", "ain", "qkv", "pr", "mx", "xh2", "inv2", "min", "sl", "hd")


def kept_shapes(total, width, ff):
    images = total // IMG_PAD
    return dict(
        xh1=((total, width), F32), inv1=((total, BLOCK), F32), ain=((total, width), BF16), qkv=((2, total, ATT), BF16),
        pr=((images * 6, IMG_PAD, IMG_PAD), BF16), mx=((2, total, 2 * BLOCK), BF16), xh2=((total, width), F32),
        inv2=((total, BLOCK), F32), min=((total, width), BF16), sl=((total, ff), BF16), hd=((total, ff), BF16))


def grad_shapes(total, width, ff):
    return dict(dg=((total, width), BF16), up=((total, ff), BF16), ag=((total, width), BF16),
                qkv=((2, total, ATT), BF16))


def layer_call(sources, load, store, out_shapes, scalars, x, u, kept_in, ff, piece):
    forward, backward = x is not None, u is not None
    total, width = (x if forward else u).shape
    ks = kept_shapes(total, width, ff)
    gs = grad_shapes(total, width, ff)
    vmem = pl.BlockSpec(memory_space=pltpu.VMEM)
    anywhere = pl.BlockSpec(memory_space=pl.ANY)
    ins, in_specs = [scalars], [pl.BlockSpec(memory_space=pltpu.SMEM)]
    outs, out_specs = [], []
    keep_out = forward and not backward
    keep_in = backward and not forward
    for a in (x, u):
        if a is not None:
            ins.append(a)
            in_specs.append(vmem)
    if keep_in:
        ins += [kept_in[k] for k in KEPT]
        in_specs += [vmem] * len(KEPT)
    ins += sources
    in_specs += [anywhere] * len(sources)
    if forward:
        outs.append(((total, width), BF16))
        out_specs.append(vmem)
    if backward:
        outs += [((total, width), F32), ((2, 16, BLOCK), F32)] + out_shapes
        out_specs += [vmem, vmem] + [anywhere] * len(out_shapes)
    if keep_out:
        outs += [ks[k] for k in KEPT]
        out_specs += [vmem] * len(KEPT)
    scratch = [pltpu.VMEM((2, 2, width, HALF), BF16), pltpu.VMEM((8, width), F32), pltpu.VMEM((2, 16, BLOCK), F32),
               pltpu.SemaphoreType.DMA]
    if backward:
        scratch += [pltpu.VMEM(*gs[k]) for k in gs]
        scratch += [pltpu.VMEM((8, width), F32), pltpu.VMEM((2, 2, width, HALF), BF16)]
    if forward and backward:
        scratch += [pltpu.VMEM(*ks[k]) for k in KEPT]

    def body(*refs):
        refs = list(refs)

        def take(n):
            got = refs[:n]
            del refs[:n]
            return got

        sc = take(1)[0]
        x_ref = take(1)[0] if forward else None
        u_ref = take(1)[0] if backward else None
        if keep_in:
            kept = dict(zip(KEPT, take(len(KEPT))))
        src = take(len(sources))
        if forward:
            out_ref = take(1)[0]
        if backward:
            in_ref, bsum = take(2)
            dst = take(len(out_shapes))
        if keep_out:
            kept = dict(zip(KEPT, take(len(KEPT))))
        w, vec, brow, sem = take(4)
        if backward:
            grad = dict(zip(gs, take(len(gs))))
            sums, g = take(2)
        if forward and backward:
            kept = dict(zip(KEPT, take(len(KEPT))))
        copies = load(sc, src, w, sem)
        for c in copies:
            c.start()
        for c in copies:
            c.wait()
        vec[...] = w[0, 0, :, MISC:UP0].astype(F32).T[:8, :]
        for t in range(2):
            brow[t] = w[t, 1, :16, ROWSB:].astype(F32)
        if forward:
            def step(n, carry):
                forward_image(n, sc, x_ref, w, vec, brow, out_ref, kept)
                return carry
            lax.fori_loop(0, total // IMG_PAD, step, 0)
        if backward:
            sums[...] = jnp.zeros_like(sums)
            bsum[...] = jnp.zeros_like(bsum)

            def back(n, carry):
                backward_image(n, sc, u_ref, w, vec, in_ref, kept, grad, sums, bsum)
                return carry
            lax.fori_loop(0, total // IMG_PAD, back, 0)
            small = jnp.concatenate([sums[...], jnp.zeros((BLOCK - 8, width), F32)], 0).T.astype(BF16)
            copies = []
            for side in range(2):
                t = jnp.where(sc[1] == 0, 1 - side, side)
                weight_grads(t, piece, kept, grad, small, bsum, g)
                out = store(sc, side, t, g, dst, sem)
                for c in out:
                    c.start()
                copies += out
            for c in copies:
                c.wait()

    got = pl.pallas_call(
        body,
        out_shape=[jax.ShapeDtypeStruct(*o) for o in outs],
        in_specs=in_specs,
        out_specs=out_specs,
        scratch_shapes=scratch,
        compiler_params=pltpu.CompilerParams(vmem_limit_bytes=56 * 2 ** 20),
    )(*ins)
    got = list(got)
    res = {}
    if forward:
        res["out"] = got.pop(0)
    if backward:
        res["in"], res["bias"] = got[:2]
        res["g"] = got[2:2 + len(out_shapes)]
        del got[:2 + len(out_shapes)]
    if keep_out:
        res["kept"] = dict(zip(KEPT, got))
    return res


def shards(tokens, image_counts, cotangent, norm_gains, row_biases, qkv_weight, qv_bias, out_weight,
           up_weight, up_bias, down_weight):
    sec = lax.axis_index("section")
    dp = lax.axis_index("dp")
    ten = lax.axis_index("tensor")
    n_dp = lax.axis_size("dp")
    m = n_dp // 2
    zi, yi = dp // 2, dp % 2
    local_rows, width = tokens.shape[1:]
    images = local_rows * n_dp // IMG_LEN
    piece = width // n_dp
    ff = 2 * up_weight.shape[2]
    direct = piece % 16 == 0

    def pt(a):
        return lax.ppermute(a, "tensor", [(0, 1), (1, 0)])

    def px(a):
        return lax.ppermute(a, "section", [(0, 1), (1, 0)])

    def py(a):
        return lax.ppermute(a, "dp", [(i, i ^ 1) for i in range(n_dp)])

    def pd(a):
        return lax.ppermute(a, ("section", "dp"), [(i, (i + n_dp) % (2 * n_dp) ^ 1) for i in range(2 * n_dp)])

    def pz(a, k):
        return lax.ppermute(a, "dp", [(2 * z + y, 2 * ((z + k) % m) + y) for z in range(m) for y in range(2)])

    def plus(*a):
        return sum(b.astype(F32) for b in a)

    batch_tokens = lax.dynamic_index_in_dim(tokens, sec, 0, keepdims=False)
    batch_cot = lax.dynamic_index_in_dim(cotangent, sec, 0, keepdims=False)
    count = lax.dynamic_index_in_dim(image_counts, sec, 0, keepdims=False)
    first = jnp.minimum((dp * local_rows + IMG_LEN - 1) // IMG_LEN, images)
    last = jnp.minimum(((dp + 1) * local_rows + IMG_LEN - 1) // IMG_LEN, images)
    held = last - first
    slots = -(-(-(-local_rows // IMG_LEN)) // 2)
    lower = held // 2
    own_first = jnp.where(ten == 0, first, first + lower)
    own_count = jnp.where(ten == 0, lower, held - lower)
    total = slots * IMG_PAD
    row = lax.broadcasted_iota(jnp.int32, (total, 1), 0)
    slot, inside = row // IMG_PAD, row % IMG_PAD
    exists = (inside < IMG_LEN) & (slot < own_count)
    target = (own_first + slot) * IMG_LEN + inside - dp * local_rows
    canvas_rows = local_rows + IMG_PAD
    select = ((lax.broadcasted_iota(jnp.int32, (total, canvas_rows), 1) == target) & exists).astype(BF16)
    scalars = jnp.stack([jnp.minimum(own_count, jnp.maximum(count - own_first, 0)), ten, sec, zi, yi]).astype(jnp.int32)

    both = jnp.stack([batch_tokens, batch_cot])
    halo = lax.ppermute(both[:, :IMG_PAD], "dp", [(i + 1, i) for i in range(n_dp - 1)])
    both = jnp.concatenate([both, halo], 1)
    x0 = nn(select, both[0]).astype(BF16)
    cot = nn(select, both[1]).astype(BF16)

    q, k, v = [[qkv_weight[0, :, i, h * HD:(h + 1) * HD] for h in range(3)] for i in range(3)]
    o = out_weight[0].T
    o = [o[:, h * HD:(h + 1) * HD] for h in range(3)]
    misc = jnp.concatenate([norm_gains[0], row_biases[0]], 0).T
    misc = jnp.pad(misc, ((0, 0), (0, BLOCK - misc.shape[1])))
    gap = jnp.zeros((HD,), BF16)
    rows = jnp.concatenate([qv_bias[0, 0], gap, gap, gap, qv_bias[0, 1], gap, up_bias[0]]).reshape(-1, BLOCK)
    rows = jnp.pad(rows, ((0, piece - rows.shape[0]), (0, 0)))
    up, down = up_weight[0], down_weight[0].T
    part0 = jnp.concatenate(
        [q[0], q[1], q[2], k[2], k[0], k[1], v[0], v[1], v[2], o[2], o[0], o[1], misc, up[:, :CHUNK]], 1)
    part1 = jnp.concatenate([up[:, CHUNK:], down, rows], 1)

    if direct:
        keep = jnp.where(sec == 0, part0, part1)
        give = jnp.where(sec == 0, part1, part0)
        got = px(give)
        start = [jnp.where(sec == 0, keep, got), jnp.where(sec == 0, got, keep)]
        half = HALF // 2

        def load(sc, src, w, sem):
            copies = []
            for side in range(2):
                t = jnp.where(sc[1] == 0, side, 1 - side)
                quad, qx, qy, qd0, qd1 = src[side * 5:side * 5 + 5]
                for kk in range(m):
                    z = lax.rem(sc[3] - kk + m, m)
                    near = pl.ds(pl.multiple_of((2 * z + sc[4]) * piece, 16), piece)
                    far = pl.ds(pl.multiple_of((2 * z + 1 - sc[4]) * piece, 16), piece)
                    for a, h, r, c in (
                            (quad, sc[2], near, slice(0, HALF)), (qx, 1 - sc[2], near, slice(0, HALF)),
                            (qy, sc[2], far, slice(0, HALF)), (qd0, 1 - sc[2], far, slice(0, half)),
                            (qd1, 1 - sc[2], far, slice(half, HALF))):
                        copies.append(pltpu.make_async_copy(a.at[kk], w.at[t, h, r, c], sem))
            return copies

        def store(sc, side, t, g, dst, sem):
            copies = []
            for hr in range(2):
                h = jnp.where(sc[2] == 0, hr, 1 - hr)
                for yr in range(2):
                    y = jnp.where(sc[4] == 0, yr, 1 - yr)
                    for kk in range(m):
                        z = lax.rem(sc[3] + kk, m)
                        r = pl.ds(pl.multiple_of((2 * z + y) * piece, 16), piece)
                        out = dst[0].at[hr, yr, kk] if side == 0 else dst[1 + hr * 2 + yr].at[kk]
                        copies.append(pltpu.make_async_copy(g.at[t, h, r, :], out, sem))
            return copies

        out_shapes = [((2, 2, m, piece, HALF), BF16)] + [((m, piece, HALF), BF16)] * 4

        def spread(a):
            quad = jnp.stack([a] + [pz(a, kk) for kk in range(1, m)])
            qx, qy = px(quad), py(quad)
            qd0, qd1 = px(qy[..., :half]), py(qx[..., half:])
            mine = [quad, qx, qy, qd0, qd1]
            return mine + [pt(b) for b in mine]

        sources = [spread(a) for a in start]
    else:
        def load(sc, src, w, sem):
            return [pltpu.make_async_copy(src[0], w, sem)]

        def store(sc, side, t, g, dst, sem):
            return [pltpu.make_async_copy(g.at[t], dst[0].at[t], sem)]

        out_shapes = [((2, 2, width, HALF), BF16)]
        a = lax.all_gather(jnp.stack([part0, part1]), "dp", axis=1, tiled=True)
        a = lax.all_gather(lax.all_gather(a, "tensor"), "section")
        sources = [[a[0]], [a[1]]]

    def call(l, x, u, kept):
        return layer_call(sources[l], load, store, out_shapes, scalars, x, u, kept, ff, piece)

    r0 = call(0, x0, None, None)
    r1 = call(1, r0["out"], cot, None)
    b0 = call(0, None, r1["in"], r0["kept"])

    if direct:
        def gather_in(g):
            theirs, keep, to_y, to_x, to_d = g
            got = pt(theirs)
            to_y = plus(to_y, got[0, 1]).astype(BF16)
            to_x = plus(to_x, got[1, 0]).astype(BF16)
            to_d = plus(to_d, got[1, 1]).astype(BF16)
            quad = plus(keep, got[0, 0], py(to_y), px(to_x), pd(to_d))
            low = quad.astype(BF16)
            return plus(quad[0], *[pz(low[kk], kk) for kk in range(1, m)])

        done = [gather_in(r1["g"]), gather_in(b0["g"])]
        mine = jnp.where(sec == 0, done[1], done[0])
        other = px(jnp.where(sec == 0, done[0], done[1]).astype(BF16)).astype(F32)
        final0 = jnp.where(sec == 0, mine, other)
        final1 = jnp.where(sec == 0, other, mine)
        small = final1[:, ROWSB:]
    else:
        g = jnp.stack([b0["g"][0], r1["g"][0]])
        g = lax.psum_scatter(g.astype(F32), "section", scatter_dimension=0)
        g = lax.psum_scatter(g, "tensor", scatter_dimension=0)
        g = lax.psum_scatter(g, "dp", scatter_dimension=1, tiled=True)
        final0, final1 = g[0], g[1]
        small = lax.psum(jnp.stack([b0["bias"], r1["bias"]]), ("section", "tensor", "dp"))
        small = lax.dynamic_index_in_dim(lax.dynamic_index_in_dim(small, sec, 0, False), ten, 0, False)

    def settled(a0, a1):
        keep = jnp.where(sec == 0, a0, a1)
        got = px(jnp.where(sec == 0, a1, a0))
        a = jnp.where(sec == 0, jnp.stack([keep, got]), jnp.stack([got, keep]))
        a = jnp.stack([tn(select, a[0]), tn(select, a[1])]).astype(BF16)
        a = a + pt(a)
        spill = lax.ppermute(a[:, local_rows:], "dp", [(i, i + 1) for i in range(n_dp - 1)])
        return jnp.concatenate([a[:, :IMG_PAD] + spill, a[:, IMG_PAD:local_rows]], 1)

    layer_outputs = settled(r0["out"], r1["out"])[None]
    input_grads = settled(b0["in"].astype(BF16), r1["in"].astype(BF16)).astype(F32)[None]

    def heads(*starts):
        return [final0[:, s * HD:(s + 1) * HD] for s in starts]

    small = small.reshape(-1)
    qkv = jnp.concatenate(heads(0, 1, 2, 4, 5, 3, 6, 7, 8), 1).reshape(1, piece, 3, 3 * HD)
    return (
        layer_outputs,
        input_grads,
        final0[:, MISC:MISC + 2].T[None],
        final0[:, MISC + 2:MISC + 6].T[None],
        qkv,
        jnp.stack([small[:3 * HD], small[6 * HD:9 * HD]])[None],
        jnp.concatenate(heads(10, 11, 9), 1).T[None],
        jnp.concatenate([final0[:, UP0:], final1[:, :DOWN]], 1)[None],
        small[ATT:ATT + ff // 2][None],
        final1[:, DOWN:ROWSB].T[None],
    )


def solution(mesh):
    in_specs = (
        P(None, "dp", None),
        P(),
        P(None, "dp", None),
        P("section", None, "dp"),
        P("section", None, "dp"),
        P("section", "dp", None, "tensor"),
        P("section", None, "tensor"),
        P("section", "tensor", "dp"),
        P("section", "dp", "tensor"),
        P("section", "tensor"),
        P("section", "tensor", "dp"),
    )
    out_specs = (
        P("section", None, "dp", None),
        P("section", None, "dp", None),
        P("section", None, "dp"),
        P("section", None, "dp"),
        P("section", "dp", None, "tensor"),
        P("section", None, "tensor"),
        P("section", "tensor", "dp"),
        P("section", "dp", "tensor"),
        P("section", "tensor"),
        P("section", "tensor", "dp"),
    )
    return jax.shard_map(shards, mesh=mesh, in_specs=in_specs, out_specs=out_specs, check_vma=False)
```

```python
import math

import jax
import jax.numpy as jnp
from jax import lax
from jax.experimental import pallas as pl
from jax.experimental.pallas import tpu as pltpu
from jax.sharding import PartitionSpec as P

IMG_LEN = 197
IMG_PAD = 208
HD = 64
EPSILON = 1e-06
NEGATIVE = -1e30
F32 = jnp.float32
BF16 = jnp.bfloat16
BLOCK = 128
HALF = 1280
COST = 10 ** 10
SCALE = 1.0 / math.sqrt(HD)


def mm(a, b, dims):
    return lax.dot_general(a, b, (dims, ((), ())), preferred_element_type=F32)


def nn(a, b):
    return mm(a, b, ((1,), (0,)))


def nt(a, b):
    return mm(a, b, ((1,), (1,)))


def tn(a, b):
    return mm(a, b, ((0,), (0,)))


def normed(x):
    centred = x - jnp.mean(x, -1, keepdims=True)
    inverse = lax.rsqrt(jnp.mean(centred * centred, -1, keepdims=True) + EPSILON)
    return centred * inverse, inverse


def norm_back(grad, xhat, inverse, gain):
    t = grad * gain
    return inverse * (
        t - jnp.mean(t, -1, keepdims=True) - xhat * jnp.mean(t * xhat, -1, keepdims=True)
    )


def gelu_parts(u):
    cdf = 0.5 * (1.0 + lax.erf(u * math.sqrt(0.5)))
    pdf = jnp.exp(-0.5 * u * u) * (1.0 / math.sqrt(2.0 * math.pi))
    return u * cdf, cdf + u * pdf


ATT = 640
OUT = 512
MISC = 768
UP0 = 896
DOWN = 384
ROWSB = 1152
CHUNK = 384


def up_at(w, t, j):
    return w[t, 0, :, UP0:] if j == 0 else w[t, 1, :, :CHUNK]


def down_at(w, t, j):
    return w[t, 1, :, DOWN + j * CHUNK:DOWN + (j + 1) * CHUNK]


def low_lanes():
    return lax.broadcasted_iota(jnp.int32, (1, BLOCK), 1) < HD


def turn(a):
    return jnp.concatenate([a[:, HD:], a[:, :HD]], 1)


def valid_rows(sc, n):
    row = lax.broadcasted_iota(jnp.int32, (IMG_PAD, 1), 0)
    return jnp.where((row < IMG_LEN) & (n < sc[0]), 1.0, 0.0)


def image_rows(n):
    return pl.ds(pl.multiple_of(n * IMG_PAD, 16), IMG_PAD)


def forward_image(n, sc, x_ref, w, vec, brow, out_ref, kept):
    r = image_rows(n)
    x = x_ref[r, :].astype(F32)
    xhat, inv = normed(x)
    attn_in = (xhat * vec[0:1, :] + vec[2:3, :]).astype(BF16)
    kept["xh1"][r, :] = xhat
    kept["inv1"][r, :] = jnp.broadcast_to(inv, (IMG_PAD, BLOCK))
    kept["ain"][r, :] = attn_in
    residual = x + vec[3:4, :]
    low = low_lanes()
    lane = lax.broadcasted_iota(jnp.int32, (1, ATT), 1)
    factor = jnp.where(lane < 192, SCALE, jnp.where(lane < 576, 1.0, 0.0))
    real = lax.broadcasted_iota(jnp.int32, (1, IMG_PAD), 1) < IMG_LEN
    for t in range(2):
        bias = jnp.concatenate([brow[t, i:i + 1, :] for i in range(5)], 1)
        p = ((nn(attn_in, w[t, 0, :, :ATT]) + bias) * factor).astype(BF16)
        kept["qkv"][t, r, :] = p
        q, qk, k, v, vx = [p[:, i * BLOCK:(i + 1) * BLOCK] for i in range(5)]
        kq, xv = turn(qk), turn(vx)
        outs = []
        for i, (qq, kk, vv) in enumerate(
                [(jnp.where(low, q, 0), k, v), (jnp.where(low, 0, q), k, v), (jnp.where(low, qk, 0), kq, xv)]):
            s = jnp.where(real, nt(qq, kk), NEGATIVE)
            e = jnp.exp(s - jnp.max(s, -1, keepdims=True))
            pr = (e * (1.0 / jnp.sum(e, -1, keepdims=True))).astype(BF16)
            kept["pr"][n * 6 + t * 3 + i] = pr
            outs.append(nn(pr, vv))
        mixed = jnp.concatenate([outs[2], jnp.where(low, outs[0], outs[1])], 1).astype(BF16)
        kept["mx"][t, r, :] = mixed
        residual = residual + nt(mixed, w[t, 0, :, OUT:MISC])
    xhat, inv = normed(residual)
    mlp_in = (xhat * vec[1:2, :] + vec[4:5, :]).astype(BF16)
    kept["xh2"][r, :] = xhat
    kept["inv2"][r, :] = jnp.broadcast_to(inv, (IMG_PAD, BLOCK))
    kept["min"][r, :] = mlp_in
    out = residual + vec[5:6, :]
    for t in range(2):
        for j in range(2):
            bias = jnp.concatenate([brow[t, 5 + j * 3 + i:6 + j * 3 + i, :] for i in range(3)], 1)
            hidden, slope = gelu_parts(nn(mlp_in, up_at(w, t, j)) + bias)
            c = slice((t * 2 + j) * CHUNK, (t * 2 + j + 1) * CHUNK)
            hidden = hidden.astype(BF16)
            kept["hd"][r, c] = hidden
            kept["sl"][r, c] = slope.astype(BF16)
            out = out + nt(hidden, down_at(w, t, j))
    out_ref[r, :] = (out * valid_rows(sc, n)).astype(BF16)


def rsum(a):
    return jnp.sum(a, 0, keepdims=True)


def backward_mlp(n, sc, u_ref, w, vec, kept, grad, sums, bsum):
    r = image_rows(n)

    masked = u_ref[r, :].astype(F32) * valid_rows(sc, n)
    sums[5:6, :] += rsum(masked)
    dg = masked.astype(BF16)
    grad["dg"][r, :] = dg
    mg = jnp.zeros(masked.shape, F32)
    for t in range(2):
        for j in range(2):
            c = slice((t * 2 + j) * CHUNK, (t * 2 + j + 1) * CHUNK)
            up = nn(dg, down_at(w, t, j)) * kept["sl"][r, c].astype(F32)
            up = up.astype(BF16)
            grad["up"][r, c] = up
            total = rsum(up.astype(F32))
            for i in range(3):
                bsum[t, 5 + j * 3 + i:6 + j * 3 + i, :] += total[:, i * BLOCK:(i + 1) * BLOCK]
            mg = mg + nt(up, up_at(w, t, j))
    xhat = kept["xh2"][r, :]
    sums[4:5, :] += rsum(mg)
    sums[1:2, :] += rsum(mg * xhat)
    res = masked + norm_back(mg, xhat, kept["inv2"][r, :1], vec[1:2, :])
    sums[3:4, :] += rsum(res)
    grad["res"][r, :] = res


def backward_attention(n, w, vec, in_ref, kept, grad, sums, bsum):
    r = image_rows(n)
    res = grad["res"][r, :]
    ag = res.astype(BF16)
    grad["ag"][r, :] = ag
    low = low_lanes()
    ig = jnp.zeros(res.shape, F32)
    for t in range(2):
        xg = nn(ag, w[t, 0, :, OUT:MISC]).astype(BF16)
        gx = jnp.where(low, 0, xg[:, :BLOCK])
        g = xg[:, BLOCK:]
        p = kept["qkv"][t, r, :]
        q, qk, k, v, vx = [p[:, i * BLOCK:(i + 1) * BLOCK] for i in range(5)]
        kq, xv = turn(qk), turn(vx)
        dq, dk, dv = [], [], []
        for i, (qq, kk, vv, gm, gg) in enumerate(
                [(q, k, v, jnp.where(low, g, 0), g), (q, k, v, jnp.where(low, 0, g), g), (qk, kq, xv, gx, turn(gx))]):
            pb = kept["pr"][n * 6 + t * 3 + i]
            pf = pb.astype(F32)
            dp = nt(gm, vv)
            ds = (pf * (dp - jnp.sum(pf * dp, -1, keepdims=True))).astype(BF16)
            dv.append(tn(pb, gg))
            dq.append(nn(ds, kk) * SCALE)
            dk.append(tn(ds, kq if i == 2 else qq))
        blocks = [
            jnp.where(low, dq[0], dq[1]), jnp.where(low, dq[2], dk[2]), jnp.where(low, dk[0], dk[1]),
            jnp.where(low, dv[0], dv[1]), dv[2],
        ]
        d = jnp.concatenate(blocks, 1).astype(BF16)
        grad["dqkv"][t, r, :] = d
        total = rsum(d.astype(F32))
        for i in range(5):
            bsum[t, i:i + 1, :] += total[:, i * BLOCK:(i + 1) * BLOCK]
        ig = ig + nt(d, w[t, 0, :, :ATT])
    xhat = kept["xh1"][r, :]
    sums[2:3, :] += rsum(ig)
    sums[0:1, :] += rsum(ig * xhat)
    in_ref[r, :] = res + norm_back(ig, xhat, kept["inv1"][r, :1], vec[0:1, :])


def weight_grads(t, piece, kept, grad, small, bsum, g):
    width = small.shape[0]
    ag, dg = grad["ag"][...], grad["dg"][...]
    ain, mlp_in = kept["ain"][...], kept["min"][...]
    high = jnp.where(low_lanes(), 0.0, 1.0)
    d = grad["dqkv"][t]
    g[t, 0, :, :OUT] = tn(ain, d[:, :OUT]).astype(BF16)
    out = tn(ag, kept["mx"][t])
    g[t, 0, :, OUT:ATT] = (tn(ain, d[:, OUT:]) + out[:, :BLOCK] * high).astype(BF16)
    g[t, 0, :, ATT:MISC] = out[:, BLOCK:].astype(BF16)
    g[t, 0, :, MISC:UP0] = small
    for j in range(2):
        c = pl.ds(pl.multiple_of((t * 2 + j) * CHUNK, BLOCK), CHUNK)
        up = tn(mlp_in, grad["up"][:, c]).astype(BF16)
        if j == 0:
            g[t, 0, :, UP0:] = up
        else:
            g[t, 1, :, :CHUNK] = up
        g[t, 1, :, DOWN + j * CHUNK:DOWN + (j + 1) * CHUNK] = tn(dg, kept["hd"][:, c]).astype(BF16)
    if piece % 16 == 0:
        rows = jnp.concatenate([bsum[t], jnp.zeros((piece - 16, BLOCK), F32)], 0).astype(BF16)
        for i in range(width // piece):
            g[t, 1, i * piece:(i + 1) * piece, ROWSB:] = rows


def kept_shapes(total, width, ff):
    images = total // IMG_PAD
    return dict(
        xh1=((total, width), F32), inv1=((total, BLOCK), F32), ain=((total, width), BF16), qkv=((2, total, ATT), BF16),
        pr=((images * 6, IMG_PAD, IMG_PAD), BF16), mx=((2, total, 2 * BLOCK), BF16), xh2=((total, width), F32),
        inv2=((total, BLOCK), F32), min=((total, width), BF16), sl=((total, ff), BF16), hd=((total, ff), BF16))


def grad_shapes(total, width, ff):
    return dict(dg=((total, width), BF16), up=((total, ff), BF16), res=((total, width), F32), sums=((8, width), F32),
                bsum=((2, 16, BLOCK), F32))


def layer_call(phases, sources, load, store, out_shapes, scalars, given, total, width, ff, piece):
    ks = kept_shapes(total, width, ff)
    gs = grad_shapes(total, width, ff)
    need = {
        "forward": ["x"], "mlp": ["u", "sl", "xh2", "inv2"],
        "attention": list(gs) + ["ain", "qkv", "pr", "mx", "xh1", "inv1", "min", "hd"],
    }
    gives = {"forward": {"out": ((total, width), BF16), **ks}, "mlp": gs, "attention": {"in": ((total, width), F32)}}
    made = {}
    for p in phases:
        made.update(gives[p])
    inputs = [n for p in phases for n in need[p] if n not in made]
    inputs = list(dict.fromkeys(inputs))
    last = phases[-1]
    shown = {"forward": list(gives["forward"]), "mlp": list(gs), "attention": ["in"]}[last]
    if last != "forward" and "forward" in phases:
        shown = ["out"] + shown
    if last == "mlp" and "forward" in phases:
        shown += [n for n in ks if n in need["attention"]]
    inner = [n for n in made if n not in shown]
    end = last == "attention"
    vmem = pl.BlockSpec(memory_space=pltpu.VMEM)
    anywhere = pl.BlockSpec(memory_space=pl.ANY)
    ends = out_shapes if end else []
    scratch = [pltpu.VMEM((2, 2, width, HALF), BF16), pltpu.VMEM((8, width), F32), pltpu.VMEM((2, 16, BLOCK), F32),
               pltpu.SemaphoreType.DMA] + [pltpu.VMEM(*made[n]) for n in inner]
    if end:
        scratch += [pltpu.VMEM((total, width), BF16), pltpu.VMEM((2, total, ATT), BF16),
                    pltpu.VMEM((2, 2, width, HALF), BF16)]
        if "mlp" not in phases:
            scratch += [pltpu.VMEM(*gs["sums"]), pltpu.VMEM(*gs["bsum"])]

    def body(*refs):
        refs = list(refs)

        def take(n):
            got = refs[:n]
            del refs[:n]
            return got

        sc = take(1)[0]
        at = dict(zip(inputs, take(len(inputs))))
        src = take(len(sources))
        at.update(zip(shown, take(len(shown))))
        if end:
            bias = take(1)[0]
        dst = take(len(ends))
        w, vec, brow, sem = take(4)
        at.update(zip(inner, take(len(inner))))
        if end:
            at["ag"], at["dqkv"], g = take(3)
            if "mlp" not in phases:
                sums, bsum = take(2)
                sums[...] = at["sums"][...]
                bsum[...] = at["bsum"][...]
                at["sums"], at["bsum"] = sums, bsum
        copies = load(sc, src, w, sem)
        for c in copies:
            c.start()
        for c in copies:
            c.wait()
        vec[...] = w[0, 0, :, MISC:UP0].astype(F32).T[:8, :]
        for t in range(2):
            brow[t] = w[t, 1, :16, ROWSB:].astype(F32)
        if "forward" in phases:
            def step(n, carry):
                forward_image(n, sc, at["x"], w, vec, brow, at["out"], at)
                return carry
            lax.fori_loop(0, total // IMG_PAD, step, 0)
        if "mlp" in phases:
            at["sums"][...] = jnp.zeros_like(at["sums"])
            at["bsum"][...] = jnp.zeros_like(at["bsum"])

            def back_mlp(n, carry):
                backward_mlp(n, sc, at["u"], w, vec, at, at, at["sums"], at["bsum"])
                return carry
            lax.fori_loop(0, total // IMG_PAD, back_mlp, 0)
        if end:
            sums, bsum = at["sums"], at["bsum"]

            def back(n, carry):
                backward_attention(n, w, vec, at["in"], at, at, sums, bsum)
                return carry
            lax.fori_loop(0, total // IMG_PAD, back, 0)
            bias[...] = bsum[...]
            small = jnp.concatenate([sums[...], jnp.zeros((BLOCK - 8, width), F32)], 0).T.astype(BF16)
            copies = []
            for side in range(2):
                t = jnp.where(sc[1] == 0, 1 - side, side)
                weight_grads(t, piece, at, at, small, bsum, g)
                out = store(sc, side, t, g, dst, sem)
                for c in out:
                    c.start()
                copies += out
            for c in copies:
                c.wait()

    outs = [made[n] for n in shown] + ([gs["bsum"]] if end else []) + ends
    got = pl.pallas_call(
        body,
        out_shape=[jax.ShapeDtypeStruct(*o) for o in outs],
        in_specs=[pl.BlockSpec(memory_space=pltpu.SMEM)] + [vmem] * len(inputs) + [anywhere] * len(sources),
        out_specs=[vmem] * (len(outs) - len(ends)) + [anywhere] * len(ends),
        scratch_shapes=scratch,
        compiler_params=pltpu.CompilerParams(vmem_limit_bytes=56 * 2 ** 20),
        cost_estimate=pl.CostEstimate(flops=COST * len(phases), transcendentals=0, bytes_accessed=2 ** 23),
    )(scalars, *[given[n] for n in inputs], *sources)
    got = list(got)
    res = dict(zip(shown, got))
    del got[:len(shown)]
    if end:
        res["bias"] = got.pop(0)
        res["g"] = got
    return res


def shards(tokens, image_counts, cotangent, norm_gains, row_biases, qkv_weight, qv_bias, out_weight,
           up_weight, up_bias, down_weight):
    sec = lax.axis_index("section")
    dp = lax.axis_index("dp")
    ten = lax.axis_index("tensor")
    n_dp = lax.axis_size("dp")
    m = n_dp // 2
    zi, yi = dp // 2, dp % 2
    local_rows, width = tokens.shape[1:]
    images = local_rows * n_dp // IMG_LEN
    piece = width // n_dp
    ff = 2 * up_weight.shape[2]
    direct = piece % 16 == 0

    def pt(a):
        return lax.ppermute(a, "tensor", [(0, 1), (1, 0)])

    def px(a):
        return lax.ppermute(a, "section", [(0, 1), (1, 0)])

    def py(a):
        return lax.ppermute(a, "dp", [(i, i ^ 1) for i in range(n_dp)])

    def pd(a):
        return lax.ppermute(a, ("section", "dp"), [(i, (i + n_dp) % (2 * n_dp) ^ 1) for i in range(2 * n_dp)])

    def pz(a, k):
        return lax.ppermute(a, "dp", [(2 * z + y, 2 * ((z + k) % m) + y) for z in range(m) for y in range(2)])

    def after(a, *b):
        return lax.optimization_barrier((a, *b))

    def plus(*a):
        return sum(b.astype(F32) for b in a)

    def add_pair(g, got):
        keep, to_y, to_x, to_d = [plus(a, b) for a, b in zip(g[1:], (got[0, 0], got[0, 1], got[1, 0], got[1, 1]))]
        return [keep, to_y.astype(BF16), to_x.astype(BF16), to_d.astype(BF16)]

    def across(sent):
        return [sent[0], py(sent[1]), px(sent[2]), pd(sent[3])]

    def along(quad):
        quad = plus(*quad)
        low = quad.astype(BF16)
        return plus(quad[0], *[pz(low[kk], kk) for kk in range(1, m)])

    batch_tokens = lax.dynamic_index_in_dim(tokens, sec, 0, keepdims=False)
    batch_cot = lax.dynamic_index_in_dim(cotangent, sec, 0, keepdims=False)
    count = lax.dynamic_index_in_dim(image_counts, sec, 0, keepdims=False)
    first = jnp.minimum((dp * local_rows + IMG_LEN - 1) // IMG_LEN, images)
    last = jnp.minimum(((dp + 1) * local_rows + IMG_LEN - 1) // IMG_LEN, images)
    held = last - first
    slots = -(-(-(-local_rows // IMG_LEN)) // 2)
    lower = held // 2
    own_first = jnp.where(ten == 0, first, first + lower)
    own_count = jnp.where(ten == 0, lower, held - lower)
    total = slots * IMG_PAD
    row = lax.broadcasted_iota(jnp.int32, (total, 1), 0)
    slot, inside = row // IMG_PAD, row % IMG_PAD
    exists = (inside < IMG_LEN) & (slot < own_count)
    target = (own_first + slot) * IMG_LEN + inside - dp * local_rows
    canvas_rows = local_rows + IMG_PAD
    select = ((lax.broadcasted_iota(jnp.int32, (total, canvas_rows), 1) == target) & exists).astype(BF16)
    scalars = jnp.stack([jnp.minimum(own_count, jnp.maximum(count - own_first, 0)), ten, sec, zi, yi]).astype(jnp.int32)

    both = jnp.stack([batch_tokens, batch_cot])
    halo = lax.ppermute(both[:, :IMG_PAD], "dp", [(i + 1, i) for i in range(n_dp - 1)])
    both = jnp.concatenate([both, halo], 1)
    x0 = nn(select, both[0]).astype(BF16)
    cot = nn(select, both[1]).astype(BF16)

    q, k, v = [[qkv_weight[0, :, i, h * HD:(h + 1) * HD] for h in range(3)] for i in range(3)]
    o = out_weight[0].T
    o = [o[:, h * HD:(h + 1) * HD] for h in range(3)]
    misc = jnp.concatenate([norm_gains[0], row_biases[0]], 0).T
    misc = jnp.pad(misc, ((0, 0), (0, BLOCK - misc.shape[1])))
    gap = jnp.zeros((HD,), BF16)
    rows = jnp.concatenate([qv_bias[0, 0], gap, gap, gap, qv_bias[0, 1], gap, up_bias[0]]).reshape(-1, BLOCK)
    rows = jnp.pad(rows, ((0, piece - rows.shape[0]), (0, 0)))
    up, down = up_weight[0], down_weight[0].T
    part0 = jnp.concatenate(
        [q[0], q[1], q[2], k[2], k[0], k[1], v[0], v[1], v[2], o[2], o[0], o[1], misc, up[:, :CHUNK]], 1)
    part1 = jnp.concatenate([up[:, CHUNK:], down, rows], 1)

    if direct:
        keep = jnp.where(sec == 0, part0, part1)
        give = jnp.where(sec == 0, part1, part0)
        got = px(give)
        start = [jnp.where(sec == 0, keep, got), jnp.where(sec == 0, got, keep)]

        def load(sc, src, w, sem):
            copies = []
            for side in range(2):
                t = jnp.where(sc[1] == 0, side, 1 - side)
                quad, qx, qy, qd = src[side * 4:side * 4 + 4]
                for kk in range(m):
                    z = lax.rem(sc[3] - kk + m, m)
                    near = pl.ds(pl.multiple_of((2 * z + sc[4]) * piece, 16), piece)
                    far = pl.ds(pl.multiple_of((2 * z + 1 - sc[4]) * piece, 16), piece)
                    for a, h, r in ((quad, sc[2], near), (qx, 1 - sc[2], near), (qy, sc[2], far), (qd, 1 - sc[2], far)):
                        copies.append(pltpu.make_async_copy(a.at[kk], w.at[t, h, r, :], sem))
            return copies

        def store(sc, side, t, g, dst, sem):
            copies = []
            for hr in range(2):
                h = jnp.where(sc[2] == 0, hr, 1 - hr)
                for yr in range(2):
                    y = jnp.where(sc[4] == 0, yr, 1 - yr)
                    for kk in range(m):
                        z = lax.rem(sc[3] + kk, m)
                        r = pl.ds(pl.multiple_of((2 * z + y) * piece, 16), piece)
                        out = dst[0].at[hr, yr, kk] if side == 0 else dst[1 + hr * 2 + yr].at[kk]
                        copies.append(pltpu.make_async_copy(g.at[t, h, r, :], out, sem))
            return copies

        out_shapes = [((2, 2, m, piece, HALF), BF16)] + [((m, piece, HALF), BF16)] * 4

        quads = [jnp.stack([a] + [pz(a, kk) for kk in range(1, m)]) for a in start]
        mine = [quads[0], px(quads[0]), py(quads[0]), pd(quads[0])]
        quads[1], mine[1] = after(quads[1], mine[1])
        sources = [mine + [pt(b) for b in mine]]
        mine = [quads[1], px(quads[1]), py(quads[1]), pd(quads[1])]
        sources.append(mine)
    else:
        def load(sc, src, w, sem):
            return [pltpu.make_async_copy(src[0], w, sem)]

        def store(sc, side, t, g, dst, sem):
            return [pltpu.make_async_copy(g.at[t], dst[0].at[t], sem)]

        out_shapes = [((2, 2, width, HALF), BF16)]
        a = lax.all_gather(jnp.stack([part0, part1]), "dp", axis=1, tiled=True)
        a = lax.all_gather(lax.all_gather(a, "tensor"), "section")
        sources = [[a[0]], [a[1]]]

    def call(l, phases, **given):
        return layer_call(phases, sources[l], load, store, out_shapes, scalars, given, total, width, ff, piece)

    r0 = call(0, ["forward"], x=x0)
    if direct:
        low0, *mine = after(r0["out"], *sources[1])
        sources[1] = mine + [pt(b) for b in mine]
    else:
        low0 = r0["out"]
    r1 = call(1, ["forward", "mlp", "attention"], x=low0, u=cot)
    if direct:
        got1 = pt(r1["g"][0])
    m0 = call(0, ["mlp"], **{**r0, "u": r1["in"]})
    if direct:
        m0["res"], got1 = after(m0["res"], got1)
        sent1 = add_pair(r1["g"], got1)
        m0["res"], *sent1 = after(m0["res"], *sent1)
        quad1 = across(sent1)
    b0 = call(0, ["attention"], **{**r0, **m0})

    if direct:
        out0, *quad1 = after(b0["g"][0], *quad1)
        got0 = pt(out0)
        sent0 = add_pair(b0["g"], got0)
        b0["in"], *sent0 = after(b0["in"], *sent0)
        done = [along(quad1), along(across(sent0))]
        mine = jnp.where(sec == 0, done[1], done[0])
        other = px(jnp.where(sec == 0, done[0], done[1]).astype(BF16)).astype(F32)
        final0 = jnp.where(sec == 0, mine, other)
        final1 = jnp.where(sec == 0, other, mine)
        small = final1[:, ROWSB:]
    else:
        g = jnp.stack([b0["g"][0], r1["g"][0]])
        g = lax.psum_scatter(g.astype(F32), "section", scatter_dimension=0)
        g = lax.psum_scatter(g, "tensor", scatter_dimension=0)
        g = lax.psum_scatter(g, "dp", scatter_dimension=1, tiled=True)
        final0, final1 = g[0], g[1]
        small = lax.psum(jnp.stack([b0["bias"], r1["bias"]]), ("section", "tensor", "dp"))
        small = lax.dynamic_index_in_dim(lax.dynamic_index_in_dim(small, sec, 0, False), ten, 0, False)

    def settled(a0, a1):
        keep = jnp.where(sec == 0, a0, a1)
        got = px(jnp.where(sec == 0, a1, a0))
        a = jnp.where(sec == 0, jnp.stack([keep, got]), jnp.stack([got, keep]))
        a = jnp.stack([tn(select, a[0]), tn(select, a[1])]).astype(BF16)
        a = a + pt(a)
        spill = lax.ppermute(a[:, local_rows:], "dp", [(i, i + 1) for i in range(n_dp - 1)])
        return jnp.concatenate([a[:, :IMG_PAD] + spill, a[:, IMG_PAD:local_rows]], 1)

    layer_outputs = settled(r0["out"], r1["out"])[None]
    input_grads = settled(b0["in"].astype(BF16), r1["in"].astype(BF16)).astype(F32)[None]

    def heads(*starts):
        return [final0[:, s * HD:(s + 1) * HD] for s in starts]

    small = small.reshape(-1)
    qkv = jnp.concatenate(heads(0, 1, 2, 4, 5, 3, 6, 7, 8), 1).reshape(1, piece, 3, 3 * HD)
    return (
        layer_outputs,
        input_grads,
        final0[:, MISC:MISC + 2].T[None],
        final0[:, MISC + 2:MISC + 6].T[None],
        qkv,
        jnp.stack([small[:3 * HD], small[6 * HD:9 * HD]])[None],
        jnp.concatenate(heads(10, 11, 9), 1).T[None],
        jnp.concatenate([final0[:, UP0:], final1[:, :DOWN]], 1)[None],
        small[ATT:ATT + ff // 2][None],
        final1[:, DOWN:ROWSB].T[None],
    )


def solution(mesh):
    in_specs = (
        P(None, "dp", None),
        P(),
        P(None, "dp", None),
        P("section", None, "dp"),
        P("section", None, "dp"),
        P("section", "dp", None, "tensor"),
        P("section", None, "tensor"),
        P("section", "tensor", "dp"),
        P("section", "dp", "tensor"),
        P("section", "tensor"),
        P("section", "tensor", "dp"),
    )
    out_specs = (
        P("section", None, "dp", None),
        P("section", None, "dp", None),
        P("section", None, "dp"),
        P("section", None, "dp"),
        P("section", "dp", None, "tensor"),
        P("section", None, "tensor"),
        P("section", "tensor", "dp"),
        P("section", "dp", "tensor"),
        P("section", "tensor"),
        P("section", "tensor", "dp"),
    )
    return jax.shard_map(shards, mesh=mesh, in_specs=in_specs, out_specs=out_specs, check_vma=False)
```

```python
import math

import jax
import jax.numpy as jnp
from jax import lax
from jax.experimental import pallas as pl
from jax.experimental.pallas import tpu as pltpu
from jax.sharding import PartitionSpec as P

IMG_LEN = 197
IMG_PAD = 208
HD = 64
EPSILON = 1e-06
NEGATIVE = -1e30
F32 = jnp.float32
BF16 = jnp.bfloat16
BLOCK = 128
HALF = 1280
COST = 10 ** 10
SCALE = 1.0 / math.sqrt(HD)


def mm(a, b, dims):
    return lax.dot_general(a, b, (dims, ((), ())), preferred_element_type=F32)


def nn(a, b):
    return mm(a, b, ((1,), (0,)))


def nt(a, b):
    return mm(a, b, ((1,), (1,)))


def tn(a, b):
    return mm(a, b, ((0,), (0,)))


def normed(x):
    centred = x - jnp.mean(x, -1, keepdims=True)
    inverse = lax.rsqrt(jnp.mean(centred * centred, -1, keepdims=True) + EPSILON)
    return centred * inverse, inverse


def norm_back(grad, xhat, inverse, gain):
    t = grad * gain
    return inverse * (
        t - jnp.mean(t, -1, keepdims=True) - xhat * jnp.mean(t * xhat, -1, keepdims=True)
    )


def gelu_parts(u):
    cdf = 0.5 * (1.0 + lax.erf(u * math.sqrt(0.5)))
    pdf = jnp.exp(-0.5 * u * u) * (1.0 / math.sqrt(2.0 * math.pi))
    return u * cdf, cdf + u * pdf


ATT = 640
OUT = 512
MISC = 768
UP0 = 896
DOWN = 384
ROWSB = 1152
CHUNK = 384


def up_at(w, t, j):
    return w[t, 0, :, UP0:] if j == 0 else w[t, 1, :, :CHUNK]


def down_at(w, t, j):
    return w[t, 1, :, DOWN + j * CHUNK:DOWN + (j + 1) * CHUNK]


def low_lanes():
    return lax.broadcasted_iota(jnp.int32, (1, BLOCK), 1) < HD


def turn(a):
    return jnp.concatenate([a[:, HD:], a[:, :HD]], 1)


def valid_rows(sc, n):
    row = lax.broadcasted_iota(jnp.int32, (IMG_PAD, 1), 0)
    return jnp.where((row < IMG_LEN) & (n < sc[0]), 1.0, 0.0)


def image_rows(n):
    return pl.ds(pl.multiple_of(n * IMG_PAD, 16), IMG_PAD)


def forward_image(n, sc, x_ref, w, vec, brow, out_ref, kept):
    r = image_rows(n)
    x = x_ref[r, :].astype(F32)
    xhat, inv = normed(x)
    attn_in = (xhat * vec[0:1, :] + vec[2:3, :]).astype(BF16)
    kept["xh1"][r, :] = xhat
    kept["inv1"][r, :] = jnp.broadcast_to(inv, (IMG_PAD, BLOCK))
    kept["ain"][r, :] = attn_in
    residual = x + vec[3:4, :]
    low = low_lanes()
    lane = lax.broadcasted_iota(jnp.int32, (1, ATT), 1)
    factor = jnp.where(lane < 192, SCALE, jnp.where(lane < 576, 1.0, 0.0))
    real = lax.broadcasted_iota(jnp.int32, (1, IMG_PAD), 1) < IMG_LEN
    for t in range(2):
        bias = jnp.concatenate([brow[t, i:i + 1, :] for i in range(5)], 1)
        p = ((nn(attn_in, w[t, 0, :, :ATT]) + bias) * factor).astype(BF16)
        kept["qkv"][t, r, :] = p
        q, qk, k, v, vx = [p[:, i * BLOCK:(i + 1) * BLOCK] for i in range(5)]
        kq, xv = turn(qk), turn(vx)
        outs = []
        for i, (qq, kk, vv) in enumerate(
                [(jnp.where(low, q, 0), k, v), (jnp.where(low, 0, q), k, v), (jnp.where(low, qk, 0), kq, xv)]):
            s = jnp.where(real, nt(qq, kk), NEGATIVE)
            e = jnp.exp(s - jnp.max(s, -1, keepdims=True))
            pr = (e * (1.0 / jnp.sum(e, -1, keepdims=True))).astype(BF16)
            kept["pr"][n * 6 + t * 3 + i] = pr
            outs.append(nn(pr, vv))
        mixed = jnp.concatenate([outs[2], jnp.where(low, outs[0], outs[1])], 1).astype(BF16)
        kept["mx"][t, r, :] = mixed
        residual = residual + nt(mixed, w[t, 0, :, OUT:MISC])
    xhat, inv = normed(residual)
    mlp_in = (xhat * vec[1:2, :] + vec[4:5, :]).astype(BF16)
    kept["xh2"][r, :] = xhat
    kept["inv2"][r, :] = jnp.broadcast_to(inv, (IMG_PAD, BLOCK))
    kept["min"][r, :] = mlp_in
    out = residual + vec[5:6, :]
    for t in range(2):
        for j in range(2):
            bias = jnp.concatenate([brow[t, 5 + j * 3 + i:6 + j * 3 + i, :] for i in range(3)], 1)
            hidden, slope = gelu_parts(nn(mlp_in, up_at(w, t, j)) + bias)
            c = slice((t * 2 + j) * CHUNK, (t * 2 + j + 1) * CHUNK)
            hidden = hidden.astype(BF16)
            kept["hd"][r, c] = hidden
            kept["sl"][r, c] = slope.astype(BF16)
            out = out + nt(hidden, down_at(w, t, j))
    out_ref[r, :] = (out * valid_rows(sc, n)).astype(BF16)


def rsum(a):
    return jnp.sum(a, 0, keepdims=True)


def backward_mlp(n, sc, u_ref, w, vec, kept, grad, sums, bsum):
    r = image_rows(n)

    masked = u_ref[r, :].astype(F32) * valid_rows(sc, n)
    sums[5:6, :] += rsum(masked)
    dg = masked.astype(BF16)
    grad["dg"][r, :] = dg
    mg = jnp.zeros(masked.shape, F32)
    for t in range(2):
        for j in range(2):
            c = slice((t * 2 + j) * CHUNK, (t * 2 + j + 1) * CHUNK)
            up = nn(dg, down_at(w, t, j)) * kept["sl"][r, c].astype(F32)
            up = up.astype(BF16)
            grad["up"][r, c] = up
            total = rsum(up.astype(F32))
            for i in range(3):
                bsum[t, 5 + j * 3 + i:6 + j * 3 + i, :] += total[:, i * BLOCK:(i + 1) * BLOCK]
            mg = mg + nt(up, up_at(w, t, j))
    xhat = kept["xh2"][r, :]
    sums[4:5, :] += rsum(mg)
    sums[1:2, :] += rsum(mg * xhat)
    res = masked + norm_back(mg, xhat, kept["inv2"][r, :1], vec[1:2, :])
    sums[3:4, :] += rsum(res)
    grad["res"][r, :] = res


def backward_attention(n, w, vec, in_ref, kept, grad, sums, bsum):
    r = image_rows(n)
    res = grad["res"][r, :]
    ag = res.astype(BF16)
    grad["ag"][r, :] = ag
    low = low_lanes()
    ig = jnp.zeros(res.shape, F32)
    for t in range(2):
        xg = nn(ag, w[t, 0, :, OUT:MISC]).astype(BF16)
        gx = jnp.where(low, 0, xg[:, :BLOCK])
        g = xg[:, BLOCK:]
        p = kept["qkv"][t, r, :]
        q, qk, k, v, vx = [p[:, i * BLOCK:(i + 1) * BLOCK] for i in range(5)]
        kq, xv = turn(qk), turn(vx)
        dq, dk, dv = [], [], []
        for i, (qq, kk, vv, gm, gg) in enumerate(
                [(q, k, v, jnp.where(low, g, 0), g), (q, k, v, jnp.where(low, 0, g), g), (qk, kq, xv, gx, turn(gx))]):
            pb = kept["pr"][n * 6 + t * 3 + i]
            pf = pb.astype(F32)
            dp = nt(gm, vv)
            ds = (pf * (dp - jnp.sum(pf * dp, -1, keepdims=True))).astype(BF16)
            dv.append(tn(pb, gg))
            dq.append(nn(ds, kk) * SCALE)
            dk.append(tn(ds, kq if i == 2 else qq))
        blocks = [
            jnp.where(low, dq[0], dq[1]), jnp.where(low, dq[2], dk[2]), jnp.where(low, dk[0], dk[1]),
            jnp.where(low, dv[0], dv[1]), dv[2],
        ]
        d = jnp.concatenate(blocks, 1).astype(BF16)
        grad["dqkv"][t, r, :] = d
        total = rsum(d.astype(F32))
        for i in range(5):
            bsum[t, i:i + 1, :] += total[:, i * BLOCK:(i + 1) * BLOCK]
        ig = ig + nt(d, w[t, 0, :, :ATT])
    xhat = kept["xh1"][r, :]
    sums[2:3, :] += rsum(ig)
    sums[0:1, :] += rsum(ig * xhat)
    in_ref[r, :] = res + norm_back(ig, xhat, kept["inv1"][r, :1], vec[0:1, :])


def weight_grads(t, piece, kept, grad, small, bsum, g):
    width = small.shape[0]
    ag, dg = grad["ag"][...], grad["dg"][...]
    ain, mlp_in = kept["ain"][...], kept["min"][...]
    high = jnp.where(low_lanes(), 0.0, 1.0)
    d = grad["dqkv"][t]
    g[t, 0, :, :OUT] = tn(ain, d[:, :OUT]).astype(BF16)
    out = tn(ag, kept["mx"][t])
    g[t, 0, :, OUT:ATT] = (tn(ain, d[:, OUT:]) + out[:, :BLOCK] * high).astype(BF16)
    g[t, 0, :, ATT:MISC] = out[:, BLOCK:].astype(BF16)
    g[t, 0, :, MISC:UP0] = small
    for j in range(2):
        c = pl.ds(pl.multiple_of((t * 2 + j) * CHUNK, BLOCK), CHUNK)
        up = tn(mlp_in, grad["up"][:, c]).astype(BF16)
        if j == 0:
            g[t, 0, :, UP0:] = up
        else:
            g[t, 1, :, :CHUNK] = up
        g[t, 1, :, DOWN + j * CHUNK:DOWN + (j + 1) * CHUNK] = tn(dg, kept["hd"][:, c]).astype(BF16)
    if piece % 16 == 0:
        rows = jnp.concatenate([bsum[t], jnp.zeros((piece - 16, BLOCK), F32)], 0).astype(BF16)
        for i in range(width // piece):
            g[t, 1, i * piece:(i + 1) * piece, ROWSB:] = rows


def kept_shapes(total, width, ff):
    images = total // IMG_PAD
    return dict(
        xh1=((total, width), F32), inv1=((total, BLOCK), F32), ain=((total, width), BF16), qkv=((2, total, ATT), BF16),
        pr=((images * 6, IMG_PAD, IMG_PAD), BF16), mx=((2, total, 2 * BLOCK), BF16), xh2=((total, width), F32),
        inv2=((total, BLOCK), F32), min=((total, width), BF16), sl=((total, ff), BF16), hd=((total, ff), BF16))


def grad_shapes(total, width, ff):
    return dict(dg=((total, width), BF16), up=((total, ff), BF16), res=((total, width), F32), sums=((8, width), F32),
                bsum=((2, 16, BLOCK), F32))


def layer_call(phases, sources, load, store, out_shapes, scalars, given, total, width, ff, piece):
    ks = kept_shapes(total, width, ff)
    gs = grad_shapes(total, width, ff)
    need = {
        "forward": ["x"], "mlp": ["u", "sl", "xh2", "inv2"],
        "attention": list(gs) + ["ain", "qkv", "pr", "mx", "xh1", "inv1", "min", "hd"],
    }
    gives = {"forward": {"out": ((total, width), BF16), **ks}, "mlp": gs, "attention": {"in": ((total, width), F32)}}
    made = {}
    for p in phases:
        made.update(gives[p])
    inputs = [n for p in phases for n in need[p] if n not in made]
    inputs = list(dict.fromkeys(inputs))
    last = phases[-1]
    shown = {"forward": list(gives["forward"]), "mlp": list(gs), "attention": ["in"]}[last]
    if last != "forward" and "forward" in phases:
        shown = ["out"] + shown
    if last == "mlp" and "forward" in phases:
        shown += [n for n in ks if n in need["attention"]]
    inner = [n for n in made if n not in shown]
    end = last == "attention"
    vmem = pl.BlockSpec(memory_space=pltpu.VMEM)
    anywhere = pl.BlockSpec(memory_space=pl.ANY)
    ends = out_shapes if end else []
    scratch = [pltpu.VMEM((2, 2, width, HALF), BF16), pltpu.VMEM((8, width), F32), pltpu.VMEM((2, 16, BLOCK), F32),
               pltpu.SemaphoreType.DMA] + [pltpu.VMEM(*made[n]) for n in inner]
    if end:
        scratch += [pltpu.VMEM((total, width), BF16), pltpu.VMEM((2, total, ATT), BF16),
                    pltpu.VMEM((2, 2, width, HALF), BF16)]
        if "mlp" not in phases:
            scratch += [pltpu.VMEM(*gs["sums"]), pltpu.VMEM(*gs["bsum"])]

    def body(*refs):
        refs = list(refs)

        def take(n):
            got = refs[:n]
            del refs[:n]
            return got

        sc = take(1)[0]
        at = dict(zip(inputs, take(len(inputs))))
        src = take(len(sources))
        at.update(zip(shown, take(len(shown))))
        if end:
            bias = take(1)[0]
        dst = take(len(ends))
        w, vec, brow, sem = take(4)
        at.update(zip(inner, take(len(inner))))
        if end:
            at["ag"], at["dqkv"], g = take(3)
            if "mlp" not in phases:
                sums, bsum = take(2)
                sums[...] = at["sums"][...]
                bsum[...] = at["bsum"][...]
                at["sums"], at["bsum"] = sums, bsum
        copies = load(sc, src, w, sem)
        for c in copies:
            c.start()
        for c in copies:
            c.wait()
        vec[...] = w[0, 0, :, MISC:UP0].astype(F32).T[:8, :]
        for t in range(2):
            brow[t] = w[t, 1, :16, ROWSB:].astype(F32)
        if "forward" in phases:
            def step(n, carry):
                forward_image(n, sc, at["x"], w, vec, brow, at["out"], at)
                return carry
            lax.fori_loop(0, total // IMG_PAD, step, 0)
        if "mlp" in phases:
            at["sums"][...] = jnp.zeros_like(at["sums"])
            at["bsum"][...] = jnp.zeros_like(at["bsum"])

            def back_mlp(n, carry):
                backward_mlp(n, sc, at["u"], w, vec, at, at, at["sums"], at["bsum"])
                return carry
            lax.fori_loop(0, total // IMG_PAD, back_mlp, 0)
        if end:
            sums, bsum = at["sums"], at["bsum"]

            def back(n, carry):
                backward_attention(n, w, vec, at["in"], at, at, sums, bsum)
                return carry
            lax.fori_loop(0, total // IMG_PAD, back, 0)
            bias[...] = bsum[...]
            small = jnp.concatenate([sums[...], jnp.zeros((BLOCK - 8, width), F32)], 0).T.astype(BF16)
            copies = []
            for side in range(2):
                t = jnp.where(sc[1] == 0, 1 - side, side)
                weight_grads(t, piece, at, at, small, bsum, g)
                out = store(sc, side, t, g, dst, sem)
                for c in out:
                    c.start()
                copies += out
            for c in copies:
                c.wait()

    outs = [made[n] for n in shown] + ([gs["bsum"]] if end else []) + ends
    got = pl.pallas_call(
        body,
        out_shape=[jax.ShapeDtypeStruct(*o) for o in outs],
        in_specs=[pl.BlockSpec(memory_space=pltpu.SMEM)] + [vmem] * len(inputs) + [anywhere] * len(sources),
        out_specs=[vmem] * (len(outs) - len(ends)) + [anywhere] * len(ends),
        scratch_shapes=scratch,
        compiler_params=pltpu.CompilerParams(vmem_limit_bytes=56 * 2 ** 20),
        cost_estimate=pl.CostEstimate(flops=COST * len(phases), transcendentals=0, bytes_accessed=2 ** 23),
    )(scalars, *[given[n] for n in inputs], *sources)
    got = list(got)
    res = dict(zip(shown, got))
    del got[:len(shown)]
    if end:
        res["bias"] = got.pop(0)
        res["g"] = got
    return res


def shards(tokens, image_counts, cotangent, norm_gains, row_biases, qkv_weight, qv_bias, out_weight,
           up_weight, up_bias, down_weight):
    sec = lax.axis_index("section")
    dp = lax.axis_index("dp")
    ten = lax.axis_index("tensor")
    n_dp = lax.axis_size("dp")
    m = n_dp // 2
    zi, yi = dp // 2, dp % 2
    local_rows, width = tokens.shape[1:]
    images = local_rows * n_dp // IMG_LEN
    piece = width // n_dp
    ff = 2 * up_weight.shape[2]
    direct = piece % 16 == 0

    def pt(a):
        return lax.ppermute(a, "tensor", [(0, 1), (1, 0)])

    def px(a):
        return lax.ppermute(a, "section", [(0, 1), (1, 0)])

    def py(a):
        return lax.ppermute(a, "dp", [(i, i ^ 1) for i in range(n_dp)])

    def pd(a):
        return lax.ppermute(a, ("section", "dp"), [(i, (i + n_dp) % (2 * n_dp) ^ 1) for i in range(2 * n_dp)])

    def pz(a, k):
        return lax.ppermute(a, "dp", [(2 * z + y, 2 * ((z + k) % m) + y) for z in range(m) for y in range(2)])

    def after(a, *b):
        return lax.optimization_barrier((a, *b))

    def plus(*a):
        return sum(b.astype(F32) for b in a)

    def add_pair(g, got):
        keep, to_y, to_x, to_d = [plus(a, b) for a, b in zip(g[1:], (got[0, 0], got[0, 1], got[1, 0], got[1, 1]))]
        return [keep, to_y.astype(BF16), to_x.astype(BF16), to_d.astype(BF16)]

    def across(sent):
        return [sent[0], py(sent[1]), px(sent[2]), pd(sent[3])]

    def along(quad):
        quad = plus(*quad)
        low = quad.astype(BF16)
        return plus(quad[0], *[pz(low[kk], kk) for kk in range(1, m)])

    def pn(a, flip):
        other = n_dp if flip else 0
        pairs = [(i, (i + other) % (2 * n_dp) + 1) for i in range(2 * n_dp) if i % n_dp < n_dp - 1]
        return lax.ppermute(a, ("section", "dp"), pairs)

    def send_rows(a0, a1):
        keep, give = jnp.where(sec == 0, a0, a1), jnp.where(sec == 0, a1, a0)
        tail = select[:, local_rows:]
        return [keep, px(give), pn(tn(tail, keep).astype(BF16), False), pn(tn(tail, give).astype(BF16), True)]

    def place_rows(keep, got, tail, got_tail):
        def place(a, b):
            a = tn(select[:, :local_rows], a).astype(BF16)
            return jnp.concatenate([a[:IMG_PAD] + b, a[IMG_PAD:]], 0)

        near, far = place(keep, tail), place(got, got_tail)
        return jnp.where(sec == 0, jnp.stack([near, far]), jnp.stack([far, near]))

    batch_tokens = lax.dynamic_index_in_dim(tokens, sec, 0, keepdims=False)
    batch_cot = lax.dynamic_index_in_dim(cotangent, sec, 0, keepdims=False)
    count = lax.dynamic_index_in_dim(image_counts, sec, 0, keepdims=False)
    first = jnp.minimum((dp * local_rows + IMG_LEN - 1) // IMG_LEN, images)
    last = jnp.minimum(((dp + 1) * local_rows + IMG_LEN - 1) // IMG_LEN, images)
    held = last - first
    slots = -(-(-(-local_rows // IMG_LEN)) // 2)
    lower = held // 2
    own_first = jnp.where(ten == 0, first, first + lower)
    own_count = jnp.where(ten == 0, lower, held - lower)
    total = slots * IMG_PAD
    row = lax.broadcasted_iota(jnp.int32, (total, 1), 0)
    slot, inside = row // IMG_PAD, row % IMG_PAD
    exists = (inside < IMG_LEN) & (slot < own_count)
    target = (own_first + slot) * IMG_LEN + inside - dp * local_rows
    canvas_rows = local_rows + IMG_PAD
    select = ((lax.broadcasted_iota(jnp.int32, (total, canvas_rows), 1) == target) & exists).astype(BF16)
    scalars = jnp.stack([jnp.minimum(own_count, jnp.maximum(count - own_first, 0)), ten, sec, zi, yi]).astype(jnp.int32)

    both = jnp.stack([batch_tokens, batch_cot])
    halo = lax.ppermute(both[:, :IMG_PAD], "dp", [(i + 1, i) for i in range(n_dp - 1)])
    q, k, v = [[qkv_weight[0, :, i, h * HD:(h + 1) * HD] for h in range(3)] for i in range(3)]
    o = out_weight[0].T
    o = [o[:, h * HD:(h + 1) * HD] for h in range(3)]
    misc = jnp.concatenate([norm_gains[0], row_biases[0]], 0).T
    misc = jnp.pad(misc, ((0, 0), (0, BLOCK - misc.shape[1])))
    gap = jnp.zeros((HD,), BF16)
    rows = jnp.concatenate([qv_bias[0, 0], gap, gap, gap, qv_bias[0, 1], gap, up_bias[0]]).reshape(-1, BLOCK)
    rows = jnp.pad(rows, ((0, piece - rows.shape[0]), (0, 0)))
    up, down = up_weight[0], down_weight[0].T
    part0 = jnp.concatenate(
        [q[0], q[1], q[2], k[2], k[0], k[1], v[0], v[1], v[2], o[2], o[0], o[1], misc, up[:, :CHUNK]], 1)
    part1 = jnp.concatenate([up[:, CHUNK:], down, rows], 1)

    if direct:
        keep = jnp.where(sec == 0, part0, part1)
        give = jnp.where(sec == 0, part1, part0)
        give, halo = after(give, halo)
        got = px(give)
        start = [jnp.where(sec == 0, keep, got), jnp.where(sec == 0, got, keep)]

        def load(sc, src, w, sem):
            copies = []
            for side in range(2):
                t = jnp.where(sc[1] == 0, side, 1 - side)
                quad, qx, qy, qd = src[side * 4:side * 4 + 4]
                for kk in range(m):
                    z = lax.rem(sc[3] - kk + m, m)
                    near = pl.ds(pl.multiple_of((2 * z + sc[4]) * piece, 16), piece)
                    far = pl.ds(pl.multiple_of((2 * z + 1 - sc[4]) * piece, 16), piece)
                    for a, h, r in ((quad, sc[2], near), (qx, 1 - sc[2], near), (qy, sc[2], far), (qd, 1 - sc[2], far)):
                        copies.append(pltpu.make_async_copy(a.at[kk], w.at[t, h, r, :], sem))
            return copies

        def store(sc, side, t, g, dst, sem):
            copies = []
            for hr in range(2):
                h = jnp.where(sc[2] == 0, hr, 1 - hr)
                for yr in range(2):
                    y = jnp.where(sc[4] == 0, yr, 1 - yr)
                    for kk in range(m):
                        z = lax.rem(sc[3] + kk, m)
                        r = pl.ds(pl.multiple_of((2 * z + y) * piece, 16), piece)
                        out = dst[0].at[hr, yr, kk] if side == 0 else dst[1 + hr * 2 + yr].at[kk]
                        copies.append(pltpu.make_async_copy(g.at[t, h, r, :], out, sem))
            return copies

        out_shapes = [((2, 2, m, piece, HALF), BF16)] + [((m, piece, HALF), BF16)] * 4

        quads = [jnp.stack([a] + [pz(a, kk) for kk in range(1, m)]) for a in start]
        mine = [quads[0], px(quads[0]), py(quads[0]), pd(quads[0])]
        quads[1], mine[1] = after(quads[1], mine[1])
        sources = [mine + [pt(b) for b in mine]]
        mine = [quads[1], px(quads[1]), py(quads[1]), pd(quads[1])]
        sources.append(mine)
    else:
        def load(sc, src, w, sem):
            return [pltpu.make_async_copy(src[0], w, sem)]

        def store(sc, side, t, g, dst, sem):
            return [pltpu.make_async_copy(g.at[t], dst[0].at[t], sem)]

        out_shapes = [((2, 2, width, HALF), BF16)]
        a = lax.all_gather(jnp.stack([part0, part1]), "dp", axis=1, tiled=True)
        a = lax.all_gather(lax.all_gather(a, "tensor"), "section")
        sources = [[a[0]], [a[1]]]

    both = jnp.concatenate([both, halo], 1)
    x0 = nn(select, both[0]).astype(BF16)
    cot = nn(select, both[1]).astype(BF16)

    def call(l, phases, **given):
        return layer_call(phases, sources[l], load, store, out_shapes, scalars, given, total, width, ff, piece)

    r0 = call(0, ["forward"], x=x0)
    if direct:
        low0, *mine = after(r0["out"], *sources[1])
        sources[1] = mine + [pt(b) for b in mine]
    else:
        low0 = r0["out"]
    r1 = call(1, ["forward", "mlp", "attention"], x=low0, u=cot)
    if direct:
        got1 = pt(r1["g"][0])
    rows = send_rows(r0["out"], r1["out"])
    m0 = call(0, ["mlp"], **{**r0, "u": r1["in"]})
    if direct:
        m0["res"], *rows = after(m0["res"], *rows)
        m0["res"], got1 = after(m0["res"], got1)
        sent1 = add_pair(r1["g"], got1)
        placed = place_rows(*rows)
        m0["res"], placed, *sent1 = after(m0["res"], placed, *sent1)
        other_core = pt(placed)
        quad1 = across(sent1)
    else:
        placed = place_rows(*rows)
        other_core = pt(placed)
    b0 = call(0, ["attention"], **{**r0, **m0})
    layer_outputs = (placed + other_core)[None]

    if direct:
        out0, *quad1 = after(b0["g"][0], *quad1)
        got0 = pt(out0)
        rows = send_rows(b0["in"].astype(BF16), r1["in"].astype(BF16))
        got0, *rows = after(got0, *rows)
        placed = place_rows(*rows)
        sent0 = add_pair(b0["g"], got0)
        placed, *sent0 = after(placed, *sent0)
        other_core, *quad0 = after(pt(placed), *across(sent0))
        done = [along(quad1), along(quad0)]
        mine = jnp.where(sec == 0, done[1], done[0])
        other = px(jnp.where(sec == 0, done[0], done[1]).astype(BF16)).astype(F32)
        final0 = jnp.where(sec == 0, mine, other)
        final1 = jnp.where(sec == 0, other, mine)
        small = final1[:, ROWSB:]
    else:
        placed = place_rows(*send_rows(b0["in"].astype(BF16), r1["in"].astype(BF16)))
        other_core = pt(placed)
        g = jnp.stack([b0["g"][0], r1["g"][0]])
        g = lax.psum_scatter(g.astype(F32), "section", scatter_dimension=0)
        g = lax.psum_scatter(g, "tensor", scatter_dimension=0)
        g = lax.psum_scatter(g, "dp", scatter_dimension=1, tiled=True)
        final0, final1 = g[0], g[1]
        small = lax.psum(jnp.stack([b0["bias"], r1["bias"]]), ("section", "tensor", "dp"))
        small = lax.dynamic_index_in_dim(lax.dynamic_index_in_dim(small, sec, 0, False), ten, 0, False)

    input_grads = (placed + other_core).astype(F32)[None]

    def heads(*starts):
        return [final0[:, s * HD:(s + 1) * HD] for s in starts]

    small = small.reshape(-1)
    qkv = jnp.concatenate(heads(0, 1, 2, 4, 5, 3, 6, 7, 8), 1).reshape(1, piece, 3, 3 * HD)
    return (
        layer_outputs,
        input_grads,
        final0[:, MISC:MISC + 2].T[None],
        final0[:, MISC + 2:MISC + 6].T[None],
        qkv,
        jnp.stack([small[:3 * HD], small[6 * HD:9 * HD]])[None],
        jnp.concatenate(heads(10, 11, 9), 1).T[None],
        jnp.concatenate([final0[:, UP0:], final1[:, :DOWN]], 1)[None],
        small[ATT:ATT + ff // 2][None],
        final1[:, DOWN:ROWSB].T[None],
    )


def solution(mesh):
    in_specs = (
        P(None, "dp", None),
        P(),
        P(None, "dp", None),
        P("section", None, "dp"),
        P("section", None, "dp"),
        P("section", "dp", None, "tensor"),
        P("section", None, "tensor"),
        P("section", "tensor", "dp"),
        P("section", "dp", "tensor"),
        P("section", "tensor"),
        P("section", "tensor", "dp"),
    )
    out_specs = (
        P("section", None, "dp", None),
        P("section", None, "dp", None),
        P("section", None, "dp"),
        P("section", None, "dp"),
        P("section", "dp", None, "tensor"),
        P("section", None, "tensor"),
        P("section", "tensor", "dp"),
        P("section", "dp", "tensor"),
        P("section", "tensor"),
        P("section", "tensor", "dp"),
    )
    return jax.shard_map(shards, mesh=mesh, in_specs=in_specs, out_specs=out_specs, check_vma=False)
```

```python
import functools
import math

import jax
import jax.numpy as jnp
from jax import lax
from jax.experimental import pallas as pl
from jax.experimental.pallas import tpu as pltpu
from jax.sharding import PartitionSpec as P

IMG_LEN = 197
IMG_PAD = 208
HD = 64
EPSILON = 1e-06
NEGATIVE = -1e30
F32 = jnp.float32
BF16 = jnp.bfloat16
BLOCK = 128
HALF = 1280
COST = 10 ** 10
SCALE = 1.0 / math.sqrt(HD)


def mm(a, b, dims):
    return lax.dot_general(a, b, (dims, ((), ())), preferred_element_type=F32)


def nn(a, b):
    return mm(a, b, ((1,), (0,)))


def nt(a, b):
    return mm(a, b, ((1,), (1,)))


def tn(a, b):
    return mm(a, b, ((0,), (0,)))


def normed(x):
    centred = x - jnp.mean(x, -1, keepdims=True)
    inverse = lax.rsqrt(jnp.mean(centred * centred, -1, keepdims=True) + EPSILON)
    return centred * inverse, inverse


def norm_back(grad, xhat, inverse, gain):
    t = grad * gain
    return inverse * (
        t - jnp.mean(t, -1, keepdims=True) - xhat * jnp.mean(t * xhat, -1, keepdims=True)
    )


def gelu_parts(u):
    cdf = 0.5 * (1.0 + lax.erf(u * math.sqrt(0.5)))
    pdf = jnp.exp(-0.5 * u * u) * (1.0 / math.sqrt(2.0 * math.pi))
    return u * cdf, cdf + u * pdf


ATT = 640
OUT = 512
MISC = 768
UP0 = 896
DOWN = 384
ROWSB = 1152
CHUNK = 384


def up_at(w, t, j):
    return w[t, 0, :, UP0:] if j == 0 else w[t, 1, :, :CHUNK]


def down_at(w, t, j):
    return w[t, 1, :, DOWN + j * CHUNK:DOWN + (j + 1) * CHUNK]


def low_lanes():
    return lax.broadcasted_iota(jnp.int32, (1, BLOCK), 1) < HD


def turn(a):
    return jnp.concatenate([a[:, HD:], a[:, :HD]], 1)


def valid_rows(sc, n):
    row = lax.broadcasted_iota(jnp.int32, (IMG_PAD, 1), 0)
    return jnp.where((row < IMG_LEN) & (n < sc[0]), 1.0, 0.0)


def image_rows(n):
    return pl.ds(pl.multiple_of(n * IMG_PAD, 16), IMG_PAD)


def forward_image(n, sc, x_ref, w, vec, brow, out_ref, kept):
    r = image_rows(n)
    x = x_ref[r, :].astype(F32)
    xhat, inv = normed(x)
    attn_in = (xhat * vec[0:1, :] + vec[2:3, :]).astype(BF16)
    kept["xh1"][r, :] = xhat
    kept["inv1"][r, :] = jnp.broadcast_to(inv, (IMG_PAD, BLOCK))
    kept["ain"][r, :] = attn_in
    residual = x + vec[3:4, :]
    low = low_lanes()
    lane = lax.broadcasted_iota(jnp.int32, (1, ATT), 1)
    factor = jnp.where(lane < 192, SCALE, jnp.where(lane < 576, 1.0, 0.0))
    real = lax.broadcasted_iota(jnp.int32, (1, IMG_PAD), 1) < IMG_LEN
    for t in range(2):
        bias = jnp.concatenate([brow[t, i:i + 1, :] for i in range(5)], 1)
        p = ((nn(attn_in, w[t, 0, :, :ATT]) + bias) * factor).astype(BF16)
        kept["qkv"][t, r, :] = p
        q, qk, k, v, vx = [p[:, i * BLOCK:(i + 1) * BLOCK] for i in range(5)]
        kq, xv = turn(qk), turn(vx)
        outs = []
        for i, (qq, kk, vv) in enumerate(
                [(jnp.where(low, q, 0), k, v), (jnp.where(low, 0, q), k, v), (jnp.where(low, qk, 0), kq, xv)]):
            s = jnp.where(real, nt(qq, kk), NEGATIVE)
            e = jnp.exp(s - jnp.max(s, -1, keepdims=True))
            pr = (e * (1.0 / jnp.sum(e, -1, keepdims=True))).astype(BF16)
            kept["pr"][n * 6 + t * 3 + i] = pr
            outs.append(nn(pr, vv))
        mixed = jnp.concatenate([outs[2], jnp.where(low, outs[0], outs[1])], 1).astype(BF16)
        kept["mx"][t, r, :] = mixed
        residual = residual + nt(mixed, w[t, 0, :, OUT:MISC])
    xhat, inv = normed(residual)
    mlp_in = (xhat * vec[1:2, :] + vec[4:5, :]).astype(BF16)
    kept["xh2"][r, :] = xhat
    kept["inv2"][r, :] = jnp.broadcast_to(inv, (IMG_PAD, BLOCK))
    kept["min"][r, :] = mlp_in
    out = residual + vec[5:6, :]
    for t in range(2):
        for j in range(2):
            bias = jnp.concatenate([brow[t, 5 + j * 3 + i:6 + j * 3 + i, :] for i in range(3)], 1)
            hidden, slope = gelu_parts(nn(mlp_in, up_at(w, t, j)) + bias)
            c = slice((t * 2 + j) * CHUNK, (t * 2 + j + 1) * CHUNK)
            hidden = hidden.astype(BF16)
            kept["hd"][r, c] = hidden
            kept["sl"][r, c] = slope.astype(BF16)
            out = out + nt(hidden, down_at(w, t, j))
    out_ref[r, :] = (out * valid_rows(sc, n)).astype(BF16)


def rsum(a):
    return jnp.sum(a, 0, keepdims=True)


def backward_mlp(n, sc, u_ref, w, vec, kept, grad, sums, bsum):
    r = image_rows(n)

    masked = u_ref[r, :].astype(F32) * valid_rows(sc, n)
    sums[5:6, :] += rsum(masked)
    dg = masked.astype(BF16)
    grad["dg"][r, :] = dg
    mg = jnp.zeros(masked.shape, F32)
    for t in range(2):
        for j in range(2):
            c = slice((t * 2 + j) * CHUNK, (t * 2 + j + 1) * CHUNK)
            up = nn(dg, down_at(w, t, j)) * kept["sl"][r, c].astype(F32)
            up = up.astype(BF16)
            grad["up"][r, c] = up
            total = rsum(up.astype(F32))
            for i in range(3):
                bsum[t, 5 + j * 3 + i:6 + j * 3 + i, :] += total[:, i * BLOCK:(i + 1) * BLOCK]
            mg = mg + nt(up, up_at(w, t, j))
    xhat = kept["xh2"][r, :]
    sums[4:5, :] += rsum(mg)
    sums[1:2, :] += rsum(mg * xhat)
    res = masked + norm_back(mg, xhat, kept["inv2"][r, :1], vec[1:2, :])
    sums[3:4, :] += rsum(res)
    grad["res"][r, :] = res


def backward_attention(n, w, vec, in_ref, kept, grad, sums, bsum):
    r = image_rows(n)
    res = grad["res"][r, :]
    ag = res.astype(BF16)
    grad["ag"][r, :] = ag
    low = low_lanes()
    ig = jnp.zeros(res.shape, F32)
    for t in range(2):
        xg = nn(ag, w[t, 0, :, OUT:MISC]).astype(BF16)
        gx = jnp.where(low, 0, xg[:, :BLOCK])
        g = xg[:, BLOCK:]
        p = kept["qkv"][t, r, :]
        q, qk, k, v, vx = [p[:, i * BLOCK:(i + 1) * BLOCK] for i in range(5)]
        kq, xv = turn(qk), turn(vx)
        dq, dk, dv = [], [], []
        for i, (qq, kk, vv, gm, gg) in enumerate(
                [(q, k, v, jnp.where(low, g, 0), g), (q, k, v, jnp.where(low, 0, g), g), (qk, kq, xv, gx, turn(gx))]):
            pb = kept["pr"][n * 6 + t * 3 + i]
            pf = pb.astype(F32)
            dp = nt(gm, vv)
            ds = (pf * (dp - jnp.sum(pf * dp, -1, keepdims=True))).astype(BF16)
            dv.append(tn(pb, gg))
            dq.append(nn(ds, kk) * SCALE)
            dk.append(tn(ds, kq if i == 2 else qq))
        blocks = [
            jnp.where(low, dq[0], dq[1]), jnp.where(low, dq[2], dk[2]), jnp.where(low, dk[0], dk[1]),
            jnp.where(low, dv[0], dv[1]), dv[2],
        ]
        d = jnp.concatenate(blocks, 1).astype(BF16)
        grad["dqkv"][t, r, :] = d
        total = rsum(d.astype(F32))
        for i in range(5):
            bsum[t, i:i + 1, :] += total[:, i * BLOCK:(i + 1) * BLOCK]
        ig = ig + nt(d, w[t, 0, :, :ATT])
    xhat = kept["xh1"][r, :]
    sums[2:3, :] += rsum(ig)
    sums[0:1, :] += rsum(ig * xhat)
    in_ref[r, :] = res + norm_back(ig, xhat, kept["inv1"][r, :1], vec[0:1, :])


def weight_grads(t, piece, kept, grad, g):
    ag, dg = grad["ag"][...], grad["dg"][...]
    ain, mlp_in = kept["ain"][...], kept["min"][...]
    width = ag.shape[1]
    high = jnp.where(low_lanes(), 0.0, 1.0)
    d = grad["dqkv"][t]
    g[0, :, :OUT] = tn(ain, d[:, :OUT]).astype(BF16)
    out = tn(ag, kept["mx"][t])
    g[0, :, OUT:ATT] = (tn(ain, d[:, OUT:]) + out[:, :BLOCK] * high).astype(BF16)
    g[0, :, ATT:MISC] = out[:, BLOCK:].astype(BF16)
    sums = jnp.concatenate([grad["sums"][...], jnp.zeros((BLOCK - 8, width), F32)], 0)
    g[0, :, MISC:UP0] = sums.T.astype(BF16)
    for j in range(2):
        c = pl.ds(pl.multiple_of((t * 2 + j) * CHUNK, BLOCK), CHUNK)
        up = tn(mlp_in, grad["up"][:, c]).astype(BF16)
        if j == 0:
            g[0, :, UP0:] = up
        else:
            g[1, :, :CHUNK] = up
        g[1, :, DOWN + j * CHUNK:DOWN + (j + 1) * CHUNK] = tn(dg, kept["hd"][:, c]).astype(BF16)
    if piece % 16 == 0:
        rows = jnp.concatenate([grad["bsum"][t], jnp.zeros((piece - 16, BLOCK), F32)], 0).astype(BF16)
        for i in range(width // piece):
            g[1, i * piece:(i + 1) * piece, ROWSB:] = rows


def kept_shapes(total, width, ff):
    images = total // IMG_PAD
    return dict(
        xh1=((total, width), F32), inv1=((total, BLOCK), F32), ain=((total, width), BF16), qkv=((2, total, ATT), BF16),
        pr=((images * 6, IMG_PAD, IMG_PAD), BF16), mx=((2, total, 2 * BLOCK), BF16), xh2=((total, width), F32),
        inv2=((total, BLOCK), F32), min=((total, width), BF16), sl=((total, ff), BF16), hd=((total, ff), BF16))


def grad_shapes(total, width, ff):
    return dict(dg=((total, width), BF16), up=((total, ff), BF16), res=((total, width), F32), sums=((8, width), F32),
                bsum=((2, 16, BLOCK), F32), ag=((total, width), BF16), dqkv=((2, total, ATT), BF16))


def layer_call(phases, sources, load, store, out_shapes, scalars, given, total, width, ff, piece):
    ks = kept_shapes(total, width, ff)
    gs = grad_shapes(total, width, ff)
    weights = ["ain", "mx", "min", "hd"] + [n for n in gs if n != "res"]
    need = {"forward": ["x"], "back": ["u"] + list(ks), "theirs": weights, "mine": weights}
    gives = {"forward": {"out": ((total, width), BF16), **ks}, "back": {"in": ((total, width), F32), **gs},
             "theirs": {}, "mine": {}}
    made = {}
    for p in phases:
        made.update(gives[p])
    inputs = list(dict.fromkeys(n for p in phases for n in need[p] if n not in made))
    if phases[-1] == "forward":
        shown = list(made)
    else:
        shown = [n for n in made if n in weights or n in ("out", "in")]
    inner = [n for n in made if n not in shown]
    side = {"theirs": 0, "mine": 1}.get(phases[-1])
    products = phases[0] != "mine"
    vmem = pl.BlockSpec(memory_space=pltpu.VMEM)
    anywhere = pl.BlockSpec(memory_space=pl.ANY)
    ends = [] if side is None else out_shapes[side]
    scratch = [pltpu.SemaphoreType.DMA] + [pltpu.VMEM(*made[n]) for n in inner]
    if products:
        scratch += [pltpu.VMEM((2, 2, width, HALF), BF16), pltpu.VMEM((8, width), F32), pltpu.VMEM((2, 16, BLOCK), F32)]
    if ends:
        scratch.append(pltpu.VMEM((2, width, HALF), BF16))

    def body(*refs):
        refs = list(refs)

        def take(n):
            got = refs[:n]
            del refs[:n]
            return got

        sc = take(1)[0]
        at = dict(zip(inputs, take(len(inputs))))
        src = take(len(sources))
        at.update(zip(shown, take(len(shown))))
        dst = take(len(ends))
        sem = take(1)[0]
        at.update(zip(inner, take(len(inner))))
        if products:
            w, vec, brow = take(3)
            copies = load(sc, src, w, sem)
            for c in copies:
                c.start()
            for c in copies:
                c.wait()
            vec[...] = w[0, 0, :, MISC:UP0].astype(F32).T[:8, :]
            for t in range(2):
                brow[t] = w[t, 1, :16, ROWSB:].astype(F32)
        if "forward" in phases:
            def step(n, carry):
                forward_image(n, sc, at["x"], w, vec, brow, at["out"], at)
                return carry
            lax.fori_loop(0, total // IMG_PAD, step, 0)
        if "back" in phases:
            sums, bsum = at["sums"], at["bsum"]
            sums[...] = jnp.zeros_like(sums)
            bsum[...] = jnp.zeros_like(bsum)

            def back(n, carry):
                backward_mlp(n, sc, at["u"], w, vec, at, at, sums, bsum)
                backward_attention(n, w, vec, at["in"], at, at, sums, bsum)
                return carry
            lax.fori_loop(0, total // IMG_PAD, back, 0)
        if ends:
            g = take(1)[0]
            t = jnp.where(sc[1] == 0, 1 - side, side)
            weight_grads(t, piece, at, at, g)
            copies = store(sc, side, g, dst, sem)
            for c in copies:
                c.start()
            for c in copies:
                c.wait()

    outs = [made[n] for n in shown] + ends
    args = [scalars, *[given[n] for n in inputs], *(sources if products else [])]
    if not products:
        sources = []
    got = pl.pallas_call(
        body,
        out_shape=[jax.ShapeDtypeStruct(*o) for o in outs],
        in_specs=[pl.BlockSpec(memory_space=pltpu.SMEM)] + [vmem] * len(inputs) + [anywhere] * len(sources),
        out_specs=[vmem] * (len(outs) - len(ends)) + [anywhere] * len(ends),
        scratch_shapes=scratch,
        compiler_params=pltpu.CompilerParams(vmem_limit_bytes=56 * 2 ** 20),
        cost_estimate=pl.CostEstimate(flops=COST * len(phases), transcendentals=0, bytes_accessed=2 ** 23),
    )(*args)
    got = list(got)
    res = dict(zip(shown, got))
    res["g"] = got[len(shown):]
    return res


def shards(tokens, image_counts, cotangent, norm_gains, row_biases, qkv_weight, qv_bias, out_weight,
           up_weight, up_bias, down_weight):
    sec = lax.axis_index("section")
    dp = lax.axis_index("dp")
    ten = lax.axis_index("tensor")
    n_dp = lax.axis_size("dp")
    m = n_dp // 2
    zi, yi = dp // 2, dp % 2
    local_rows, width = tokens.shape[1:]
    images = local_rows * n_dp // IMG_LEN
    piece = width // n_dp
    ff = 2 * up_weight.shape[2]
    direct = piece % 16 == 0

    def pt(a):
        return lax.ppermute(a, "tensor", [(0, 1), (1, 0)])

    def px(a):
        return lax.ppermute(a, "section", [(0, 1), (1, 0)])

    def py(a):
        return lax.ppermute(a, "dp", [(i, i ^ 1) for i in range(n_dp)])

    def pd(a):
        return lax.ppermute(a, ("section", "dp"), [(i, (i + n_dp) % (2 * n_dp) ^ 1) for i in range(2 * n_dp)])

    def pz(a, k):
        return lax.ppermute(a, "dp", [(2 * z + y, 2 * ((z + k) % m) + y) for z in range(m) for y in range(2)])

    def after(a, *b):
        return lax.optimization_barrier((a, *b))

    def plus(*a):
        return sum(b.astype(F32) for b in a)

    def add_pair(g, got):
        keep, to_y, to_x, to_d = [plus(a, b) for a, b in zip(g, (got[0, 0], got[0, 1], got[1, 0], got[1, 1]))]
        return [keep, to_y.astype(BF16), to_x.astype(BF16), to_d.astype(BF16)]

    def across(sent):
        return [sent[0], py(sent[1]), px(sent[2]), pd(sent[3])]

    def along(quad):
        quad = plus(*quad)
        low = quad.astype(BF16)
        return plus(quad[0], *[pz(low[kk], kk) for kk in range(1, m)])

    def pn(a, flip):
        other = n_dp if flip else 0
        pairs = [(i, (i + other) % (2 * n_dp) + 1) for i in range(2 * n_dp) if i % n_dp < n_dp - 1]
        return lax.ppermute(a, ("section", "dp"), pairs)

    def send_rows(a0, a1):
        keep, give = jnp.where(sec == 0, a0, a1), jnp.where(sec == 0, a1, a0)
        tail = select[:, local_rows:]
        tails = [pn(tn(tail, keep).astype(BF16), False), pn(tn(tail, give).astype(BF16), True)]
        return [keep, px(give)] + tails

    def place_rows(keep, got, tail, got_tail):
        def place(a, b):
            a = tn(select[:, :local_rows], a).astype(BF16)
            return jnp.concatenate([a[:IMG_PAD] + b, a[IMG_PAD:]], 0)

        near, far = place(keep, tail), place(got, got_tail)
        return jnp.where(sec == 0, jnp.stack([near, far]), jnp.stack([far, near]))

    batch_tokens = lax.dynamic_index_in_dim(tokens, sec, 0, keepdims=False)
    batch_cot = lax.dynamic_index_in_dim(cotangent, sec, 0, keepdims=False)
    count = lax.dynamic_index_in_dim(image_counts, sec, 0, keepdims=False)
    first = jnp.minimum((dp * local_rows + IMG_LEN - 1) // IMG_LEN, images)
    last = jnp.minimum(((dp + 1) * local_rows + IMG_LEN - 1) // IMG_LEN, images)
    held = last - first
    slots = -(-(-(-local_rows // IMG_LEN)) // 2)
    lower = held // 2
    own_first = jnp.where(ten == 0, first, first + lower)
    own_count = jnp.where(ten == 0, lower, held - lower)
    total = slots * IMG_PAD
    row = lax.broadcasted_iota(jnp.int32, (total, 1), 0)
    slot, inside = row // IMG_PAD, row % IMG_PAD
    exists = (inside < IMG_LEN) & (slot < own_count)
    target = (own_first + slot) * IMG_LEN + inside - dp * local_rows
    canvas_rows = local_rows + IMG_PAD
    select = ((lax.broadcasted_iota(jnp.int32, (total, canvas_rows), 1) == target) & exists).astype(BF16)
    scalars = jnp.stack([jnp.minimum(own_count, jnp.maximum(count - own_first, 0)), ten, sec, zi, yi]).astype(jnp.int32)

    both = jnp.stack([batch_tokens, batch_cot])
    halo = lax.ppermute(both[:, :IMG_PAD], "dp", [(i + 1, i) for i in range(n_dp - 1)])
    q, k, v = [[qkv_weight[0, :, i, h * HD:(h + 1) * HD] for h in range(3)] for i in range(3)]
    o = out_weight[0].T
    o = [o[:, h * HD:(h + 1) * HD] for h in range(3)]
    misc = jnp.concatenate([norm_gains[0], row_biases[0]], 0).T
    misc = jnp.pad(misc, ((0, 0), (0, BLOCK - misc.shape[1])))
    gap = jnp.zeros((HD,), BF16)
    rows = jnp.concatenate([qv_bias[0, 0], gap, gap, gap, qv_bias[0, 1], gap, up_bias[0]]).reshape(-1, BLOCK)
    rows = jnp.pad(rows, ((0, piece - rows.shape[0]), (0, 0)))
    up, down = up_weight[0], down_weight[0].T
    part0 = jnp.concatenate(
        [q[0], q[1], q[2], k[2], k[0], k[1], v[0], v[1], v[2], o[2], o[0], o[1], misc, up[:, :CHUNK]], 1)
    part1 = jnp.concatenate([up[:, CHUNK:], down, rows], 1)

    if direct:
        keep = jnp.where(sec == 0, part0, part1)
        give = jnp.where(sec == 0, part1, part0)
        got, halo = after(px(give), halo)
        start = [jnp.where(sec == 0, keep, got), jnp.where(sec == 0, got, keep)]

        def load(l, sc, src, w, sem):
            copies = []
            for side in range(2):
                t = jnp.where(sc[1] == 0, side, 1 - side)
                own = src[side * 8:side * 8 + 8]
                for kk in range(m):
                    z = lax.rem(sc[3] - kk + m, m)
                    near = pl.ds(pl.multiple_of((2 * z + sc[4]) * piece, 16), piece)
                    far = pl.ds(pl.multiple_of((2 * z + 1 - sc[4]) * piece, 16), piece)
                    for i, (h, r) in enumerate(((sc[2], near), (1 - sc[2], near), (sc[2], far), (1 - sc[2], far))):
                        a = own[i].at[l] if kk == 0 else own[4 + i].at[kk - 1]
                        copies.append(pltpu.make_async_copy(a, w.at[t, h, r, :], sem))
            return copies

        def store(sc, side, g, dst, sem):
            copies = []
            for hr in range(2):
                h = jnp.where(sc[2] == 0, hr, 1 - hr)
                for yr in range(2):
                    y = jnp.where(sc[4] == 0, yr, 1 - yr)
                    for kk in range(m):
                        z = lax.rem(sc[3] + kk, m)
                        r = pl.ds(pl.multiple_of((2 * z + y) * piece, 16), piece)
                        out = dst[0].at[hr, yr, kk] if side == 0 else dst[hr * 2 + yr].at[kk]
                        copies.append(pltpu.make_async_copy(g.at[h, r, :], out, sem))
            return copies

        out_shapes = [[((2, 2, m, piece, HALF), BF16)], [((m, piece, HALF), BF16)] * 4]
        own = jnp.stack(start)
        firsts = [own, px(own), py(own), pd(own)]
        columns = [jnp.stack([pz(start[0], kk) for kk in range(1, m)])]
        columns[0], start[1], *firsts = after(columns[0], start[1], *firsts)
        columns.append(jnp.stack([pz(start[1], kk) for kk in range(1, m)]))
        rest = [columns[0], px(columns[0]), py(columns[0]), pd(columns[0])]
        columns[1], *rest = after(columns[1], *rest)
        twins = [pt(a) for a in firsts]
        sources = [firsts + rest + twins + [pt(a) for a in rest]]
        sources.append(columns[1:] + [px(columns[1]), py(columns[1]), pd(columns[1])])
    else:
        def load(l, sc, src, w, sem):
            return [pltpu.make_async_copy(src[0], w, sem)]

        def store(sc, side, g, dst, sem):
            return [pltpu.make_async_copy(g, dst[0], sem)]

        out_shapes = [[((2, width, HALF), BF16)]] * 2
        a = lax.all_gather(jnp.stack([part0, part1]), "dp", axis=1, tiled=True)
        a = lax.all_gather(lax.all_gather(a, "tensor"), "section")
        sources = [[a[0]], [a[1]]]

    batch = jnp.concatenate([both, halo], 1)
    x0 = nn(select, batch[0]).astype(BF16)
    cot = nn(select, batch[1]).astype(BF16)

    def call(l, phases, **given):
        return layer_call(phases, sources[l], functools.partial(load, l), store, out_shapes, scalars, given, total,
                          width, ff, piece)

    r0 = call(0, ["forward"], x=x0)
    low0 = r0["out"]
    if direct:
        low0, *rest = after(low0, *sources[1])
        sources[1] = firsts + rest + twins + [pt(a) for a in rest]
    r1 = call(1, ["forward", "back", "theirs"], x=low0, u=cot)
    if direct:
        got1 = pt(r1["g"][0])
    rows = send_rows(low0, r1["out"])
    m1 = call(1, ["mine"], **r1)
    if direct:
        first, got1, *rows = after(m1["g"][0], got1, *rows)
        sent1 = add_pair([first] + m1["g"][1:], got1)
        u, *sent1 = after(r1["in"], *sent1)
        quad1 = across(sent1)
    else:
        u = r1["in"]
    placed = place_rows(*rows)
    b0 = call(0, ["back", "theirs"], **{**r0, "u": u})
    if direct:
        b0["dg"], b0["g"][0], placed, *quad1 = after(b0["dg"], b0["g"][0], placed, *quad1)
        got0 = pt(b0["g"][0])
    layer_outputs = (placed + pt(placed))[None]
    rows = send_rows(b0["in"].astype(BF16), r1["in"].astype(BF16))
    m0 = call(0, ["mine"], **{**r0, **b0})

    if direct:
        first, got0 = after(m0["g"][0], got0)
        sent0 = add_pair([first] + m0["g"][1:], got0)
        rows[0], *sent0 = after(rows[0], *sent0)
        placed = place_rows(*rows)
        other_core, *quad0 = after(pt(placed), *across(sent0))
        done = [along(quad1), along(quad0)]
        mine = jnp.where(sec == 0, done[1], done[0])
        other = px(jnp.where(sec == 0, done[0], done[1]).astype(BF16)).astype(F32)
        final0 = jnp.where(sec == 0, mine, other)
        final1 = jnp.where(sec == 0, other, mine)
        small = final1[:, ROWSB:]
    else:
        placed = place_rows(*rows)
        other_core = pt(placed)

        def by_core(a, b):
            return jnp.where(ten == 0, jnp.stack([b, a]), jnp.stack([a, b]))

        g = jnp.stack([by_core(b0["g"][0], m0["g"][0]), by_core(r1["g"][0], m1["g"][0])])
        g = lax.psum_scatter(g.astype(F32), "section", scatter_dimension=0)
        g = lax.psum_scatter(g, "tensor", scatter_dimension=0)
        g = lax.psum_scatter(g, "dp", scatter_dimension=1, tiled=True)
        final0, final1 = g[0], g[1]
        small = lax.psum(jnp.stack([b0["bsum"], r1["bsum"]]), ("section", "tensor", "dp"))
        small = lax.dynamic_index_in_dim(lax.dynamic_index_in_dim(small, sec, 0, False), ten, 0, False)

    input_grads = (placed + other_core).astype(F32)[None]

    def heads(*starts):
        return [final0[:, s * HD:(s + 1) * HD] for s in starts]

    small = small.reshape(-1)
    qkv = jnp.concatenate(heads(0, 1, 2, 4, 5, 3, 6, 7, 8), 1).reshape(1, piece, 3, 3 * HD)
    return (
        layer_outputs,
        input_grads,
        final0[:, MISC:MISC + 2].T[None],
        final0[:, MISC + 2:MISC + 6].T[None],
        qkv,
        jnp.stack([small[:3 * HD], small[6 * HD:9 * HD]])[None],
        jnp.concatenate(heads(10, 11, 9), 1).T[None],
        jnp.concatenate([final0[:, UP0:], final1[:, :DOWN]], 1)[None],
        small[ATT:ATT + ff // 2][None],
        final1[:, DOWN:ROWSB].T[None],
    )


def solution(mesh):
    in_specs = (
        P(None, "dp", None),
        P(),
        P(None, "dp", None),
        P("section", None, "dp"),
        P("section", None, "dp"),
        P("section", "dp", None, "tensor"),
        P("section", None, "tensor"),
        P("section", "tensor", "dp"),
        P("section", "dp", "tensor"),
        P("section", "tensor"),
        P("section", "tensor", "dp"),
    )
    out_specs = (
        P("section", None, "dp", None),
        P("section", None, "dp", None),
        P("section", None, "dp"),
        P("section", None, "dp"),
        P("section", "dp", None, "tensor"),
        P("section", None, "tensor"),
        P("section", "tensor", "dp"),
        P("section", "dp", "tensor"),
        P("section", "tensor"),
        P("section", "tensor", "dp"),
    )
    return jax.shard_map(shards, mesh=mesh, in_specs=in_specs, out_specs=out_specs, check_vma=False)
```

```python
import functools
import math

import jax
import jax.numpy as jnp
from jax import lax
from jax.experimental import pallas as pl
from jax.experimental.pallas import tpu as pltpu
from jax.sharding import PartitionSpec as P

IMG_LEN = 197
IMG_PAD = 208
HD = 64
EPSILON = 1e-06
NEGATIVE = -1e30
F32 = jnp.float32
BF16 = jnp.bfloat16
BLOCK = 128
HALF = 1280
COST = 10 ** 10
SCALE = 1.0 / math.sqrt(HD)


def mm(a, b, dims):
    return lax.dot_general(a, b, (dims, ((), ())), preferred_element_type=F32)


def nn(a, b):
    return mm(a, b, ((1,), (0,)))


def nt(a, b):
    return mm(a, b, ((1,), (1,)))


def tn(a, b):
    return mm(a, b, ((0,), (0,)))


def normed(x):
    centred = x - jnp.mean(x, -1, keepdims=True)
    inverse = lax.rsqrt(jnp.mean(centred * centred, -1, keepdims=True) + EPSILON)
    return centred * inverse, inverse


def norm_back(grad, xhat, inverse, gain):
    t = grad * gain
    return inverse * (
        t - jnp.mean(t, -1, keepdims=True) - xhat * jnp.mean(t * xhat, -1, keepdims=True)
    )


def gelu_parts(u):
    cdf = 0.5 * (1.0 + lax.erf(u * math.sqrt(0.5)))
    pdf = jnp.exp(-0.5 * u * u) * (1.0 / math.sqrt(2.0 * math.pi))
    return u * cdf, cdf + u * pdf


ATT = 640
OUT = 512
MISC = 768
UP0 = 896
DOWN = 384
ROWSB = 1152
CHUNK = 384


def up_at(w, t, j):
    return w[t, 0, :, UP0:] if j == 0 else w[t, 1, :, :CHUNK]


def down_at(w, t, j):
    return w[t, 1, :, DOWN + j * CHUNK:DOWN + (j + 1) * CHUNK]


def low_lanes():
    return lax.broadcasted_iota(jnp.int32, (1, BLOCK), 1) < HD


def turn(a):
    return jnp.concatenate([a[:, HD:], a[:, :HD]], 1)


def valid_rows(sc, n):
    row = lax.broadcasted_iota(jnp.int32, (IMG_PAD, 1), 0)
    return jnp.where((row < IMG_LEN) & (n < sc[0]), 1.0, 0.0)


def image_rows(n):
    return pl.ds(pl.multiple_of(n * IMG_PAD, 16), IMG_PAD)


def forward_image(n, sc, x_ref, w, vec, brow, out_ref, kept):
    r = image_rows(n)
    x = x_ref[r, :].astype(F32)
    xhat, inv = normed(x)
    attn_in = (xhat * vec[0:1, :] + vec[2:3, :]).astype(BF16)
    kept["xh1"][r, :] = xhat
    kept["inv1"][r, :] = jnp.broadcast_to(inv, (IMG_PAD, BLOCK))
    kept["ain"][r, :] = attn_in
    residual = x + vec[3:4, :]
    low = low_lanes()
    lane = lax.broadcasted_iota(jnp.int32, (1, ATT), 1)
    factor = jnp.where(lane < 192, SCALE, jnp.where(lane < 576, 1.0, 0.0))
    real = lax.broadcasted_iota(jnp.int32, (1, IMG_PAD), 1) < IMG_LEN
    for t in range(2):
        bias = jnp.concatenate([brow[t, i:i + 1, :] for i in range(5)], 1)
        p = ((nn(attn_in, w[t, 0, :, :ATT]) + bias) * factor).astype(BF16)
        kept["qkv"][t, r, :] = p
        q, qk, k, v, vx = [p[:, i * BLOCK:(i + 1) * BLOCK] for i in range(5)]
        kq, xv = turn(qk), turn(vx)
        outs = []
        for i, (qq, kk, vv) in enumerate(
                [(jnp.where(low, q, 0), k, v), (jnp.where(low, 0, q), k, v), (jnp.where(low, qk, 0), kq, xv)]):
            s = jnp.where(real, nt(qq, kk), NEGATIVE)
            e = jnp.exp(s - jnp.max(s, -1, keepdims=True))
            pr = (e * (1.0 / jnp.sum(e, -1, keepdims=True))).astype(BF16)
            kept["pr"][n * 6 + t * 3 + i] = pr
            outs.append(nn(pr, vv))
        mixed = jnp.concatenate([outs[2], jnp.where(low, outs[0], outs[1])], 1).astype(BF16)
        kept["mx"][t, r, :] = mixed
        residual = residual + nt(mixed, w[t, 0, :, OUT:MISC])
    xhat, inv = normed(residual)
    mlp_in = (xhat * vec[1:2, :] + vec[4:5, :]).astype(BF16)
    kept["xh2"][r, :] = xhat
    kept["inv2"][r, :] = jnp.broadcast_to(inv, (IMG_PAD, BLOCK))
    kept["min"][r, :] = mlp_in
    out = residual + vec[5:6, :]
    for t in range(2):
        for j in range(2):
            bias = jnp.concatenate([brow[t, 5 + j * 3 + i:6 + j * 3 + i, :] for i in range(3)], 1)
            hidden, slope = gelu_parts(nn(mlp_in, up_at(w, t, j)) + bias)
            c = slice((t * 2 + j) * CHUNK, (t * 2 + j + 1) * CHUNK)
            hidden = hidden.astype(BF16)
            kept["hd"][r, c] = hidden
            kept["sl"][r, c] = slope.astype(BF16)
            out = out + nt(hidden, down_at(w, t, j))
    out_ref[r, :] = (out * valid_rows(sc, n)).astype(BF16)


def rsum(a):
    return jnp.sum(a, 0, keepdims=True)


def backward_mlp(n, sc, u_ref, w, vec, kept, grad, sums, bsum):
    r = image_rows(n)

    masked = u_ref[r, :].astype(F32) * valid_rows(sc, n)
    sums[5:6, :] += rsum(masked)
    dg = masked.astype(BF16)
    grad["dg"][r, :] = dg
    mg = jnp.zeros(masked.shape, F32)
    for t in range(2):
        for j in range(2):
            c = slice((t * 2 + j) * CHUNK, (t * 2 + j + 1) * CHUNK)
            up = nn(dg, down_at(w, t, j)) * kept["sl"][r, c].astype(F32)
            up = up.astype(BF16)
            grad["up"][r, c] = up
            total = rsum(up.astype(F32))
            for i in range(3):
                bsum[t, 5 + j * 3 + i:6 + j * 3 + i, :] += total[:, i * BLOCK:(i + 1) * BLOCK]
            mg = mg + nt(up, up_at(w, t, j))
    xhat = kept["xh2"][r, :]
    sums[4:5, :] += rsum(mg)
    sums[1:2, :] += rsum(mg * xhat)
    res = masked + norm_back(mg, xhat, kept["inv2"][r, :1], vec[1:2, :])
    sums[3:4, :] += rsum(res)
    grad["res"][r, :] = res


def backward_attention(n, w, vec, in_ref, kept, grad, sums, bsum):
    r = image_rows(n)
    res = grad["res"][r, :]
    ag = res.astype(BF16)
    grad["ag"][r, :] = ag
    low = low_lanes()
    ig = jnp.zeros(res.shape, F32)
    for t in range(2):
        xg = nn(ag, w[t, 0, :, OUT:MISC]).astype(BF16)
        gx = jnp.where(low, 0, xg[:, :BLOCK])
        g = xg[:, BLOCK:]
        p = kept["qkv"][t, r, :]
        q, qk, k, v, vx = [p[:, i * BLOCK:(i + 1) * BLOCK] for i in range(5)]
        kq, xv = turn(qk), turn(vx)
        dq, dk, dv = [], [], []
        for i, (qq, kk, vv, gm, gg) in enumerate(
                [(q, k, v, jnp.where(low, g, 0), g), (q, k, v, jnp.where(low, 0, g), g), (qk, kq, xv, gx, turn(gx))]):
            pb = kept["pr"][n * 6 + t * 3 + i]
            pf = pb.astype(F32)
            dp = nt(gm, vv)
            ds = (pf * (dp - jnp.sum(pf * dp, -1, keepdims=True))).astype(BF16)
            dv.append(tn(pb, gg))
            dq.append(nn(ds, kk) * SCALE)
            dk.append(tn(ds, kq if i == 2 else qq))
        blocks = [
            jnp.where(low, dq[0], dq[1]), jnp.where(low, dq[2], dk[2]), jnp.where(low, dk[0], dk[1]),
            jnp.where(low, dv[0], dv[1]), dv[2],
        ]
        d = jnp.concatenate(blocks, 1).astype(BF16)
        grad["dqkv"][t, r, :] = d
        total = rsum(d.astype(F32))
        for i in range(5):
            bsum[t, i:i + 1, :] += total[:, i * BLOCK:(i + 1) * BLOCK]
        ig = ig + nt(d, w[t, 0, :, :ATT])
    xhat = kept["xh1"][r, :]
    sums[2:3, :] += rsum(ig)
    sums[0:1, :] += rsum(ig * xhat)
    in_ref[r, :] = res + norm_back(ig, xhat, kept["inv1"][r, :1], vec[0:1, :])


def weight_grads(t, piece, kept, grad, g):
    ag, dg = grad["ag"][...], grad["dg"][...]
    ain, mlp_in = kept["ain"][...], kept["min"][...]
    width = ag.shape[1]
    high = jnp.where(low_lanes(), 0.0, 1.0)
    d = grad["dqkv"][t]
    g[0, :, :OUT] = tn(ain, d[:, :OUT]).astype(BF16)
    out = tn(ag, kept["mx"][t])
    g[0, :, OUT:ATT] = (tn(ain, d[:, OUT:]) + out[:, :BLOCK] * high).astype(BF16)
    g[0, :, ATT:MISC] = out[:, BLOCK:].astype(BF16)
    sums = jnp.concatenate([grad["sums"][...], jnp.zeros((BLOCK - 8, width), F32)], 0)
    g[0, :, MISC:UP0] = sums.T.astype(BF16)
    for j in range(2):
        c = pl.ds(pl.multiple_of((t * 2 + j) * CHUNK, BLOCK), CHUNK)
        up = tn(mlp_in, grad["up"][:, c]).astype(BF16)
        if j == 0:
            g[0, :, UP0:] = up
        else:
            g[1, :, :CHUNK] = up
        g[1, :, DOWN + j * CHUNK:DOWN + (j + 1) * CHUNK] = tn(dg, kept["hd"][:, c]).astype(BF16)
    if piece % 16 == 0:
        rows = jnp.concatenate([grad["bsum"][t], jnp.zeros((piece - 16, BLOCK), F32)], 0).astype(BF16)
        for i in range(width // piece):
            g[1, i * piece:(i + 1) * piece, ROWSB:] = rows


def kept_shapes(total, width, ff):
    images = total // IMG_PAD
    return dict(
        xh1=((total, width), F32), inv1=((total, BLOCK), F32), ain=((total, width), BF16), qkv=((2, total, ATT), BF16),
        pr=((images * 6, IMG_PAD, IMG_PAD), BF16), mx=((2, total, 2 * BLOCK), BF16), xh2=((total, width), F32),
        inv2=((total, BLOCK), F32), min=((total, width), BF16), sl=((total, ff), BF16), hd=((total, ff), BF16))


def grad_shapes(total, width, ff):
    return dict(dg=((total, width), BF16), up=((total, ff), BF16), res=((total, width), F32), sums=((8, width), F32),
                bsum=((2, 16, BLOCK), F32), ag=((total, width), BF16), dqkv=((2, total, ATT), BF16))


def layer_call(phases, sources, load, store, out_shapes, scalars, given, total, width, ff, piece):
    ks = kept_shapes(total, width, ff)
    gs = grad_shapes(total, width, ff)
    weights = ["ain", "mx", "min", "hd"] + [n for n in gs if n != "res"]
    need = {"forward": ["x"], "back": ["u"] + list(ks), "theirs": weights, "mine": weights}
    gives = {"forward": {"out": ((total, width), BF16), **ks}, "back": {"keep": ((total, width), BF16), "give": ((total, width), BF16), "in": ((total, width), F32), **gs},
             "theirs": {}, "mine": {}}
    made = {}
    for p in phases:
        made.update(gives[p])
    inputs = list(dict.fromkeys(n for p in phases for n in need[p] if n not in made))
    if phases[-1] == "forward":
        shown = list(made)
    else:
        shown = [n for n in made if n in weights or n in ("keep", "give")]
        if "forward" in phases:
            shown.append("in")
    inner = [n for n in made if n not in shown]
    side = {"theirs": 0, "mine": 1}.get(phases[-1])
    products = phases[0] != "mine"
    vmem = pl.BlockSpec(memory_space=pltpu.VMEM)
    anywhere = pl.BlockSpec(memory_space=pl.ANY)
    ends = [] if side is None else out_shapes[side]
    scratch = [pltpu.SemaphoreType.DMA] + [pltpu.VMEM(*made[n]) for n in inner]
    if products:
        scratch += [pltpu.VMEM((2, 2, width, HALF), BF16), pltpu.VMEM((8, width), F32), pltpu.VMEM((2, 16, BLOCK), F32)]
    if ends:
        scratch.append(pltpu.VMEM((2, width, HALF), BF16))

    def body(*refs):
        refs = list(refs)

        def take(n):
            got = refs[:n]
            del refs[:n]
            return got

        sc = take(1)[0]
        at = dict(zip(inputs, take(len(inputs))))
        src = take(len(sources))
        at.update(zip(shown, take(len(shown))))
        dst = take(len(ends))
        sem = take(1)[0]
        at.update(zip(inner, take(len(inner))))
        if products:
            w, vec, brow = take(3)
            copies = load(sc, src, w, sem)
            for c in copies:
                c.start()
            for c in copies:
                c.wait()
            vec[...] = w[0, 0, :, MISC:UP0].astype(F32).T[:8, :]
            for t in range(2):
                brow[t] = w[t, 1, :16, ROWSB:].astype(F32)
        if "forward" in phases:
            def step(n, carry):
                forward_image(n, sc, at["x"], w, vec, brow, at["out"], at)
                return carry
            lax.fori_loop(0, total // IMG_PAD, step, 0)
        if "back" in phases:
            sums, bsum = at["sums"], at["bsum"]
            sums[...] = jnp.zeros_like(sums)
            bsum[...] = jnp.zeros_like(bsum)

            def back(n, carry):
                backward_mlp(n, sc, at["u"], w, vec, at, at, sums, bsum)
                backward_attention(n, w, vec, at["in"], at, at, sums, bsum)
                return carry
            lax.fori_loop(0, total // IMG_PAD, back, 0)
            rows = [at[n] for n in (("x", "out") if "forward" in phases else ("in", "u"))]
            for here in range(2):
                @pl.when(sc[2] == here)
                def _():
                    at["keep"][...] = rows[here][...].astype(BF16)
                    at["give"][...] = rows[1 - here][...].astype(BF16)
        if ends:
            g = take(1)[0]
            t = jnp.where(sc[1] == 0, 1 - side, side)
            weight_grads(t, piece, at, at, g)
            copies = store(sc, side, g, dst, sem)
            for c in copies:
                c.start()
            for c in copies:
                c.wait()

    outs = [made[n] for n in shown] + ends
    args = [scalars, *[given[n] for n in inputs], *(sources if products else [])]
    if not products:
        sources = []
    got = pl.pallas_call(
        body,
        out_shape=[jax.ShapeDtypeStruct(*o) for o in outs],
        in_specs=[pl.BlockSpec(memory_space=pltpu.SMEM)] + [vmem] * len(inputs) + [anywhere] * len(sources),
        out_specs=[vmem] * (len(outs) - len(ends)) + [anywhere] * len(ends),
        scratch_shapes=scratch,
        compiler_params=pltpu.CompilerParams(vmem_limit_bytes=56 * 2 ** 20),
        cost_estimate=pl.CostEstimate(flops=COST * len(phases), transcendentals=0, bytes_accessed=2 ** 23),
    )(*args)
    got = list(got)
    res = dict(zip(shown, got))
    res["g"] = got[len(shown):]
    return res


def shards(tokens, image_counts, cotangent, norm_gains, row_biases, qkv_weight, qv_bias, out_weight,
           up_weight, up_bias, down_weight):
    sec = lax.axis_index("section")
    dp = lax.axis_index("dp")
    ten = lax.axis_index("tensor")
    n_dp = lax.axis_size("dp")
    m = n_dp // 2
    zi, yi = dp // 2, dp % 2
    local_rows, width = tokens.shape[1:]
    images = local_rows * n_dp // IMG_LEN
    piece = width // n_dp
    ff = 2 * up_weight.shape[2]
    direct = piece % 16 == 0 and m == 4

    def pt(a):
        return lax.ppermute(a, "tensor", [(0, 1), (1, 0)])

    def px(a):
        return lax.ppermute(a, "section", [(0, 1), (1, 0)])

    def py(a):
        return lax.ppermute(a, "dp", [(i, i ^ 1) for i in range(n_dp)])

    def pd(a):
        return lax.ppermute(a, ("section", "dp"), [(i, (i + n_dp) % (2 * n_dp) ^ 1) for i in range(2 * n_dp)])

    def pz(a, k):
        return lax.ppermute(a, "dp", [(2 * z + y, 2 * ((z + k) % m) + y) for z in range(m) for y in range(2)])

    def after(a, *b):
        return lax.optimization_barrier((a, *b))

    def plus(*a):
        return sum(b.astype(F32) for b in a)

    def add_pair(g, got):
        keep, to_y, to_x, to_d = [plus(a, b) for a, b in zip(g, (got[0, 0], got[0, 1], got[1, 0], got[1, 1]))]
        return [keep, to_y.astype(BF16), to_x.astype(BF16), to_d.astype(BF16)]

    def across(sent):
        return [sent[0], py(sent[1]), px(sent[2]), pd(sent[3])]

    def pz_to(a, kk):
        return lax.ppermute(a, "dp", [(i, i ^ (2 * kk)) for i in range(n_dp)])

    def along(quad):
        quad = plus(*quad)
        low = quad.astype(BF16)
        return plus(quad[:, 0], *[pz_to(low[:, kk], kk) for kk in range(1, m)])

    def along_steps(quad):
        quad = plus(*quad)
        got = pz_to(quad[:, 1::2].astype(BF16), 1)
        quad = plus(quad[:, 0::2], got)
        return plus(quad[:, 0], pz_to(quad[:, 1].astype(BF16), 2))

    def pn(a):
        return lax.ppermute(a, ("dp", "tensor"), [(2 * i + 1, 2 * i + 3) for i in range(n_dp - 1)])

    def tails(keep, got):
        tail = select[:, local_rows:]
        return pn(jnp.stack([tn(tail, keep), tn(tail, got)]).astype(BF16))

    def placed(keep, got, tail):
        def place(a, b):
            a = tn(select[:, :local_rows], a).astype(BF16)
            return jnp.concatenate([a[:IMG_PAD] + b, a[IMG_PAD:]], 0)

        return jnp.stack([place(keep, tail[0]), place(got, tail[1])])

    def ordered(a, b):
        a = a + b
        return jnp.where(sec == 0, a, a[::-1])[None]

    batch_tokens = lax.dynamic_index_in_dim(tokens, sec, 0, keepdims=False)
    batch_cot = lax.dynamic_index_in_dim(cotangent, sec, 0, keepdims=False)
    count = lax.dynamic_index_in_dim(image_counts, sec, 0, keepdims=False)
    first = jnp.minimum((dp * local_rows + IMG_LEN - 1) // IMG_LEN, images)
    last = jnp.minimum(((dp + 1) * local_rows + IMG_LEN - 1) // IMG_LEN, images)
    held = last - first
    slots = -(-(-(-local_rows // IMG_LEN)) // 2)
    lower = held // 2
    own_first = jnp.where(ten == 0, first, first + lower)
    own_count = jnp.where(ten == 0, lower, held - lower)
    total = slots * IMG_PAD
    row = lax.broadcasted_iota(jnp.int32, (total, 1), 0)
    slot, inside = row // IMG_PAD, row % IMG_PAD
    exists = (inside < IMG_LEN) & (slot < own_count)
    target = (own_first + slot) * IMG_LEN + inside - dp * local_rows
    canvas_rows = local_rows + IMG_PAD
    select = ((lax.broadcasted_iota(jnp.int32, (total, canvas_rows), 1) == target) & exists).astype(BF16)
    scalars = jnp.stack([jnp.minimum(own_count, jnp.maximum(count - own_first, 0)), ten, sec, zi, yi]).astype(jnp.int32)

    both = jnp.stack([batch_tokens, batch_cot])
    halo = lax.ppermute(both[:, :IMG_PAD], ("dp", "tensor"), [(2 * i + 3, 2 * i + 1) for i in range(n_dp - 1)])
    q, k, v = [[qkv_weight[0, :, i, h * HD:(h + 1) * HD] for h in range(3)] for i in range(3)]
    o = out_weight[0].T
    o = [o[:, h * HD:(h + 1) * HD] for h in range(3)]
    misc = jnp.concatenate([norm_gains[0], row_biases[0]], 0).T
    misc = jnp.pad(misc, ((0, 0), (0, BLOCK - misc.shape[1])))
    gap = jnp.zeros((HD,), BF16)
    rows = jnp.concatenate([qv_bias[0, 0], gap, gap, gap, qv_bias[0, 1], gap, up_bias[0]]).reshape(-1, BLOCK)
    rows = jnp.pad(rows, ((0, piece - rows.shape[0]), (0, 0)))
    up, down = up_weight[0], down_weight[0].T
    part0 = jnp.concatenate(
        [q[0], q[1], q[2], k[2], k[0], k[1], v[0], v[1], v[2], o[2], o[0], o[1], misc, up[:, :CHUNK]], 1)
    part1 = jnp.concatenate([up[:, CHUNK:], down, rows], 1)

    if direct:
        keep = jnp.where(sec == 0, part0, part1)
        give = jnp.where(sec == 0, part1, part0)
        got, halo = after(px(give), halo)
        start = [jnp.where(sec == 0, keep, got), jnp.where(sec == 0, got, keep)]

        def load(l, sc, src, w, sem):
            copies = []
            for side in range(2):
                t = jnp.where(sc[1] == 0, side, 1 - side)
                own = src[side * 8:side * 8 + 8]
                for kk in range(m):
                    z = lax.rem(sc[3] - kk + m, m)
                    near = pl.ds(pl.multiple_of((2 * z + sc[4]) * piece, 16), piece)
                    far = pl.ds(pl.multiple_of((2 * z + 1 - sc[4]) * piece, 16), piece)
                    for i, (h, r) in enumerate(((sc[2], near), (1 - sc[2], near), (sc[2], far), (1 - sc[2], far))):
                        a = own[i].at[l] if kk == 0 else own[4 + i].at[kk - 1]
                        copies.append(pltpu.make_async_copy(a, w.at[t, h, r, :], sem))
            return copies

        def store(sc, side, g, dst, sem):
            copies = []
            for hr in range(2):
                h = jnp.where(sc[2] == 0, hr, 1 - hr)
                for yr in range(2):
                    y = jnp.where(sc[4] == 0, yr, 1 - yr)
                    for kk in range(m):
                        z = lax.bitwise_xor(sc[3], kk)
                        r = pl.ds(pl.multiple_of((2 * z + y) * piece, 16), piece)
                        out = dst[0].at[hr, yr] if side == 0 else dst[hr * 2 + yr]
                        for c in range(2):
                            a = g.at[h, r, c * part:(c + 1) * part]
                            copies.append(pltpu.make_async_copy(a, out.at[c, kk], sem))
            return copies

        part = HALF // 2
        out_shapes = [[((2, 2, 2, m, piece, part), BF16)], [((2, m, piece, part), BF16)] * 4]
        own = jnp.stack(start)
        firsts = [own, px(own), py(own), pd(own)]
        columns = [jnp.stack([pz(start[0], kk) for kk in range(1, m)])]
        rest = [columns[0], px(columns[0]), py(columns[0]), pd(columns[0])]
        start[1], _, *firsts = after(start[1], columns[0], *firsts)
        columns.append(jnp.stack([pz(start[1], kk) for kk in range(1, m)]))
        columns[1], *rest = after(columns[1], *rest)
        twins = [pt(a) for a in firsts]
        sources = [firsts + rest + twins + [pt(a) for a in rest]]
        sources.append(columns[1:] + [px(columns[1]), py(columns[1]), pd(columns[1])])
    else:
        def load(l, sc, src, w, sem):
            return [pltpu.make_async_copy(src[0], w, sem)]

        def store(sc, side, g, dst, sem):
            return [pltpu.make_async_copy(g, dst[0], sem)]

        out_shapes = [[((2, width, HALF), BF16)]] * 2
        a = lax.all_gather(jnp.stack([part0, part1]), "dp", axis=1, tiled=True)
        a = lax.all_gather(lax.all_gather(a, "tensor"), "section")
        sources = [[a[0]], [a[1]]]

    batch = jnp.concatenate([both, halo], 1)
    x0 = nn(select, batch[0]).astype(BF16)
    cot = nn(select, batch[1]).astype(BF16)

    def call(l, phases, **given):
        return layer_call(phases, sources[l], functools.partial(load, l), store, out_shapes, scalars, given, total,
                          width, ff, piece)

    r0 = call(0, ["forward"], x=x0)
    low0 = r0["out"]
    if direct:
        low0, *rest = after(low0, *sources[1])
        sources[1] = firsts + rest + twins + [pt(a) for a in rest]
    r1 = call(1, ["forward", "back", "theirs"], x=low0, u=cot)
    if direct:
        got1 = pt(r1["g"][0])
    low_got = px(r1["give"])
    m1 = call(1, ["mine"], **r1)
    u = r1["in"]
    if direct:
        first, got1, low_got = after(m1["g"][0], got1, low_got)
        sent1 = add_pair([first] + m1["g"][1:], got1)
        low_tails = tails(r1["keep"], low_got)
        u, *sent1 = after(u, *sent1)
        quad1 = across(sent1)
    else:
        low_tails = tails(r1["keep"], low_got)
    b0 = call(0, ["back", "theirs"], **{**r0, "u": u})
    if direct:
        b0["dg"], b0["g"][0], low_tails, *quad1 = after(b0["dg"], b0["g"][0], low_tails, *quad1)
        got0 = pt(b0["g"][0])
    low_rows = placed(r1["keep"], low_got, low_tails)
    low_twin = pt(low_rows)
    in_got = px(b0["give"])
    m0 = call(0, ["mine"], **{**r0, **b0})

    if direct:
        first, got0, in_got, low_twin = after(m0["g"][0], got0, in_got, low_twin)
        sent0 = add_pair([first] + m0["g"][1:], got0)
        both = after(in_got, *sent0, *quad1)
        in_got, sent0, quad1 = both[0], both[1:5], both[5:]
        in_tails = tails(b0["keep"], in_got)
        quad0 = [across([a[c:c + 1] for a in sent0]) for c in range(2)]
        in_rows = placed(b0["keep"], in_got, in_tails)
        in_twin, *quad0[1] = after(pt(in_rows), *quad0[1])
        done1 = along_steps(quad1)
        done0 = [along_steps(quad0[0])]
        done1, done0[0], *quad0[1] = after(done1, done0[0], *quad0[1])
        done0 = jnp.concatenate(done0 + [along(quad0[1])])
        mine = jnp.where(sec == 0, done0, done1)
        other = px(jnp.where(sec == 0, done1, done0).astype(BF16)).astype(F32)
        final0 = jnp.where(sec == 0, mine, other)
        final1 = jnp.where(sec == 0, other, mine)
        final0, final1 = [jnp.concatenate([a[0], a[1]], 1) for a in (final0, final1)]
        small = final1[:, ROWSB:]
    else:
        in_rows = placed(b0["keep"], in_got, tails(b0["keep"], in_got))
        in_twin = pt(in_rows)

        def by_core(a, b):
            return jnp.where(ten == 0, jnp.stack([b, a]), jnp.stack([a, b]))

        g = jnp.stack([by_core(b0["g"][0], m0["g"][0]), by_core(r1["g"][0], m1["g"][0])])
        g = lax.psum_scatter(g.astype(F32), "section", scatter_dimension=0)
        g = lax.psum_scatter(g, "tensor", scatter_dimension=0)
        g = lax.psum_scatter(g, "dp", scatter_dimension=1, tiled=True)
        final0, final1 = g[0], g[1]
        small = lax.psum(jnp.stack([b0["bsum"], r1["bsum"]]), ("section", "tensor", "dp"))
        small = lax.dynamic_index_in_dim(lax.dynamic_index_in_dim(small, sec, 0, False), ten, 0, False)

    layer_outputs = ordered(low_rows, low_twin)
    input_grads = ordered(in_rows, in_twin).astype(F32)

    def heads(*starts):
        return [final0[:, s * HD:(s + 1) * HD] for s in starts]

    small = small.reshape(-1)
    qkv = jnp.concatenate(heads(0, 1, 2, 4, 5, 3, 6, 7, 8), 1).reshape(1, piece, 3, 3 * HD)
    return (
        layer_outputs,
        input_grads,
        final0[:, MISC:MISC + 2].T[None],
        final0[:, MISC + 2:MISC + 6].T[None],
        qkv,
        jnp.stack([small[:3 * HD], small[6 * HD:9 * HD]])[None],
        jnp.concatenate(heads(10, 11, 9), 1).T[None],
        jnp.concatenate([final0[:, UP0:], final1[:, :DOWN]], 1)[None],
        small[ATT:ATT + ff // 2][None],
        final1[:, DOWN:ROWSB].T[None],
    )


def solution(mesh):
    in_specs = (
        P(None, "dp", None),
        P(),
        P(None, "dp", None),
        P("section", None, "dp"),
        P("section", None, "dp"),
        P("section", "dp", None, "tensor"),
        P("section", None, "tensor"),
        P("section", "tensor", "dp"),
        P("section", "dp", "tensor"),
        P("section", "tensor"),
        P("section", "tensor", "dp"),
    )
    out_specs = (
        P("section", None, "dp", None),
        P("section", None, "dp", None),
        P("section", None, "dp"),
        P("section", None, "dp"),
        P("section", "dp", None, "tensor"),
        P("section", None, "tensor"),
        P("section", "tensor", "dp"),
        P("section", "dp", "tensor"),
        P("section", "tensor"),
        P("section", "tensor", "dp"),
    )
    return jax.shard_map(shards, mesh=mesh, in_specs=in_specs, out_specs=out_specs, check_vma=False)
```

```python
import functools
import math

import jax
import jax.numpy as jnp
from jax import lax
from jax.experimental import pallas as pl
from jax.experimental.pallas import tpu as pltpu
from jax.sharding import PartitionSpec as P

IMG_LEN = 197
IMG_PAD = 208
HD = 64
EPSILON = 1e-06
NEGATIVE = -1e30
F32 = jnp.float32
BF16 = jnp.bfloat16
BLOCK = 128
HALF = 1280
COST = 10 ** 10
SCALE = 1.0 / math.sqrt(HD)


def mm(a, b, dims):
    return lax.dot_general(a, b, (dims, ((), ())), preferred_element_type=F32)


def nn(a, b):
    return mm(a, b, ((1,), (0,)))


def nt(a, b):
    return mm(a, b, ((1,), (1,)))


def tn(a, b):
    return mm(a, b, ((0,), (0,)))


def normed(x):
    centred = x - jnp.mean(x, -1, keepdims=True)
    inverse = lax.rsqrt(jnp.mean(centred * centred, -1, keepdims=True) + EPSILON)
    return centred * inverse, inverse


def norm_back(grad, xhat, inverse, gain):
    t = grad * gain
    return inverse * (
        t - jnp.mean(t, -1, keepdims=True) - xhat * jnp.mean(t * xhat, -1, keepdims=True)
    )


def gelu_parts(u):
    cdf = 0.5 * (1.0 + lax.erf(u * math.sqrt(0.5)))
    pdf = jnp.exp(-0.5 * u * u) * (1.0 / math.sqrt(2.0 * math.pi))
    return u * cdf, cdf + u * pdf


ATT = 640
OUT = 512
MISC = 768
UP0 = 896
DOWN = 384
ROWSB = 1152
CHUNK = 384


def up_at(w, t, j):
    return w[t, 0, :, UP0:] if j == 0 else w[t, 1, :, :CHUNK]


def down_at(w, t, j):
    return w[t, 1, :, DOWN + j * CHUNK:DOWN + (j + 1) * CHUNK]


def low_lanes():
    return lax.broadcasted_iota(jnp.int32, (1, BLOCK), 1) < HD


def turn(a):
    return jnp.concatenate([a[:, HD:], a[:, :HD]], 1)


def valid_rows(sc, n):
    row = lax.broadcasted_iota(jnp.int32, (IMG_PAD, 1), 0)
    return jnp.where((row < IMG_LEN) & (n < sc[0]), 1.0, 0.0)


def image_rows(n):
    return pl.ds(pl.multiple_of(n * IMG_PAD, 16), IMG_PAD)


def forward_image(n, sc, x_ref, w, vec, brow, out_ref, kept):
    r = image_rows(n)
    x = x_ref[r, :].astype(F32)
    xhat, inv = normed(x)
    attn_in = (xhat * vec[0:1, :] + vec[2:3, :]).astype(BF16)
    kept["xh1"][r, :] = xhat
    kept["inv1"][r, :] = jnp.broadcast_to(inv, (IMG_PAD, BLOCK))
    kept["ain"][r, :] = attn_in
    residual = x + vec[3:4, :]
    low = low_lanes()
    lane = lax.broadcasted_iota(jnp.int32, (1, ATT), 1)
    factor = jnp.where(lane < 192, SCALE, jnp.where(lane < 576, 1.0, 0.0))
    real = lax.broadcasted_iota(jnp.int32, (1, IMG_PAD), 1) < IMG_LEN
    for t in range(2):
        bias = jnp.concatenate([brow[t, i:i + 1, :] for i in range(5)], 1)
        p = ((nn(attn_in, w[t, 0, :, :ATT]) + bias) * factor).astype(BF16)
        kept["qkv"][t, r, :] = p
        q, qk, k, v, vx = [p[:, i * BLOCK:(i + 1) * BLOCK] for i in range(5)]
        kq, xv = turn(qk), turn(vx)
        outs = []
        for i, (qq, kk, vv) in enumerate(
                [(jnp.where(low, q, 0), k, v), (jnp.where(low, 0, q), k, v), (jnp.where(low, qk, 0), kq, xv)]):
            s = jnp.where(real, nt(qq, kk), NEGATIVE)
            e = jnp.exp(s - jnp.max(s, -1, keepdims=True))
            pr = (e * (1.0 / jnp.sum(e, -1, keepdims=True))).astype(BF16)
            kept["pr"][n * 6 + t * 3 + i] = pr
            outs.append(nn(pr, vv))
        mixed = jnp.concatenate([outs[2], jnp.where(low, outs[0], outs[1])], 1).astype(BF16)
        kept["mx"][t, r, :] = mixed
        residual = residual + nt(mixed, w[t, 0, :, OUT:MISC])
    xhat, inv = normed(residual)
    mlp_in = (xhat * vec[1:2, :] + vec[4:5, :]).astype(BF16)
    kept["xh2"][r, :] = xhat
    kept["inv2"][r, :] = jnp.broadcast_to(inv, (IMG_PAD, BLOCK))
    kept["min"][r, :] = mlp_in
    out = residual + vec[5:6, :]
    for t in range(2):
        for j in range(2):
            bias = jnp.concatenate([brow[t, 5 + j * 3 + i:6 + j * 3 + i, :] for i in range(3)], 1)
            hidden, slope = gelu_parts(nn(mlp_in, up_at(w, t, j)) + bias)
            c = slice((t * 2 + j) * CHUNK, (t * 2 + j + 1) * CHUNK)
            hidden = hidden.astype(BF16)
            kept["hd"][r, c] = hidden
            kept["sl"][r, c] = slope.astype(BF16)
            out = out + nt(hidden, down_at(w, t, j))
    out_ref[r, :] = (out * valid_rows(sc, n)).astype(BF16)


def rsum(a):
    return jnp.sum(a, 0, keepdims=True)


def backward_mlp(n, sc, u_ref, w, vec, kept, grad, sums, bsum):
    r = image_rows(n)

    masked = u_ref[r, :].astype(F32) * valid_rows(sc, n)
    sums[5:6, :] += rsum(masked)
    dg = masked.astype(BF16)
    grad["dg"][r, :] = dg
    mg = jnp.zeros(masked.shape, F32)
    for t in range(2):
        for j in range(2):
            c = slice((t * 2 + j) * CHUNK, (t * 2 + j + 1) * CHUNK)
            up = nn(dg, down_at(w, t, j)) * kept["sl"][r, c].astype(F32)
            up = up.astype(BF16)
            grad["up"][r, c] = up
            total = rsum(up.astype(F32))
            for i in range(3):
                bsum[t, 5 + j * 3 + i:6 + j * 3 + i, :] += total[:, i * BLOCK:(i + 1) * BLOCK]
            mg = mg + nt(up, up_at(w, t, j))
    xhat = kept["xh2"][r, :]
    sums[4:5, :] += rsum(mg)
    sums[1:2, :] += rsum(mg * xhat)
    res = masked + norm_back(mg, xhat, kept["inv2"][r, :1], vec[1:2, :])
    sums[3:4, :] += rsum(res)
    grad["res"][r, :] = res


def backward_attention(n, w, vec, in_ref, kept, grad, sums, bsum):
    r = image_rows(n)
    res = grad["res"][r, :]
    ag = res.astype(BF16)
    grad["ag"][r, :] = ag
    low = low_lanes()
    ig = jnp.zeros(res.shape, F32)
    for t in range(2):
        xg = nn(ag, w[t, 0, :, OUT:MISC]).astype(BF16)
        gx = jnp.where(low, 0, xg[:, :BLOCK])
        g = xg[:, BLOCK:]
        p = kept["qkv"][t, r, :]
        q, qk, k, v, vx = [p[:, i * BLOCK:(i + 1) * BLOCK] for i in range(5)]
        kq, xv = turn(qk), turn(vx)
        dq, dk, dv = [], [], []
        for i, (qq, kk, vv, gm, gg) in enumerate(
                [(q, k, v, jnp.where(low, g, 0), g), (q, k, v, jnp.where(low, 0, g), g), (qk, kq, xv, gx, turn(gx))]):
            pb = kept["pr"][n * 6 + t * 3 + i]
            pf = pb.astype(F32)
            dp = nt(gm, vv)
            ds = (pf * (dp - jnp.sum(pf * dp, -1, keepdims=True))).astype(BF16)
            dv.append(tn(pb, gg))
            dq.append(nn(ds, kk) * SCALE)
            dk.append(tn(ds, kq if i == 2 else qq))
        blocks = [
            jnp.where(low, dq[0], dq[1]), jnp.where(low, dq[2], dk[2]), jnp.where(low, dk[0], dk[1]),
            jnp.where(low, dv[0], dv[1]), dv[2],
        ]
        d = jnp.concatenate(blocks, 1).astype(BF16)
        grad["dqkv"][t, r, :] = d
        total = rsum(d.astype(F32))
        for i in range(5):
            bsum[t, i:i + 1, :] += total[:, i * BLOCK:(i + 1) * BLOCK]
        ig = ig + nt(d, w[t, 0, :, :ATT])
    xhat = kept["xh1"][r, :]
    sums[2:3, :] += rsum(ig)
    sums[0:1, :] += rsum(ig * xhat)
    in_ref[r, :] = res + norm_back(ig, xhat, kept["inv1"][r, :1], vec[0:1, :])


def weight_grads(t, piece, kept, grad, g):
    ag, dg = grad["ag"][...], grad["dg"][...]
    ain, mlp_in = kept["ain"][...], kept["min"][...]
    width = ag.shape[1]
    high = jnp.where(low_lanes(), 0.0, 1.0)
    d = grad["dqkv"][t]
    g[0, :, :OUT] = tn(ain, d[:, :OUT]).astype(BF16)
    out = tn(ag, kept["mx"][t])
    g[0, :, OUT:ATT] = (tn(ain, d[:, OUT:]) + out[:, :BLOCK] * high).astype(BF16)
    g[0, :, ATT:MISC] = out[:, BLOCK:].astype(BF16)
    sums = jnp.concatenate([grad["sums"][...], jnp.zeros((BLOCK - 8, width), F32)], 0)
    g[0, :, MISC:UP0] = sums.T.astype(BF16)
    for j in range(2):
        c = pl.ds(pl.multiple_of((t * 2 + j) * CHUNK, BLOCK), CHUNK)
        up = tn(mlp_in, grad["up"][:, c]).astype(BF16)
        if j == 0:
            g[0, :, UP0:] = up
        else:
            g[1, :, :CHUNK] = up
        g[1, :, DOWN + j * CHUNK:DOWN + (j + 1) * CHUNK] = tn(dg, kept["hd"][:, c]).astype(BF16)
    if piece % 16 == 0:
        rows = jnp.concatenate([grad["bsum"][t], jnp.zeros((piece - 16, BLOCK), F32)], 0).astype(BF16)
        for i in range(width // piece):
            g[1, i * piece:(i + 1) * piece, ROWSB:] = rows


def kept_shapes(total, width, ff):
    images = total // IMG_PAD
    return dict(
        xh1=((total, width), F32), inv1=((total, BLOCK), F32), ain=((total, width), BF16), qkv=((2, total, ATT), BF16),
        pr=((images * 6, IMG_PAD, IMG_PAD), BF16), mx=((2, total, 2 * BLOCK), BF16), xh2=((total, width), F32),
        inv2=((total, BLOCK), F32), min=((total, width), BF16), sl=((total, ff), BF16), hd=((total, ff), BF16))


def grad_shapes(total, width, ff):
    return dict(dg=((total, width), BF16), up=((total, ff), BF16), res=((total, width), F32), sums=((8, width), F32),
                bsum=((2, 16, BLOCK), F32), ag=((total, width), BF16), dqkv=((2, total, ATT), BF16))


def layer_call(phases, sources, load, store, out_shapes, scalars, given, total, width, ff, piece):
    ks = kept_shapes(total, width, ff)
    gs = grad_shapes(total, width, ff)
    weights = ["ain", "mx", "min", "hd"] + [n for n in gs if n != "res"]
    need = {"forward": ["x"], "back": ["u"] + list(ks), "theirs": weights, "mine": weights}
    gives = {"forward": {"out": ((total, width), BF16), **ks}, "back": {"keep": ((total, width), BF16), "give": ((total, width), BF16), "in": ((total, width), F32), **gs},
             "theirs": {}, "mine": {}}
    made = {}
    for p in phases:
        made.update(gives[p])
    inputs = list(dict.fromkeys(n for p in phases for n in need[p] if n not in made))
    if phases[-1] == "forward":
        shown = list(made)
    else:
        shown = [n for n in made if n in weights or n in ("keep", "give")]
        if "forward" in phases:
            shown.append("in")
    inner = [n for n in made if n not in shown]
    side = {"theirs": 0, "mine": 1}.get(phases[-1])
    products = phases[0] != "mine"
    vmem = pl.BlockSpec(memory_space=pltpu.VMEM)
    anywhere = pl.BlockSpec(memory_space=pl.ANY)
    ends = [] if side is None else out_shapes[side]
    scratch = [pltpu.SemaphoreType.DMA] + [pltpu.VMEM(*made[n]) for n in inner]
    if products:
        scratch += [pltpu.VMEM((2, 2, width, HALF), BF16), pltpu.VMEM((8, width), F32), pltpu.VMEM((2, 16, BLOCK), F32)]
    if ends:
        scratch.append(pltpu.VMEM((2, width, HALF), BF16))

    def body(*refs):
        refs = list(refs)

        def take(n):
            got = refs[:n]
            del refs[:n]
            return got

        sc = take(1)[0]
        at = dict(zip(inputs, take(len(inputs))))
        src = take(len(sources))
        at.update(zip(shown, take(len(shown))))
        dst = take(len(ends))
        sem = take(1)[0]
        at.update(zip(inner, take(len(inner))))
        if products:
            w, vec, brow = take(3)
            copies = load(sc, src, w, sem)
            for c in copies:
                c.start()
            for c in copies:
                c.wait()
            vec[...] = w[0, 0, :, MISC:UP0].astype(F32).T[:8, :]
            for t in range(2):
                brow[t] = w[t, 1, :16, ROWSB:].astype(F32)
        if "forward" in phases:
            def step(n, carry):
                forward_image(n, sc, at["x"], w, vec, brow, at["out"], at)
                return carry
            lax.fori_loop(0, total // IMG_PAD, step, 0)
        if "back" in phases:
            sums, bsum = at["sums"], at["bsum"]
            sums[...] = jnp.zeros_like(sums)
            bsum[...] = jnp.zeros_like(bsum)

            def back(n, carry):
                backward_mlp(n, sc, at["u"], w, vec, at, at, sums, bsum)
                backward_attention(n, w, vec, at["in"], at, at, sums, bsum)
                return carry
            lax.fori_loop(0, total // IMG_PAD, back, 0)
            rows = [at[n] for n in (("x", "out") if "forward" in phases else ("in", "u"))]
            for here in range(2):
                @pl.when(sc[2] == here)
                def _():
                    at["keep"][...] = rows[here][...].astype(BF16)
                    at["give"][...] = rows[1 - here][...].astype(BF16)
        if ends:
            g = take(1)[0]
            t = jnp.where(sc[1] == 0, 1 - side, side)
            weight_grads(t, piece, at, at, g)
            copies = store(sc, side, g, dst, sem)
            for c in copies:
                c.start()
            for c in copies:
                c.wait()

    outs = [made[n] for n in shown] + ends
    args = [scalars, *[given[n] for n in inputs], *(sources if products else [])]
    if not products:
        sources = []
    got = pl.pallas_call(
        body,
        out_shape=[jax.ShapeDtypeStruct(*o) for o in outs],
        in_specs=[pl.BlockSpec(memory_space=pltpu.SMEM)] + [vmem] * len(inputs) + [anywhere] * len(sources),
        out_specs=[vmem] * (len(outs) - len(ends)) + [anywhere] * len(ends),
        scratch_shapes=scratch,
        compiler_params=pltpu.CompilerParams(vmem_limit_bytes=56 * 2 ** 20),
        cost_estimate=pl.CostEstimate(flops=COST * len(phases), transcendentals=0, bytes_accessed=2 ** 23),
    )(*args)
    got = list(got)
    res = dict(zip(shown, got))
    res["g"] = got[len(shown):]
    return res


def shards(tokens, image_counts, cotangent, norm_gains, row_biases, qkv_weight, qv_bias, out_weight,
           up_weight, up_bias, down_weight):
    sec = lax.axis_index("section")
    dp = lax.axis_index("dp")
    ten = lax.axis_index("tensor")
    n_dp = lax.axis_size("dp")
    m = n_dp // 2
    zi, yi = dp // 2, dp % 2
    local_rows, width = tokens.shape[1:]
    images = local_rows * n_dp // IMG_LEN
    piece = width // n_dp
    ff = 2 * up_weight.shape[2]
    direct = piece % 16 == 0 and m == 4

    def pt(a):
        return lax.ppermute(a, "tensor", [(0, 1), (1, 0)])

    def px(a):
        return lax.ppermute(a, "section", [(0, 1), (1, 0)])

    def py(a):
        return lax.ppermute(a, "dp", [(i, i ^ 1) for i in range(n_dp)])

    def pd(a):
        return lax.ppermute(a, ("section", "dp"), [(i, (i + n_dp) % (2 * n_dp) ^ 1) for i in range(2 * n_dp)])

    def after(a, *b):
        return lax.optimization_barrier((a, *b))

    def plus(*a):
        return sum(b.astype(F32) for b in a)

    def add_pair(g, got):
        keep, to_y, to_x, to_d = [plus(a, b) for a, b in zip(g, (got[0, 0], got[0, 1], got[1, 0], got[1, 1]))]
        return [keep, to_y.astype(BF16), to_x.astype(BF16), to_d.astype(BF16)]

    def across(sent):
        return [sent[0], py(sent[1]), px(sent[2]), pd(sent[3])]

    def pz_to(a, kk):
        return lax.ppermute(a, "dp", [(i, i ^ (2 * kk)) for i in range(n_dp)])

    def along(quad):
        quad = plus(*quad)
        low = quad.astype(BF16)
        return plus(quad[:, 0], *[pz_to(low[:, kk], kk) for kk in range(1, m)])

    def along_steps(quad):
        quad = plus(*quad)
        got = pz_to(quad[:, 1::2].astype(BF16), 1)
        quad = plus(quad[:, 0::2], got)
        return plus(quad[:, 0], pz_to(quad[:, 1].astype(BF16), 2))

    def pn(a):
        return lax.ppermute(a, ("dp", "tensor"), [(2 * i + 1, 2 * i + 3) for i in range(n_dp - 1)])

    def tails(keep, got):
        tail = select[:, local_rows:]
        return pn(jnp.stack([tn(tail, keep), tn(tail, got)]).astype(BF16))

    def placed(keep, got, tail):
        def place(a, b):
            a = tn(select[:, :local_rows], a).astype(BF16)
            return jnp.concatenate([a[:IMG_PAD] + b, a[IMG_PAD:]], 0)

        return jnp.stack([place(keep, tail[0]), place(got, tail[1])])

    def ordered(a, b):
        a = a + b
        return jnp.where(sec == 0, a, a[::-1])[None]

    batch_tokens = lax.dynamic_index_in_dim(tokens, sec, 0, keepdims=False)
    batch_cot = lax.dynamic_index_in_dim(cotangent, sec, 0, keepdims=False)
    count = lax.dynamic_index_in_dim(image_counts, sec, 0, keepdims=False)
    first = jnp.minimum((dp * local_rows + IMG_LEN - 1) // IMG_LEN, images)
    last = jnp.minimum(((dp + 1) * local_rows + IMG_LEN - 1) // IMG_LEN, images)
    held = last - first
    slots = -(-(-(-local_rows // IMG_LEN)) // 2)
    lower = held // 2
    own_first = jnp.where(ten == 0, first, first + lower)
    own_count = jnp.where(ten == 0, lower, held - lower)
    total = slots * IMG_PAD
    row = lax.broadcasted_iota(jnp.int32, (total, 1), 0)
    slot, inside = row // IMG_PAD, row % IMG_PAD
    exists = (inside < IMG_LEN) & (slot < own_count)
    target = (own_first + slot) * IMG_LEN + inside - dp * local_rows
    canvas_rows = local_rows + IMG_PAD
    select = ((lax.broadcasted_iota(jnp.int32, (total, canvas_rows), 1) == target) & exists).astype(BF16)
    scalars = jnp.stack([jnp.minimum(own_count, jnp.maximum(count - own_first, 0)), ten, sec, zi, yi]).astype(jnp.int32)

    both = jnp.stack([batch_tokens, batch_cot])
    halo = lax.ppermute(both[:, :IMG_PAD], ("dp", "tensor"), [(2 * i + 3, 2 * i + 1) for i in range(n_dp - 1)])
    q, k, v = [[qkv_weight[0, :, i, h * HD:(h + 1) * HD] for h in range(3)] for i in range(3)]
    o = out_weight[0].T
    o = [o[:, h * HD:(h + 1) * HD] for h in range(3)]
    misc = jnp.concatenate([norm_gains[0], row_biases[0]], 0).T
    misc = jnp.pad(misc, ((0, 0), (0, BLOCK - misc.shape[1])))
    gap = jnp.zeros((HD,), BF16)
    rows = jnp.concatenate([qv_bias[0, 0], gap, gap, gap, qv_bias[0, 1], gap, up_bias[0]]).reshape(-1, BLOCK)
    rows = jnp.pad(rows, ((0, piece - rows.shape[0]), (0, 0)))
    up, down = up_weight[0], down_weight[0].T
    part0 = jnp.concatenate(
        [q[0], q[1], q[2], k[2], k[0], k[1], v[0], v[1], v[2], o[2], o[0], o[1], misc, up[:, :CHUNK]], 1)
    part1 = jnp.concatenate([up[:, CHUNK:], down, rows], 1)

    if direct:
        keep = jnp.where(sec == 0, part0, part1)
        give = jnp.where(sec == 0, part1, part0)
        got, halo = after(px(give), halo)
        start = [jnp.where(sec == 0, keep, got), jnp.where(sec == 0, got, keep)]

        def load(l, sc, src, w, sem):
            copies = []
            for side in range(2):
                t = jnp.where(sc[1] == 0, side, 1 - side)
                own = src[side * 8:side * 8 + 8]
                for kk in range(m):
                    z = lax.bitwise_xor(sc[3], kk)
                    near = pl.ds(pl.multiple_of((2 * z + sc[4]) * piece, 16), piece)
                    far = pl.ds(pl.multiple_of((2 * z + 1 - sc[4]) * piece, 16), piece)
                    for i, (h, r) in enumerate(((sc[2], near), (1 - sc[2], near), (sc[2], far), (1 - sc[2], far))):
                        a = own[i].at[l] if kk == 0 else own[4 + i].at[kk - 1]
                        copies.append(pltpu.make_async_copy(a, w.at[t, h, r, :], sem))
            return copies

        def store(sc, side, g, dst, sem):
            copies = []
            for hr in range(2):
                h = jnp.where(sc[2] == 0, hr, 1 - hr)
                for yr in range(2):
                    y = jnp.where(sc[4] == 0, yr, 1 - yr)
                    for kk in range(m):
                        z = lax.bitwise_xor(sc[3], kk)
                        r = pl.ds(pl.multiple_of((2 * z + y) * piece, 16), piece)
                        out = dst[0].at[hr, yr] if side == 0 else dst[hr * 2 + yr]
                        for c in range(2):
                            a = g.at[h, r, c * part:(c + 1) * part]
                            copies.append(pltpu.make_async_copy(a, out.at[c, kk], sem))
            return copies

        part = HALF // 2
        out_shapes = [[((2, 2, 2, m, piece, part), BF16)], [((2, m, piece, part), BF16)] * 4]
        own = jnp.stack(start)
        firsts = [own, px(own), py(own), pd(own)]
        columns = [jnp.stack([pz_to(start[0], kk) for kk in range(1, m)])]
        start[1], columns[0] = after(start[1], columns[0])
        columns[0], *firsts = after(columns[0], *firsts)
        rest = [columns[0], px(columns[0]), py(columns[0]), pd(columns[0])]
        near = pz_to(start[1], 1)
        columns.append(jnp.concatenate([near[None], pz_to(jnp.stack([start[1], near]), 2)]))
        columns[1], *rest = after(columns[1], *rest)
        twins = [pt(a) for a in firsts]
        sources = [firsts + rest + twins + [pt(a) for a in rest]]
        sources.append(columns[1:] + [px(columns[1]), py(columns[1]), pd(columns[1])])
    else:
        def load(l, sc, src, w, sem):
            return [pltpu.make_async_copy(src[0], w, sem)]

        def store(sc, side, g, dst, sem):
            return [pltpu.make_async_copy(g, dst[0], sem)]

        out_shapes = [[((2, width, HALF), BF16)]] * 2
        a = lax.all_gather(jnp.stack([part0, part1]), "dp", axis=1, tiled=True)
        a = lax.all_gather(lax.all_gather(a, "tensor"), "section")
        sources = [[a[0]], [a[1]]]

    batch = jnp.concatenate([both, halo], 1)
    x0 = nn(select, batch[0]).astype(BF16)
    cot = nn(select, batch[1]).astype(BF16)

    def call(l, phases, **given):
        return layer_call(phases, sources[l], functools.partial(load, l), store, out_shapes, scalars, given, total,
                          width, ff, piece)

    r0 = call(0, ["forward"], x=x0)
    low0 = r0["out"]
    if direct:
        low0, *rest = after(low0, *sources[1])
        sources[1] = firsts + rest + twins + [pt(a) for a in rest]
    r1 = call(1, ["forward", "back", "theirs"], x=low0, u=cot)
    if direct:
        got1 = pt(r1["g"][0])
    low_got = px(r1["give"])
    m1 = call(1, ["mine"], **r1)
    u = r1["in"]
    if direct:
        first, got1 = after(m1["g"][0], got1)
        sent1 = add_pair([first] + m1["g"][1:], got1)
        u, low_got, *sent1 = after(u, low_got, *sent1)
        low_tails = tails(r1["keep"], low_got)
        quad1 = across(sent1)
    else:
        low_tails = tails(r1["keep"], low_got)
    b0 = call(0, ["back", "theirs"], **{**r0, "u": u})
    if direct:
        b0["dg"], b0["g"][0], low_tails, *quad1 = after(b0["dg"], b0["g"][0], low_tails, *quad1)
        got0 = pt(b0["g"][0])
    low_rows = placed(r1["keep"], low_got, low_tails)
    low_twin = pt(low_rows)
    in_got = px(b0["give"])
    m0 = call(0, ["mine"], **{**r0, **b0})

    if direct:
        first, got0, low_twin = after(m0["g"][0], got0, low_twin)
        sent0 = add_pair([first] + m0["g"][1:], got0)
        both = after(in_got, *sent0, *quad1)
        in_got, sent0, quad1 = both[0], both[1:5], both[5:]
        in_tails = tails(b0["keep"], in_got)
        quad0 = [across([a[c:c + 1] for a in sent0]) for c in range(2)]
        in_rows = placed(b0["keep"], in_got, in_tails)
        in_twin, *quad0[1] = after(pt(in_rows), *quad0[1])
        done1 = along_steps(quad1)
        done0 = [along_steps(quad0[0])]
        done0 = jnp.concatenate(done0 + [along(quad0[1])])
        mine = jnp.where(sec == 0, done0, done1)
        other = px(jnp.where(sec == 0, done1, done0).astype(BF16)).astype(F32)
        final0 = jnp.where(sec == 0, mine, other)
        final1 = jnp.where(sec == 0, other, mine)
        final0, final1 = [jnp.concatenate([a[0], a[1]], 1) for a in (final0, final1)]
        small = final1[:, ROWSB:]
    else:
        in_rows = placed(b0["keep"], in_got, tails(b0["keep"], in_got))
        in_twin = pt(in_rows)

        def by_core(a, b):
            return jnp.where(ten == 0, jnp.stack([b, a]), jnp.stack([a, b]))

        g = jnp.stack([by_core(b0["g"][0], m0["g"][0]), by_core(r1["g"][0], m1["g"][0])])
        g = lax.psum_scatter(g.astype(F32), "section", scatter_dimension=0)
        g = lax.psum_scatter(g, "tensor", scatter_dimension=0)
        g = lax.psum_scatter(g, "dp", scatter_dimension=1, tiled=True)
        final0, final1 = g[0], g[1]
        small = lax.psum(jnp.stack([b0["bsum"], r1["bsum"]]), ("section", "tensor", "dp"))
        small = lax.dynamic_index_in_dim(lax.dynamic_index_in_dim(small, sec, 0, False), ten, 0, False)

    layer_outputs = ordered(low_rows, low_twin)
    input_grads = ordered(in_rows, in_twin).astype(F32)

    def heads(*starts):
        return [final0[:, s * HD:(s + 1) * HD] for s in starts]

    small = small.reshape(-1)
    qkv = jnp.concatenate(heads(0, 1, 2, 4, 5, 3, 6, 7, 8), 1).reshape(1, piece, 3, 3 * HD)
    return (
        layer_outputs,
        input_grads,
        final0[:, MISC:MISC + 2].T[None],
        final0[:, MISC + 2:MISC + 6].T[None],
        qkv,
        jnp.stack([small[:3 * HD], small[6 * HD:9 * HD]])[None],
        jnp.concatenate(heads(10, 11, 9), 1).T[None],
        jnp.concatenate([final0[:, UP0:], final1[:, :DOWN]], 1)[None],
        small[ATT:ATT + ff // 2][None],
        final1[:, DOWN:ROWSB].T[None],
    )


def solution(mesh):
    in_specs = (
        P(None, "dp", None),
        P(),
        P(None, "dp", None),
        P("section", None, "dp"),
        P("section", None, "dp"),
        P("section", "dp", None, "tensor"),
        P("section", None, "tensor"),
        P("section", "tensor", "dp"),
        P("section", "dp", "tensor"),
        P("section", "tensor"),
        P("section", "tensor", "dp"),
    )
    out_specs = (
        P("section", None, "dp", None),
        P("section", None, "dp", None),
        P("section", None, "dp"),
        P("section", None, "dp"),
        P("section", "dp", None, "tensor"),
        P("section", None, "tensor"),
        P("section", "tensor", "dp"),
        P("section", "dp", "tensor"),
        P("section", "tensor"),
        P("section", "tensor", "dp"),
    )
    return jax.shard_map(shards, mesh=mesh, in_specs=in_specs, out_specs=out_specs, check_vma=False)
```

```python
import functools
import math

import jax
import jax.numpy as jnp
from jax import lax
from jax.experimental import pallas as pl
from jax.experimental.pallas import tpu as pltpu
from jax.sharding import PartitionSpec as P

IMG_LEN = 197
IMG_PAD = 208
HD = 64
EPSILON = 1e-06
NEGATIVE = -1e30
F32 = jnp.float32
BF16 = jnp.bfloat16
BLOCK = 128
HALF = 1280
COST = 10 ** 10
SCALE = 1.0 / math.sqrt(HD)


def mm(a, b, dims):
    return lax.dot_general(a, b, (dims, ((), ())), preferred_element_type=F32)


def nn(a, b):
    return mm(a, b, ((1,), (0,)))


def nt(a, b):
    return mm(a, b, ((1,), (1,)))


def tn(a, b):
    return mm(a, b, ((0,), (0,)))


def normed(x):
    centred = x - jnp.mean(x, -1, keepdims=True)
    inverse = lax.rsqrt(jnp.mean(centred * centred, -1, keepdims=True) + EPSILON)
    return centred * inverse, inverse


def norm_back(grad, xhat, inverse, gain):
    t = grad * gain
    return inverse * (
        t - jnp.mean(t, -1, keepdims=True) - xhat * jnp.mean(t * xhat, -1, keepdims=True)
    )


def gelu_parts(u):
    cdf = 0.5 * (1.0 + lax.erf(u * math.sqrt(0.5)))
    pdf = jnp.exp(-0.5 * u * u) * (1.0 / math.sqrt(2.0 * math.pi))
    return u * cdf, cdf + u * pdf


QK = 384
V = 256
OUT = 128
MISC = 384
MLP = 512
ATT = QK + V


def low_lanes():
    return lax.broadcasted_iota(jnp.int32, (1, BLOCK), 1) < HD


def turn(a):
    return jnp.concatenate([a[:, HD:], a[:, :HD]], 1)


def valid_rows(sc, n):
    row = lax.broadcasted_iota(jnp.int32, (IMG_PAD, 1), 0)
    return jnp.where((row < IMG_LEN) & (n < sc[0]), 1.0, 0.0)


def image_rows(n):
    return pl.ds(pl.multiple_of(n * IMG_PAD, 16), IMG_PAD)


def forward_image(n, sc, x_ref, w, vec, brow, out_ref, kept, ready):
    r = image_rows(n)
    x = x_ref[r, :].astype(F32)
    xhat, inv = normed(x)
    attn_in = (xhat * vec[0:1, :] + vec[2:3, :]).astype(BF16)
    kept["xh1"][r, :] = xhat
    kept["inv1"][r, :] = jnp.broadcast_to(inv, (IMG_PAD, BLOCK))
    kept["ain"][r, :] = attn_in
    residual = x + vec[3:4, :]
    low = low_lanes()
    lane = lax.broadcasted_iota(jnp.int32, (1, ATT), 1)
    factor = jnp.where(lane < 192, SCALE, jnp.where(lane < 576, 1.0, 0.0))
    real = lax.broadcasted_iota(jnp.int32, (1, IMG_PAD), 1) < IMG_LEN
    for t in range(2):
        bias = jnp.concatenate([brow[t, i:i + 1, :] for i in range(5)], 1)
        p = jnp.concatenate([nn(attn_in, w[t, 0, :, :QK]), nn(attn_in, w[t, 1, :, :V])], 1)
        p = ((p + bias) * factor).astype(BF16)
        kept["qkv"][t, r, :] = p
        q, qk, k, v, vx = [p[:, i * BLOCK:(i + 1) * BLOCK] for i in range(5)]
        kq, xv = turn(qk), turn(vx)
        outs = []
        for i, (qq, kk, vv) in enumerate(
                [(jnp.where(low, q, 0), k, v), (jnp.where(low, 0, q), k, v), (jnp.where(low, qk, 0), kq, xv)]):
            s = jnp.where(real, nt(qq, kk), NEGATIVE)
            e = jnp.exp(s - jnp.max(s, -1, keepdims=True))
            pr = (e * (1.0 / jnp.sum(e, -1, keepdims=True))).astype(BF16)
            kept["pr"][n * 6 + t * 3 + i] = pr
            outs.append(nn(pr, vv))
        mixed = jnp.concatenate([outs[2], jnp.where(low, outs[0], outs[1])], 1).astype(BF16)
        kept["mx"][t, r, :] = mixed
        residual = residual + nt(mixed, w[t, 1, :, OUT:MISC])
    xhat, inv = normed(residual)
    mlp_in = (xhat * vec[1:2, :] + vec[4:5, :]).astype(BF16)
    kept["xh2"][r, :] = xhat
    kept["inv2"][r, :] = jnp.broadcast_to(inv, (IMG_PAD, BLOCK))
    kept["min"][r, :] = mlp_in
    out = residual + vec[5:6, :]
    ready(1)
    ff = kept["hd"].shape[1] // 2
    for t in range(2):
        bias = jnp.concatenate([brow[t, 5 + i:6 + i, :] for i in range(ff // BLOCK)], 1)
        hidden, slope = gelu_parts(nn(mlp_in, w[t, 0, :, MLP:]) + bias)
        hidden = hidden.astype(BF16)
        kept["hd"][r, t * ff:(t + 1) * ff] = hidden
        kept["sl"][r, t * ff:(t + 1) * ff] = slope.astype(BF16)
        out = out + nt(hidden, w[t, 1, :, MLP:])
    out_ref[r, :] = (out * valid_rows(sc, n)).astype(BF16)


def rsum(a):
    return jnp.sum(a, 0, keepdims=True)


def backward_mlp(n, sc, u_ref, w, vec, kept, grad, sums, bsum):
    r = image_rows(n)

    masked = u_ref[r, :].astype(F32) * valid_rows(sc, n)
    sums[5:6, :] += rsum(masked)
    dg = masked.astype(BF16)
    grad["dg"][r, :] = dg
    mg = jnp.zeros(masked.shape, F32)
    ff = kept["hd"].shape[1] // 2
    for t in range(2):
        c = slice(t * ff, (t + 1) * ff)
        up = (nn(dg, w[t, 1, :, MLP:]) * kept["sl"][r, c].astype(F32)).astype(BF16)
        grad["up"][r, c] = up
        total = rsum(up.astype(F32))
        for i in range(ff // BLOCK):
            bsum[t, 5 + i:6 + i, :] += total[:, i * BLOCK:(i + 1) * BLOCK]
        mg = mg + nt(up, w[t, 0, :, MLP:])
    xhat = kept["xh2"][r, :]
    sums[4:5, :] += rsum(mg)
    sums[1:2, :] += rsum(mg * xhat)
    res = masked + norm_back(mg, xhat, kept["inv2"][r, :1], vec[1:2, :])
    sums[3:4, :] += rsum(res)
    grad["res"][r, :] = res


def backward_attention(n, w, vec, in_ref, kept, grad, sums, bsum):
    r = image_rows(n)
    res = grad["res"][r, :]
    ag = res.astype(BF16)
    grad["ag"][r, :] = ag
    low = low_lanes()
    ig = jnp.zeros(res.shape, F32)
    for t in range(2):
        xg = nn(ag, w[t, 1, :, OUT:MISC]).astype(BF16)
        gx = jnp.where(low, 0, xg[:, :BLOCK])
        g = xg[:, BLOCK:]
        p = kept["qkv"][t, r, :]
        q, qk, k, v, vx = [p[:, i * BLOCK:(i + 1) * BLOCK] for i in range(5)]
        kq, xv = turn(qk), turn(vx)
        dq, dk, dv = [], [], []
        for i, (qq, kk, vv, gm, gg) in enumerate(
                [(q, k, v, jnp.where(low, g, 0), g), (q, k, v, jnp.where(low, 0, g), g), (qk, kq, xv, gx, turn(gx))]):
            pb = kept["pr"][n * 6 + t * 3 + i]
            pf = pb.astype(F32)
            dp = nt(gm, vv)
            ds = (pf * (dp - jnp.sum(pf * dp, -1, keepdims=True))).astype(BF16)
            dv.append(tn(pb, gg))
            dq.append(nn(ds, kk) * SCALE)
            dk.append(tn(ds, kq if i == 2 else qq))
        blocks = [
            jnp.where(low, dq[0], dq[1]), jnp.where(low, dq[2], dk[2]), jnp.where(low, dk[0], dk[1]),
            jnp.where(low, dv[0], dv[1]), dv[2],
        ]
        d = jnp.concatenate(blocks, 1).astype(BF16)
        grad["dqkv"][t, r, :] = d
        total = rsum(d.astype(F32))
        for i in range(5):
            bsum[t, i:i + 1, :] += total[:, i * BLOCK:(i + 1) * BLOCK]
        ig = ig + nt(d[:, :QK], w[t, 0, :, :QK]) + nt(d[:, QK:], w[t, 1, :, :V])
    xhat = kept["xh1"][r, :]
    sums[2:3, :] += rsum(ig)
    sums[0:1, :] += rsum(ig * xhat)
    in_ref[r, :] = res + norm_back(ig, xhat, kept["inv1"][r, :1], vec[0:1, :])


def weight_grads(t, piece, kept, grad, g):
    ag, dg = grad["ag"][...], grad["dg"][...]
    ain, mlp_in = kept["ain"][...], kept["min"][...]
    width = ag.shape[1]
    high = jnp.where(low_lanes(), 0.0, 1.0)
    d = grad["dqkv"][t]
    g[0, :, :QK] = tn(ain, d[:, :QK]).astype(BF16)
    val = tn(ain, d[:, QK:])
    out = tn(ag, kept["mx"][t])
    g[1, :, :OUT] = val[:, :BLOCK].astype(BF16)
    g[1, :, OUT:V] = (val[:, BLOCK:] + out[:, :BLOCK] * high).astype(BF16)
    g[1, :, V:MISC] = out[:, BLOCK:].astype(BF16)
    sums = jnp.concatenate([grad["sums"][...], jnp.zeros((BLOCK - 8, width), F32)], 0)
    g[0, :, MISC:MLP] = sums.T.astype(BF16)
    ff = kept["hd"].shape[1] // 2
    c = pl.ds(pl.multiple_of(t * ff, BLOCK), ff)
    g[0, :, MLP:] = tn(mlp_in, grad["up"][:, c]).astype(BF16)
    g[1, :, MLP:] = tn(dg, kept["hd"][:, c]).astype(BF16)
    if piece % 16 == 0:
        rows = jnp.concatenate([grad["bsum"][t], jnp.zeros((piece - 16, BLOCK), F32)], 0).astype(BF16)
        for i in range(width // piece):
            g[1, i * piece:(i + 1) * piece, MISC:MLP] = rows


def kept_shapes(total, width, ff):
    images = total // IMG_PAD
    return dict(
        xh1=((total, width), F32), inv1=((total, BLOCK), F32), ain=((total, width), BF16), qkv=((2, total, ATT), BF16),
        pr=((images * 6, IMG_PAD, IMG_PAD), BF16), mx=((2, total, 2 * BLOCK), BF16), xh2=((total, width), F32),
        inv2=((total, BLOCK), F32), min=((total, width), BF16), sl=((total, ff), BF16), hd=((total, ff), BF16))


def grad_shapes(total, width, ff):
    return dict(dg=((total, width), BF16), up=((total, ff), BF16), res=((total, width), F32), sums=((8, width), F32),
                bsum=((2, 16, BLOCK), F32), ag=((total, width), BF16), dqkv=((2, total, ATT), BF16))


def layer_call(phases, sources, load, store, out_shapes, scalars, given, total, width, ff, piece):
    ks = kept_shapes(total, width, ff)
    gs = grad_shapes(total, width, ff)
    weights = ["ain", "mx", "min", "hd"] + [n for n in gs if n != "res"]
    need = {"forward": ["x"], "back": ["u"] + list(ks), "theirs": weights, "mine": weights}
    gives = {"forward": {"out": ((total, width), BF16), **ks}, "back": {"keep": ((total, width), BF16), "give": ((total, width), BF16), "in": ((total, width), F32), **gs},
             "theirs": {}, "mine": {}}
    made = {}
    for p in phases:
        made.update(gives[p])
    inputs = list(dict.fromkeys(n for p in phases for n in need[p] if n not in made))
    if phases[-1] == "forward":
        shown = list(made)
    else:
        shown = [n for n in made if n in weights or n in ("keep", "give")]
        if "forward" in phases:
            shown.append("in")
    inner = [n for n in made if n not in shown]
    side = {"theirs": 0, "mine": 1}.get(phases[-1])
    products = phases[0] != "mine"
    vmem = pl.BlockSpec(memory_space=pltpu.VMEM)
    anywhere = pl.BlockSpec(memory_space=pl.ANY)
    ends = [] if side is None else out_shapes[side]
    scratch = [pltpu.SemaphoreType.DMA((2,))] + [pltpu.VMEM(*made[n]) for n in inner]
    if products:
        scratch += [pltpu.VMEM((2, 2, width, HALF), BF16), pltpu.VMEM((8, width), F32), pltpu.VMEM((2, 16, BLOCK), F32)]
    if ends:
        scratch.append(pltpu.VMEM((2, width, HALF), BF16))

    def body(*refs):
        refs = list(refs)

        def take(n):
            got = refs[:n]
            del refs[:n]
            return got

        sc = take(1)[0]
        at = dict(zip(inputs, take(len(inputs))))
        src = take(len(sources))
        at.update(zip(shown, take(len(shown))))
        dst = take(len(ends))
        sem = take(1)[0]
        at.update(zip(inner, take(len(inner))))
        if products:
            w, vec, brow = take(3)
            pending = [load(sc, src, w, sem, c) for c in range(2)]
            for part in pending if "forward" in phases else pending[::-1]:
                for c in part:
                    c.start()

            def ready(c):
                for copy in pending[c]:
                    copy.wait()
                if c == 0 and pending[c]:
                    vec[...] = w[0, 0, :, MISC:MLP].astype(F32).T[:8, :]
                    for t in range(2):
                        brow[t] = w[t, 1, :16, MISC:MLP].astype(F32)
                pending[c] = []

            ready(0 if "forward" in phases else 1)
        if "forward" in phases:
            for n in range(total // IMG_PAD):
                forward_image(n, sc, at["x"], w, vec, brow, at["out"], at, ready)
        if "back" in phases:
            sums, bsum = at["sums"], at["bsum"]
            sums[...] = jnp.zeros_like(sums)
            bsum[...] = jnp.zeros_like(bsum)
            ready(0)

            def back(n, carry):
                backward_mlp(n, sc, at["u"], w, vec, at, at, sums, bsum)
                backward_attention(n, w, vec, at["in"], at, at, sums, bsum)
                return carry
            lax.fori_loop(0, total // IMG_PAD, back, 0)
            rows = [at[n] for n in (("x", "out") if "forward" in phases else ("in", "u"))]
            for here in range(2):
                @pl.when(sc[2] == here)
                def _():
                    at["keep"][...] = rows[here][...].astype(BF16)
                    at["give"][...] = rows[1 - here][...].astype(BF16)
        if ends:
            g = take(1)[0]
            t = jnp.where(sc[1] == 0, 1 - side, side)
            weight_grads(t, piece, at, at, g)
            copies = store(sc, side, g, dst, sem.at[0])
            for c in copies:
                c.start()
            for c in copies:
                c.wait()

    outs = [made[n] for n in shown] + ends
    args = [scalars, *[given[n] for n in inputs], *(sources if products else [])]
    if not products:
        sources = []
    got = pl.pallas_call(
        body,
        out_shape=[jax.ShapeDtypeStruct(*o) for o in outs],
        in_specs=[pl.BlockSpec(memory_space=pltpu.SMEM)] + [vmem] * len(inputs) + [anywhere] * len(sources),
        out_specs=[vmem] * (len(outs) - len(ends)) + [anywhere] * len(ends),
        scratch_shapes=scratch,
        compiler_params=pltpu.CompilerParams(vmem_limit_bytes=56 * 2 ** 20),
        cost_estimate=pl.CostEstimate(flops=COST * len(phases), transcendentals=0, bytes_accessed=2 ** 23),
    )(*args)
    got = list(got)
    res = dict(zip(shown, got))
    res["g"] = got[len(shown):]
    return res


def shards(tokens, image_counts, cotangent, norm_gains, row_biases, qkv_weight, qv_bias, out_weight,
           up_weight, up_bias, down_weight):
    sec = lax.axis_index("section")
    dp = lax.axis_index("dp")
    ten = lax.axis_index("tensor")
    n_dp = lax.axis_size("dp")
    m = n_dp // 2
    zi, yi = dp // 2, dp % 2
    local_rows, width = tokens.shape[1:]
    images = local_rows * n_dp // IMG_LEN
    piece = width // n_dp
    ff = 2 * up_weight.shape[2]
    direct = piece % 16 == 0 and m == 4

    def pt(a):
        return lax.ppermute(a, "tensor", [(0, 1), (1, 0)])

    def px(a):
        return lax.ppermute(a, "section", [(0, 1), (1, 0)])

    def py(a):
        return lax.ppermute(a, "dp", [(i, i ^ 1) for i in range(n_dp)])

    def pd(a):
        return lax.ppermute(a, ("section", "dp"), [(i, (i + n_dp) % (2 * n_dp) ^ 1) for i in range(2 * n_dp)])

    def after(a, *b):
        return lax.optimization_barrier((a, *b))

    def plus(*a):
        return sum(b.astype(F32) for b in a)

    def add_pair(g, got):
        keep, to_y, to_x, to_d = [plus(a, b) for a, b in zip(g, (got[0, 0], got[0, 1], got[1, 0], got[1, 1]))]
        return [keep, to_y.astype(BF16), to_x.astype(BF16), to_d.astype(BF16)]

    def across(sent):
        return [sent[0], py(sent[1]), px(sent[2]), pd(sent[3])]

    def pz_to(a, kk):
        return lax.ppermute(a, "dp", [(i, i ^ (2 * kk)) for i in range(n_dp)])

    def along(quad):
        quad = plus(*quad)
        low = quad.astype(BF16)
        return plus(quad[:, 0], *[pz_to(low[:, kk], kk) for kk in range(1, m)])

    def along_steps(quad):
        quad = plus(*quad)
        got = pz_to(quad[:, 1::2].astype(BF16), 1)
        quad = plus(quad[:, 0::2], got)
        return plus(quad[:, 0], pz_to(quad[:, 1].astype(BF16), 2))

    def pn(a):
        return lax.ppermute(a, ("dp", "tensor"), [(2 * i + 1, 2 * i + 3) for i in range(n_dp - 1)])

    def tails(keep, got):
        tail = select[:, local_rows:]
        return pn(jnp.stack([tn(tail, keep), tn(tail, got)]).astype(BF16))

    def placed(keep, got, tail):
        def place(a, b):
            a = tn(select[:, :local_rows], a).astype(BF16)
            return jnp.concatenate([a[:IMG_PAD] + b, a[IMG_PAD:]], 0)

        return jnp.stack([place(keep, tail[0]), place(got, tail[1])])

    def ordered(a, b):
        a = a + b
        return jnp.where(sec == 0, a, a[::-1])[None]

    batch_tokens = lax.dynamic_index_in_dim(tokens, sec, 0, keepdims=False)
    batch_cot = lax.dynamic_index_in_dim(cotangent, sec, 0, keepdims=False)
    count = lax.dynamic_index_in_dim(image_counts, sec, 0, keepdims=False)
    first = jnp.minimum((dp * local_rows + IMG_LEN - 1) // IMG_LEN, images)
    last = jnp.minimum(((dp + 1) * local_rows + IMG_LEN - 1) // IMG_LEN, images)
    held = last - first
    slots = -(-(-(-local_rows // IMG_LEN)) // 2)
    lower = held // 2
    own_first = jnp.where(ten == 0, first, first + lower)
    own_count = jnp.where(ten == 0, lower, held - lower)
    total = slots * IMG_PAD
    row = lax.broadcasted_iota(jnp.int32, (total, 1), 0)
    slot, inside = row // IMG_PAD, row % IMG_PAD
    exists = (inside < IMG_LEN) & (slot < own_count)
    target = (own_first + slot) * IMG_LEN + inside - dp * local_rows
    canvas_rows = local_rows + IMG_PAD
    select = ((lax.broadcasted_iota(jnp.int32, (total, canvas_rows), 1) == target) & exists).astype(BF16)
    scalars = jnp.stack([jnp.minimum(own_count, jnp.maximum(count - own_first, 0)), ten, sec, zi, yi]).astype(jnp.int32)

    both = jnp.stack([batch_tokens, batch_cot])
    halo = lax.ppermute(both[:, :IMG_PAD], ("dp", "tensor"), [(2 * i + 3, 2 * i + 1) for i in range(n_dp - 1)])
    q, k, v = [[qkv_weight[0, :, i, h * HD:(h + 1) * HD] for h in range(3)] for i in range(3)]
    o = out_weight[0].T
    o = [o[:, h * HD:(h + 1) * HD] for h in range(3)]
    misc = jnp.concatenate([norm_gains[0], row_biases[0]], 0).T
    misc = jnp.pad(misc, ((0, 0), (0, BLOCK - misc.shape[1])))
    gap = jnp.zeros((HD,), BF16)
    rows = jnp.concatenate([qv_bias[0, 0], gap, gap, gap, qv_bias[0, 1], gap, up_bias[0]]).reshape(-1, BLOCK)
    rows = jnp.pad(rows, ((0, piece - rows.shape[0]), (0, 0)))
    up, down = up_weight[0], down_weight[0].T
    part0 = jnp.concatenate([q[0], q[1], q[2], k[2], k[0], k[1], misc, up], 1)
    part1 = jnp.concatenate([v[0], v[1], v[2], o[2], o[0], o[1], rows, down], 1)

    if direct:
        keep = jnp.where(sec == 0, part0, part1)
        give = jnp.where(sec == 0, part1, part0)
        got, halo = after(px(give), halo)
        start = [jnp.where(sec == 0, keep, got), jnp.where(sec == 0, got, keep)]

        def load(l, sc, src, w, sem, c):
            copies = []
            cols = slice(0, MLP) if c == 0 else slice(MLP, HALF)
            for side in range(2):
                t = jnp.where(sc[1] == 0, side, 1 - side)
                own = src[side * 8:side * 8 + 8]
                for kk in range(m):
                    z = lax.bitwise_xor(sc[3], kk)
                    near = pl.ds(pl.multiple_of((2 * z + sc[4]) * piece, 16), piece)
                    far = pl.ds(pl.multiple_of((2 * z + 1 - sc[4]) * piece, 16), piece)
                    for i, (h, r) in enumerate(((sc[2], near), (1 - sc[2], near), (sc[2], far), (1 - sc[2], far))):
                        a = own[i].at[l, :, cols] if kk == 0 else own[4 + i].at[kk - 1, :, cols]
                        copies.append(pltpu.make_async_copy(a, w.at[t, h, r, cols], sem.at[c]))
            return copies

        def store(sc, side, g, dst, sem):
            copies = []
            for hr in range(2):
                h = jnp.where(sc[2] == 0, hr, 1 - hr)
                for yr in range(2):
                    y = jnp.where(sc[4] == 0, yr, 1 - yr)
                    for kk in range(m):
                        z = lax.bitwise_xor(sc[3], kk)
                        r = pl.ds(pl.multiple_of((2 * z + y) * piece, 16), piece)
                        out = dst[0].at[hr, yr] if side == 0 else dst[hr * 2 + yr]
                        for c in range(2):
                            a = g.at[h, r, c * part:(c + 1) * part]
                            copies.append(pltpu.make_async_copy(a, out.at[c, kk], sem))
            return copies

        part = HALF // 2
        out_shapes = [[((2, 2, 2, m, piece, part), BF16)], [((2, m, piece, part), BF16)] * 4]
        own = jnp.stack(start)
        firsts = [own, px(own), py(own), pd(own)]
        columns = [jnp.stack([pz_to(start[0], kk) for kk in range(1, m)])]
        start[1], columns[0] = after(start[1], columns[0])
        columns[0], *firsts = after(columns[0], *firsts)
        rest = [columns[0], px(columns[0]), py(columns[0]), pd(columns[0])]
        near = pz_to(start[1], 1)
        columns.append(jnp.concatenate([near[None], pz_to(jnp.stack([start[1], near]), 2)]))
        columns[1], *rest = after(columns[1], *rest)
        twins = [pt(a) for a in firsts]
        sources = [firsts + rest + twins + [pt(a) for a in rest]]
        sources.append(columns[1:] + [px(columns[1]), py(columns[1]), pd(columns[1])])
    else:
        def load(l, sc, src, w, sem, c):
            return [pltpu.make_async_copy(src[0], w, sem.at[c])] if c == 0 else []

        def store(sc, side, g, dst, sem):
            return [pltpu.make_async_copy(g, dst[0], sem)]

        out_shapes = [[((2, width, HALF), BF16)]] * 2
        a = lax.all_gather(jnp.stack([part0, part1]), "dp", axis=1, tiled=True)
        a = lax.all_gather(lax.all_gather(a, "tensor"), "section")
        sources = [[a[0]], [a[1]]]

    batch = jnp.concatenate([both, halo], 1)
    x0 = nn(select, batch[0]).astype(BF16)
    cot = nn(select, batch[1]).astype(BF16)

    def call(l, phases, **given):
        return layer_call(phases, sources[l], functools.partial(load, l), store, out_shapes, scalars, given, total,
                          width, ff, piece)

    r0 = call(0, ["forward"], x=x0)
    low0 = r0["out"]
    if direct:
        low0, *rest = after(low0, *sources[1])
        sources[1] = firsts + rest + twins + [pt(a) for a in rest]
    r1 = call(1, ["forward", "back", "theirs"], x=low0, u=cot)
    if direct:
        got1 = pt(r1["g"][0])
    low_got = px(r1["give"])
    m1 = call(1, ["mine"], **r1)
    u = r1["in"]
    if direct:
        first, got1 = after(m1["g"][0], got1)
        sent1 = add_pair([first] + m1["g"][1:], got1)
        u, low_got, *sent1 = after(u, low_got, *sent1)
        low_tails = tails(r1["keep"], low_got)
        quad1 = across(sent1)
    else:
        low_tails = tails(r1["keep"], low_got)
    b0 = call(0, ["back", "theirs"], **{**r0, "u": u})
    if direct:
        b0["dg"], b0["g"][0], low_tails, *quad1 = after(b0["dg"], b0["g"][0], low_tails, *quad1)
        got0 = pt(b0["g"][0])
    low_rows = placed(r1["keep"], low_got, low_tails)
    low_twin = pt(low_rows)
    in_got = px(b0["give"])
    m0 = call(0, ["mine"], **{**r0, **b0})

    if direct:
        first, got0, low_twin = after(m0["g"][0], got0, low_twin)
        sent0 = add_pair([first] + m0["g"][1:], got0)
        both = after(in_got, *sent0, *quad1)
        in_got, sent0, quad1 = both[0], both[1:5], both[5:]
        in_tails = tails(b0["keep"], in_got)
        quad0 = [across([a[c:c + 1] for a in sent0]) for c in range(2)]
        in_rows = placed(b0["keep"], in_got, in_tails)
        in_twin, *quad0[1] = after(pt(in_rows), *quad0[1])
        done1 = along_steps(quad1)
        done0 = [along_steps(quad0[0])]
        done0 = jnp.concatenate(done0 + [along(quad0[1])])
        mine = jnp.where(sec == 0, done0, done1)
        other = px(jnp.where(sec == 0, done1, done0).astype(BF16)).astype(F32)
        final0 = jnp.where(sec == 0, mine, other)
        final1 = jnp.where(sec == 0, other, mine)
        final0, final1 = [jnp.concatenate([a[0], a[1]], 1) for a in (final0, final1)]
        small = final1[:, MISC:MLP]
    else:
        in_rows = placed(b0["keep"], in_got, tails(b0["keep"], in_got))
        in_twin = pt(in_rows)

        def by_core(a, b):
            return jnp.where(ten == 0, jnp.stack([b, a]), jnp.stack([a, b]))

        g = jnp.stack([by_core(b0["g"][0], m0["g"][0]), by_core(r1["g"][0], m1["g"][0])])
        g = lax.psum_scatter(g.astype(F32), "section", scatter_dimension=0)
        g = lax.psum_scatter(g, "tensor", scatter_dimension=0)
        g = lax.psum_scatter(g, "dp", scatter_dimension=1, tiled=True)
        final0, final1 = g[0], g[1]
        small = lax.psum(jnp.stack([b0["bsum"], r1["bsum"]]), ("section", "tensor", "dp"))
        small = lax.dynamic_index_in_dim(lax.dynamic_index_in_dim(small, sec, 0, False), ten, 0, False)

    layer_outputs = ordered(low_rows, low_twin)
    input_grads = ordered(in_rows, in_twin).astype(F32)

    def heads(a, *starts):
        return [a[:, s * HD:(s + 1) * HD] for s in starts]

    small = small.reshape(-1)
    qkv = jnp.concatenate(heads(final0, 0, 1, 2, 4, 5, 3) + heads(final1, 0, 1, 2), 1).reshape(1, piece, 3, 3 * HD)
    return (
        layer_outputs,
        input_grads,
        final0[:, MISC:MISC + 2].T[None],
        final0[:, MISC + 2:MISC + 6].T[None],
        qkv,
        jnp.stack([small[:3 * HD], small[6 * HD:9 * HD]])[None],
        jnp.concatenate(heads(final1, 4, 5, 3), 1).T[None],
        final0[:, MLP:][None],
        small[ATT:ATT + ff // 2][None],
        final1[:, MLP:].T[None],
    )


def solution(mesh):
    in_specs = (
        P(None, "dp", None),
        P(),
        P(None, "dp", None),
        P("section", None, "dp"),
        P("section", None, "dp"),
        P("section", "dp", None, "tensor"),
        P("section", None, "tensor"),
        P("section", "tensor", "dp"),
        P("section", "dp", "tensor"),
        P("section", "tensor"),
        P("section", "tensor", "dp"),
    )
    out_specs = (
        P("section", None, "dp", None),
        P("section", None, "dp", None),
        P("section", None, "dp"),
        P("section", None, "dp"),
        P("section", "dp", None, "tensor"),
        P("section", None, "tensor"),
        P("section", "tensor", "dp"),
        P("section", "dp", "tensor"),
        P("section", "tensor"),
        P("section", "tensor", "dp"),
    )
    return jax.shard_map(shards, mesh=mesh, in_specs=in_specs, out_specs=out_specs, check_vma=False)
```

```python
import functools
import math

import jax
import jax.numpy as jnp
from jax import lax
from jax.experimental import pallas as pl
from jax.experimental.pallas import tpu as pltpu
from jax.sharding import PartitionSpec as P

IMG_LEN = 197
IMG_PAD = 208
HD = 64
EPSILON = 1e-06
NEGATIVE = -1e30
F32 = jnp.float32
BF16 = jnp.bfloat16
BLOCK = 128
HALF = 1280
COST = 10 ** 10
SCALE = 1.0 / math.sqrt(HD)


def mm(a, b, dims):
    return lax.dot_general(a, b, (dims, ((), ())), preferred_element_type=F32)


def nn(a, b):
    return mm(a, b, ((1,), (0,)))


def nt(a, b):
    return mm(a, b, ((1,), (1,)))


def tn(a, b):
    return mm(a, b, ((0,), (0,)))


def normed(x):
    centred = x - jnp.mean(x, -1, keepdims=True)
    inverse = lax.rsqrt(jnp.mean(centred * centred, -1, keepdims=True) + EPSILON)
    return centred * inverse, inverse


def norm_back(grad, xhat, inverse, gain):
    t = grad * gain
    return inverse * (
        t - jnp.mean(t, -1, keepdims=True) - xhat * jnp.mean(t * xhat, -1, keepdims=True)
    )


def gelu_parts(u):
    cdf = 0.5 * (1.0 + lax.erf(u * math.sqrt(0.5)))
    pdf = jnp.exp(-0.5 * u * u) * (1.0 / math.sqrt(2.0 * math.pi))
    return u * cdf, cdf + u * pdf


QK = 384
V = 256
OUT = 128
MISC = 384
MLP = 512
ATT = QK + V


def low_lanes():
    return lax.broadcasted_iota(jnp.int32, (1, BLOCK), 1) < HD


def turn(a):
    return jnp.concatenate([a[:, HD:], a[:, :HD]], 1)


def valid_rows(sc, n):
    row = lax.broadcasted_iota(jnp.int32, (IMG_PAD, 1), 0)
    return jnp.where((row < IMG_LEN) & (n < sc[0]), 1.0, 0.0)


def image_rows(n):
    return pl.ds(pl.multiple_of(n * IMG_PAD, 16), IMG_PAD)


def forward_image(n, sc, x_ref, w, vec, brow, out_ref, kept, ready):
    r = image_rows(n)
    x = x_ref[r, :].astype(F32)
    xhat, inv = normed(x)
    attn_in = (xhat * vec[0:1, :] + vec[2:3, :]).astype(BF16)
    kept["xh1"][r, :] = xhat
    kept["inv1"][r, :] = jnp.broadcast_to(inv, (IMG_PAD, BLOCK))
    kept["ain"][r, :] = attn_in
    residual = x + vec[3:4, :]
    low = low_lanes()
    lane = lax.broadcasted_iota(jnp.int32, (1, ATT), 1)
    factor = jnp.where(lane < 192, SCALE, jnp.where(lane < 576, 1.0, 0.0))
    real = lax.broadcasted_iota(jnp.int32, (1, IMG_PAD), 1) < IMG_LEN
    for t in range(2):
        bias = jnp.concatenate([brow[t, i:i + 1, :] for i in range(5)], 1)
        p = jnp.concatenate([nn(attn_in, w[t, 0, :, :QK]), nn(attn_in, w[t, 1, :, :V])], 1)
        p = ((p + bias) * factor).astype(BF16)
        kept["qkv"][t, r, :] = p
        q, qk, k, v, vx = [p[:, i * BLOCK:(i + 1) * BLOCK] for i in range(5)]
        kq, xv = turn(qk), turn(vx)
        outs = []
        for i, (qq, kk, vv) in enumerate(
                [(jnp.where(low, q, 0), k, v), (jnp.where(low, 0, q), k, v), (jnp.where(low, qk, 0), kq, xv)]):
            s = jnp.where(real, nt(qq, kk), NEGATIVE)
            e = jnp.exp(s - jnp.max(s, -1, keepdims=True))
            pr = (e * (1.0 / jnp.sum(e, -1, keepdims=True))).astype(BF16)
            kept["pr"][n * 6 + t * 3 + i] = pr
            outs.append(nn(pr, vv))
        mixed = jnp.concatenate([outs[2], jnp.where(low, outs[0], outs[1])], 1).astype(BF16)
        kept["mx"][t, r, :] = mixed
        residual = residual + nt(mixed, w[t, 1, :, OUT:MISC])
    xhat, inv = normed(residual)
    mlp_in = (xhat * vec[1:2, :] + vec[4:5, :]).astype(BF16)
    kept["xh2"][r, :] = xhat
    kept["inv2"][r, :] = jnp.broadcast_to(inv, (IMG_PAD, BLOCK))
    kept["min"][r, :] = mlp_in
    out = residual + vec[5:6, :]
    ready(1)
    ff = kept["hd"].shape[1] // 2
    for t in range(2):
        bias = jnp.concatenate([brow[t, 5 + i:6 + i, :] for i in range(ff // BLOCK)], 1)
        hidden, slope = gelu_parts(nn(mlp_in, w[t, 0, :, MLP:]) + bias)
        hidden = hidden.astype(BF16)
        kept["hd"][r, t * ff:(t + 1) * ff] = hidden
        kept["sl"][r, t * ff:(t + 1) * ff] = slope.astype(BF16)
        out = out + nt(hidden, w[t, 1, :, MLP:])
    out_ref[r, :] = (out * valid_rows(sc, n)).astype(BF16)


def rsum(a):
    return jnp.sum(a, 0, keepdims=True)


def backward_mlp(n, sc, u_ref, w, vec, kept, grad, sums, bsum):
    r = image_rows(n)

    masked = u_ref[r, :].astype(F32) * valid_rows(sc, n)
    sums[5:6, :] += rsum(masked)
    dg = masked.astype(BF16)
    grad["dg"][r, :] = dg
    mg = jnp.zeros(masked.shape, F32)
    ff = kept["hd"].shape[1] // 2
    for t in range(2):
        c = slice(t * ff, (t + 1) * ff)
        up = (nn(dg, w[t, 1, :, MLP:]) * kept["sl"][r, c].astype(F32)).astype(BF16)
        grad["up"][r, c] = up
        total = rsum(up.astype(F32))
        for i in range(ff // BLOCK):
            bsum[t, 5 + i:6 + i, :] += total[:, i * BLOCK:(i + 1) * BLOCK]
        mg = mg + nt(up, w[t, 0, :, MLP:])
    xhat = kept["xh2"][r, :]
    sums[4:5, :] += rsum(mg)
    sums[1:2, :] += rsum(mg * xhat)
    res = masked + norm_back(mg, xhat, kept["inv2"][r, :1], vec[1:2, :])
    sums[3:4, :] += rsum(res)
    grad["res"][r, :] = res


def backward_attention(n, w, vec, in_ref, kept, grad, sums, bsum):
    r = image_rows(n)
    res = grad["res"][r, :]
    ag = res.astype(BF16)
    grad["ag"][r, :] = ag
    low = low_lanes()
    ig = jnp.zeros(res.shape, F32)
    for t in range(2):
        xg = nn(ag, w[t, 1, :, OUT:MISC]).astype(BF16)
        gx = jnp.where(low, 0, xg[:, :BLOCK])
        g = xg[:, BLOCK:]
        p = kept["qkv"][t, r, :]
        q, qk, k, v, vx = [p[:, i * BLOCK:(i + 1) * BLOCK] for i in range(5)]
        kq, xv = turn(qk), turn(vx)
        dq, dk, dv = [], [], []
        for i, (qq, kk, vv, gm, gg) in enumerate(
                [(q, k, v, jnp.where(low, g, 0), g), (q, k, v, jnp.where(low, 0, g), g), (qk, kq, xv, gx, turn(gx))]):
            pb = kept["pr"][n * 6 + t * 3 + i]
            pf = pb.astype(F32)
            dp = nt(gm, vv)
            ds = (pf * (dp - jnp.sum(pf * dp, -1, keepdims=True))).astype(BF16)
            dv.append(tn(pb, gg))
            dq.append(nn(ds, kk) * SCALE)
            dk.append(tn(ds, kq if i == 2 else qq))
        blocks = [
            jnp.where(low, dq[0], dq[1]), jnp.where(low, dq[2], dk[2]), jnp.where(low, dk[0], dk[1]),
            jnp.where(low, dv[0], dv[1]), dv[2],
        ]
        d = jnp.concatenate(blocks, 1).astype(BF16)
        grad["dqkv"][t, r, :] = d
        total = rsum(d.astype(F32))
        for i in range(5):
            bsum[t, i:i + 1, :] += total[:, i * BLOCK:(i + 1) * BLOCK]
        ig = ig + nt(d[:, :QK], w[t, 0, :, :QK]) + nt(d[:, QK:], w[t, 1, :, :V])
    xhat = kept["xh1"][r, :]
    sums[2:3, :] += rsum(ig)
    sums[0:1, :] += rsum(ig * xhat)
    in_ref[r, :] = res + norm_back(ig, xhat, kept["inv1"][r, :1], vec[0:1, :])


def weight_grads(t, piece, kept, grad, g):
    ag, dg = grad["ag"][...], grad["dg"][...]
    ain, mlp_in = kept["ain"][...], kept["min"][...]
    width = ag.shape[1]
    high = jnp.where(low_lanes(), 0.0, 1.0)
    d = grad["dqkv"][t]
    g[0, :, :QK] = tn(ain, d[:, :QK]).astype(BF16)
    val = tn(ain, d[:, QK:])
    out = tn(ag, kept["mx"][t])
    g[1, :, :OUT] = val[:, :BLOCK].astype(BF16)
    g[1, :, OUT:V] = (val[:, BLOCK:] + out[:, :BLOCK] * high).astype(BF16)
    g[1, :, V:MISC] = out[:, BLOCK:].astype(BF16)
    sums = jnp.concatenate([grad["sums"][...], jnp.zeros((BLOCK - 8, width), F32)], 0)
    g[0, :, MISC:MLP] = sums.T.astype(BF16)
    ff = kept["hd"].shape[1] // 2
    c = pl.ds(pl.multiple_of(t * ff, BLOCK), ff)
    g[0, :, MLP:] = tn(mlp_in, grad["up"][:, c]).astype(BF16)
    g[1, :, MLP:] = tn(dg, kept["hd"][:, c]).astype(BF16)
    if piece % 16 == 0:
        rows = jnp.concatenate([grad["bsum"][t], jnp.zeros((piece - 16, BLOCK), F32)], 0).astype(BF16)
        for i in range(width // piece):
            g[1, i * piece:(i + 1) * piece, MISC:MLP] = rows


def kept_shapes(total, width, ff):
    images = total // IMG_PAD
    return dict(
        xh1=((total, width), F32), inv1=((total, BLOCK), F32), ain=((total, width), BF16), qkv=((2, total, ATT), BF16),
        pr=((images * 6, IMG_PAD, IMG_PAD), BF16), mx=((2, total, 2 * BLOCK), BF16), xh2=((total, width), F32),
        inv2=((total, BLOCK), F32), min=((total, width), BF16), sl=((total, ff), BF16), hd=((total, ff), BF16))


def grad_shapes(total, width, ff):
    return dict(dg=((total, width), BF16), up=((total, ff), BF16), res=((total, width), F32), sums=((8, width), F32),
                bsum=((2, 16, BLOCK), F32), ag=((total, width), BF16), dqkv=((2, total, ATT), BF16))


def layer_call(phases, sources, load, store, out_shapes, scalars, given, total, width, ff, piece):
    ks = kept_shapes(total, width, ff)
    gs = grad_shapes(total, width, ff)
    weights = ["ain", "mx", "min", "hd"] + [n for n in gs if n != "res"]
    need = {"forward": ["x"], "back": ["u"] + list(ks), "theirs": weights, "mine": weights}
    gives = {"forward": {"out": ((total, width), BF16), **ks}, "back": {"keep": ((total, width), BF16), "give": ((total, width), BF16), "in": ((total, width), F32), **gs},
             "theirs": {}, "mine": {}}
    made = {}
    for p in phases:
        made.update(gives[p])
    inputs = list(dict.fromkeys(n for p in phases for n in need[p] if n not in made))
    if phases[-1] == "forward":
        shown = list(made)
    else:
        shown = [n for n in made if n in weights or n in ("keep", "give")]
        if "forward" in phases:
            shown.append("in")
    inner = [n for n in made if n not in shown]
    side = {"theirs": 0, "mine": 1}.get(phases[-1])
    products = phases[0] != "mine"
    vmem = pl.BlockSpec(memory_space=pltpu.VMEM)
    anywhere = pl.BlockSpec(memory_space=pl.ANY)
    ends = [] if side is None else out_shapes[side]
    scratch = [pltpu.SemaphoreType.DMA((2,))] + [pltpu.VMEM(*made[n]) for n in inner]
    if products:
        scratch += [pltpu.VMEM((2, 2, width, HALF), BF16), pltpu.VMEM((8, width), F32), pltpu.VMEM((2, 16, BLOCK), F32)]
    if ends:
        scratch.append(pltpu.VMEM((2, width, HALF), BF16))

    def body(*refs):
        refs = list(refs)

        def take(n):
            got = refs[:n]
            del refs[:n]
            return got

        sc = take(1)[0]
        at = dict(zip(inputs, take(len(inputs))))
        src = take(len(sources))
        at.update(zip(shown, take(len(shown))))
        dst = take(len(ends))
        sem = take(1)[0]
        at.update(zip(inner, take(len(inner))))
        if products:
            w, vec, brow = take(3)
            pending = [load(sc, src, w, sem, c) for c in range(2)]
            for part in pending if "forward" in phases else pending[::-1]:
                for c in part:
                    c.start()

            def ready(c):
                for copy in pending[c]:
                    copy.wait()
                if c == 0 and pending[c]:
                    vec[...] = w[0, 0, :, MISC:MLP].astype(F32).T[:8, :]
                    for t in range(2):
                        brow[t] = w[t, 1, :16, MISC:MLP].astype(F32)
                pending[c] = []

            ready(0 if "forward" in phases else 1)
        if "forward" in phases:
            for n in range(total // IMG_PAD):
                forward_image(n, sc, at["x"], w, vec, brow, at["out"], at, ready)
        if "back" in phases:
            sums, bsum = at["sums"], at["bsum"]
            sums[...] = jnp.zeros_like(sums)
            bsum[...] = jnp.zeros_like(bsum)
            ready(0)

            def back(n, carry):
                backward_mlp(n, sc, at["u"], w, vec, at, at, sums, bsum)
                backward_attention(n, w, vec, at["in"], at, at, sums, bsum)
                return carry
            lax.fori_loop(0, total // IMG_PAD, back, 0)
            rows = [at[n] for n in (("x", "out") if "forward" in phases else ("in", "u"))]
            for here in range(2):
                @pl.when(sc[2] == here)
                def _():
                    at["keep"][...] = rows[here][...].astype(BF16)
                    at["give"][...] = rows[1 - here][...].astype(BF16)
        if ends:
            g = take(1)[0]
            t = jnp.where(sc[1] == 0, 1 - side, side)
            weight_grads(t, piece, at, at, g)
            copies = store(sc, side, g, dst, sem.at[0])
            for c in copies:
                c.start()
            for c in copies:
                c.wait()

    outs = [made[n] for n in shown] + ends
    args = [scalars, *[given[n] for n in inputs], *(sources if products else [])]
    if not products:
        sources = []
    got = pl.pallas_call(
        body,
        out_shape=[jax.ShapeDtypeStruct(*o) for o in outs],
        in_specs=[pl.BlockSpec(memory_space=pltpu.SMEM)] + [vmem] * len(inputs) + [anywhere] * len(sources),
        out_specs=[vmem] * (len(outs) - len(ends)) + [anywhere] * len(ends),
        scratch_shapes=scratch,
        compiler_params=pltpu.CompilerParams(vmem_limit_bytes=34 * 2 ** 20),
        cost_estimate=pl.CostEstimate(flops=COST * len(phases), transcendentals=0, bytes_accessed=2 ** 23),
    )(*args)
    got = list(got)
    res = dict(zip(shown, got))
    res["g"] = got[len(shown):]
    return res


def parts(a, b, ff):
    small = a[:, MISC:MLP].T
    rows = b[:16, MISC:MLP]

    def heads(c, pair, single):
        return jnp.concatenate([c[:, pair:pair + BLOCK], c[:, single:single + HD]], 1)

    def lanes(first, last):
        return jnp.concatenate([rows[i:i + 1, :] for i in range(first, last)], 1)

    size = 3 * HD
    qkv = jnp.stack([heads(a, 0, BLOCK), heads(a, 2 * BLOCK, BLOCK + HD), heads(b, 0, BLOCK)])
    biases = jnp.concatenate([lanes(0, 2)[:, :size], lanes(3, 5)[:, :size]], 0)
    out = heads(b, 2 * BLOCK, BLOCK + HD)
    return small[:2], small[2:6], qkv, biases, out, a[:, MLP:], lanes(5, 5 + ff // BLOCK), b[:, MLP:]


def finish(scalars, mine, other, ff):
    piece = mine.shape[0]

    def body(sc, mine_ref, other_ref, *outs):
        first = sc[2] == 0
        a, b = mine_ref[...], other_ref[...].astype(F32)
        for ref, got in zip(outs, parts(jnp.where(first, a, b), jnp.where(first, b, a), ff)):
            ref[...] = got

    vmem = pl.BlockSpec(memory_space=pltpu.VMEM)
    shapes = [(2, piece), (4, piece), (3, piece, 3 * HD), (2, 3 * HD), (piece, 3 * HD), (piece, ff), (1, ff), (piece, ff)]
    return pl.pallas_call(
        body,
        out_shape=[jax.ShapeDtypeStruct(s, F32) for s in shapes],
        in_specs=[pl.BlockSpec(memory_space=pltpu.SMEM), vmem, vmem],
        out_specs=[vmem] * len(shapes),
    )(scalars, mine, other)


def shards(tokens, image_counts, cotangent, norm_gains, row_biases, qkv_weight, qv_bias, out_weight,
           up_weight, up_bias, down_weight):
    sec = lax.axis_index("section")
    dp = lax.axis_index("dp")
    ten = lax.axis_index("tensor")
    n_dp = lax.axis_size("dp")
    m = n_dp // 2
    zi, yi = dp // 2, dp % 2
    local_rows, width = tokens.shape[1:]
    images = local_rows * n_dp // IMG_LEN
    piece = width // n_dp
    ff = 2 * up_weight.shape[2]
    direct = piece % 16 == 0 and m == 4

    def pt(a):
        return lax.ppermute(a, "tensor", [(0, 1), (1, 0)])

    def px(a):
        return lax.ppermute(a, "section", [(0, 1), (1, 0)])

    def py(a):
        return lax.ppermute(a, "dp", [(i, i ^ 1) for i in range(n_dp)])

    def pd(a):
        return lax.ppermute(a, ("section", "dp"), [(i, (i + n_dp) % (2 * n_dp) ^ 1) for i in range(2 * n_dp)])

    def after(a, *b):
        return lax.optimization_barrier((a, *b))

    def plus(*a):
        return sum(b.astype(F32) for b in a)

    def add_pair(g, got):
        keep, to_y, to_x, to_d = [plus(a, b) for a, b in zip(g, (got[0, 0], got[0, 1], got[1, 0], got[1, 1]))]
        return [keep, to_y.astype(BF16), to_x.astype(BF16), to_d.astype(BF16)]

    def across(sent):
        return [sent[0], py(sent[1]), px(sent[2]), pd(sent[3])]

    def pz_to(a, kk):
        return lax.ppermute(a, "dp", [(i, i ^ (2 * kk)) for i in range(n_dp)])

    def along(quad):
        quad = plus(*quad)
        low = quad.astype(BF16)
        return plus(quad[:, 0], *[pz_to(low[:, kk], kk) for kk in range(1, m)])

    def along_steps(quad):
        quad = plus(*quad)
        got = pz_to(quad[:, 1::2].astype(BF16), 1)
        quad = plus(quad[:, 0::2], got)
        return plus(quad[:, 0], pz_to(quad[:, 1].astype(BF16), 2))

    def pn(a):
        return lax.ppermute(a, ("dp", "tensor"), [(2 * i + 1, 2 * i + 3) for i in range(n_dp - 1)])

    def tails(keep, got):
        tail = select[:, local_rows:]
        return pn(jnp.stack([tn(tail, keep), tn(tail, got)]).astype(BF16))

    def placed(keep, got, tail):
        def place(a, b):
            a = tn(select[:, :local_rows], a).astype(BF16)
            return jnp.concatenate([a[:IMG_PAD] + b, a[IMG_PAD:]], 0)

        return jnp.stack([place(keep, tail[0]), place(got, tail[1])])

    def ordered(a, b):
        a = a + b
        return jnp.where(sec == 0, a, a[::-1])[None]

    batch_tokens = lax.dynamic_index_in_dim(tokens, sec, 0, keepdims=False)
    batch_cot = lax.dynamic_index_in_dim(cotangent, sec, 0, keepdims=False)
    count = lax.dynamic_index_in_dim(image_counts, sec, 0, keepdims=False)
    first = jnp.minimum((dp * local_rows + IMG_LEN - 1) // IMG_LEN, images)
    last = jnp.minimum(((dp + 1) * local_rows + IMG_LEN - 1) // IMG_LEN, images)
    held = last - first
    slots = -(-(-(-local_rows // IMG_LEN)) // 2)
    lower = held // 2
    own_first = jnp.where(ten == 0, first, first + lower)
    own_count = jnp.where(ten == 0, lower, held - lower)
    total = slots * IMG_PAD
    row = lax.broadcasted_iota(jnp.int32, (total, 1), 0)
    slot, inside = row // IMG_PAD, row % IMG_PAD
    exists = (inside < IMG_LEN) & (slot < own_count)
    target = (own_first + slot) * IMG_LEN + inside - dp * local_rows
    canvas_rows = local_rows + IMG_PAD
    select = ((lax.broadcasted_iota(jnp.int32, (total, canvas_rows), 1) == target) & exists).astype(BF16)
    scalars = jnp.stack([jnp.minimum(own_count, jnp.maximum(count - own_first, 0)), ten, sec, zi, yi]).astype(jnp.int32)

    both = jnp.stack([batch_tokens, batch_cot])
    halo = lax.ppermute(both[:, :IMG_PAD], ("dp", "tensor"), [(2 * i + 3, 2 * i + 1) for i in range(n_dp - 1)])
    q, k, v = [[qkv_weight[0, :, i, h * HD:(h + 1) * HD] for h in range(3)] for i in range(3)]
    o = out_weight[0].T
    o = [o[:, h * HD:(h + 1) * HD] for h in range(3)]
    misc = jnp.concatenate([norm_gains[0], row_biases[0]], 0).T
    misc = jnp.pad(misc, ((0, 0), (0, BLOCK - misc.shape[1])))
    gap = jnp.zeros((HD,), BF16)
    rows = jnp.concatenate([qv_bias[0, 0], gap, gap, gap, qv_bias[0, 1], gap, up_bias[0]]).reshape(-1, BLOCK)
    rows = jnp.pad(rows, ((0, piece - rows.shape[0]), (0, 0)))
    up, down = up_weight[0], down_weight[0].T
    part0 = jnp.concatenate([q[0], q[1], q[2], k[2], k[0], k[1], misc, up], 1)
    part1 = jnp.concatenate([v[0], v[1], v[2], o[2], o[0], o[1], rows, down], 1)

    if direct:
        keep = jnp.where(sec == 0, part0, part1)
        give = jnp.where(sec == 0, part1, part0)
        got, halo = after(px(give), halo)
        start = [jnp.where(sec == 0, keep, got), jnp.where(sec == 0, got, keep)]

        def load(l, sc, src, w, sem, c):
            copies = []
            cols = slice(0, MLP) if c == 0 else slice(MLP, HALF)
            for side in range(2):
                t = jnp.where(sc[1] == 0, side, 1 - side)
                own = src[side * 8:side * 8 + 8]
                for kk in range(m):
                    z = lax.bitwise_xor(sc[3], kk)
                    near = pl.ds(pl.multiple_of((2 * z + sc[4]) * piece, 16), piece)
                    far = pl.ds(pl.multiple_of((2 * z + 1 - sc[4]) * piece, 16), piece)
                    for i, (h, r) in enumerate(((sc[2], near), (1 - sc[2], near), (sc[2], far), (1 - sc[2], far))):
                        a = own[i].at[l, :, cols] if kk == 0 else own[4 + i].at[kk - 1, :, cols]
                        copies.append(pltpu.make_async_copy(a, w.at[t, h, r, cols], sem.at[c]))
            return copies

        def store(l, sc, side, g, dst, sem):
            chunks = 2 - l
            part = HALF // chunks
            copies = []
            for hr in range(2):
                h = jnp.where(sc[2] == 0, hr, 1 - hr)
                for yr in range(2):
                    y = jnp.where(sc[4] == 0, yr, 1 - yr)
                    for kk in range(m):
                        z = lax.bitwise_xor(sc[3], kk)
                        r = pl.ds(pl.multiple_of((2 * z + y) * piece, 16), piece)
                        out = dst[0].at[hr, yr] if side == 0 else dst[hr * 2 + yr]
                        for c in range(chunks):
                            a = g.at[h, r, c * part:(c + 1) * part]
                            copies.append(pltpu.make_async_copy(a, out.at[c, kk], sem))
            return copies

        shapes = [(c, m, piece, HALF // c) for c in (2, 1)]
        out_shapes = [[[((2, 2) + s, BF16)], [(s, BF16)] * 4] for s in shapes]
        own = jnp.stack(start)
        firsts = [own, px(own), py(own), pd(own)]
        columns = [jnp.stack([pz_to(start[0], kk) for kk in range(1, m)])]
        start[1], columns[0] = after(start[1], columns[0])
        columns[0], *firsts = after(columns[0], *firsts)
        rest = [columns[0], px(columns[0]), py(columns[0]), pd(columns[0])]
        near = pz_to(start[1], 1)
        columns.append(jnp.concatenate([near[None], pz_to(jnp.stack([start[1], near]), 2)]))
        columns[1], *rest = after(columns[1], *rest)
        twins = [pt(a) for a in firsts]
        sources = [firsts + rest + twins + [pt(a) for a in rest]]
        sources.append(columns[1:] + [px(columns[1]), py(columns[1]), pd(columns[1])])
    else:
        def load(l, sc, src, w, sem, c):
            return [pltpu.make_async_copy(src[0], w, sem.at[c])] if c == 0 else []

        def store(l, sc, side, g, dst, sem):
            return [pltpu.make_async_copy(g, dst[0], sem)]

        out_shapes = [[[((2, width, HALF), BF16)]] * 2] * 2
        a = lax.all_gather(jnp.stack([part0, part1]), "dp", axis=1, tiled=True)
        a = lax.all_gather(lax.all_gather(a, "tensor"), "section")
        sources = [[a[0]], [a[1]]]

    batch = jnp.concatenate([both, halo], 1)
    x0 = nn(select, batch[0]).astype(BF16)
    cot = nn(select, batch[1]).astype(BF16)
    x0, cot = after(x0, cot)

    def call(l, phases, **given):
        return layer_call(phases, sources[l], functools.partial(load, l), functools.partial(store, l), out_shapes[l],
                          scalars, given, total, width, ff, piece)

    r0 = call(0, ["forward"], x=x0)
    low0 = r0["out"]
    if direct:
        low0, *rest = after(low0, *sources[1])
        sources[1] = firsts + rest + twins + [pt(a) for a in rest]
    r1 = call(1, ["forward", "back", "theirs"], x=low0, u=cot)
    if direct:
        got1 = pt(r1["g"][0])
    low_got = px(r1["give"])
    m1 = call(1, ["mine"], **r1)
    u = r1["in"]
    if direct:
        first, got1 = after(m1["g"][0], got1)
        sent1 = add_pair([first] + m1["g"][1:], got1)
        u, low_got, *sent1 = after(u, low_got, *sent1)
        low_tails = tails(r1["keep"], low_got)
        quad1 = across(sent1)
    else:
        low_tails = tails(r1["keep"], low_got)
    b0 = call(0, ["back", "theirs"], **{**r0, "u": u})
    if direct:
        b0["dg"], b0["g"][0], low_tails, *quad1 = after(b0["dg"], b0["g"][0], low_tails, *quad1)
        got0 = pt(b0["g"][0])
    low_rows = placed(r1["keep"], low_got, low_tails)
    low_twin = pt(low_rows)
    in_got = px(b0["give"])
    m0 = call(0, ["mine"], **{**r0, **b0})

    if direct:
        first, got0, low_twin = after(m0["g"][0], got0, low_twin)
        sent0 = add_pair([first] + m0["g"][1:], got0)
        both = after(in_got, *sent0, *quad1)
        in_got, sent0, quad1 = both[0], both[1:5], both[5:]
        in_tails = tails(b0["keep"], in_got)
        quad0 = [across([a[c:c + 1] for a in sent0]) for c in range(2)]
        in_rows = placed(b0["keep"], in_got, in_tails)
        in_twin, *quad0[1] = after(pt(in_rows), *quad0[1])
        done1 = along_steps(quad1)[0]
        done1, *quad0[0] = after(done1, *quad0[0])
        done0 = jnp.concatenate([along_steps(quad0[0])[0], along(quad0[1])[0]], 1)
        mine = jnp.where(sec == 0, done0, done1)
        other = px(jnp.where(sec == 0, done1, done0).astype(BF16))
        g_gain, g_bias, g_qkv, g_qv, g_out, g_up, g_up_bias, g_down = finish(scalars, mine, other, ff // 2)
    else:
        in_rows = placed(b0["keep"], in_got, tails(b0["keep"], in_got))
        in_twin = pt(in_rows)

        def by_core(a, b):
            return jnp.where(ten == 0, jnp.stack([b, a]), jnp.stack([a, b]))

        g = jnp.stack([by_core(b0["g"][0], m0["g"][0]), by_core(r1["g"][0], m1["g"][0])])
        g = lax.psum_scatter(g.astype(F32), "section", scatter_dimension=0)
        g = lax.psum_scatter(g, "tensor", scatter_dimension=0)
        g = lax.psum_scatter(g, "dp", scatter_dimension=1, tiled=True)
        small = lax.psum(jnp.stack([b0["bsum"], r1["bsum"]]), ("section", "tensor", "dp"))
        small = lax.dynamic_index_in_dim(lax.dynamic_index_in_dim(small, sec, 0, False), ten, 0, False)
        g_gain, g_bias, g_qkv, _, g_out, g_up, _, g_down = parts(g[0], g[1], ff // 2)
        small = jnp.pad(small, ((0, 0), (MISC, HALF - MLP)))
        _, _, _, g_qv, _, _, g_up_bias, _ = parts(small, small, ff // 2)

    layer_outputs = ordered(low_rows, low_twin)
    input_grads = ordered(in_rows, in_twin).astype(F32)

    return (
        layer_outputs,
        input_grads,
        g_gain[None],
        g_bias[None],
        g_qkv.transpose(1, 0, 2)[None],
        g_qv[None],
        g_out.T[None],
        g_up[None],
        g_up_bias,
        g_down.T[None],
    )


def solution(mesh):
    in_specs = (
        P(None, "dp", None),
        P(),
        P(None, "dp", None),
        P("section", None, "dp"),
        P("section", None, "dp"),
        P("section", "dp", None, "tensor"),
        P("section", None, "tensor"),
        P("section", "tensor", "dp"),
        P("section", "dp", "tensor"),
        P("section", "tensor"),
        P("section", "tensor", "dp"),
    )
    out_specs = (
        P("section", None, "dp", None),
        P("section", None, "dp", None),
        P("section", None, "dp"),
        P("section", None, "dp"),
        P("section", "dp", None, "tensor"),
        P("section", None, "tensor"),
        P("section", "tensor", "dp"),
        P("section", "dp", "tensor"),
        P("section", "tensor"),
        P("section", "tensor", "dp"),
    )
    return jax.shard_map(shards, mesh=mesh, in_specs=in_specs, out_specs=out_specs, check_vma=False)
```

```python
import functools
import math

import jax
import jax.numpy as jnp
from jax import lax
from jax.experimental import pallas as pl
from jax.experimental.pallas import tpu as pltpu
from jax.sharding import PartitionSpec as P

IMG_LEN = 197
IMG_PAD = 208
HD = 64
EPSILON = 1e-06
NEGATIVE = -1e30
F32 = jnp.float32
BF16 = jnp.bfloat16
BLOCK = 128
HALF = 1280
COST = 10 ** 10
SCALE = 1.0 / math.sqrt(HD)


def mm(a, b, dims):
    return lax.dot_general(a, b, (dims, ((), ())), preferred_element_type=F32)


def nn(a, b):
    return mm(a, b, ((1,), (0,)))


def nt(a, b):
    return mm(a, b, ((1,), (1,)))


def tn(a, b):
    return mm(a, b, ((0,), (0,)))


def normed(x):
    centred = x - jnp.mean(x, -1, keepdims=True)
    inverse = lax.rsqrt(jnp.mean(centred * centred, -1, keepdims=True) + EPSILON)
    return centred * inverse, inverse


def norm_back(grad, xhat, inverse, gain):
    t = grad * gain
    return inverse * (
        t - jnp.mean(t, -1, keepdims=True) - xhat * jnp.mean(t * xhat, -1, keepdims=True)
    )


def gelu_parts(u):
    cdf = 0.5 * (1.0 + lax.erf(u * math.sqrt(0.5)))
    pdf = jnp.exp(-0.5 * u * u) * (1.0 / math.sqrt(2.0 * math.pi))
    return u * cdf, cdf + u * pdf


QK = 384
V = 256
OUT = 128
MISC = 384
MLP = 512
ATT = QK + V


def low_lanes():
    return lax.broadcasted_iota(jnp.int32, (1, BLOCK), 1) < HD


def turn(a):
    return jnp.concatenate([a[:, HD:], a[:, :HD]], 1)


def valid_rows(sc, n):
    row = lax.broadcasted_iota(jnp.int32, (IMG_PAD, 1), 0)
    return jnp.where((row < IMG_LEN) & (n < sc[0]), 1.0, 0.0)


def image_rows(n):
    return pl.ds(pl.multiple_of(n * IMG_PAD, 16), IMG_PAD)


def forward_image(n, sc, x_ref, w, vec, brow, out_ref, kept, ready):
    r = image_rows(n)
    x = x_ref[r, :].astype(F32)
    xhat, inv = normed(x)
    attn_in = (xhat * vec[0:1, :] + vec[2:3, :]).astype(BF16)
    kept["xh1"][r, :] = xhat
    kept["inv1"][r, :] = jnp.broadcast_to(inv, (IMG_PAD, BLOCK))
    kept["ain"][r, :] = attn_in
    residual = x + vec[3:4, :]
    low = low_lanes()
    lane = lax.broadcasted_iota(jnp.int32, (1, ATT), 1)
    factor = jnp.where(lane < 192, SCALE, jnp.where(lane < 576, 1.0, 0.0))
    real = lax.broadcasted_iota(jnp.int32, (1, IMG_PAD), 1) < IMG_LEN
    for t in range(2):
        bias = jnp.concatenate([brow[t, i:i + 1, :] for i in range(5)], 1)
        p = jnp.concatenate([nn(attn_in, w[t, 0, :, :QK]), nn(attn_in, w[t, 1, :, :V])], 1)
        p = ((p + bias) * factor).astype(BF16)
        kept["qkv"][t, r, :] = p
        q, qk, k, v, vx = [p[:, i * BLOCK:(i + 1) * BLOCK] for i in range(5)]
        kq, xv = turn(qk), turn(vx)
        outs = []
        for i, (qq, kk, vv) in enumerate(
                [(jnp.where(low, q, 0), k, v), (jnp.where(low, 0, q), k, v), (jnp.where(low, qk, 0), kq, xv)]):
            s = jnp.where(real, nt(qq, kk), NEGATIVE)
            e = jnp.exp(s - jnp.max(s, -1, keepdims=True))
            pr = (e * (1.0 / jnp.sum(e, -1, keepdims=True))).astype(BF16)
            kept["pr"][n * 6 + t * 3 + i] = pr
            outs.append(nn(pr, vv))
        mixed = jnp.concatenate([outs[2], jnp.where(low, outs[0], outs[1])], 1).astype(BF16)
        kept["mx"][t, r, :] = mixed
        residual = residual + nt(mixed, w[t, 1, :, OUT:MISC])
    xhat, inv = normed(residual)
    mlp_in = (xhat * vec[1:2, :] + vec[4:5, :]).astype(BF16)
    kept["xh2"][r, :] = xhat
    kept["inv2"][r, :] = jnp.broadcast_to(inv, (IMG_PAD, BLOCK))
    kept["min"][r, :] = mlp_in
    out = residual + vec[5:6, :]
    ready(1)
    ff = kept["hd"].shape[1] // 2
    for t in range(2):
        bias = jnp.concatenate([brow[t, 5 + i:6 + i, :] for i in range(ff // BLOCK)], 1)
        hidden, slope = gelu_parts(nn(mlp_in, w[t, 0, :, MLP:]) + bias)
        hidden = hidden.astype(BF16)
        kept["hd"][r, t * ff:(t + 1) * ff] = hidden
        kept["sl"][r, t * ff:(t + 1) * ff] = slope.astype(BF16)
        out = out + nt(hidden, w[t, 1, :, MLP:])
    out_ref[r, :] = (out * valid_rows(sc, n)).astype(BF16)


def rsum(a):
    return jnp.sum(a, 0, keepdims=True)


def backward_mlp(n, sc, u_ref, w, vec, kept, grad, sums, bsum):
    r = image_rows(n)

    masked = u_ref[r, :].astype(F32) * valid_rows(sc, n)
    sums[5:6, :] += rsum(masked)
    dg = masked.astype(BF16)
    grad["dg"][r, :] = dg
    mg = jnp.zeros(masked.shape, F32)
    ff = kept["hd"].shape[1] // 2
    for t in range(2):
        c = slice(t * ff, (t + 1) * ff)
        up = (nn(dg, w[t, 1, :, MLP:]) * kept["sl"][r, c].astype(F32)).astype(BF16)
        grad["up"][r, c] = up
        total = rsum(up.astype(F32))
        for i in range(ff // BLOCK):
            bsum[t, 5 + i:6 + i, :] += total[:, i * BLOCK:(i + 1) * BLOCK]
        mg = mg + nt(up, w[t, 0, :, MLP:])
    xhat = kept["xh2"][r, :]
    sums[4:5, :] += rsum(mg)
    sums[1:2, :] += rsum(mg * xhat)
    res = masked + norm_back(mg, xhat, kept["inv2"][r, :1], vec[1:2, :])
    sums[3:4, :] += rsum(res)
    grad["res"][r, :] = res


def backward_attention(n, w, vec, in_ref, kept, grad, sums, bsum):
    r = image_rows(n)
    res = grad["res"][r, :]
    ag = res.astype(BF16)
    grad["ag"][r, :] = ag
    low = low_lanes()
    ig = jnp.zeros(res.shape, F32)
    for t in range(2):
        xg = nn(ag, w[t, 1, :, OUT:MISC]).astype(BF16)
        gx = jnp.where(low, 0, xg[:, :BLOCK])
        g = xg[:, BLOCK:]
        p = kept["qkv"][t, r, :]
        q, qk, k, v, vx = [p[:, i * BLOCK:(i + 1) * BLOCK] for i in range(5)]
        kq, xv = turn(qk), turn(vx)
        dq, dk, dv = [], [], []
        for i, (qq, kk, vv, gm, gg) in enumerate(
                [(q, k, v, jnp.where(low, g, 0), g), (q, k, v, jnp.where(low, 0, g), g), (qk, kq, xv, gx, turn(gx))]):
            pb = kept["pr"][n * 6 + t * 3 + i]
            pf = pb.astype(F32)
            dp = nt(gm, vv)
            ds = (pf * (dp - jnp.sum(pf * dp, -1, keepdims=True))).astype(BF16)
            dv.append(tn(pb, gg))
            dq.append(nn(ds, kk) * SCALE)
            dk.append(tn(ds, kq if i == 2 else qq))
        blocks = [
            jnp.where(low, dq[0], dq[1]), jnp.where(low, dq[2], dk[2]), jnp.where(low, dk[0], dk[1]),
            jnp.where(low, dv[0], dv[1]), dv[2],
        ]
        d = jnp.concatenate(blocks, 1).astype(BF16)
        grad["dqkv"][t, r, :] = d
        total = rsum(d.astype(F32))
        for i in range(5):
            bsum[t, i:i + 1, :] += total[:, i * BLOCK:(i + 1) * BLOCK]
        ig = ig + nt(d[:, :QK], w[t, 0, :, :QK]) + nt(d[:, QK:], w[t, 1, :, :V])
    xhat = kept["xh1"][r, :]
    sums[2:3, :] += rsum(ig)
    sums[0:1, :] += rsum(ig * xhat)
    in_ref[r, :] = res + norm_back(ig, xhat, kept["inv1"][r, :1], vec[0:1, :])


def weight_grads(t, piece, kept, grad, g):
    ag, dg = grad["ag"][...], grad["dg"][...]
    ain, mlp_in = kept["ain"][...], kept["min"][...]
    width = ag.shape[1]
    high = jnp.where(low_lanes(), 0.0, 1.0)
    d = grad["dqkv"][t]
    g[0, :, :QK] = tn(ain, d[:, :QK]).astype(BF16)
    val = tn(ain, d[:, QK:])
    out = tn(ag, kept["mx"][t])
    g[1, :, :OUT] = val[:, :BLOCK].astype(BF16)
    g[1, :, OUT:V] = (val[:, BLOCK:] + out[:, :BLOCK] * high).astype(BF16)
    g[1, :, V:MISC] = out[:, BLOCK:].astype(BF16)
    sums = jnp.concatenate([grad["sums"][...], jnp.zeros((BLOCK - 8, width), F32)], 0)
    g[0, :, MISC:MLP] = sums.T.astype(BF16)
    ff = kept["hd"].shape[1] // 2
    c = pl.ds(pl.multiple_of(t * ff, BLOCK), ff)
    g[0, :, MLP:] = tn(mlp_in, grad["up"][:, c]).astype(BF16)
    g[1, :, MLP:] = tn(dg, kept["hd"][:, c]).astype(BF16)
    if piece % 16 == 0:
        rows = jnp.concatenate([grad["bsum"][t], jnp.zeros((piece - 16, BLOCK), F32)], 0).astype(BF16)
        for i in range(width // piece):
            g[1, i * piece:(i + 1) * piece, MISC:MLP] = rows


def kept_shapes(total, width, ff):
    images = total // IMG_PAD
    return dict(
        xh1=((total, width), F32), inv1=((total, BLOCK), F32), ain=((total, width), BF16), qkv=((2, total, ATT), BF16),
        pr=((images * 6, IMG_PAD, IMG_PAD), BF16), mx=((2, total, 2 * BLOCK), BF16), xh2=((total, width), F32),
        inv2=((total, BLOCK), F32), min=((total, width), BF16), sl=((total, ff), BF16), hd=((total, ff), BF16))


def grad_shapes(total, width, ff):
    return dict(dg=((total, width), BF16), up=((total, ff), BF16), res=((total, width), F32), sums=((8, width), F32),
                bsum=((2, 16, BLOCK), F32), ag=((total, width), BF16), dqkv=((2, total, ATT), BF16))


def layer_call(phases, sources, load, store, out_shapes, scalars, given, total, width, ff, piece):
    ks = kept_shapes(total, width, ff)
    gs = grad_shapes(total, width, ff)
    weights = ["ain", "mx", "min", "hd"] + [n for n in gs if n != "res"]
    need = {"forward": ["x"], "back": ["u"] + list(ks), "theirs": weights, "mine": weights}
    gives = {"forward": {"out": ((total, width), BF16), **ks}, "back": {"keep": ((total, width), BF16), "give": ((total, width), BF16), "in": ((total, width), F32), **gs},
             "theirs": {}, "mine": {}}
    made = {}
    for p in phases:
        made.update(gives[p])
    inputs = list(dict.fromkeys(n for p in phases for n in need[p] if n not in made))
    if phases[-1] == "forward":
        shown = list(made)
    else:
        shown = [n for n in made if n in weights or n in ("keep", "give")]
        if "forward" in phases:
            shown.append("in")
    inner = [n for n in made if n not in shown]
    side = {"theirs": 0, "mine": 1}.get(phases[-1])
    products = phases[0] != "mine"
    vmem = pl.BlockSpec(memory_space=pltpu.VMEM)
    anywhere = pl.BlockSpec(memory_space=pl.ANY)
    ends = [] if side is None else out_shapes[side]
    scratch = [pltpu.SemaphoreType.DMA((2,))] + [pltpu.VMEM(*made[n]) for n in inner]
    if products:
        scratch += [pltpu.VMEM((2, 2, width, HALF), BF16), pltpu.VMEM((8, width), F32), pltpu.VMEM((2, 16, BLOCK), F32)]
    if ends:
        scratch.append(pltpu.VMEM((2, width, HALF), BF16))

    def body(*refs):
        refs = list(refs)

        def take(n):
            got = refs[:n]
            del refs[:n]
            return got

        sc = take(1)[0]
        at = dict(zip(inputs, take(len(inputs))))
        src = take(len(sources))
        at.update(zip(shown, take(len(shown))))
        dst = take(len(ends))
        sem = take(1)[0]
        at.update(zip(inner, take(len(inner))))
        if products:
            w, vec, brow = take(3)
            pending = [load(sc, src, w, sem, c) for c in range(2)]
            for part in pending if "forward" in phases else pending[::-1]:
                for c in part:
                    c.start()

            def ready(c):
                for copy in pending[c]:
                    copy.wait()
                if c == 0 and pending[c]:
                    vec[...] = w[0, 0, :, MISC:MLP].astype(F32).T[:8, :]
                    for t in range(2):
                        brow[t] = w[t, 1, :16, MISC:MLP].astype(F32)
                pending[c] = []

            ready(0 if "forward" in phases else 1)
        if "forward" in phases:
            if "back" in phases:
                ready(1)

                def step(n, carry):
                    forward_image(n, sc, at["x"], w, vec, brow, at["out"], at, ready)
                    return carry
                lax.fori_loop(0, total // IMG_PAD, step, 0)
            else:
                for n in range(total // IMG_PAD):
                    forward_image(n, sc, at["x"], w, vec, brow, at["out"], at, ready)
        if "back" in phases:
            sums, bsum = at["sums"], at["bsum"]
            sums[...] = jnp.zeros_like(sums)
            bsum[...] = jnp.zeros_like(bsum)
            ready(0)

            def back(n, carry):
                backward_mlp(n, sc, at["u"], w, vec, at, at, sums, bsum)
                backward_attention(n, w, vec, at["in"], at, at, sums, bsum)
                return carry
            lax.fori_loop(0, total // IMG_PAD, back, 0)
            rows = [at[n] for n in (("x", "out") if "forward" in phases else ("in", "u"))]
            for here in range(2):
                @pl.when(sc[2] == here)
                def _():
                    at["keep"][...] = rows[here][...].astype(BF16)
                    at["give"][...] = rows[1 - here][...].astype(BF16)
        if ends:
            g = take(1)[0]
            t = jnp.where(sc[1] == 0, 1 - side, side)
            weight_grads(t, piece, at, at, g)
            copies = store(sc, side, g, dst, sem.at[0])
            for c in copies:
                c.start()
            for c in copies:
                c.wait()

    outs = [made[n] for n in shown] + ends
    args = [scalars, *[given[n] for n in inputs], *(sources if products else [])]
    if not products:
        sources = []
    got = pl.pallas_call(
        body,
        out_shape=[jax.ShapeDtypeStruct(*o) for o in outs],
        in_specs=[pl.BlockSpec(memory_space=pltpu.SMEM)] + [vmem] * len(inputs) + [anywhere] * len(sources),
        out_specs=[vmem] * (len(outs) - len(ends)) + [anywhere] * len(ends),
        scratch_shapes=scratch,
        compiler_params=pltpu.CompilerParams(vmem_limit_bytes=34 * 2 ** 20),
        cost_estimate=pl.CostEstimate(flops=COST * len(phases), transcendentals=0, bytes_accessed=2 ** 23),
    )(*args)
    got = list(got)
    res = dict(zip(shown, got))
    res["g"] = got[len(shown):]
    return res


def parts(a, b, ff):
    small = a[:, MISC:MLP].T
    rows = b[:16, MISC:MLP]

    def heads(c, pair, single):
        return jnp.concatenate([c[:, pair:pair + BLOCK], c[:, single:single + HD]], 1)

    def lanes(first, last):
        return jnp.concatenate([rows[i:i + 1, :] for i in range(first, last)], 1)

    size = 3 * HD
    qkv = jnp.stack([heads(a, 0, BLOCK), heads(a, 2 * BLOCK, BLOCK + HD), heads(b, 0, BLOCK)])
    biases = jnp.concatenate([lanes(0, 2)[:, :size], lanes(3, 5)[:, :size]], 0)
    out = heads(b, 2 * BLOCK, BLOCK + HD)
    return small[:2], small[2:6], qkv, biases, out, a[:, MLP:], lanes(5, 5 + ff // BLOCK), b[:, MLP:]


def finish(scalars, mine, other, ff):
    piece = mine.shape[0]

    def body(sc, mine_ref, other_ref, *outs):
        first = sc[2] == 0
        a, b = mine_ref[...], other_ref[...].astype(F32)
        for ref, got in zip(outs, parts(jnp.where(first, a, b), jnp.where(first, b, a), ff)):
            ref[...] = got

    vmem = pl.BlockSpec(memory_space=pltpu.VMEM)
    shapes = [(2, piece), (4, piece), (3, piece, 3 * HD), (2, 3 * HD), (piece, 3 * HD), (piece, ff), (1, ff), (piece, ff)]
    return pl.pallas_call(
        body,
        out_shape=[jax.ShapeDtypeStruct(s, F32) for s in shapes],
        in_specs=[pl.BlockSpec(memory_space=pltpu.SMEM), vmem, vmem],
        out_specs=[vmem] * len(shapes),
    )(scalars, mine, other)


def shards(tokens, image_counts, cotangent, norm_gains, row_biases, qkv_weight, qv_bias, out_weight,
           up_weight, up_bias, down_weight):
    sec = lax.axis_index("section")
    dp = lax.axis_index("dp")
    ten = lax.axis_index("tensor")
    n_dp = lax.axis_size("dp")
    m = n_dp // 2
    zi, yi = dp // 2, dp % 2
    local_rows, width = tokens.shape[1:]
    images = local_rows * n_dp // IMG_LEN
    piece = width // n_dp
    ff = 2 * up_weight.shape[2]
    direct = piece % 16 == 0 and m == 4

    def pt(a):
        return lax.ppermute(a, "tensor", [(0, 1), (1, 0)])

    def px(a):
        return lax.ppermute(a, "section", [(0, 1), (1, 0)])

    def py(a):
        return lax.ppermute(a, "dp", [(i, i ^ 1) for i in range(n_dp)])

    def pd(a):
        return lax.ppermute(a, ("section", "dp"), [(i, (i + n_dp) % (2 * n_dp) ^ 1) for i in range(2 * n_dp)])

    def after(a, *b):
        return lax.optimization_barrier((a, *b))

    def plus(*a):
        return sum(b.astype(F32) for b in a)

    def chip_sums(g, got):
        keep0, give0, keep1, give1 = [plus(a, got[i // 2, i % 2]) for i, a in enumerate(g)]
        return [keep0, give0.astype(BF16), keep1, give1.astype(BF16)]

    def cross_first(s):
        return [s[0], px(s[1]), s[2], py(s[3])]

    def cross_second(s):
        a, b = plus(s[0], s[1]), plus(s[2], s[3])
        return [a[0], py(a[1].astype(BF16)), b[0], px(b[1].astype(BF16))]

    def crossed(s):
        return jnp.stack([plus(s[0], s[1]), plus(s[2], s[3])])

    def pz_to(a, kk):
        return lax.ppermute(a, "dp", [(i, i ^ (2 * kk)) for i in range(n_dp)])

    def along(quad):
        low = quad.astype(BF16)
        return plus(quad[:, 0], *[pz_to(low[:, kk], kk) for kk in range(1, m)])

    def along_steps(quad):
        got = pz_to(quad[:, 1::2].astype(BF16), 1)
        quad = plus(quad[:, 0::2], got)
        return plus(quad[:, 0], pz_to(quad[:, 1].astype(BF16), 2))

    def pn(a):
        return lax.ppermute(a, ("dp", "tensor"), [(2 * i + 1, 2 * i + 3) for i in range(n_dp - 1)])

    def tails(keep, got):
        tail = select[:, local_rows:]
        return pn(jnp.stack([tn(tail, keep), tn(tail, got)]).astype(BF16))

    def placed(keep, got, tail):
        def place(a, b):
            a = tn(select[:, :local_rows], a).astype(BF16)
            return jnp.concatenate([a[:IMG_PAD] + b, a[IMG_PAD:]], 0)

        return jnp.stack([place(keep, tail[0]), place(got, tail[1])])

    def ordered(a, b):
        a = a + b
        return jnp.where(sec == 0, a, a[::-1])[None]

    batch_tokens = lax.dynamic_index_in_dim(tokens, sec, 0, keepdims=False)
    batch_cot = lax.dynamic_index_in_dim(cotangent, sec, 0, keepdims=False)
    count = lax.dynamic_index_in_dim(image_counts, sec, 0, keepdims=False)
    first = jnp.minimum((dp * local_rows + IMG_LEN - 1) // IMG_LEN, images)
    last = jnp.minimum(((dp + 1) * local_rows + IMG_LEN - 1) // IMG_LEN, images)
    held = last - first
    slots = -(-(-(-local_rows // IMG_LEN)) // 2)
    lower = held // 2
    own_first = jnp.where(ten == 0, first, first + lower)
    own_count = jnp.where(ten == 0, lower, held - lower)
    total = slots * IMG_PAD
    row = lax.broadcasted_iota(jnp.int32, (total, 1), 0)
    slot, inside = row // IMG_PAD, row % IMG_PAD
    exists = (inside < IMG_LEN) & (slot < own_count)
    target = (own_first + slot) * IMG_LEN + inside - dp * local_rows
    canvas_rows = local_rows + IMG_PAD
    select = ((lax.broadcasted_iota(jnp.int32, (total, canvas_rows), 1) == target) & exists).astype(BF16)
    scalars = jnp.stack([jnp.minimum(own_count, jnp.maximum(count - own_first, 0)), ten, sec, zi, yi]).astype(jnp.int32)

    both = jnp.stack([batch_tokens, batch_cot])
    halo = lax.ppermute(both[:, :IMG_PAD], ("dp", "tensor"), [(2 * i + 3, 2 * i + 1) for i in range(n_dp - 1)])
    q, k, v = [[qkv_weight[0, :, i, h * HD:(h + 1) * HD] for h in range(3)] for i in range(3)]
    o = out_weight[0].T
    o = [o[:, h * HD:(h + 1) * HD] for h in range(3)]
    misc = jnp.concatenate([norm_gains[0], row_biases[0]], 0).T
    misc = jnp.pad(misc, ((0, 0), (0, BLOCK - misc.shape[1])))
    gap = jnp.zeros((HD,), BF16)
    rows = jnp.concatenate([qv_bias[0, 0], gap, gap, gap, qv_bias[0, 1], gap, up_bias[0]]).reshape(-1, BLOCK)
    rows = jnp.pad(rows, ((0, piece - rows.shape[0]), (0, 0)))
    up, down = up_weight[0], down_weight[0].T
    part0 = jnp.concatenate([q[0], q[1], q[2], k[2], k[0], k[1], misc, up], 1)
    part1 = jnp.concatenate([v[0], v[1], v[2], o[2], o[0], o[1], rows, down], 1)

    if direct:
        keep = jnp.where(sec == 0, part0, part1)
        give = jnp.where(sec == 0, part1, part0)
        got, halo = after(px(give), halo)
        start = [jnp.where(sec == 0, keep, got), jnp.where(sec == 0, got, keep)]

        def load(l, sc, src, w, sem, c):
            copies = []
            cols = slice(0, MLP) if c == 0 else slice(MLP, HALF)
            for side in range(2):
                t = jnp.where(sc[1] == 0, side, 1 - side)
                own = src[side * 8:side * 8 + 8]
                for kk in range(m):
                    z = lax.bitwise_xor(sc[3], kk)
                    near = pl.ds(pl.multiple_of((2 * z + sc[4]) * piece, 16), piece)
                    far = pl.ds(pl.multiple_of((2 * z + 1 - sc[4]) * piece, 16), piece)
                    for i, (h, r) in enumerate(((sc[2], near), (1 - sc[2], near), (sc[2], far), (1 - sc[2], far))):
                        a = own[i].at[l, :, cols] if kk == 0 else own[4 + i].at[kk - 1, :, cols]
                        copies.append(pltpu.make_async_copy(a, w.at[t, h, r, cols], sem.at[c]))
            return copies

        part = HALF // 2

        def store(sc, side, g, dst, sem):
            copies = []
            for c in range(2):
                for i in range(2):
                    for j in range(2):
                        hr, yr = (i, j) if c == 0 else (j, i)
                        h = lax.bitwise_xor(sc[2], hr)
                        y = lax.bitwise_xor(sc[4], yr)
                        out = dst[0].at[c, i, j] if side == 0 else dst[2 * c + i].at[j]
                        for kk in range(m):
                            z = lax.bitwise_xor(sc[3], kk)
                            r = pl.ds(pl.multiple_of((2 * z + y) * piece, 16), piece)
                            a = g.at[h, r, c * part:(c + 1) * part]
                            copies.append(pltpu.make_async_copy(a, out.at[kk], sem))
            return copies

        out_shapes = [[((2, 2, 2, m, piece, part), BF16)], [((2, m, piece, part), BF16)] * 4]
        own = jnp.stack(start)
        firsts = [own, px(own), py(own), pd(own)]
        columns = [jnp.stack([pz_to(start[0], kk) for kk in range(1, m)])]
        start[1] = after(start[1], columns[0])[0]
        near = pz_to(start[1], 1)
        columns[0], near, *firsts = after(columns[0], near, *firsts)
        rest = [columns[0], px(columns[0]), py(columns[0]), pd(columns[0])]
        columns.append(jnp.concatenate([near[None], pz_to(jnp.stack([start[1], near]), 2)]))
        columns[1], *rest = after(columns[1], *rest)
        twins = [pt(a) for a in firsts]
        sources = [firsts + rest + twins + [pt(a) for a in rest]]
        sources.append(columns[1:] + [px(columns[1]), py(columns[1]), pd(columns[1])])
    else:
        def load(l, sc, src, w, sem, c):
            return [pltpu.make_async_copy(src[0], w, sem.at[c])] if c == 0 else []

        def store(sc, side, g, dst, sem):
            return [pltpu.make_async_copy(g, dst[0], sem)]

        out_shapes = [[((2, width, HALF), BF16)]] * 2
        a = lax.all_gather(jnp.stack([part0, part1]), "dp", axis=1, tiled=True)
        a = lax.all_gather(lax.all_gather(a, "tensor"), "section")
        sources = [[a[0]], [a[1]]]

    batch = jnp.concatenate([both, halo], 1)
    x0 = nn(select, batch[0]).astype(BF16)
    cot = nn(select, batch[1]).astype(BF16)
    x0, cot = after(x0, cot)

    def call(l, phases, **given):
        return layer_call(phases, sources[l], functools.partial(load, l), store, out_shapes, scalars, given,
                          total, width, ff, piece)

    r0 = call(0, ["forward"], x=x0)
    low0 = r0["out"]
    if direct:
        low0, *rest = after(low0, *sources[1])
        sources[1] = firsts + rest + twins + [pt(a) for a in rest]
    r1 = call(1, ["forward", "back", "theirs"], x=low0, u=cot)
    if direct:
        got1 = pt(r1["g"][0])
    low_got = px(r1["give"])
    m1 = call(1, ["mine"], **r1)
    u = r1["in"]
    if direct:
        first, got1 = after(m1["g"][0], got1)
        sent1 = chip_sums([first] + m1["g"][1:], got1)
        u = after(u, sent1[1], sent1[3])[0]
        low_got = after(low_got, sent1[1], sent1[3])[0]
        low_tails = tails(r1["keep"], low_got)
        quad1 = cross_first(sent1)
    else:
        low_tails = tails(r1["keep"], low_got)
    b0 = call(0, ["back", "theirs"], **{**r0, "u": u})
    if direct:
        b0["dg"], b0["g"][0], low_tails, *quad1 = after(b0["dg"], b0["g"][0], low_tails, *quad1)
        got0 = pt(b0["g"][0])
        quad1 = cross_second(quad1)
    low_rows = placed(r1["keep"], low_got, low_tails)
    low_twin = pt(low_rows)
    in_got = px(b0["give"])
    m0 = call(0, ["mine"], **{**r0, **b0})

    if direct:
        first, got0, low_twin = after(m0["g"][0], got0, low_twin)
        sent0 = chip_sums([first] + m0["g"][1:], got0)
        in_got, *quad1 = after(in_got, *quad1, sent0[1], sent0[3])[:5]
        in_tails = tails(b0["keep"], in_got)
        quad0 = cross_second(after(*cross_first(sent0)))
        in_rows = placed(b0["keep"], in_got, in_tails)
        done1 = along_steps(crossed(quad1))
        in_twin, done1, *quad0 = after(pt(in_rows), done1, *quad0)
        done0 = along(crossed(quad0))
        done0, done1 = [jnp.concatenate([a[0], a[1]], 1) for a in (done0, done1)]
        mine = jnp.where(sec == 0, done0, done1)
        other = px(jnp.where(sec == 0, done1, done0).astype(BF16))
        g_gain, g_bias, g_qkv, g_qv, g_out, g_up, g_up_bias, g_down = finish(scalars, mine, other, ff // 2)
    else:
        in_rows = placed(b0["keep"], in_got, tails(b0["keep"], in_got))
        in_twin = pt(in_rows)

        def by_core(a, b):
            return jnp.where(ten == 0, jnp.stack([b, a]), jnp.stack([a, b]))

        g = jnp.stack([by_core(b0["g"][0], m0["g"][0]), by_core(r1["g"][0], m1["g"][0])])
        g = lax.psum_scatter(g.astype(F32), "section", scatter_dimension=0)
        g = lax.psum_scatter(g, "tensor", scatter_dimension=0)
        g = lax.psum_scatter(g, "dp", scatter_dimension=1, tiled=True)
        small = lax.psum(jnp.stack([b0["bsum"], r1["bsum"]]), ("section", "tensor", "dp"))
        small = lax.dynamic_index_in_dim(lax.dynamic_index_in_dim(small, sec, 0, False), ten, 0, False)
        g_gain, g_bias, g_qkv, _, g_out, g_up, _, g_down = parts(g[0], g[1], ff // 2)
        small = jnp.pad(small, ((0, 0), (MISC, HALF - MLP)))
        _, _, _, g_qv, _, _, g_up_bias, _ = parts(small, small, ff // 2)

    layer_outputs = ordered(low_rows, low_twin)
    input_grads = ordered(in_rows, in_twin).astype(F32)

    return (
        layer_outputs,
        input_grads,
        g_gain[None],
        g_bias[None],
        g_qkv.transpose(1, 0, 2)[None],
        g_qv[None],
        g_out.T[None],
        g_up[None],
        g_up_bias,
        g_down.T[None],
    )


def solution(mesh):
    in_specs = (
        P(None, "dp", None),
        P(),
        P(None, "dp", None),
        P("section", None, "dp"),
        P("section", None, "dp"),
        P("section", "dp", None, "tensor"),
        P("section", None, "tensor"),
        P("section", "tensor", "dp"),
        P("section", "dp", "tensor"),
        P("section", "tensor"),
        P("section", "tensor", "dp"),
    )
    out_specs = (
        P("section", None, "dp", None),
        P("section", None, "dp", None),
        P("section", None, "dp"),
        P("section", None, "dp"),
        P("section", "dp", None, "tensor"),
        P("section", None, "tensor"),
        P("section", "tensor", "dp"),
        P("section", "dp", "tensor"),
        P("section", "tensor"),
        P("section", "tensor", "dp"),
    )
    return jax.shard_map(shards, mesh=mesh, in_specs=in_specs, out_specs=out_specs, check_vma=False)
```

```python
import functools
import math

import jax
import jax.numpy as jnp
from jax import lax
from jax.experimental import pallas as pl
from jax.experimental.pallas import tpu as pltpu
from jax.sharding import PartitionSpec as P

IMG_LEN = 197
IMG_PAD = 208
HD = 64
EPSILON = 1e-06
NEGATIVE = -1e30
F32 = jnp.float32
BF16 = jnp.bfloat16
BLOCK = 128
HALF = 1280
COST = 10 ** 10
SCALE = 1.0 / math.sqrt(HD)


def mm(a, b, dims):
    return lax.dot_general(a, b, (dims, ((), ())), preferred_element_type=F32)


def nn(a, b):
    return mm(a, b, ((1,), (0,)))


def nt(a, b):
    return mm(a, b, ((1,), (1,)))


def tn(a, b):
    return mm(a, b, ((0,), (0,)))


def normed(x):
    centred = x - jnp.mean(x, -1, keepdims=True)
    inverse = lax.rsqrt(jnp.mean(centred * centred, -1, keepdims=True) + EPSILON)
    return centred * inverse, inverse


def norm_back(grad, xhat, inverse, gain):
    t = grad * gain
    return inverse * (
        t - jnp.mean(t, -1, keepdims=True) - xhat * jnp.mean(t * xhat, -1, keepdims=True)
    )


def gelu_parts(u):
    cdf = 0.5 * (1.0 + lax.erf(u * math.sqrt(0.5)))
    pdf = jnp.exp(-0.5 * u * u) * (1.0 / math.sqrt(2.0 * math.pi))
    return u * cdf, cdf + u * pdf


QK = 384
V = 256
OUT = 128
MISC = 384
MLP = 512
ATT = QK + V


def low_lanes():
    return lax.broadcasted_iota(jnp.int32, (1, BLOCK), 1) < HD


def turn(a):
    return jnp.concatenate([a[:, HD:], a[:, :HD]], 1)


def valid_rows(sc, n):
    row = lax.broadcasted_iota(jnp.int32, (IMG_PAD, 1), 0)
    return jnp.where((row < IMG_LEN) & (n < sc[0]), 1.0, 0.0)


def image_rows(n):
    return pl.ds(pl.multiple_of(n * IMG_PAD, 16), IMG_PAD)


def forward_image(n, sc, x_ref, w, vec, brow, out_ref, kept, ready):
    r = image_rows(n)
    x = x_ref[r, :].astype(F32)
    xhat, inv = normed(x)
    attn_in = (xhat * vec[0:1, :] + vec[2:3, :]).astype(BF16)
    kept["xh1"][r, :] = xhat
    kept["inv1"][r, :] = jnp.broadcast_to(inv, (IMG_PAD, BLOCK))
    kept["ain"][r, :] = attn_in
    residual = x + vec[3:4, :]
    low = low_lanes()
    lane = lax.broadcasted_iota(jnp.int32, (1, ATT), 1)
    factor = jnp.where(lane < 192, SCALE, jnp.where(lane < 576, 1.0, 0.0))
    real = lax.broadcasted_iota(jnp.int32, (1, IMG_PAD), 1) < IMG_LEN
    for t in range(2):
        bias = jnp.concatenate([brow[t, i:i + 1, :] for i in range(5)], 1)
        p = jnp.concatenate([nn(attn_in, w[t, 0, :, :QK]), nn(attn_in, w[t, 1, :, :V])], 1)
        p = ((p + bias) * factor).astype(BF16)
        kept["qkv"][t, r, :] = p
        q, qk, k, v, vx = [p[:, i * BLOCK:(i + 1) * BLOCK] for i in range(5)]
        kq, xv = turn(qk), turn(vx)
        outs = []
        for i, (qq, kk, vv) in enumerate(
                [(jnp.where(low, q, 0), k, v), (jnp.where(low, 0, q), k, v), (jnp.where(low, qk, 0), kq, xv)]):
            s = jnp.where(real, nt(qq, kk), NEGATIVE)
            e = jnp.exp(s - jnp.max(s, -1, keepdims=True))
            pr = (e * (1.0 / jnp.sum(e, -1, keepdims=True))).astype(BF16)
            kept["pr"][n * 6 + t * 3 + i] = pr
            outs.append(nn(pr, vv))
        mixed = jnp.concatenate([outs[2], jnp.where(low, outs[0], outs[1])], 1).astype(BF16)
        kept["mx"][t, r, :] = mixed
        residual = residual + nt(mixed, w[t, 1, :, OUT:MISC])
    xhat, inv = normed(residual)
    mlp_in = (xhat * vec[1:2, :] + vec[4:5, :]).astype(BF16)
    kept["xh2"][r, :] = xhat
    kept["inv2"][r, :] = jnp.broadcast_to(inv, (IMG_PAD, BLOCK))
    kept["min"][r, :] = mlp_in
    out = residual + vec[5:6, :]
    ready(1)
    ff = kept["hd"].shape[1] // 2
    for t in range(2):
        bias = jnp.concatenate([brow[t, 5 + i:6 + i, :] for i in range(ff // BLOCK)], 1)
        hidden, slope = gelu_parts(nn(mlp_in, w[t, 0, :, MLP:]) + bias)
        hidden = hidden.astype(BF16)
        kept["hd"][r, t * ff:(t + 1) * ff] = hidden
        kept["sl"][r, t * ff:(t + 1) * ff] = slope.astype(BF16)
        out = out + nt(hidden, w[t, 1, :, MLP:])
    out_ref[r, :] = (out * valid_rows(sc, n)).astype(BF16)


def rsum(a):
    return jnp.sum(a, 0, keepdims=True)


def backward_mlp(n, sc, u_ref, w, vec, kept, grad, sums, bsum):
    r = image_rows(n)

    masked = u_ref[r, :].astype(F32) * valid_rows(sc, n)
    sums[5:6, :] += rsum(masked)
    dg = masked.astype(BF16)
    grad["dg"][r, :] = dg
    mg = jnp.zeros(masked.shape, F32)
    ff = kept["hd"].shape[1] // 2
    for t in range(2):
        c = slice(t * ff, (t + 1) * ff)
        up = (nn(dg, w[t, 1, :, MLP:]) * kept["sl"][r, c].astype(F32)).astype(BF16)
        grad["up"][r, c] = up
        total = rsum(up.astype(F32))
        for i in range(ff // BLOCK):
            bsum[t, 5 + i:6 + i, :] += total[:, i * BLOCK:(i + 1) * BLOCK]
        mg = mg + nt(up, w[t, 0, :, MLP:])
    xhat = kept["xh2"][r, :]
    sums[4:5, :] += rsum(mg)
    sums[1:2, :] += rsum(mg * xhat)
    res = masked + norm_back(mg, xhat, kept["inv2"][r, :1], vec[1:2, :])
    sums[3:4, :] += rsum(res)
    grad["res"][r, :] = res


def backward_attention(n, w, vec, in_ref, kept, grad, sums, bsum):
    r = image_rows(n)
    res = grad["res"][r, :]
    ag = res.astype(BF16)
    grad["ag"][r, :] = ag
    low = low_lanes()
    ig = jnp.zeros(res.shape, F32)
    for t in range(2):
        xg = nn(ag, w[t, 1, :, OUT:MISC]).astype(BF16)
        gx = jnp.where(low, 0, xg[:, :BLOCK])
        g = xg[:, BLOCK:]
        p = kept["qkv"][t, r, :]
        q, qk, k, v, vx = [p[:, i * BLOCK:(i + 1) * BLOCK] for i in range(5)]
        kq, xv = turn(qk), turn(vx)
        dq, dk, dv = [], [], []
        for i, (qq, kk, vv, gm, gg) in enumerate(
                [(q, k, v, jnp.where(low, g, 0), g), (q, k, v, jnp.where(low, 0, g), g), (qk, kq, xv, gx, turn(gx))]):
            pb = kept["pr"][n * 6 + t * 3 + i]
            pf = pb.astype(F32)
            dp = nt(gm, vv)
            ds = (pf * (dp - jnp.sum(pf * dp, -1, keepdims=True))).astype(BF16)
            dv.append(tn(pb, gg))
            dq.append(nn(ds, kk) * SCALE)
            dk.append(tn(ds, kq if i == 2 else qq))
        blocks = [
            jnp.where(low, dq[0], dq[1]), jnp.where(low, dq[2], dk[2]), jnp.where(low, dk[0], dk[1]),
            jnp.where(low, dv[0], dv[1]), dv[2],
        ]
        d = jnp.concatenate(blocks, 1).astype(BF16)
        grad["dqkv"][t, r, :] = d
        total = rsum(d.astype(F32))
        for i in range(5):
            bsum[t, i:i + 1, :] += total[:, i * BLOCK:(i + 1) * BLOCK]
        ig = ig + nt(d[:, :QK], w[t, 0, :, :QK]) + nt(d[:, QK:], w[t, 1, :, :V])
    xhat = kept["xh1"][r, :]
    sums[2:3, :] += rsum(ig)
    sums[0:1, :] += rsum(ig * xhat)
    in_ref[r, :] = res + norm_back(ig, xhat, kept["inv1"][r, :1], vec[0:1, :])


def weight_grads(t, piece, kept, grad, g):
    ag, dg = grad["ag"][...], grad["dg"][...]
    ain, mlp_in = kept["ain"][...], kept["min"][...]
    width = ag.shape[1]
    high = jnp.where(low_lanes(), 0.0, 1.0)
    d = grad["dqkv"][t]
    g[0, :, :QK] = tn(ain, d[:, :QK]).astype(BF16)
    val = tn(ain, d[:, QK:])
    out = tn(ag, kept["mx"][t])
    g[1, :, :OUT] = val[:, :BLOCK].astype(BF16)
    g[1, :, OUT:V] = (val[:, BLOCK:] + out[:, :BLOCK] * high).astype(BF16)
    g[1, :, V:MISC] = out[:, BLOCK:].astype(BF16)
    sums = jnp.concatenate([grad["sums"][...], jnp.zeros((BLOCK - 8, width), F32)], 0)
    g[0, :, MISC:MLP] = sums.T.astype(BF16)
    ff = kept["hd"].shape[1] // 2
    c = pl.ds(pl.multiple_of(t * ff, BLOCK), ff)
    g[0, :, MLP:] = tn(mlp_in, grad["up"][:, c]).astype(BF16)
    g[1, :, MLP:] = tn(dg, kept["hd"][:, c]).astype(BF16)
    if piece % 16 == 0:
        rows = jnp.concatenate([grad["bsum"][t], jnp.zeros((piece - 16, BLOCK), F32)], 0).astype(BF16)
        for i in range(width // piece):
            g[1, i * piece:(i + 1) * piece, MISC:MLP] = rows


def kept_shapes(total, width, ff):
    images = total // IMG_PAD
    return dict(
        xh1=((total, width), F32), inv1=((total, BLOCK), F32), ain=((total, width), BF16), qkv=((2, total, ATT), BF16),
        pr=((images * 6, IMG_PAD, IMG_PAD), BF16), mx=((2, total, 2 * BLOCK), BF16), xh2=((total, width), F32),
        inv2=((total, BLOCK), F32), min=((total, width), BF16), sl=((total, ff), BF16), hd=((total, ff), BF16))


def grad_shapes(total, width, ff):
    return dict(dg=((total, width), BF16), up=((total, ff), BF16), res=((total, width), F32), sums=((8, width), F32),
                bsum=((2, 16, BLOCK), F32), ag=((total, width), BF16), dqkv=((2, total, ATT), BF16))


def layer_call(phases, sources, load, store, out_shapes, scalars, given, total, width, ff, piece):
    ks = kept_shapes(total, width, ff)
    gs = grad_shapes(total, width, ff)
    weights = ["ain", "mx", "min", "hd"] + [n for n in gs if n != "res"]
    need = {"forward": ["x"], "back": ["u"] + list(ks), "theirs": weights, "mine": weights}
    gives = {"forward": {"out": ((total, width), BF16), **ks}, "back": {"keep": ((total, width), BF16), "give": ((total, width), BF16), "in": ((total, width), F32), **gs},
             "theirs": {}, "mine": {}}
    made = {}
    for p in phases:
        made.update(gives[p])
    inputs = list(dict.fromkeys(n for p in phases for n in need[p] if n not in made))
    if phases[-1] == "forward":
        shown = list(made)
    else:
        shown = [n for n in made if n in weights or n in ("keep", "give")]
        if "forward" in phases:
            shown.append("in")
    inner = [n for n in made if n not in shown]
    side = {"theirs": 0, "mine": 1}.get(phases[-1])
    products = phases[0] != "mine"
    vmem = pl.BlockSpec(memory_space=pltpu.VMEM)
    anywhere = pl.BlockSpec(memory_space=pl.ANY)
    ends = [] if side is None else out_shapes[side]
    scratch = [pltpu.SemaphoreType.DMA((2,))] + [pltpu.VMEM(*made[n]) for n in inner]
    if products:
        scratch += [pltpu.VMEM((2, 2, width, HALF), BF16), pltpu.VMEM((8, width), F32), pltpu.VMEM((2, 16, BLOCK), F32)]
    if ends:
        scratch.append(pltpu.VMEM((2, width, HALF), BF16))

    def body(*refs):
        refs = list(refs)

        def take(n):
            got = refs[:n]
            del refs[:n]
            return got

        sc = take(1)[0]
        at = dict(zip(inputs, take(len(inputs))))
        src = take(len(sources))
        at.update(zip(shown, take(len(shown))))
        dst = take(len(ends))
        sem = take(1)[0]
        at.update(zip(inner, take(len(inner))))
        if products:
            w, vec, brow = take(3)
            pending = [load(sc, src, w, sem, c) for c in range(2)]
            for part in pending if "forward" in phases else pending[::-1]:
                for c in part:
                    c.start()

            def ready(c):
                for copy in pending[c]:
                    copy.wait()
                if c == 0 and pending[c]:
                    vec[...] = w[0, 0, :, MISC:MLP].astype(F32).T[:8, :]
                    for t in range(2):
                        brow[t] = w[t, 1, :16, MISC:MLP].astype(F32)
                pending[c] = []

            ready(0 if "forward" in phases else 1)
        if "forward" in phases:
            if "back" in phases:
                ready(1)

                def step(n, carry):
                    forward_image(n, sc, at["x"], w, vec, brow, at["out"], at, ready)
                    return carry
                lax.fori_loop(0, total // IMG_PAD, step, 0)
            else:
                for n in range(total // IMG_PAD):
                    forward_image(n, sc, at["x"], w, vec, brow, at["out"], at, ready)
        if "back" in phases:
            sums, bsum = at["sums"], at["bsum"]
            sums[...] = jnp.zeros_like(sums)
            bsum[...] = jnp.zeros_like(bsum)
            ready(0)

            def back(n, carry):
                backward_mlp(n, sc, at["u"], w, vec, at, at, sums, bsum)
                backward_attention(n, w, vec, at["in"], at, at, sums, bsum)
                return carry
            lax.fori_loop(0, total // IMG_PAD, back, 0)
            rows = [at[n] for n in (("x", "out") if "forward" in phases else ("in", "u"))]
            for here in range(2):
                @pl.when(sc[2] == here)
                def _():
                    at["keep"][...] = rows[here][...].astype(BF16)
                    at["give"][...] = rows[1 - here][...].astype(BF16)
        if ends:
            g = take(1)[0]
            t = jnp.where(sc[1] == 0, 1 - side, side)
            weight_grads(t, piece, at, at, g)
            copies = store(sc, side, g, dst, sem.at[0])
            for c in copies:
                c.start()
            for c in copies:
                c.wait()

    outs = [made[n] for n in shown] + ends
    args = [scalars, *[given[n] for n in inputs], *(sources if products else [])]
    if not products:
        sources = []
    got = pl.pallas_call(
        body,
        out_shape=[jax.ShapeDtypeStruct(*o) for o in outs],
        in_specs=[pl.BlockSpec(memory_space=pltpu.SMEM)] + [vmem] * len(inputs) + [anywhere] * len(sources),
        out_specs=[vmem] * (len(outs) - len(ends)) + [anywhere] * len(ends),
        scratch_shapes=scratch,
        compiler_params=pltpu.CompilerParams(vmem_limit_bytes=34 * 2 ** 20),
        cost_estimate=pl.CostEstimate(flops=COST * len(phases), transcendentals=0, bytes_accessed=2 ** 23),
    )(*args)
    got = list(got)
    res = dict(zip(shown, got))
    res["g"] = got[len(shown):]
    return res


def parts(a, b, ff):
    small = a[:, MISC:MLP].T
    rows = b[:16, MISC:MLP]

    def heads(c, pair, single):
        return jnp.concatenate([c[:, pair:pair + BLOCK], c[:, single:single + HD]], 1)

    def lanes(first, last):
        return jnp.concatenate([rows[i:i + 1, :] for i in range(first, last)], 1)

    size = 3 * HD
    qkv = jnp.stack([heads(a, 0, BLOCK), heads(a, 2 * BLOCK, BLOCK + HD), heads(b, 0, BLOCK)])
    biases = jnp.concatenate([lanes(0, 2)[:, :size], lanes(3, 5)[:, :size]], 0)
    out = heads(b, 2 * BLOCK, BLOCK + HD)
    return small[:2], small[2:6], qkv, biases, out, a[:, MLP:], lanes(5, 5 + ff // BLOCK), b[:, MLP:]


def finish(scalars, mine, other, ff):
    piece = mine.shape[0]

    def body(sc, mine_ref, other_ref, *outs):
        first = sc[2] == 0
        a, b = mine_ref[...], other_ref[...].astype(F32)
        for ref, got in zip(outs, parts(jnp.where(first, a, b), jnp.where(first, b, a), ff)):
            ref[...] = got

    vmem = pl.BlockSpec(memory_space=pltpu.VMEM)
    shapes = [(2, piece), (4, piece), (3, piece, 3 * HD), (2, 3 * HD), (piece, 3 * HD), (piece, ff), (1, ff), (piece, ff)]
    return pl.pallas_call(
        body,
        out_shape=[jax.ShapeDtypeStruct(s, F32) for s in shapes],
        in_specs=[pl.BlockSpec(memory_space=pltpu.SMEM), vmem, vmem],
        out_specs=[vmem] * len(shapes),
    )(scalars, mine, other)


def shards(tokens, image_counts, cotangent, norm_gains, row_biases, qkv_weight, qv_bias, out_weight,
           up_weight, up_bias, down_weight):
    sec = lax.axis_index("section")
    dp = lax.axis_index("dp")
    ten = lax.axis_index("tensor")
    n_dp = lax.axis_size("dp")
    m = n_dp // 2
    zi, yi = dp // 2, dp % 2
    local_rows, width = tokens.shape[1:]
    images = local_rows * n_dp // IMG_LEN
    piece = width // n_dp
    ff = 2 * up_weight.shape[2]
    direct = piece % 16 == 0 and m == 4

    def pt(a):
        return lax.ppermute(a, "tensor", [(0, 1), (1, 0)])

    def px(a):
        return lax.ppermute(a, "section", [(0, 1), (1, 0)])

    def py(a):
        return lax.ppermute(a, "dp", [(i, i ^ 1) for i in range(n_dp)])

    def pd(a):
        return lax.ppermute(a, ("section", "dp"), [(i, (i + n_dp) % (2 * n_dp) ^ 1) for i in range(2 * n_dp)])

    def after(a, *b):
        return lax.optimization_barrier((a, *b))

    def plus(*a):
        return sum(b.astype(F32) for b in a)

    def chip_sums(g, got):
        keep0, give0, keep1, give1 = [plus(a, got[i // 2, i % 2]) for i, a in enumerate(g)]
        return [keep0, give0.astype(BF16), keep1, give1.astype(BF16)]

    def cross_first(s):
        return [s[0], px(s[1]), s[2], py(s[3])]

    def cross_second(s):
        a, b = plus(s[0], s[1]), plus(s[2], s[3])
        return [a[0], py(a[1].astype(BF16)), b[0], px(b[1].astype(BF16))]

    def crossed(s):
        return jnp.stack([plus(s[0], s[1]), plus(s[2], s[3])])

    def pz_to(a, kk):
        return lax.ppermute(a, "dp", [(i, i ^ (2 * kk)) for i in range(n_dp)])

    def along(quad):
        low = quad.astype(BF16)
        return plus(quad[:, 0], *[pz_to(low[:, kk], kk) for kk in range(1, m)])

    def along_steps(quad, *before):
        got = pz_to(quad[:, 1::2].astype(BF16), 1)
        quad = after(plus(quad[:, 0::2], got), *before)[0]
        return plus(quad[:, 0], pz_to(quad[:, 1].astype(BF16), 2))

    def pn(a):
        return lax.ppermute(a, ("dp", "tensor"), [(2 * i + 1, 2 * i + 3) for i in range(n_dp - 1)])

    def placed(rows, *before):
        tail = select[:, local_rows:]
        tails = after(pn(jnp.stack([tn(tail, a) for a in rows]).astype(BF16)), *before)[0]

        def place(a, b):
            a = tn(select[:, :local_rows], a).astype(BF16)
            return jnp.concatenate([a[:IMG_PAD] + b, a[IMG_PAD:]], 0)

        return jnp.stack([place(a, tails[i]) for i, a in enumerate(rows)])

    def ordered(a, b):
        a = a + b
        return jnp.where(sec == 0, a, a[::-1])[None]

    batch_tokens = lax.dynamic_index_in_dim(tokens, sec, 0, keepdims=False)
    batch_cot = lax.dynamic_index_in_dim(cotangent, sec, 0, keepdims=False)
    count = lax.dynamic_index_in_dim(image_counts, sec, 0, keepdims=False)
    first = jnp.minimum((dp * local_rows + IMG_LEN - 1) // IMG_LEN, images)
    last = jnp.minimum(((dp + 1) * local_rows + IMG_LEN - 1) // IMG_LEN, images)
    held = last - first
    slots = -(-(-(-local_rows // IMG_LEN)) // 2)
    lower = held // 2
    own_first = jnp.where(ten == 0, first, first + lower)
    own_count = jnp.where(ten == 0, lower, held - lower)
    total = slots * IMG_PAD
    row = lax.broadcasted_iota(jnp.int32, (total, 1), 0)
    slot, inside = row // IMG_PAD, row % IMG_PAD
    exists = (inside < IMG_LEN) & (slot < own_count)
    target = (own_first + slot) * IMG_LEN + inside - dp * local_rows
    canvas_rows = local_rows + IMG_PAD
    select = ((lax.broadcasted_iota(jnp.int32, (total, canvas_rows), 1) == target) & exists).astype(BF16)
    scalars = jnp.stack([jnp.minimum(own_count, jnp.maximum(count - own_first, 0)), ten, sec, zi, yi]).astype(jnp.int32)

    both = jnp.stack([batch_tokens, batch_cot])
    halo = lax.ppermute(both[:, :IMG_PAD], ("dp", "tensor"), [(2 * i + 3, 2 * i + 1) for i in range(n_dp - 1)])
    q, k, v = [[qkv_weight[0, :, i, h * HD:(h + 1) * HD] for h in range(3)] for i in range(3)]
    o = out_weight[0].T
    o = [o[:, h * HD:(h + 1) * HD] for h in range(3)]
    misc = jnp.concatenate([norm_gains[0], row_biases[0]], 0).T
    misc = jnp.pad(misc, ((0, 0), (0, BLOCK - misc.shape[1])))
    gap = jnp.zeros((HD,), BF16)
    rows = jnp.concatenate([qv_bias[0, 0], gap, gap, gap, qv_bias[0, 1], gap, up_bias[0]]).reshape(-1, BLOCK)
    rows = jnp.pad(rows, ((0, piece - rows.shape[0]), (0, 0)))
    up, down = up_weight[0], down_weight[0].T
    part0 = jnp.concatenate([q[0], q[1], q[2], k[2], k[0], k[1], misc, up], 1)
    part1 = jnp.concatenate([v[0], v[1], v[2], o[2], o[0], o[1], rows, down], 1)

    if direct:
        keep = jnp.where(sec == 0, part0, part1)
        give = jnp.where(sec == 0, part1, part0)
        got, halo = after(px(give), halo)
        start = [jnp.where(sec == 0, keep, got), jnp.where(sec == 0, got, keep)]

        def load(l, sc, src, w, sem, c):
            copies = []
            cols = slice(0, MLP) if c == 0 else slice(MLP, HALF)
            for side in range(2):
                t = jnp.where(sc[1] == 0, side, 1 - side)
                own = src[side * 8:side * 8 + 8]
                for kk in range(m):
                    z = lax.bitwise_xor(sc[3], kk)
                    near = pl.ds(pl.multiple_of((2 * z + sc[4]) * piece, 16), piece)
                    far = pl.ds(pl.multiple_of((2 * z + 1 - sc[4]) * piece, 16), piece)
                    for i, (h, r) in enumerate(((sc[2], near), (1 - sc[2], near), (sc[2], far), (1 - sc[2], far))):
                        a = own[i].at[l, :, cols] if kk == 0 else own[4 + i].at[kk - 1, :, cols]
                        copies.append(pltpu.make_async_copy(a, w.at[t, h, r, cols], sem.at[c]))
            return copies

        part = HALF // 2

        def store(sc, side, g, dst, sem):
            copies = []
            for c in range(2):
                for i in range(2):
                    for j in range(2):
                        hr, yr = (i, j) if c == 0 else (j, i)
                        h = lax.bitwise_xor(sc[2], hr)
                        y = lax.bitwise_xor(sc[4], yr)
                        out = dst[0].at[c, i, j] if side == 0 else dst[2 * c + i].at[j]
                        for kk in range(m):
                            z = lax.bitwise_xor(sc[3], kk)
                            r = pl.ds(pl.multiple_of((2 * z + y) * piece, 16), piece)
                            a = g.at[h, r, c * part:(c + 1) * part]
                            copies.append(pltpu.make_async_copy(a, out.at[kk], sem))
            return copies

        out_shapes = [[((2, 2, 2, m, piece, part), BF16)], [((2, m, piece, part), BF16)] * 4]
        own = jnp.stack(start)
        firsts = [own, px(own), py(own), pd(own)]
        columns = [jnp.stack([pz_to(start[0], kk) for kk in range(1, m)])]
        start[1] = after(start[1], columns[0])[0]
        near = pz_to(start[1], 1)
        columns[0], near, *firsts = after(columns[0], near, *firsts)
        rest = [columns[0], px(columns[0]), py(columns[0]), pd(columns[0])]
        columns.append(jnp.concatenate([near[None], pz_to(jnp.stack([start[1], near]), 2)]))
        columns[1], *rest = after(columns[1], *rest)
        twins = [pt(a) for a in firsts]
        sources = [firsts + rest + twins + [pt(a) for a in rest]]
        sources.append(columns[1:] + [px(columns[1]), py(columns[1]), pd(columns[1])])
    else:
        def load(l, sc, src, w, sem, c):
            return [pltpu.make_async_copy(src[0], w, sem.at[c])] if c == 0 else []

        def store(sc, side, g, dst, sem):
            return [pltpu.make_async_copy(g, dst[0], sem)]

        out_shapes = [[((2, width, HALF), BF16)]] * 2
        a = lax.all_gather(jnp.stack([part0, part1]), "dp", axis=1, tiled=True)
        a = lax.all_gather(lax.all_gather(a, "tensor"), "section")
        sources = [[a[0]], [a[1]]]

    batch = jnp.concatenate([both, halo], 1)
    x0 = nn(select, batch[0]).astype(BF16)
    cot = nn(select, batch[1]).astype(BF16)
    x0, cot = after(x0, cot)

    def call(l, phases, **given):
        return layer_call(phases, sources[l], functools.partial(load, l), store, out_shapes, scalars, given,
                          total, width, ff, piece)

    r0 = call(0, ["forward"], x=x0)
    low0 = r0["out"]
    if direct:
        low0, *rest = after(low0, *sources[1])
        sources[1] = firsts + rest + twins + [pt(a) for a in rest]
    r1 = call(1, ["forward", "back", "theirs"], x=low0, u=cot)
    if direct:
        got1 = pt(r1["g"][0])
    low_got = px(r1["give"])
    m1 = call(1, ["mine"], **r1)
    u = r1["in"]
    if direct:
        first, got1 = after(m1["g"][0], got1)
        sent1 = chip_sums([first] + m1["g"][1:], got1)
        u = after(u, sent1[1], sent1[3])[0]
        quad1 = cross_first(sent1)
    b0 = call(0, ["back", "theirs"], **{**r0, "u": u})
    if direct:
        b0["dg"], b0["g"][0], *quad1 = after(b0["dg"], b0["g"][0], *quad1)
        got0 = pt(b0["g"][0])
        quad1 = cross_second(quad1)
    in_got = px(b0["give"])
    m0 = call(0, ["mine"], **{**r0, **b0})

    if direct:
        first, got0 = after(m0["g"][0], got0)
        sent0 = chip_sums([first] + m0["g"][1:], got0)
        in_got, low_got, *quad1 = after(in_got, low_got, *quad1, sent0[1], sent0[3])[:6]
        quad0 = after(*cross_first(sent0))
        rows = placed([r1["keep"], low_got, b0["keep"], in_got], quad0[1], quad0[3])
        done1 = along_steps(crossed(quad1), quad0[1], quad0[3])
        quad0 = cross_second(quad0)
        done1, *quad0 = after(done1, *quad0)
        twin, done0 = after(pt(rows), along(crossed(quad0)))
        done0, done1 = [jnp.concatenate([a[0], a[1]], 1) for a in (done0, done1)]
        mine = jnp.where(sec == 0, done0, done1)
        other = px(jnp.where(sec == 0, done1, done0).astype(BF16))
        g_gain, g_bias, g_qkv, g_qv, g_out, g_up, g_up_bias, g_down = finish(scalars, mine, other, ff // 2)
    else:
        rows = placed([r1["keep"], low_got, b0["keep"], in_got])
        twin = pt(rows)

        def by_core(a, b):
            return jnp.where(ten == 0, jnp.stack([b, a]), jnp.stack([a, b]))

        g = jnp.stack([by_core(b0["g"][0], m0["g"][0]), by_core(r1["g"][0], m1["g"][0])])
        g = lax.psum_scatter(g.astype(F32), "section", scatter_dimension=0)
        g = lax.psum_scatter(g, "tensor", scatter_dimension=0)
        g = lax.psum_scatter(g, "dp", scatter_dimension=1, tiled=True)
        small = lax.psum(jnp.stack([b0["bsum"], r1["bsum"]]), ("section", "tensor", "dp"))
        small = lax.dynamic_index_in_dim(lax.dynamic_index_in_dim(small, sec, 0, False), ten, 0, False)
        g_gain, g_bias, g_qkv, _, g_out, g_up, _, g_down = parts(g[0], g[1], ff // 2)
        small = jnp.pad(small, ((0, 0), (MISC, HALF - MLP)))
        _, _, _, g_qv, _, _, g_up_bias, _ = parts(small, small, ff // 2)

    layer_outputs = ordered(rows[:2], twin[:2])
    input_grads = ordered(rows[2:], twin[2:]).astype(F32)

    return (
        layer_outputs,
        input_grads,
        g_gain[None],
        g_bias[None],
        g_qkv.transpose(1, 0, 2)[None],
        g_qv[None],
        g_out.T[None],
        g_up[None],
        g_up_bias,
        g_down.T[None],
    )


def solution(mesh):
    in_specs = (
        P(None, "dp", None),
        P(),
        P(None, "dp", None),
        P("section", None, "dp"),
        P("section", None, "dp"),
        P("section", "dp", None, "tensor"),
        P("section", None, "tensor"),
        P("section", "tensor", "dp"),
        P("section", "dp", "tensor"),
        P("section", "tensor"),
        P("section", "tensor", "dp"),
    )
    out_specs = (
        P("section", None, "dp", None),
        P("section", None, "dp", None),
        P("section", None, "dp"),
        P("section", None, "dp"),
        P("section", "dp", None, "tensor"),
        P("section", None, "tensor"),
        P("section", "tensor", "dp"),
        P("section", "dp", "tensor"),
        P("section", "tensor"),
        P("section", "tensor", "dp"),
    )
    return jax.shard_map(shards, mesh=mesh, in_specs=in_specs, out_specs=out_specs, check_vma=False)
```

```python
import functools
import math

import jax
import jax.numpy as jnp
from jax import lax
from jax.experimental import pallas as pl
from jax.experimental.pallas import tpu as pltpu
from jax.sharding import PartitionSpec as P

IMG_LEN = 197
IMG_PAD = 208
HD = 64
EPSILON = 1e-06
NEGATIVE = -1e30
F32 = jnp.float32
BF16 = jnp.bfloat16
BLOCK = 128
HALF = 1280
COST = 10 ** 10
SCALE = 1.0 / math.sqrt(HD)


def mm(a, b, dims):
    return lax.dot_general(a, b, (dims, ((), ())), preferred_element_type=F32)


def nn(a, b):
    return mm(a, b, ((1,), (0,)))


def nt(a, b):
    return mm(a, b, ((1,), (1,)))


def tn(a, b):
    return mm(a, b, ((0,), (0,)))


def normed(x):
    centred = x - jnp.mean(x, -1, keepdims=True)
    inverse = lax.rsqrt(jnp.mean(centred * centred, -1, keepdims=True) + EPSILON)
    return centred * inverse, inverse


def norm_back(grad, xhat, inverse, gain):
    t = grad * gain
    return inverse * (
        t - jnp.mean(t, -1, keepdims=True) - xhat * jnp.mean(t * xhat, -1, keepdims=True)
    )


def gelu_parts(u):
    cdf = 0.5 * (1.0 + lax.erf(u * math.sqrt(0.5)))
    pdf = jnp.exp(-0.5 * u * u) * (1.0 / math.sqrt(2.0 * math.pi))
    return u * cdf, cdf + u * pdf


QK = 384
V = 256
OUT = 128
MISC = 384
MLP = 512
ATT = QK + V


def low_lanes():
    return lax.broadcasted_iota(jnp.int32, (1, BLOCK), 1) < HD


def turn(a):
    return jnp.concatenate([a[:, HD:], a[:, :HD]], 1)


def valid_rows(sc, n):
    row = lax.broadcasted_iota(jnp.int32, (IMG_PAD, 1), 0)
    return jnp.where((row < IMG_LEN) & (n < sc[0]), 1.0, 0.0)


def image_rows(n):
    return pl.ds(pl.multiple_of(n * IMG_PAD, 16), IMG_PAD)


def forward_image(n, sc, x_ref, w, vec, brow, out_ref, kept, ready):
    r = image_rows(n)
    x = x_ref[r, :].astype(F32)
    xhat, inv = normed(x)
    attn_in = (xhat * vec[0:1, :] + vec[2:3, :]).astype(BF16)
    kept["xh1"][r, :] = xhat
    kept["inv1"][r, :] = jnp.broadcast_to(inv, (IMG_PAD, BLOCK))
    kept["ain"][r, :] = attn_in
    residual = x + vec[3:4, :]
    low = low_lanes()
    lane = lax.broadcasted_iota(jnp.int32, (1, ATT), 1)
    factor = jnp.where(lane < 192, SCALE, jnp.where(lane < 576, 1.0, 0.0))
    real = lax.broadcasted_iota(jnp.int32, (1, IMG_PAD), 1) < IMG_LEN
    for t in range(2):
        bias = jnp.concatenate([brow[t, i:i + 1, :] for i in range(5)], 1)
        p = jnp.concatenate([nn(attn_in, w[t, 0, :, :QK]), nn(attn_in, w[t, 1, :, :V])], 1)
        p = ((p + bias) * factor).astype(BF16)
        kept["qkv"][t, r, :] = p
        q, qk, k, v, vx = [p[:, i * BLOCK:(i + 1) * BLOCK] for i in range(5)]
        kq, xv = turn(qk), turn(vx)
        outs = []
        for i, (qq, kk, vv) in enumerate(
                [(jnp.where(low, q, 0), k, v), (jnp.where(low, 0, q), k, v), (jnp.where(low, qk, 0), kq, xv)]):
            s = jnp.where(real, nt(qq, kk), NEGATIVE)
            e = jnp.exp(s - jnp.max(s, -1, keepdims=True))
            pr = (e * (1.0 / jnp.sum(e, -1, keepdims=True))).astype(BF16)
            kept["pr"][n * 6 + t * 3 + i] = pr
            outs.append(nn(pr, vv))
        mixed = jnp.concatenate([outs[2], jnp.where(low, outs[0], outs[1])], 1).astype(BF16)
        kept["mx"][t, r, :] = mixed
        residual = residual + nt(mixed, w[t, 1, :, OUT:MISC])
    xhat, inv = normed(residual)
    mlp_in = (xhat * vec[1:2, :] + vec[4:5, :]).astype(BF16)
    kept["xh2"][r, :] = xhat
    kept["inv2"][r, :] = jnp.broadcast_to(inv, (IMG_PAD, BLOCK))
    kept["min"][r, :] = mlp_in
    out = residual + vec[5:6, :]
    ready(1)
    ff = kept["hd"].shape[1] // 2
    for t in range(2):
        bias = jnp.concatenate([brow[t, 5 + i:6 + i, :] for i in range(ff // BLOCK)], 1)
        hidden, slope = gelu_parts(nn(mlp_in, w[t, 0, :, MLP:]) + bias)
        hidden = hidden.astype(BF16)
        kept["hd"][r, t * ff:(t + 1) * ff] = hidden
        kept["sl"][r, t * ff:(t + 1) * ff] = slope.astype(BF16)
        out = out + nt(hidden, w[t, 1, :, MLP:])
    out_ref[r, :] = (out * valid_rows(sc, n)).astype(BF16)


def rsum(a):
    return jnp.sum(a, 0, keepdims=True)


def backward_mlp(n, sc, u_ref, w, vec, kept, grad, sums, bsum):
    r = image_rows(n)

    masked = u_ref[r, :].astype(F32) * valid_rows(sc, n)
    sums[5:6, :] += rsum(masked)
    dg = masked.astype(BF16)
    grad["dg"][r, :] = dg
    mg = jnp.zeros(masked.shape, F32)
    ff = kept["hd"].shape[1] // 2
    for t in range(2):
        c = slice(t * ff, (t + 1) * ff)
        up = (nn(dg, w[t, 1, :, MLP:]) * kept["sl"][r, c].astype(F32)).astype(BF16)
        grad["up"][r, c] = up
        total = rsum(up.astype(F32))
        for i in range(ff // BLOCK):
            bsum[t, 5 + i:6 + i, :] += total[:, i * BLOCK:(i + 1) * BLOCK]
        mg = mg + nt(up, w[t, 0, :, MLP:])
    xhat = kept["xh2"][r, :]
    sums[4:5, :] += rsum(mg)
    sums[1:2, :] += rsum(mg * xhat)
    res = masked + norm_back(mg, xhat, kept["inv2"][r, :1], vec[1:2, :])
    sums[3:4, :] += rsum(res)
    grad["res"][r, :] = res


def backward_attention(n, w, vec, in_ref, kept, grad, sums, bsum):
    r = image_rows(n)
    res = grad["res"][r, :]
    ag = res.astype(BF16)
    grad["ag"][r, :] = ag
    low = low_lanes()
    ig = jnp.zeros(res.shape, F32)
    for t in range(2):
        xg = nn(ag, w[t, 1, :, OUT:MISC]).astype(BF16)
        gx = jnp.where(low, 0, xg[:, :BLOCK])
        g = xg[:, BLOCK:]
        p = kept["qkv"][t, r, :]
        q, qk, k, v, vx = [p[:, i * BLOCK:(i + 1) * BLOCK] for i in range(5)]
        kq, xv = turn(qk), turn(vx)
        dq, dk, dv = [], [], []
        for i, (qq, kk, vv, gm, gg) in enumerate(
                [(q, k, v, jnp.where(low, g, 0), g), (q, k, v, jnp.where(low, 0, g), g), (qk, kq, xv, gx, turn(gx))]):
            pb = kept["pr"][n * 6 + t * 3 + i]
            pf = pb.astype(F32)
            dp = nt(gm, vv)
            ds = (pf * (dp - jnp.sum(pf * dp, -1, keepdims=True))).astype(BF16)
            dv.append(tn(pb, gg))
            dq.append(nn(ds, kk) * SCALE)
            dk.append(tn(ds, kq if i == 2 else qq))
        blocks = [
            jnp.where(low, dq[0], dq[1]), jnp.where(low, dq[2], dk[2]), jnp.where(low, dk[0], dk[1]),
            jnp.where(low, dv[0], dv[1]), dv[2],
        ]
        d = jnp.concatenate(blocks, 1).astype(BF16)
        grad["dqkv"][t, r, :] = d
        total = rsum(d.astype(F32))
        for i in range(5):
            bsum[t, i:i + 1, :] += total[:, i * BLOCK:(i + 1) * BLOCK]
        ig = ig + nt(d[:, :QK], w[t, 0, :, :QK]) + nt(d[:, QK:], w[t, 1, :, :V])
    xhat = kept["xh1"][r, :]
    sums[2:3, :] += rsum(ig)
    sums[0:1, :] += rsum(ig * xhat)
    in_ref[r, :] = res + norm_back(ig, xhat, kept["inv1"][r, :1], vec[0:1, :])


def weight_grads(t, piece, kept, grad, g):
    ag, dg = grad["ag"][...], grad["dg"][...]
    ain, mlp_in = kept["ain"][...], kept["min"][...]
    width = ag.shape[1]
    high = jnp.where(low_lanes(), 0.0, 1.0)
    d = grad["dqkv"][t]
    g[0, :, :QK] = tn(ain, d[:, :QK]).astype(BF16)
    val = tn(ain, d[:, QK:])
    out = tn(ag, kept["mx"][t])
    g[1, :, :OUT] = val[:, :BLOCK].astype(BF16)
    g[1, :, OUT:V] = (val[:, BLOCK:] + out[:, :BLOCK] * high).astype(BF16)
    g[1, :, V:MISC] = out[:, BLOCK:].astype(BF16)
    sums = jnp.concatenate([grad["sums"][...], jnp.zeros((BLOCK - 8, width), F32)], 0)
    g[0, :, MISC:MLP] = sums.T.astype(BF16)
    ff = kept["hd"].shape[1] // 2
    c = pl.ds(pl.multiple_of(t * ff, BLOCK), ff)
    g[0, :, MLP:] = tn(mlp_in, grad["up"][:, c]).astype(BF16)
    g[1, :, MLP:] = tn(dg, kept["hd"][:, c]).astype(BF16)
    if piece % 16 == 0:
        rows = jnp.concatenate([grad["bsum"][t], jnp.zeros((piece - 16, BLOCK), F32)], 0).astype(BF16)
        for i in range(width // piece):
            g[1, i * piece:(i + 1) * piece, MISC:MLP] = rows


def kept_shapes(total, width, ff):
    images = total // IMG_PAD
    return dict(
        xh1=((total, width), F32), inv1=((total, BLOCK), F32), ain=((total, width), BF16), qkv=((2, total, ATT), BF16),
        pr=((images * 6, IMG_PAD, IMG_PAD), BF16), mx=((2, total, 2 * BLOCK), BF16), xh2=((total, width), F32),
        inv2=((total, BLOCK), F32), min=((total, width), BF16), sl=((total, ff), BF16), hd=((total, ff), BF16))


def grad_shapes(total, width, ff):
    return dict(dg=((total, width), BF16), up=((total, ff), BF16), res=((total, width), F32), sums=((8, width), F32),
                bsum=((2, 16, BLOCK), F32), ag=((total, width), BF16), dqkv=((2, total, ATT), BF16))


def layer_call(phases, sources, load, store, out_shapes, scalars, given, total, width, ff, piece):
    ks = kept_shapes(total, width, ff)
    gs = grad_shapes(total, width, ff)
    weights = ["ain", "mx", "min", "hd"] + [n for n in gs if n != "res"]
    need = {"forward": ["x"], "back": ["u"] + list(ks), "theirs": weights, "mine": weights}
    gives = {"forward": {"out": ((total, width), BF16), **ks}, "back": {"keep": ((total, width), BF16), "give": ((total, width), BF16), "in": ((total, width), F32), **gs},
             "theirs": {}, "mine": {}}
    made = {}
    for p in phases:
        made.update(gives[p])
    inputs = list(dict.fromkeys(n for p in phases for n in need[p] if n not in made))
    if phases[-1] == "forward":
        shown = list(made)
    else:
        shown = [n for n in made if n in weights or n in ("keep", "give")]
        if "forward" in phases:
            shown.append("in")
    inner = [n for n in made if n not in shown]
    side = {"theirs": 0, "mine": 1}.get(phases[-1])
    products = phases[0] != "mine"
    vmem = pl.BlockSpec(memory_space=pltpu.VMEM)
    anywhere = pl.BlockSpec(memory_space=pl.ANY)
    ends = [] if side is None else out_shapes[side]
    scratch = [pltpu.SemaphoreType.DMA((2,))] + [pltpu.VMEM(*made[n]) for n in inner]
    if products:
        scratch += [pltpu.VMEM((2, 2, width, HALF), BF16), pltpu.VMEM((8, width), F32), pltpu.VMEM((2, 16, BLOCK), F32)]
    if ends:
        scratch.append(pltpu.VMEM((2, width, HALF), BF16))

    def body(*refs):
        refs = list(refs)

        def take(n):
            got = refs[:n]
            del refs[:n]
            return got

        sc = take(1)[0]
        at = dict(zip(inputs, take(len(inputs))))
        src = take(len(sources))
        at.update(zip(shown, take(len(shown))))
        dst = take(len(ends))
        sem = take(1)[0]
        at.update(zip(inner, take(len(inner))))
        if products:
            w, vec, brow = take(3)
            pending = [load(sc, src, w, sem, c) for c in range(2)]
            for part in pending if "forward" in phases else pending[::-1]:
                for c in part:
                    c.start()

            def ready(c):
                for copy in pending[c]:
                    copy.wait()
                if c == 0 and pending[c]:
                    vec[...] = w[0, 0, :, MISC:MLP].astype(F32).T[:8, :]
                    for t in range(2):
                        brow[t] = w[t, 1, :16, MISC:MLP].astype(F32)
                pending[c] = []

            ready(0 if "forward" in phases else 1)
        if "forward" in phases:
            if "back" in phases:
                ready(1)

                def step(n, carry):
                    forward_image(n, sc, at["x"], w, vec, brow, at["out"], at, ready)
                    return carry
                lax.fori_loop(0, total // IMG_PAD, step, 0)
            else:
                for n in range(total // IMG_PAD):
                    forward_image(n, sc, at["x"], w, vec, brow, at["out"], at, ready)
        if "back" in phases:
            sums, bsum = at["sums"], at["bsum"]
            sums[...] = jnp.zeros_like(sums)
            bsum[...] = jnp.zeros_like(bsum)
            ready(0)

            def back(n, carry):
                backward_mlp(n, sc, at["u"], w, vec, at, at, sums, bsum)
                backward_attention(n, w, vec, at["in"], at, at, sums, bsum)
                return carry
            lax.fori_loop(0, total // IMG_PAD, back, 0)
            rows = [at[n] for n in (("x", "out") if "forward" in phases else ("in", "u"))]
            for here in range(2):
                @pl.when(sc[2] == here)
                def _():
                    at["keep"][...] = rows[here][...].astype(BF16)
                    at["give"][...] = rows[1 - here][...].astype(BF16)
        if ends:
            g = take(1)[0]
            t = jnp.where(sc[1] == 0, 1 - side, side)
            weight_grads(t, piece, at, at, g)
            copies = store(sc, side, g, dst, sem.at[0])
            for c in copies:
                c.start()
            for c in copies:
                c.wait()

    outs = [made[n] for n in shown] + ends
    args = [scalars, *[given[n] for n in inputs], *(sources if products else [])]
    if not products:
        sources = []
    got = pl.pallas_call(
        body,
        out_shape=[jax.ShapeDtypeStruct(*o) for o in outs],
        in_specs=[pl.BlockSpec(memory_space=pltpu.SMEM)] + [vmem] * len(inputs) + [anywhere] * len(sources),
        out_specs=[vmem] * (len(outs) - len(ends)) + [anywhere] * len(ends),
        scratch_shapes=scratch,
        compiler_params=pltpu.CompilerParams(vmem_limit_bytes=34 * 2 ** 20),
        cost_estimate=pl.CostEstimate(flops=COST * len(phases), transcendentals=0, bytes_accessed=2 ** 23),
    )(*args)
    got = list(got)
    res = dict(zip(shown, got))
    res["g"] = got[len(shown):]
    return res


def parts(a, b, ff):
    small = a[:, MISC:MLP].T
    rows = b[:16, MISC:MLP]

    def heads(c, pair, single):
        return jnp.concatenate([c[:, pair:pair + BLOCK], c[:, single:single + HD]], 1)

    def lanes(first, last):
        return jnp.concatenate([rows[i:i + 1, :] for i in range(first, last)], 1)

    size = 3 * HD
    qkv = jnp.stack([heads(a, 0, BLOCK), heads(a, 2 * BLOCK, BLOCK + HD), heads(b, 0, BLOCK)])
    biases = jnp.concatenate([lanes(0, 2)[:, :size], lanes(3, 5)[:, :size]], 0)
    out = heads(b, 2 * BLOCK, BLOCK + HD)
    return small[:2], small[2:6], qkv, biases, out, a[:, MLP:], lanes(5, 5 + ff // BLOCK), b[:, MLP:]


def finish(scalars, mine, other, ff):
    piece = mine.shape[0]

    def body(sc, mine_ref, other_ref, *outs):
        first = sc[2] == 0
        a, b = mine_ref[...], other_ref[...].astype(F32)
        for ref, got in zip(outs, parts(jnp.where(first, a, b), jnp.where(first, b, a), ff)):
            ref[...] = got

    vmem = pl.BlockSpec(memory_space=pltpu.VMEM)
    shapes = [(2, piece), (4, piece), (3, piece, 3 * HD), (2, 3 * HD), (piece, 3 * HD), (piece, ff), (1, ff), (piece, ff)]
    return pl.pallas_call(
        body,
        out_shape=[jax.ShapeDtypeStruct(s, F32) for s in shapes],
        in_specs=[pl.BlockSpec(memory_space=pltpu.SMEM), vmem, vmem],
        out_specs=[vmem] * len(shapes),
    )(scalars, mine, other)


def shards(tokens, image_counts, cotangent, norm_gains, row_biases, qkv_weight, qv_bias, out_weight,
           up_weight, up_bias, down_weight):
    sec = lax.axis_index("section")
    dp = lax.axis_index("dp")
    ten = lax.axis_index("tensor")
    n_dp = lax.axis_size("dp")
    m = n_dp // 2
    zi, yi = dp // 2, dp % 2
    local_rows, width = tokens.shape[1:]
    images = local_rows * n_dp // IMG_LEN
    piece = width // n_dp
    ff = 2 * up_weight.shape[2]
    direct = piece % 16 == 0 and m == 4

    def pt(a):
        return lax.ppermute(a, "tensor", [(0, 1), (1, 0)])

    def px(a):
        return lax.ppermute(a, "section", [(0, 1), (1, 0)])

    def py(a):
        return lax.ppermute(a, "dp", [(i, i ^ 1) for i in range(n_dp)])

    def pd(a):
        return lax.ppermute(a, ("section", "dp"), [(i, (i + n_dp) % (2 * n_dp) ^ 1) for i in range(2 * n_dp)])

    def after(a, *b):
        return lax.optimization_barrier((a, *b))

    def plus(*a):
        return sum(b.astype(F32) for b in a)

    def chip_sums(g, got):
        keep0, give0, keep1, give1 = [plus(a, got[i // 2, i % 2]) for i, a in enumerate(g)]
        return [keep0, give0.astype(BF16), keep1, give1.astype(BF16)]

    def cross_first(s):
        return [s[0], px(s[1]), s[2], py(s[3])]

    def cross_second(s):
        a, b = plus(s[0], s[1]), plus(s[2], s[3])
        return [a[0], py(a[1].astype(BF16)), b[0], px(b[1].astype(BF16))]

    def crossed(s):
        return jnp.stack([plus(s[0], s[1]), plus(s[2], s[3])])

    def pz_to(a, kk):
        return lax.ppermute(a, "dp", [(i, i ^ (2 * kk)) for i in range(n_dp)])

    def along(quad):
        low = quad.astype(BF16)
        return plus(quad[:, 0], *[pz_to(low[:, kk], kk) for kk in range(1, m)])

    def along_steps(quad, *before):
        got = pz_to(quad[:, 1::2].astype(BF16), 1)
        quad = after(plus(quad[:, 0::2], got), *before)[0]
        return plus(quad[:, 0], pz_to(quad[:, 1].astype(BF16), 2))

    def pn(a):
        return lax.ppermute(a, ("dp", "tensor"), [(2 * i + 1, 2 * i + 3) for i in range(n_dp - 1)])

    def placed(rows, *before):
        tail = select[:, local_rows:]
        tails = after(pn(jnp.stack([tn(tail, a) for a in rows]).astype(BF16)), *before)[0]

        def place(a, b):
            a = tn(select[:, :local_rows], a).astype(BF16)
            return jnp.concatenate([a[:IMG_PAD] + b, a[IMG_PAD:]], 0)

        return jnp.stack([place(a, tails[i]) for i, a in enumerate(rows)])

    def ordered(a, b):
        a = a + b
        return jnp.where(sec == 0, a, a[::-1])[None]

    batch_tokens = lax.dynamic_index_in_dim(tokens, sec, 0, keepdims=False)
    batch_cot = lax.dynamic_index_in_dim(cotangent, sec, 0, keepdims=False)
    count = lax.dynamic_index_in_dim(image_counts, sec, 0, keepdims=False)
    first = jnp.minimum((dp * local_rows + IMG_LEN - 1) // IMG_LEN, images)
    last = jnp.minimum(((dp + 1) * local_rows + IMG_LEN - 1) // IMG_LEN, images)
    held = last - first
    slots = -(-(-(-local_rows // IMG_LEN)) // 2)
    lower = held // 2
    own_first = jnp.where(ten == 0, first, first + lower)
    own_count = jnp.where(ten == 0, lower, held - lower)
    total = slots * IMG_PAD
    row = lax.broadcasted_iota(jnp.int32, (total, 1), 0)
    slot, inside = row // IMG_PAD, row % IMG_PAD
    exists = (inside < IMG_LEN) & (slot < own_count)
    target = (own_first + slot) * IMG_LEN + inside - dp * local_rows
    canvas_rows = local_rows + IMG_PAD
    select = ((lax.broadcasted_iota(jnp.int32, (total, canvas_rows), 1) == target) & exists).astype(BF16)
    scalars = jnp.stack([jnp.minimum(own_count, jnp.maximum(count - own_first, 0)), ten, sec, zi, yi]).astype(jnp.int32)

    both = jnp.stack([batch_tokens, batch_cot])
    halo = lax.ppermute(both[:, :IMG_PAD], ("dp", "tensor"), [(2 * i + 3, 2 * i + 1) for i in range(n_dp - 1)])
    q, k, v = [[qkv_weight[0, :, i, h * HD:(h + 1) * HD] for h in range(3)] for i in range(3)]
    o = out_weight[0].T
    o = [o[:, h * HD:(h + 1) * HD] for h in range(3)]
    misc = jnp.concatenate([norm_gains[0], row_biases[0]], 0).T
    misc = jnp.pad(misc, ((0, 0), (0, BLOCK - misc.shape[1])))
    gap = jnp.zeros((HD,), BF16)
    rows = jnp.concatenate([qv_bias[0, 0], gap, gap, gap, qv_bias[0, 1], gap, up_bias[0]]).reshape(-1, BLOCK)
    rows = jnp.pad(rows, ((0, piece - rows.shape[0]), (0, 0)))
    up, down = up_weight[0], down_weight[0].T
    part0 = jnp.concatenate([q[0], q[1], q[2], k[2], k[0], k[1], misc, up], 1)
    part1 = jnp.concatenate([v[0], v[1], v[2], o[2], o[0], o[1], rows, down], 1)

    if direct:
        keep = jnp.where(sec == 0, part0, part1)
        give = jnp.where(sec == 0, part1, part0)
        got, halo = after(px(give), halo)
        start = [jnp.where(sec == 0, keep, got), jnp.where(sec == 0, got, keep)]

        def load(l, sc, src, w, sem, c):
            copies = []
            cols = slice(0, MLP) if c == 0 else slice(MLP, HALF)
            early, late = src[8:10]
            for side in range(2):
                t = jnp.where(sc[1] == 0, side, 1 - side)
                for kk in range(m):
                    z = lax.bitwise_xor(sc[3], kk)
                    near = pl.ds(pl.multiple_of((2 * z + sc[4]) * piece, 16), piece)
                    far = pl.ds(pl.multiple_of((2 * z + 1 - sc[4]) * piece, 16), piece)
                    for i, (h, r) in enumerate(((sc[2], near), (1 - sc[2], near), (sc[2], far), (1 - sc[2], far))):
                        if side == 0:
                            a, at = (src[i], l) if kk == 0 else (src[4 + i], kk - 1)
                        elif kk == 0:
                            a, at = early, 2 * i + l
                        elif i == 0:
                            a, at = (early, 7 + kk) if l == 0 else (src[10], kk - 1)
                        else:
                            a, at = late, (i - 1) * (m - 1) + kk - 1
                        a = a.at[at, :, cols]
                        copies.append(pltpu.make_async_copy(a, w.at[t, h, r, cols], sem.at[c]))
            return copies

        part = HALF // 2

        def store(sc, side, g, dst, sem):
            copies = []
            for c in range(2):
                for i in range(2):
                    for j in range(2):
                        hr, yr = (i, j) if c == 0 else (j, i)
                        h = lax.bitwise_xor(sc[2], hr)
                        y = lax.bitwise_xor(sc[4], yr)
                        out = dst[0].at[c, i, j] if side == 0 else dst[2 * c + i].at[j]
                        for kk in range(m):
                            z = lax.bitwise_xor(sc[3], kk)
                            r = pl.ds(pl.multiple_of((2 * z + y) * piece, 16), piece)
                            a = g.at[h, r, c * part:(c + 1) * part]
                            copies.append(pltpu.make_async_copy(a, out.at[kk], sem))
            return copies

        out_shapes = [[((2, 2, 2, m, piece, part), BF16)], [((2, m, piece, part), BF16)] * 4]
        own = jnp.stack(start)
        firsts = [own, px(own), py(own), pd(own)]
        columns = [jnp.stack([pz_to(start[0], kk) for kk in range(1, m)])]
        start[1] = after(start[1], columns[0])[0]
        near = pz_to(start[1], 1)
        columns[0], near, *firsts = after(columns[0], near, *firsts)
        rest = [columns[0], px(columns[0]), py(columns[0]), pd(columns[0])]
        columns.append(jnp.concatenate([near[None], pz_to(jnp.stack([start[1], near]), 2)]))
        early = pt(jnp.concatenate(firsts + columns[:1]))
        early, *rest = after(early, *rest, columns[1])[:-1]
        sources = [firsts + rest + [early, pt(jnp.concatenate(rest[1:]))]]
        rest = [px(columns[1]), py(columns[1]), pd(columns[1])]
        column_twin = pt(columns[1])
    else:
        def load(l, sc, src, w, sem, c):
            return [pltpu.make_async_copy(src[0], w, sem.at[c])] if c == 0 else []

        def store(sc, side, g, dst, sem):
            return [pltpu.make_async_copy(g, dst[0], sem)]

        out_shapes = [[((2, width, HALF), BF16)]] * 2
        a = lax.all_gather(jnp.stack([part0, part1]), "dp", axis=1, tiled=True)
        a = lax.all_gather(lax.all_gather(a, "tensor"), "section")
        sources = [[a[0]], [a[1]]]

    batch = jnp.concatenate([both, halo], 1)
    x0 = nn(select, batch[0]).astype(BF16)
    cot = nn(select, batch[1]).astype(BF16)
    x0, cot = after(x0, cot)
    if direct:
        x0, column_twin = after(x0, column_twin)

    def call(l, phases, **given):
        return layer_call(phases, sources[l] if phases[0] != "mine" else [], functools.partial(load, l), store, out_shapes, scalars, given,
                          total, width, ff, piece)

    r0 = call(0, ["forward"], x=x0)
    low0 = r0["out"]
    if direct:
        low0, *rest = after(low0, *rest)
        sources.append(firsts + columns[1:] + rest + [early, pt(jnp.concatenate(rest)), column_twin])
    r1 = call(1, ["forward", "back", "theirs"], x=low0, u=cot)
    if direct:
        got1 = pt(r1["g"][0])
    low_got = px(r1["give"])
    m1 = call(1, ["mine"], **r1)
    u = r1["in"]
    if direct:
        first, got1 = after(m1["g"][0], got1)
        sent1 = chip_sums([first] + m1["g"][1:], got1)
        u = after(u, sent1[1], sent1[3])[0]
        quad1 = cross_first(sent1)
    b0 = call(0, ["back", "theirs"], **{**r0, "u": u})
    if direct:
        b0["dg"], b0["g"][0], *quad1 = after(b0["dg"], b0["g"][0], *quad1)
        got0 = pt(b0["g"][0])
        quad1 = cross_second(quad1)
    in_got = px(b0["give"])
    m0 = call(0, ["mine"], **{**r0, **b0})

    if direct:
        first, got0 = after(m0["g"][0], got0)
        sent0 = chip_sums([first] + m0["g"][1:], got0)
        in_got, low_got, *quad1 = after(in_got, low_got, *quad1, sent0[1], sent0[3])[:6]
        quad0 = after(*cross_first(sent0))
        rows = placed([r1["keep"], low_got, b0["keep"], in_got], quad0[1], quad0[3])
        done1 = along_steps(crossed(quad1), quad0[1], quad0[3])
        quad0 = cross_second(quad0)
        twin, done0 = after(pt(rows), along(crossed(quad0)))
        done0, done1 = [jnp.concatenate([a[0], a[1]], 1) for a in (done0, done1)]
        mine = jnp.where(sec == 0, done0, done1)
        other = px(jnp.where(sec == 0, done1, done0).astype(BF16))
        g_gain, g_bias, g_qkv, g_qv, g_out, g_up, g_up_bias, g_down = finish(scalars, mine, other, ff // 2)
    else:
        rows = placed([r1["keep"], low_got, b0["keep"], in_got])
        twin = pt(rows)

        def by_core(a, b):
            return jnp.where(ten == 0, jnp.stack([b, a]), jnp.stack([a, b]))

        g = jnp.stack([by_core(b0["g"][0], m0["g"][0]), by_core(r1["g"][0], m1["g"][0])])
        g = lax.psum_scatter(g.astype(F32), "section", scatter_dimension=0)
        g = lax.psum_scatter(g, "tensor", scatter_dimension=0)
        g = lax.psum_scatter(g, "dp", scatter_dimension=1, tiled=True)
        small = lax.psum(jnp.stack([b0["bsum"], r1["bsum"]]), ("section", "tensor", "dp"))
        small = lax.dynamic_index_in_dim(lax.dynamic_index_in_dim(small, sec, 0, False), ten, 0, False)
        g_gain, g_bias, g_qkv, _, g_out, g_up, _, g_down = parts(g[0], g[1], ff // 2)
        small = jnp.pad(small, ((0, 0), (MISC, HALF - MLP)))
        _, _, _, g_qv, _, _, g_up_bias, _ = parts(small, small, ff // 2)

    layer_outputs = ordered(rows[:2], twin[:2])
    input_grads = ordered(rows[2:], twin[2:]).astype(F32)

    return (
        layer_outputs,
        input_grads,
        g_gain[None],
        g_bias[None],
        g_qkv.transpose(1, 0, 2)[None],
        g_qv[None],
        g_out.T[None],
        g_up[None],
        g_up_bias,
        g_down.T[None],
    )


def solution(mesh):
    in_specs = (
        P(None, "dp", None),
        P(),
        P(None, "dp", None),
        P("section", None, "dp"),
        P("section", None, "dp"),
        P("section", "dp", None, "tensor"),
        P("section", None, "tensor"),
        P("section", "tensor", "dp"),
        P("section", "dp", "tensor"),
        P("section", "tensor"),
        P("section", "tensor", "dp"),
    )
    out_specs = (
        P("section", None, "dp", None),
        P("section", None, "dp", None),
        P("section", None, "dp"),
        P("section", None, "dp"),
        P("section", "dp", None, "tensor"),
        P("section", None, "tensor"),
        P("section", "tensor", "dp"),
        P("section", "dp", "tensor"),
        P("section", "tensor"),
        P("section", "tensor", "dp"),
    )
    return jax.shard_map(shards, mesh=mesh, in_specs=in_specs, out_specs=out_specs, check_vma=False)
```

```python
import functools
import math

import jax
import jax.numpy as jnp
from jax import lax
from jax.experimental import pallas as pl
from jax.experimental.pallas import tpu as pltpu
from jax.sharding import PartitionSpec as P

IMG_LEN = 197
IMG_PAD = 208
HD = 64
EPSILON = 1e-06
NEGATIVE = -1e30
F32 = jnp.float32
BF16 = jnp.bfloat16
BLOCK = 128
HALF = 1280
COST = 10 ** 10
SCALE = 1.0 / math.sqrt(HD)


def mm(a, b, dims):
    return lax.dot_general(a, b, (dims, ((), ())), preferred_element_type=F32)


def nn(a, b):
    return mm(a, b, ((1,), (0,)))


def nt(a, b):
    return mm(a, b, ((1,), (1,)))


def tn(a, b):
    return mm(a, b, ((0,), (0,)))


def normed(x):
    centred = x - jnp.mean(x, -1, keepdims=True)
    inverse = lax.rsqrt(jnp.mean(centred * centred, -1, keepdims=True) + EPSILON)
    return centred * inverse, inverse


def norm_back(grad, xhat, inverse, gain):
    t = grad * gain
    return inverse * (
        t - jnp.mean(t, -1, keepdims=True) - xhat * jnp.mean(t * xhat, -1, keepdims=True)
    )


def gelu_parts(u):
    cdf = 0.5 * (1.0 + lax.erf(u * math.sqrt(0.5)))
    pdf = jnp.exp(-0.5 * u * u) * (1.0 / math.sqrt(2.0 * math.pi))
    return u * cdf, cdf + u * pdf


QK = 384
V = 256
OUT = 128
MISC = 384
MLP = 512
ATT = QK + V


def low_lanes():
    return lax.broadcasted_iota(jnp.int32, (1, BLOCK), 1) < HD


def turn(a):
    return jnp.concatenate([a[:, HD:], a[:, :HD]], 1)


def valid_rows(sc, n):
    row = lax.broadcasted_iota(jnp.int32, (IMG_PAD, 1), 0)
    return jnp.where((row < IMG_LEN) & (n < sc[0]), 1.0, 0.0)


def image_rows(n):
    return pl.ds(pl.multiple_of(n * IMG_PAD, 16), IMG_PAD)


def forward_image(n, sc, x_ref, w, vec, brow, out_ref, kept, ready):
    r = image_rows(n)
    x = x_ref[r, :].astype(F32)
    xhat, inv = normed(x)
    attn_in = (xhat * vec[0:1, :] + vec[2:3, :]).astype(BF16)
    kept["xh1"][r, :] = xhat
    kept["inv1"][r, :] = jnp.broadcast_to(inv, (IMG_PAD, BLOCK))
    kept["ain"][r, :] = attn_in
    residual = x + vec[3:4, :]
    low = low_lanes()
    lane = lax.broadcasted_iota(jnp.int32, (1, ATT), 1)
    factor = jnp.where(lane < 192, SCALE, jnp.where(lane < 576, 1.0, 0.0))
    real = lax.broadcasted_iota(jnp.int32, (1, IMG_PAD), 1) < IMG_LEN
    for t in range(2):
        bias = jnp.concatenate([brow[t, i:i + 1, :] for i in range(5)], 1)
        p = jnp.concatenate([nn(attn_in, w[t, 0, :, :QK]), nn(attn_in, w[t, 1, :, :V])], 1)
        p = ((p + bias) * factor).astype(BF16)
        kept["qkv"][t, r, :] = p
        q, qk, k, v, vx = [p[:, i * BLOCK:(i + 1) * BLOCK] for i in range(5)]
        kq, xv = turn(qk), turn(vx)
        outs = []
        for i, (qq, kk, vv) in enumerate(
                [(jnp.where(low, q, 0), k, v), (jnp.where(low, 0, q), k, v), (jnp.where(low, qk, 0), kq, xv)]):
            s = jnp.where(real, nt(qq, kk), NEGATIVE)
            e = jnp.exp(s - jnp.max(s, -1, keepdims=True))
            pr = (e * (1.0 / jnp.sum(e, -1, keepdims=True))).astype(BF16)
            kept["pr"][n * 6 + t * 3 + i] = pr
            outs.append(nn(pr, vv))
        mixed = jnp.concatenate([outs[2], jnp.where(low, outs[0], outs[1])], 1).astype(BF16)
        kept["mx"][t, r, :] = mixed
        residual = residual + nt(mixed, w[t, 1, :, OUT:MISC])
    xhat, inv = normed(residual)
    mlp_in = (xhat * vec[1:2, :] + vec[4:5, :]).astype(BF16)
    kept["xh2"][r, :] = xhat
    kept["inv2"][r, :] = jnp.broadcast_to(inv, (IMG_PAD, BLOCK))
    kept["min"][r, :] = mlp_in
    out = residual + vec[5:6, :]
    ready(1)
    ff = kept["hd"].shape[1] // 2
    for t in range(2):
        bias = jnp.concatenate([brow[t, 5 + i:6 + i, :] for i in range(ff // BLOCK)], 1)
        hidden, slope = gelu_parts(nn(mlp_in, w[t, 0, :, MLP:]) + bias)
        hidden = hidden.astype(BF16)
        kept["hd"][r, t * ff:(t + 1) * ff] = hidden
        kept["sl"][r, t * ff:(t + 1) * ff] = slope.astype(BF16)
        out = out + nt(hidden, w[t, 1, :, MLP:])
    out_ref[r, :] = (out * valid_rows(sc, n)).astype(BF16)


def rsum(a):
    return jnp.sum(a, 0, keepdims=True)


def backward_mlp(n, sc, u_ref, w, vec, kept, grad, sums, bsum):
    r = image_rows(n)

    masked = u_ref[r, :].astype(F32) * valid_rows(sc, n)
    sums[5:6, :] += rsum(masked)
    dg = masked.astype(BF16)
    grad["dg"][r, :] = dg
    mg = jnp.zeros(masked.shape, F32)
    ff = kept["hd"].shape[1] // 2
    for t in range(2):
        c = slice(t * ff, (t + 1) * ff)
        up = (nn(dg, w[t, 1, :, MLP:]) * kept["sl"][r, c].astype(F32)).astype(BF16)
        grad["up"][r, c] = up
        total = rsum(up.astype(F32))
        for i in range(ff // BLOCK):
            bsum[t, 5 + i:6 + i, :] += total[:, i * BLOCK:(i + 1) * BLOCK]
        mg = mg + nt(up, w[t, 0, :, MLP:])
    xhat = kept["xh2"][r, :]
    sums[4:5, :] += rsum(mg)
    sums[1:2, :] += rsum(mg * xhat)
    res = masked + norm_back(mg, xhat, kept["inv2"][r, :1], vec[1:2, :])
    sums[3:4, :] += rsum(res)
    grad["res"][r, :] = res


def backward_attention(n, w, vec, in_ref, kept, grad, sums, bsum):
    r = image_rows(n)
    res = grad["res"][r, :]
    ag = res.astype(BF16)
    grad["ag"][r, :] = ag
    low = low_lanes()
    ig = jnp.zeros(res.shape, F32)
    for t in range(2):
        xg = nn(ag, w[t, 1, :, OUT:MISC]).astype(BF16)
        gx = jnp.where(low, 0, xg[:, :BLOCK])
        g = xg[:, BLOCK:]
        p = kept["qkv"][t, r, :]
        q, qk, k, v, vx = [p[:, i * BLOCK:(i + 1) * BLOCK] for i in range(5)]
        kq, xv = turn(qk), turn(vx)
        dq, dk, dv = [], [], []
        for i, (qq, kk, vv, gm, gg) in enumerate(
                [(q, k, v, jnp.where(low, g, 0), g), (q, k, v, jnp.where(low, 0, g), g), (qk, kq, xv, gx, turn(gx))]):
            pb = kept["pr"][n * 6 + t * 3 + i]
            pf = pb.astype(F32)
            dp = nt(gm, vv)
            ds = (pf * (dp - jnp.sum(pf * dp, -1, keepdims=True))).astype(BF16)
            dv.append(tn(pb, gg))
            dq.append(nn(ds, kk) * SCALE)
            dk.append(tn(ds, kq if i == 2 else qq))
        blocks = [
            jnp.where(low, dq[0], dq[1]), jnp.where(low, dq[2], dk[2]), jnp.where(low, dk[0], dk[1]),
            jnp.where(low, dv[0], dv[1]), dv[2],
        ]
        d = jnp.concatenate(blocks, 1).astype(BF16)
        grad["dqkv"][t, r, :] = d
        total = rsum(d.astype(F32))
        for i in range(5):
            bsum[t, i:i + 1, :] += total[:, i * BLOCK:(i + 1) * BLOCK]
        ig = ig + nt(d[:, :QK], w[t, 0, :, :QK]) + nt(d[:, QK:], w[t, 1, :, :V])
    xhat = kept["xh1"][r, :]
    sums[2:3, :] += rsum(ig)
    sums[0:1, :] += rsum(ig * xhat)
    in_ref[r, :] = res + norm_back(ig, xhat, kept["inv1"][r, :1], vec[0:1, :])


def weight_grads(t, piece, kept, grad, g):
    ag, dg = grad["ag"][...], grad["dg"][...]
    ain, mlp_in = kept["ain"][...], kept["min"][...]
    width = ag.shape[1]
    high = jnp.where(low_lanes(), 0.0, 1.0)
    d = grad["dqkv"][t]
    g[0, :, :QK] = tn(ain, d[:, :QK]).astype(BF16)
    val = tn(ain, d[:, QK:])
    out = tn(ag, kept["mx"][t])
    g[1, :, :OUT] = val[:, :BLOCK].astype(BF16)
    g[1, :, OUT:V] = (val[:, BLOCK:] + out[:, :BLOCK] * high).astype(BF16)
    g[1, :, V:MISC] = out[:, BLOCK:].astype(BF16)
    sums = jnp.concatenate([grad["sums"][...], jnp.zeros((BLOCK - 8, width), F32)], 0)
    g[0, :, MISC:MLP] = sums.T.astype(BF16)
    ff = kept["hd"].shape[1] // 2
    c = pl.ds(pl.multiple_of(t * ff, BLOCK), ff)
    g[0, :, MLP:] = tn(mlp_in, grad["up"][:, c]).astype(BF16)
    g[1, :, MLP:] = tn(dg, kept["hd"][:, c]).astype(BF16)
    if piece % 16 == 0:
        rows = jnp.concatenate([grad["bsum"][t], jnp.zeros((piece - 16, BLOCK), F32)], 0).astype(BF16)
        for i in range(width // piece):
            g[1, i * piece:(i + 1) * piece, MISC:MLP] = rows


def kept_shapes(total, width, ff):
    images = total // IMG_PAD
    return dict(
        xh1=((total, width), F32), inv1=((total, BLOCK), F32), ain=((total, width), BF16), qkv=((2, total, ATT), BF16),
        pr=((images * 6, IMG_PAD, IMG_PAD), BF16), mx=((2, total, 2 * BLOCK), BF16), xh2=((total, width), F32),
        inv2=((total, BLOCK), F32), min=((total, width), BF16), sl=((total, ff), BF16), hd=((total, ff), BF16))


def grad_shapes(total, width, ff):
    return dict(dg=((total, width), BF16), up=((total, ff), BF16), res=((total, width), F32), sums=((8, width), F32),
                bsum=((2, 16, BLOCK), F32), ag=((total, width), BF16), dqkv=((2, total, ATT), BF16))


def layer_call(phases, sources, load, store, out_shapes, scalars, given, total, width, ff, piece):
    ks = kept_shapes(total, width, ff)
    gs = grad_shapes(total, width, ff)
    weights = ["ain", "mx", "min", "hd"] + [n for n in gs if n != "res"]
    need = {"forward": ["x"], "back": ["u"] + list(ks), "theirs": weights, "mine": weights}
    gives = {"forward": {"out": ((total, width), BF16), **ks}, "back": {"keep": ((total, width), BF16), "give": ((total, width), BF16), "in": ((total, width), F32), **gs},
             "theirs": {}, "mine": {}}
    made = {}
    for p in phases:
        made.update(gives[p])
    inputs = list(dict.fromkeys(n for p in phases for n in need[p] if n not in made))
    if phases[-1] == "forward":
        shown = list(made)
    else:
        shown = [n for n in made if n in weights or n in ("keep", "give")]
        if "forward" in phases:
            shown.append("in")
    inner = [n for n in made if n not in shown]
    side = {"theirs": 0, "mine": 1}.get(phases[-1])
    products = phases[0] != "mine"
    vmem = pl.BlockSpec(memory_space=pltpu.VMEM)
    anywhere = pl.BlockSpec(memory_space=pl.ANY)
    ends = [] if side is None else out_shapes[side]
    scratch = [pltpu.SemaphoreType.DMA((2,))] + [pltpu.VMEM(*made[n]) for n in inner]
    if products:
        scratch += [pltpu.VMEM((2, 2, width, HALF), BF16), pltpu.VMEM((8, width), F32), pltpu.VMEM((2, 16, BLOCK), F32)]
    if ends:
        scratch.append(pltpu.VMEM((2, width, HALF), BF16))

    def body(*refs):
        refs = list(refs)

        def take(n):
            got = refs[:n]
            del refs[:n]
            return got

        sc = take(1)[0]
        at = dict(zip(inputs, take(len(inputs))))
        src = take(len(sources))
        at.update(zip(shown, take(len(shown))))
        dst = take(len(ends))
        sem = take(1)[0]
        at.update(zip(inner, take(len(inner))))
        if products:
            w, vec, brow = take(3)
            pending = [load(sc, src, w, sem, c) for c in range(2)]
            for part in pending if "forward" in phases else pending[::-1]:
                for c in part:
                    c.start()

            def ready(c):
                for copy in pending[c]:
                    copy.wait()
                if c == 0 and pending[c]:
                    vec[...] = w[0, 0, :, MISC:MLP].astype(F32).T[:8, :]
                    for t in range(2):
                        brow[t] = w[t, 1, :16, MISC:MLP].astype(F32)
                pending[c] = []

            ready(0 if "forward" in phases else 1)
        if "forward" in phases:
            if "back" in phases:
                ready(1)

                def step(n, carry):
                    forward_image(n, sc, at["x"], w, vec, brow, at["out"], at, ready)
                    return carry
                lax.fori_loop(0, total // IMG_PAD, step, 0)
            else:
                for n in range(total // IMG_PAD):
                    forward_image(n, sc, at["x"], w, vec, brow, at["out"], at, ready)
        if "back" in phases:
            sums, bsum = at["sums"], at["bsum"]
            sums[...] = jnp.zeros_like(sums)
            bsum[...] = jnp.zeros_like(bsum)
            ready(0)

            def back(n, carry):
                backward_mlp(n, sc, at["u"], w, vec, at, at, sums, bsum)
                backward_attention(n, w, vec, at["in"], at, at, sums, bsum)
                return carry
            lax.fori_loop(0, total // IMG_PAD, back, 0)
            rows = [at[n] for n in (("x", "out") if "forward" in phases else ("in", "u"))]
            for here in range(2):
                @pl.when(sc[2] == here)
                def _():
                    at["keep"][...] = rows[here][...].astype(BF16)
                    at["give"][...] = rows[1 - here][...].astype(BF16)
        if ends:
            g = take(1)[0]
            t = jnp.where(sc[1] == 0, 1 - side, side)
            weight_grads(t, piece, at, at, g)
            copies = store(sc, side, g, dst, sem.at[0])
            for c in copies:
                c.start()
            for c in copies:
                c.wait()

    outs = [made[n] for n in shown] + ends
    args = [scalars, *[given[n] for n in inputs], *(sources if products else [])]
    if not products:
        sources = []
    got = pl.pallas_call(
        body,
        out_shape=[jax.ShapeDtypeStruct(*o) for o in outs],
        in_specs=[pl.BlockSpec(memory_space=pltpu.SMEM)] + [vmem] * len(inputs) + [anywhere] * len(sources),
        out_specs=[vmem] * (len(outs) - len(ends)) + [anywhere] * len(ends),
        scratch_shapes=scratch,
        compiler_params=pltpu.CompilerParams(vmem_limit_bytes=34 * 2 ** 20),
        cost_estimate=pl.CostEstimate(flops=COST * len(phases), transcendentals=0, bytes_accessed=2 ** 23),
    )(*args)
    got = list(got)
    res = dict(zip(shown, got))
    res["g"] = got[len(shown):]
    return res


def parts(a, b, ff):
    small = a[:, MISC:MLP].T
    rows = b[:16, MISC:MLP]

    def heads(c, pair, single):
        return jnp.concatenate([c[:, pair:pair + BLOCK], c[:, single:single + HD]], 1)

    def lanes(first, last):
        return jnp.concatenate([rows[i:i + 1, :] for i in range(first, last)], 1)

    size = 3 * HD
    qkv = jnp.stack([heads(a, 0, BLOCK), heads(a, 2 * BLOCK, BLOCK + HD), heads(b, 0, BLOCK)])
    biases = jnp.concatenate([lanes(0, 2)[:, :size], lanes(3, 5)[:, :size]], 0)
    out = heads(b, 2 * BLOCK, BLOCK + HD)
    return small[:2], small[2:6], qkv, biases, out, a[:, MLP:], lanes(5, 5 + ff // BLOCK), b[:, MLP:]


def finish(scalars, mine, other, ff):
    piece = mine.shape[0]

    def body(sc, mine_ref, other_ref, *outs):
        first = sc[2] == 0
        a, b = mine_ref[...], other_ref[...].astype(F32)
        for ref, got in zip(outs, parts(jnp.where(first, a, b), jnp.where(first, b, a), ff)):
            ref[...] = got

    vmem = pl.BlockSpec(memory_space=pltpu.VMEM)
    shapes = [(2, piece), (4, piece), (3, piece, 3 * HD), (2, 3 * HD), (piece, 3 * HD), (piece, ff), (1, ff), (piece, ff)]
    return pl.pallas_call(
        body,
        out_shape=[jax.ShapeDtypeStruct(s, F32) for s in shapes],
        in_specs=[pl.BlockSpec(memory_space=pltpu.SMEM), vmem, vmem],
        out_specs=[vmem] * len(shapes),
    )(scalars, mine, other)


def shards(tokens, image_counts, cotangent, norm_gains, row_biases, qkv_weight, qv_bias, out_weight,
           up_weight, up_bias, down_weight):
    sec = lax.axis_index("section")
    dp = lax.axis_index("dp")
    ten = lax.axis_index("tensor")
    n_dp = lax.axis_size("dp")
    m = n_dp // 2
    zi, yi = dp // 2, dp % 2
    local_rows, width = tokens.shape[1:]
    images = local_rows * n_dp // IMG_LEN
    piece = width // n_dp
    ff = 2 * up_weight.shape[2]
    direct = piece % 16 == 0 and m == 4

    def pt(a):
        return lax.ppermute(a, "tensor", [(0, 1), (1, 0)])

    def px(a):
        return lax.ppermute(a, "section", [(0, 1), (1, 0)])

    def py(a):
        return lax.ppermute(a, "dp", [(i, i ^ 1) for i in range(n_dp)])

    def pd(a):
        return lax.ppermute(a, ("section", "dp"), [(i, (i + n_dp) % (2 * n_dp) ^ 1) for i in range(2 * n_dp)])

    def after(a, *b):
        return lax.optimization_barrier((a, *b))

    def plus(*a):
        return sum(b.astype(F32) for b in a)

    def chip_sums(g, got):
        keep0, give0, keep1, give1 = [plus(a, got[i // 2, i % 2]) for i, a in enumerate(g)]
        return [keep0, give0.astype(BF16), keep1, give1.astype(BF16)]

    def cross_first(s):
        return [s[0], px(s[1]), s[2], py(s[3])]

    def cross_second(s):
        a, b = plus(s[0], s[1]), plus(s[2], s[3])
        return [a[0], py(a[1].astype(BF16)), b[0], px(b[1].astype(BF16))]

    def crossed(s):
        return jnp.stack([plus(s[0], s[1]), plus(s[2], s[3])])

    def pz_to(a, kk):
        return lax.ppermute(a, "dp", [(i, i ^ (2 * kk)) for i in range(n_dp)])

    def along(quad, *before):
        low = quad.astype(BF16)
        got = [pz_to(low[:, kk], kk) for kk in range(1, m)]
        return plus(quad[:, 0], *after(*got, *before)[:m - 1])

    def along_steps(quad, *before):
        got = pz_to(quad[:, 1::2].astype(BF16), 1)
        quad = after(plus(quad[:, 0::2], got), *before)[0]
        return plus(quad[:, 0], pz_to(quad[:, 1].astype(BF16), 2))

    def pn(a):
        return lax.ppermute(a, ("dp", "tensor"), [(2 * i + 1, 2 * i + 3) for i in range(n_dp - 1)])

    def placed(rows, *before):
        tail = select[:, local_rows:]
        tails = after(pn(jnp.stack([tn(tail, a) for a in rows]).astype(BF16)), *before)[0]

        def place(a, b):
            a = tn(select[:, :local_rows], a).astype(BF16)
            return jnp.concatenate([a[:IMG_PAD] + b, a[IMG_PAD:]], 0)

        return jnp.stack([place(a, tails[i]) for i, a in enumerate(rows)])

    def ordered(a, b):
        a = a + b
        return jnp.where(sec == 0, a, a[::-1])[None]

    batch_tokens = lax.dynamic_index_in_dim(tokens, sec, 0, keepdims=False)
    batch_cot = lax.dynamic_index_in_dim(cotangent, sec, 0, keepdims=False)
    count = lax.dynamic_index_in_dim(image_counts, sec, 0, keepdims=False)
    first = jnp.minimum((dp * local_rows + IMG_LEN - 1) // IMG_LEN, images)
    last = jnp.minimum(((dp + 1) * local_rows + IMG_LEN - 1) // IMG_LEN, images)
    held = last - first
    slots = -(-(-(-local_rows // IMG_LEN)) // 2)
    lower = held // 2
    own_first = jnp.where(ten == 0, first, first + lower)
    own_count = jnp.where(ten == 0, lower, held - lower)
    total = slots * IMG_PAD
    row = lax.broadcasted_iota(jnp.int32, (total, 1), 0)
    slot, inside = row // IMG_PAD, row % IMG_PAD
    exists = (inside < IMG_LEN) & (slot < own_count)
    target = (own_first + slot) * IMG_LEN + inside - dp * local_rows
    canvas_rows = local_rows + IMG_PAD
    select = ((lax.broadcasted_iota(jnp.int32, (total, canvas_rows), 1) == target) & exists).astype(BF16)
    scalars = jnp.stack([jnp.minimum(own_count, jnp.maximum(count - own_first, 0)), ten, sec, zi, yi]).astype(jnp.int32)

    both = jnp.stack([batch_tokens, batch_cot])
    halo = lax.ppermute(both[:, :IMG_PAD], ("dp", "tensor"), [(2 * i + 3, 2 * i + 1) for i in range(n_dp - 1)])
    q, k, v = [[qkv_weight[0, :, i, h * HD:(h + 1) * HD] for h in range(3)] for i in range(3)]
    o = out_weight[0].T
    o = [o[:, h * HD:(h + 1) * HD] for h in range(3)]
    misc = jnp.concatenate([norm_gains[0], row_biases[0]], 0).T
    misc = jnp.pad(misc, ((0, 0), (0, BLOCK - misc.shape[1])))
    gap = jnp.zeros((HD,), BF16)
    rows = jnp.concatenate([qv_bias[0, 0], gap, gap, gap, qv_bias[0, 1], gap, up_bias[0]]).reshape(-1, BLOCK)
    rows = jnp.pad(rows, ((0, piece - rows.shape[0]), (0, 0)))
    up, down = up_weight[0], down_weight[0].T
    part0 = jnp.concatenate([q[0], q[1], q[2], k[2], k[0], k[1], misc, up], 1)
    part1 = jnp.concatenate([v[0], v[1], v[2], o[2], o[0], o[1], rows, down], 1)

    if direct:
        keep = jnp.where(sec == 0, part0, part1)
        give = jnp.where(sec == 0, part1, part0)
        got, halo = after(px(give), halo)
        start = [jnp.where(sec == 0, keep, got), jnp.where(sec == 0, got, keep)]

        def load(l, sc, src, w, sem, c):
            copies = []
            cols = slice(0, MLP) if c == 0 else slice(MLP, HALF)
            for side in range(2):
                t = jnp.where(sc[1] == 0, side, 1 - side)
                own = src[side * 8:side * 8 + 8]
                for kk in range(m):
                    z = lax.bitwise_xor(sc[3], kk)
                    near = pl.ds(pl.multiple_of((2 * z + sc[4]) * piece, 16), piece)
                    far = pl.ds(pl.multiple_of((2 * z + 1 - sc[4]) * piece, 16), piece)
                    for i, (h, r) in enumerate(((sc[2], near), (1 - sc[2], near), (sc[2], far), (1 - sc[2], far))):
                        a = own[i].at[l, :, cols] if kk == 0 else own[4 + i].at[kk - 1, :, cols]
                        copies.append(pltpu.make_async_copy(a, w.at[t, h, r, cols], sem.at[c]))
            return copies

        part = HALF // 2

        def store(sc, side, g, dst, sem):
            copies = []
            for c in range(2):
                for i in range(2):
                    for j in range(2):
                        hr, yr = (i, j) if c == 0 else (j, i)
                        h = lax.bitwise_xor(sc[2], hr)
                        y = lax.bitwise_xor(sc[4], yr)
                        out = dst[0].at[c, i, j] if side == 0 else dst[2 * c + i].at[j]
                        for kk in range(m):
                            z = lax.bitwise_xor(sc[3], kk)
                            r = pl.ds(pl.multiple_of((2 * z + y) * piece, 16), piece)
                            a = g.at[h, r, c * part:(c + 1) * part]
                            copies.append(pltpu.make_async_copy(a, out.at[kk], sem))
            return copies

        out_shapes = [[((2, 2, 2, m, piece, part), BF16)], [((2, m, piece, part), BF16)] * 4]
        own = jnp.stack(start)
        firsts = [own, px(own), py(own), pd(own)]
        columns = [jnp.stack([pz_to(start[0], kk) for kk in range(1, m)])]
        start[1] = after(start[1], columns[0])[0]
        near = pz_to(start[1], 1)
        columns[0], near, *firsts = after(columns[0], near, *firsts)
        rest = [columns[0], px(columns[0]), py(columns[0]), pd(columns[0])]
        columns.append(jnp.concatenate([near[None], pz_to(jnp.stack([start[1], near]), 2)]))
        columns[1], *rest = after(columns[1], *rest)
        twins = [pt(a) for a in firsts]
        sources = [firsts + rest + twins + [pt(a) for a in rest]]
        sources.append(columns[1:] + [px(columns[1]), py(columns[1]), pd(columns[1])])
    else:
        def load(l, sc, src, w, sem, c):
            return [pltpu.make_async_copy(src[0], w, sem.at[c])] if c == 0 else []

        def store(sc, side, g, dst, sem):
            return [pltpu.make_async_copy(g, dst[0], sem)]

        out_shapes = [[((2, width, HALF), BF16)]] * 2
        a = lax.all_gather(jnp.stack([part0, part1]), "dp", axis=1, tiled=True)
        a = lax.all_gather(lax.all_gather(a, "tensor"), "section")
        sources = [[a[0]], [a[1]]]

    batch = jnp.concatenate([both, halo], 1)
    x0 = nn(select, batch[0]).astype(BF16)
    cot = nn(select, batch[1]).astype(BF16)
    x0, cot = after(x0, cot)

    def call(l, phases, **given):
        return layer_call(phases, sources[l], functools.partial(load, l), store, out_shapes, scalars, given,
                          total, width, ff, piece)

    r0 = call(0, ["forward"], x=x0)
    low0 = r0["out"]
    if direct:
        low0, *rest = after(low0, *sources[1])
        sources[1] = firsts + rest + twins + [pt(a) for a in rest]
    r1 = call(1, ["forward", "back", "theirs"], x=low0, u=cot)
    if direct:
        got1 = pt(r1["g"][0])
    low_got = px(r1["give"])
    m1 = call(1, ["mine"], **r1)
    u = r1["in"]
    if direct:
        first, got1 = after(m1["g"][0], got1)
        sent1 = chip_sums([first] + m1["g"][1:], got1)
        u = after(u, sent1[1], sent1[3])[0]
        quad1 = cross_first(sent1)
    b0 = call(0, ["back", "theirs"], **{**r0, "u": u})
    if direct:
        b0["dg"], b0["g"][0], *quad1 = after(b0["dg"], b0["g"][0], *quad1)
        got0 = pt(b0["g"][0])
        quad1 = cross_second(quad1)
    in_got = px(b0["give"])
    m0 = call(0, ["mine"], **{**r0, **b0})

    if direct:
        first, got0 = after(m0["g"][0], got0)
        sent0 = chip_sums([first] + m0["g"][1:], got0)
        in_got, low_got, *quad1 = after(in_got, low_got, *quad1, sent0[1], sent0[3])[:6]
        quad0 = after(*cross_first(sent0))
        in_got, low_got = after(in_got, low_got, quad0[1], quad0[3])[:2]
        rows = placed([r1["keep"], low_got, b0["keep"], in_got])
        quad0 = cross_second(quad0)
        done1 = along(crossed(quad1), quad0[1], quad0[3])
        twin, done0 = after(pt(rows), along(crossed(quad0)))
        done0, done1 = [jnp.concatenate([a[0], a[1]], 1) for a in (done0, done1)]
        mine = jnp.where(sec == 0, done0, done1)
        other = px(jnp.where(sec == 0, done1, done0).astype(BF16))
        g_gain, g_bias, g_qkv, g_qv, g_out, g_up, g_up_bias, g_down = finish(scalars, mine, other, ff // 2)
    else:
        rows = placed([r1["keep"], low_got, b0["keep"], in_got])
        twin = pt(rows)

        def by_core(a, b):
            return jnp.where(ten == 0, jnp.stack([b, a]), jnp.stack([a, b]))

        g = jnp.stack([by_core(b0["g"][0], m0["g"][0]), by_core(r1["g"][0], m1["g"][0])])
        g = lax.psum_scatter(g.astype(F32), "section", scatter_dimension=0)
        g = lax.psum_scatter(g, "tensor", scatter_dimension=0)
        g = lax.psum_scatter(g, "dp", scatter_dimension=1, tiled=True)
        small = lax.psum(jnp.stack([b0["bsum"], r1["bsum"]]), ("section", "tensor", "dp"))
        small = lax.dynamic_index_in_dim(lax.dynamic_index_in_dim(small, sec, 0, False), ten, 0, False)
        g_gain, g_bias, g_qkv, _, g_out, g_up, _, g_down = parts(g[0], g[1], ff // 2)
        small = jnp.pad(small, ((0, 0), (MISC, HALF - MLP)))
        _, _, _, g_qv, _, _, g_up_bias, _ = parts(small, small, ff // 2)

    layer_outputs = ordered(rows[:2], twin[:2])
    input_grads = ordered(rows[2:], twin[2:]).astype(F32)

    return (
        layer_outputs,
        input_grads,
        g_gain[None],
        g_bias[None],
        g_qkv.transpose(1, 0, 2)[None],
        g_qv[None],
        g_out.T[None],
        g_up[None],
        g_up_bias,
        g_down.T[None],
    )


def solution(mesh):
    in_specs = (
        P(None, "dp", None),
        P(),
        P(None, "dp", None),
        P("section", None, "dp"),
        P("section", None, "dp"),
        P("section", "dp", None, "tensor"),
        P("section", None, "tensor"),
        P("section", "tensor", "dp"),
        P("section", "dp", "tensor"),
        P("section", "tensor"),
        P("section", "tensor", "dp"),
    )
    out_specs = (
        P("section", None, "dp", None),
        P("section", None, "dp", None),
        P("section", None, "dp"),
        P("section", None, "dp"),
        P("section", "dp", None, "tensor"),
        P("section", None, "tensor"),
        P("section", "tensor", "dp"),
        P("section", "dp", "tensor"),
        P("section", "tensor"),
        P("section", "tensor", "dp"),
    )
    return jax.shard_map(shards, mesh=mesh, in_specs=in_specs, out_specs=out_specs, check_vma=False)
```

```python
import functools
import math

import jax
import jax.numpy as jnp
from jax import lax
from jax.experimental import pallas as pl
from jax.experimental.pallas import tpu as pltpu
from jax.sharding import PartitionSpec as P

IMG_LEN = 197
IMG_PAD = 208
HD = 64
EPSILON = 1e-06
NEGATIVE = -1e30
F32 = jnp.float32
BF16 = jnp.bfloat16
BLOCK = 128
HALF = 1280
COST = 10 ** 10
SCALE = 1.0 / math.sqrt(HD)


def mm(a, b, dims):
    return lax.dot_general(a, b, (dims, ((), ())), preferred_element_type=F32)


def nn(a, b):
    return mm(a, b, ((1,), (0,)))


def nt(a, b):
    return mm(a, b, ((1,), (1,)))


def tn(a, b):
    return mm(a, b, ((0,), (0,)))


def normed(x):
    centred = x - jnp.mean(x, -1, keepdims=True)
    inverse = lax.rsqrt(jnp.mean(centred * centred, -1, keepdims=True) + EPSILON)
    return centred * inverse, inverse


def norm_back(grad, xhat, inverse, gain):
    t = grad * gain
    return inverse * (
        t - jnp.mean(t, -1, keepdims=True) - xhat * jnp.mean(t * xhat, -1, keepdims=True)
    )


def gelu_parts(u):
    cdf = 0.5 * (1.0 + lax.erf(u * math.sqrt(0.5)))
    pdf = jnp.exp(-0.5 * u * u) * (1.0 / math.sqrt(2.0 * math.pi))
    return u * cdf, cdf + u * pdf


QK = 384
V = 256
OUT = 128
MISC = 384
MLP = 512
ATT = QK + V


def low_lanes():
    return lax.broadcasted_iota(jnp.int32, (1, BLOCK), 1) < HD


def turn(a):
    return jnp.concatenate([a[:, HD:], a[:, :HD]], 1)


def valid_rows(sc, n):
    row = lax.broadcasted_iota(jnp.int32, (IMG_PAD, 1), 0)
    return jnp.where((row < IMG_LEN) & (n < sc[0]), 1.0, 0.0)


def image_rows(n):
    return pl.ds(pl.multiple_of(n * IMG_PAD, 16), IMG_PAD)


def forward_image(n, sc, x_ref, w, vec, brow, out_ref, kept, ready):
    r = image_rows(n)
    x = x_ref[r, :].astype(F32)
    xhat, inv = normed(x)
    attn_in = (xhat * vec[0:1, :] + vec[2:3, :]).astype(BF16)
    kept["xh1"][r, :] = xhat
    kept["inv1"][r, :] = jnp.broadcast_to(inv, (IMG_PAD, BLOCK))
    kept["ain"][r, :] = attn_in
    residual = x + vec[3:4, :]
    low = low_lanes()
    lane = lax.broadcasted_iota(jnp.int32, (1, ATT), 1)
    factor = jnp.where(lane < 192, SCALE, jnp.where(lane < 576, 1.0, 0.0))
    real = lax.broadcasted_iota(jnp.int32, (1, IMG_PAD), 1) < IMG_LEN
    for t in range(2):
        bias = jnp.concatenate([brow[t, i:i + 1, :] for i in range(5)], 1)
        p = jnp.concatenate([nn(attn_in, w[t, 0, :, :QK]), nn(attn_in, w[t, 1, :, :V])], 1)
        p = ((p + bias) * factor).astype(BF16)
        kept["qkv"][t, r, :] = p
        q, qk, k, v, vx = [p[:, i * BLOCK:(i + 1) * BLOCK] for i in range(5)]
        kq, xv = turn(qk), turn(vx)
        outs = []
        for i, (qq, kk, vv) in enumerate(
                [(jnp.where(low, q, 0), k, v), (jnp.where(low, 0, q), k, v), (jnp.where(low, qk, 0), kq, xv)]):
            s = jnp.where(real, nt(qq, kk), NEGATIVE)
            e = jnp.exp(s - jnp.max(s, -1, keepdims=True))
            pr = (e * (1.0 / jnp.sum(e, -1, keepdims=True))).astype(BF16)
            kept["pr"][n * 6 + t * 3 + i] = pr
            outs.append(nn(pr, vv))
        mixed = jnp.concatenate([outs[2], jnp.where(low, outs[0], outs[1])], 1).astype(BF16)
        kept["mx"][t, r, :] = mixed
        residual = residual + nt(mixed, w[t, 1, :, OUT:MISC])
    xhat, inv = normed(residual)
    mlp_in = (xhat * vec[1:2, :] + vec[4:5, :]).astype(BF16)
    kept["xh2"][r, :] = xhat
    kept["inv2"][r, :] = jnp.broadcast_to(inv, (IMG_PAD, BLOCK))
    kept["min"][r, :] = mlp_in
    out = residual + vec[5:6, :]
    ready(1)
    ff = kept["hd"].shape[1] // 2
    for t in range(2):
        bias = jnp.concatenate([brow[t, 5 + i:6 + i, :] for i in range(ff // BLOCK)], 1)
        hidden, slope = gelu_parts(nn(mlp_in, w[t, 0, :, MLP:]) + bias)
        hidden = hidden.astype(BF16)
        kept["hd"][r, t * ff:(t + 1) * ff] = hidden
        kept["sl"][r, t * ff:(t + 1) * ff] = slope.astype(BF16)
        out = out + nt(hidden, w[t, 1, :, MLP:])
    out_ref[r, :] = (out * valid_rows(sc, n)).astype(BF16)


def rsum(a):
    return jnp.sum(a, 0, keepdims=True)


def backward_mlp(n, sc, u_ref, w, vec, kept, grad, sums, bsum):
    r = image_rows(n)

    masked = u_ref[r, :].astype(F32) * valid_rows(sc, n)
    sums[5:6, :] += rsum(masked)
    dg = masked.astype(BF16)
    grad["dg"][r, :] = dg
    mg = jnp.zeros(masked.shape, F32)
    ff = kept["hd"].shape[1] // 2
    for t in range(2):
        c = slice(t * ff, (t + 1) * ff)
        up = (nn(dg, w[t, 1, :, MLP:]) * kept["sl"][r, c].astype(F32)).astype(BF16)
        grad["up"][r, c] = up
        total = rsum(up.astype(F32))
        for i in range(ff // BLOCK):
            bsum[t, 5 + i:6 + i, :] += total[:, i * BLOCK:(i + 1) * BLOCK]
        mg = mg + nt(up, w[t, 0, :, MLP:])
    xhat = kept["xh2"][r, :]
    sums[4:5, :] += rsum(mg)
    sums[1:2, :] += rsum(mg * xhat)
    res = masked + norm_back(mg, xhat, kept["inv2"][r, :1], vec[1:2, :])
    sums[3:4, :] += rsum(res)
    grad["res"][r, :] = res


def backward_attention(n, w, vec, in_ref, kept, grad, sums, bsum):
    r = image_rows(n)
    res = grad["res"][r, :]
    ag = res.astype(BF16)
    grad["ag"][r, :] = ag
    low = low_lanes()
    ig = jnp.zeros(res.shape, F32)
    for t in range(2):
        xg = nn(ag, w[t, 1, :, OUT:MISC]).astype(BF16)
        gx = jnp.where(low, 0, xg[:, :BLOCK])
        g = xg[:, BLOCK:]
        p = kept["qkv"][t, r, :]
        q, qk, k, v, vx = [p[:, i * BLOCK:(i + 1) * BLOCK] for i in range(5)]
        kq, xv = turn(qk), turn(vx)
        dq, dk, dv = [], [], []
        for i, (qq, kk, vv, gm, gg) in enumerate(
                [(q, k, v, jnp.where(low, g, 0), g), (q, k, v, jnp.where(low, 0, g), g), (qk, kq, xv, gx, turn(gx))]):
            pb = kept["pr"][n * 6 + t * 3 + i]
            pf = pb.astype(F32)
            dp = nt(gm, vv)
            ds = (pf * (dp - jnp.sum(pf * dp, -1, keepdims=True))).astype(BF16)
            dv.append(tn(pb, gg))
            dq.append(nn(ds, kk) * SCALE)
            dk.append(tn(ds, kq if i == 2 else qq))
        blocks = [
            jnp.where(low, dq[0], dq[1]), jnp.where(low, dq[2], dk[2]), jnp.where(low, dk[0], dk[1]),
            jnp.where(low, dv[0], dv[1]), dv[2],
        ]
        d = jnp.concatenate(blocks, 1).astype(BF16)
        grad["dqkv"][t, r, :] = d
        total = rsum(d.astype(F32))
        for i in range(5):
            bsum[t, i:i + 1, :] += total[:, i * BLOCK:(i + 1) * BLOCK]
        ig = ig + nt(d[:, :QK], w[t, 0, :, :QK]) + nt(d[:, QK:], w[t, 1, :, :V])
    xhat = kept["xh1"][r, :]
    sums[2:3, :] += rsum(ig)
    sums[0:1, :] += rsum(ig * xhat)
    in_ref[r, :] = res + norm_back(ig, xhat, kept["inv1"][r, :1], vec[0:1, :])


def weight_grads(t, piece, kept, grad, g):
    ag, dg = grad["ag"][...], grad["dg"][...]
    ain, mlp_in = kept["ain"][...], kept["min"][...]
    width = ag.shape[1]
    high = jnp.where(low_lanes(), 0.0, 1.0)
    d = grad["dqkv"][t]
    g[0, :, :QK] = tn(ain, d[:, :QK]).astype(BF16)
    val = tn(ain, d[:, QK:])
    out = tn(ag, kept["mx"][t])
    g[1, :, :OUT] = val[:, :BLOCK].astype(BF16)
    g[1, :, OUT:V] = (val[:, BLOCK:] + out[:, :BLOCK] * high).astype(BF16)
    g[1, :, V:MISC] = out[:, BLOCK:].astype(BF16)
    sums = jnp.concatenate([grad["sums"][...], jnp.zeros((BLOCK - 8, width), F32)], 0)
    g[0, :, MISC:MLP] = sums.T.astype(BF16)
    ff = kept["hd"].shape[1] // 2
    c = pl.ds(pl.multiple_of(t * ff, BLOCK), ff)
    g[0, :, MLP:] = tn(mlp_in, grad["up"][:, c]).astype(BF16)
    g[1, :, MLP:] = tn(dg, kept["hd"][:, c]).astype(BF16)
    if piece % 16 == 0:
        rows = jnp.concatenate([grad["bsum"][t], jnp.zeros((piece - 16, BLOCK), F32)], 0).astype(BF16)
        for i in range(width // piece):
            g[1, i * piece:(i + 1) * piece, MISC:MLP] = rows


def kept_shapes(total, width, ff):
    images = total // IMG_PAD
    return dict(
        xh1=((total, width), F32), inv1=((total, BLOCK), F32), ain=((total, width), BF16), qkv=((2, total, ATT), BF16),
        pr=((images * 6, IMG_PAD, IMG_PAD), BF16), mx=((2, total, 2 * BLOCK), BF16), xh2=((total, width), F32),
        inv2=((total, BLOCK), F32), min=((total, width), BF16), sl=((total, ff), BF16), hd=((total, ff), BF16))


def grad_shapes(total, width, ff):
    return dict(dg=((total, width), BF16), up=((total, ff), BF16), res=((total, width), F32), sums=((8, width), F32),
                bsum=((2, 16, BLOCK), F32), ag=((total, width), BF16), dqkv=((2, total, ATT), BF16))


def layer_call(phases, sources, load, store, out_shapes, scalars, given, total, width, ff, piece):
    ks = kept_shapes(total, width, ff)
    gs = grad_shapes(total, width, ff)
    weights = ["ain", "mx", "min", "hd"] + [n for n in gs if n != "res"]
    need = {"forward": ["x"], "back": ["u"] + list(ks), "theirs": weights, "mine": weights}
    gives = {"forward": {"out": ((total, width), BF16), **ks}, "back": {"keep": ((total, width), BF16), "give": ((total, width), BF16), "in": ((total, width), F32), **gs},
             "theirs": {}, "mine": {}}
    made = {}
    for p in phases:
        made.update(gives[p])
    inputs = list(dict.fromkeys(n for p in phases for n in need[p] if n not in made))
    if phases[-1] == "forward":
        shown = list(made)
    else:
        shown = [n for n in made if n in weights or n in ("keep", "give")]
        if "forward" in phases:
            shown.append("in")
    inner = [n for n in made if n not in shown]
    side = {"theirs": 0, "mine": 1}.get(phases[-1])
    products = phases[0] != "mine"
    vmem = pl.BlockSpec(memory_space=pltpu.VMEM)
    anywhere = pl.BlockSpec(memory_space=pl.ANY)
    ends = [] if side is None else out_shapes[side]
    scratch = [pltpu.SemaphoreType.DMA((2,))] + [pltpu.VMEM(*made[n]) for n in inner]
    if products:
        scratch += [pltpu.VMEM((2, 2, width, HALF), BF16), pltpu.VMEM((8, width), F32), pltpu.VMEM((2, 16, BLOCK), F32)]
    if ends:
        scratch.append(pltpu.VMEM((2, width, HALF), BF16))

    def body(*refs):
        refs = list(refs)

        def take(n):
            got = refs[:n]
            del refs[:n]
            return got

        sc = take(1)[0]
        at = dict(zip(inputs, take(len(inputs))))
        src = take(len(sources))
        at.update(zip(shown, take(len(shown))))
        dst = take(len(ends))
        sem = take(1)[0]
        at.update(zip(inner, take(len(inner))))
        if products:
            w, vec, brow = take(3)
            pending = [load(sc, src, w, sem, c) for c in range(2)]
            for part in pending if "forward" in phases else pending[::-1]:
                for c in part:
                    c.start()

            def ready(c):
                for copy in pending[c]:
                    copy.wait()
                if c == 0 and pending[c]:
                    vec[...] = w[0, 0, :, MISC:MLP].astype(F32).T[:8, :]
                    for t in range(2):
                        brow[t] = w[t, 1, :16, MISC:MLP].astype(F32)
                pending[c] = []

            ready(0 if "forward" in phases else 1)
        if "forward" in phases:
            if "back" in phases:
                ready(1)

                def step(n, carry):
                    forward_image(n, sc, at["x"], w, vec, brow, at["out"], at, ready)
                    return carry
                lax.fori_loop(0, total // IMG_PAD, step, 0)
            else:
                for n in range(total // IMG_PAD):
                    forward_image(n, sc, at["x"], w, vec, brow, at["out"], at, ready)
        if "back" in phases:
            sums, bsum = at["sums"], at["bsum"]
            sums[...] = jnp.zeros_like(sums)
            bsum[...] = jnp.zeros_like(bsum)
            ready(0)

            def back(n, carry):
                backward_mlp(n, sc, at["u"], w, vec, at, at, sums, bsum)
                backward_attention(n, w, vec, at["in"], at, at, sums, bsum)
                return carry
            lax.fori_loop(0, total // IMG_PAD, back, 0)
            rows = [at[n] for n in (("x", "out") if "forward" in phases else ("in", "u"))]
            for here in range(2):
                @pl.when(sc[2] == here)
                def _():
                    at["keep"][...] = rows[here][...].astype(BF16)
                    at["give"][...] = rows[1 - here][...].astype(BF16)
        if ends:
            g = take(1)[0]
            t = jnp.where(sc[1] == 0, 1 - side, side)
            weight_grads(t, piece, at, at, g)
            copies = store(sc, side, g, dst, sem.at[0])
            for c in copies:
                c.start()
            for c in copies:
                c.wait()

    outs = [made[n] for n in shown] + ends
    args = [scalars, *[given[n] for n in inputs], *(sources if products else [])]
    if not products:
        sources = []
    got = pl.pallas_call(
        body,
        out_shape=[jax.ShapeDtypeStruct(*o) for o in outs],
        in_specs=[pl.BlockSpec(memory_space=pltpu.SMEM)] + [vmem] * len(inputs) + [anywhere] * len(sources),
        out_specs=[vmem] * (len(outs) - len(ends)) + [anywhere] * len(ends),
        scratch_shapes=scratch,
        compiler_params=pltpu.CompilerParams(vmem_limit_bytes=34 * 2 ** 20),
        cost_estimate=pl.CostEstimate(flops=COST * len(phases), transcendentals=0, bytes_accessed=2 ** 23),
    )(*args)
    got = list(got)
    res = dict(zip(shown, got))
    res["g"] = got[len(shown):]
    return res


def parts(a, b, ff):
    small = a[:, MISC:MLP].T
    rows = b[:16, MISC:MLP]

    def heads(c, pair, single):
        return jnp.concatenate([c[:, pair:pair + BLOCK], c[:, single:single + HD]], 1)

    def lanes(first, last):
        return jnp.concatenate([rows[i:i + 1, :] for i in range(first, last)], 1)

    size = 3 * HD
    qkv = jnp.stack([heads(a, 0, BLOCK), heads(a, 2 * BLOCK, BLOCK + HD), heads(b, 0, BLOCK)])
    biases = jnp.concatenate([lanes(0, 2)[:, :size], lanes(3, 5)[:, :size]], 0)
    out = heads(b, 2 * BLOCK, BLOCK + HD)
    return small[:2], small[2:6], qkv, biases, out, a[:, MLP:], lanes(5, 5 + ff // BLOCK), b[:, MLP:]


def finish(scalars, mine, other, ff):
    piece = mine.shape[0]

    def body(sc, mine_ref, other_ref, *outs):
        first = sc[2] == 0
        a, b = mine_ref[...], other_ref[...].astype(F32)
        for ref, got in zip(outs, parts(jnp.where(first, a, b), jnp.where(first, b, a), ff)):
            ref[...] = got

    vmem = pl.BlockSpec(memory_space=pltpu.VMEM)
    shapes = [(2, piece), (4, piece), (3, piece, 3 * HD), (2, 3 * HD), (piece, 3 * HD), (piece, ff), (1, ff), (piece, ff)]
    return pl.pallas_call(
        body,
        out_shape=[jax.ShapeDtypeStruct(s, F32) for s in shapes],
        in_specs=[pl.BlockSpec(memory_space=pltpu.SMEM), vmem, vmem],
        out_specs=[vmem] * len(shapes),
    )(scalars, mine, other)


def shards(tokens, image_counts, cotangent, norm_gains, row_biases, qkv_weight, qv_bias, out_weight,
           up_weight, up_bias, down_weight):
    sec = lax.axis_index("section")
    dp = lax.axis_index("dp")
    ten = lax.axis_index("tensor")
    n_dp = lax.axis_size("dp")
    m = n_dp // 2
    zi, yi = dp // 2, dp % 2
    local_rows, width = tokens.shape[1:]
    images = local_rows * n_dp // IMG_LEN
    piece = width // n_dp
    ff = 2 * up_weight.shape[2]
    direct = piece % 16 == 0 and m == 4

    def pt(a):
        return lax.ppermute(a, "tensor", [(0, 1), (1, 0)])

    def px(a):
        return lax.ppermute(a, "section", [(0, 1), (1, 0)])

    def py(a):
        return lax.ppermute(a, "dp", [(i, i ^ 1) for i in range(n_dp)])

    def pd(a):
        return lax.ppermute(a, ("section", "dp"), [(i, (i + n_dp) % (2 * n_dp) ^ 1) for i in range(2 * n_dp)])

    def after(a, *b):
        return lax.optimization_barrier((a, *b))

    def plus(*a):
        return sum(b.astype(F32) for b in a)

    def chip_sums(g, got):
        keep0, give0, keep1, give1 = [plus(a, got[i // 2, i % 2]) for i, a in enumerate(g)]
        return [keep0, give0.astype(BF16), keep1, give1.astype(BF16)]

    def cross_first(s):
        return [s[0], px(s[1]), s[2], py(s[3])]

    def cross_second(s):
        a, b = plus(s[0], s[1]), plus(s[2], s[3])
        return [a[0], py(a[1].astype(BF16)), b[0], px(b[1].astype(BF16))]

    def crossed(s):
        return jnp.stack([plus(s[0], s[1]), plus(s[2], s[3])])

    def pz_to(a, kk):
        return lax.ppermute(a, "dp", [(i, i ^ (2 * kk)) for i in range(n_dp)])

    def along(quad):
        low = quad.astype(BF16)
        return plus(quad[:, 0], *[pz_to(low[:, kk], kk) for kk in range(1, m)])

    def along_steps(quad, *before):
        got = pz_to(quad[:, 1::2].astype(BF16), 1)
        quad = after(plus(quad[:, 0::2], got), *before)[0]
        return plus(quad[:, 0], pz_to(quad[:, 1].astype(BF16), 2))

    def pn(a):
        return lax.ppermute(a, ("dp", "tensor"), [(2 * i + 1, 2 * i + 3) for i in range(n_dp - 1)])

    def placed(rows, *before):
        tail = select[:, local_rows:]
        tails = after(pn(jnp.stack([tn(tail, a) for a in rows]).astype(BF16)), *before)[0]

        def place(a, b):
            a = tn(select[:, :local_rows], a).astype(BF16)
            return jnp.concatenate([a[:IMG_PAD] + b, a[IMG_PAD:]], 0)

        return jnp.stack([place(a, tails[i]) for i, a in enumerate(rows)])

    def ordered(a, b):
        a = a + b
        return jnp.where(sec == 0, a, a[::-1])[None]

    batch_tokens = lax.dynamic_index_in_dim(tokens, sec, 0, keepdims=False)
    batch_cot = lax.dynamic_index_in_dim(cotangent, sec, 0, keepdims=False)
    count = lax.dynamic_index_in_dim(image_counts, sec, 0, keepdims=False)
    first = jnp.minimum((dp * local_rows + IMG_LEN - 1) // IMG_LEN, images)
    last = jnp.minimum(((dp + 1) * local_rows + IMG_LEN - 1) // IMG_LEN, images)
    held = last - first
    slots = -(-(-(-local_rows // IMG_LEN)) // 2)
    lower = held // 2
    own_first = jnp.where(ten == 0, first, first + lower)
    own_count = jnp.where(ten == 0, lower, held - lower)
    total = slots * IMG_PAD
    row = lax.broadcasted_iota(jnp.int32, (total, 1), 0)
    slot, inside = row // IMG_PAD, row % IMG_PAD
    exists = (inside < IMG_LEN) & (slot < own_count)
    target = (own_first + slot) * IMG_LEN + inside - dp * local_rows
    canvas_rows = local_rows + IMG_PAD
    select = ((lax.broadcasted_iota(jnp.int32, (total, canvas_rows), 1) == target) & exists).astype(BF16)
    scalars = jnp.stack([jnp.minimum(own_count, jnp.maximum(count - own_first, 0)), ten, sec, zi, yi]).astype(jnp.int32)

    both = jnp.stack([batch_tokens, batch_cot])
    halo = lax.ppermute(both[:, :IMG_PAD], ("dp", "tensor"), [(2 * i + 3, 2 * i + 1) for i in range(n_dp - 1)])
    q, k, v = [[qkv_weight[0, :, i, h * HD:(h + 1) * HD] for h in range(3)] for i in range(3)]
    o = out_weight[0].T
    o = [o[:, h * HD:(h + 1) * HD] for h in range(3)]
    misc = jnp.concatenate([norm_gains[0], row_biases[0]], 0).T
    misc = jnp.pad(misc, ((0, 0), (0, BLOCK - misc.shape[1])))
    gap = jnp.zeros((HD,), BF16)
    rows = jnp.concatenate([qv_bias[0, 0], gap, gap, gap, qv_bias[0, 1], gap, up_bias[0]]).reshape(-1, BLOCK)
    rows = jnp.pad(rows, ((0, piece - rows.shape[0]), (0, 0)))
    up, down = up_weight[0], down_weight[0].T
    part0 = jnp.concatenate([q[0], q[1], q[2], k[2], k[0], k[1], misc, up], 1)
    part1 = jnp.concatenate([v[0], v[1], v[2], o[2], o[0], o[1], rows, down], 1)

    if direct:
        keep = jnp.where(sec == 0, part0, part1)
        give = jnp.where(sec == 0, part1, part0)
        got, halo = after(px(give), halo)
        start = [jnp.where(sec == 0, keep, got), jnp.where(sec == 0, got, keep)]

        def load(l, sc, src, w, sem, c):
            copies = []
            cols = slice(0, MLP) if c == 0 else slice(MLP, HALF)
            for side in range(2):
                t = jnp.where(sc[1] == 0, side, 1 - side)
                own = src[side * 8:side * 8 + 8]
                for kk in range(m):
                    z = lax.bitwise_xor(sc[3], kk)
                    near = pl.ds(pl.multiple_of((2 * z + sc[4]) * piece, 16), piece)
                    far = pl.ds(pl.multiple_of((2 * z + 1 - sc[4]) * piece, 16), piece)
                    for i, (h, r) in enumerate(((sc[2], near), (1 - sc[2], near), (sc[2], far), (1 - sc[2], far))):
                        a = own[i].at[l, :, cols] if kk == 0 else own[4 + i].at[kk - 1, :, cols]
                        copies.append(pltpu.make_async_copy(a, w.at[t, h, r, cols], sem.at[c]))
            return copies

        part = HALF // 2

        def store(sc, side, g, dst, sem):
            copies = []
            for c in range(2):
                for i in range(2):
                    for j in range(2):
                        hr, yr = (i, j) if c == 0 else (j, i)
                        h = lax.bitwise_xor(sc[2], hr)
                        y = lax.bitwise_xor(sc[4], yr)
                        out = dst[0].at[c, i, j] if side == 0 else dst[2 * c + i].at[j]
                        for kk in range(m):
                            z = lax.bitwise_xor(sc[3], kk)
                            r = pl.ds(pl.multiple_of((2 * z + y) * piece, 16), piece)
                            a = g.at[h, r, c * part:(c + 1) * part]
                            copies.append(pltpu.make_async_copy(a, out.at[kk], sem))
            return copies

        out_shapes = [[((2, 2, 2, m, piece, part), BF16)], [((2, m, piece, part), BF16)] * 4]
        own = jnp.stack(start)
        firsts = [own, px(own), py(own), pd(own)]
        columns = [jnp.stack([pz_to(start[0], kk) for kk in range(1, m)])]
        start[1] = after(start[1], columns[0])[0]
        near = pz_to(start[1], 1)
        columns[0], *firsts = after(columns[0], *firsts)
        rest = [columns[0], px(columns[0]), py(columns[0]), pd(columns[0])]
        pair = after(jnp.stack([start[1], near]), *firsts)[0]
        columns.append(jnp.concatenate([near[None], pz_to(pair, 2)]))
        columns[1], *rest = after(columns[1], *rest)
        twins = [pt(a) for a in firsts]
        sources = [firsts + rest + twins + [pt(a) for a in rest]]
        sources.append(columns[1:] + [px(columns[1]), py(columns[1]), pd(columns[1])])
    else:
        def load(l, sc, src, w, sem, c):
            return [pltpu.make_async_copy(src[0], w, sem.at[c])] if c == 0 else []

        def store(sc, side, g, dst, sem):
            return [pltpu.make_async_copy(g, dst[0], sem)]

        out_shapes = [[((2, width, HALF), BF16)]] * 2
        a = lax.all_gather(jnp.stack([part0, part1]), "dp", axis=1, tiled=True)
        a = lax.all_gather(lax.all_gather(a, "tensor"), "section")
        sources = [[a[0]], [a[1]]]

    batch = jnp.concatenate([both, halo], 1)
    x0 = nn(select, batch[0]).astype(BF16)
    cot = nn(select, batch[1]).astype(BF16)
    x0, cot = after(x0, cot)

    def call(l, phases, **given):
        return layer_call(phases, sources[l], functools.partial(load, l), store, out_shapes, scalars, given,
                          total, width, ff, piece)

    r0 = call(0, ["forward"], x=x0)
    low0 = r0["out"]
    if direct:
        low0, *rest = after(low0, *sources[1])
        sources[1] = firsts + rest + twins + [pt(a) for a in rest]
    r1 = call(1, ["forward", "back", "theirs"], x=low0, u=cot)
    if direct:
        got1 = pt(r1["g"][0])
    low_got = px(r1["give"])
    m1 = call(1, ["mine"], **r1)
    u = r1["in"]
    if direct:
        first, got1 = after(m1["g"][0], got1)
        sent1 = chip_sums([first] + m1["g"][1:], got1)
        u = after(u, sent1[1], sent1[3])[0]
        quad1 = cross_first(sent1)
    b0 = call(0, ["back", "theirs"], **{**r0, "u": u})
    if direct:
        b0["dg"], b0["g"][0], *quad1 = after(b0["dg"], b0["g"][0], *quad1)
        got0 = pt(b0["g"][0])
        quad1 = cross_second(quad1)
    in_got = px(b0["give"])
    m0 = call(0, ["mine"], **{**r0, **b0})

    if direct:
        first, got0 = after(m0["g"][0], got0)
        sent0 = chip_sums([first] + m0["g"][1:], got0)
        in_got, low_got, *quad1 = after(in_got, low_got, *quad1, sent0[1], sent0[3])[:6]
        quad0 = after(*cross_first(sent0))
        rows = placed([r1["keep"], low_got, b0["keep"], in_got], quad0[1], quad0[3])
        done1 = along_steps(crossed(quad1), quad0[1], quad0[3])
        quad0 = cross_second(quad0)
        done1, *quad0 = after(done1, *quad0)
        twin, done0 = after(pt(rows), along(crossed(quad0)))
        done0, done1 = [jnp.concatenate([a[0], a[1]], 1) for a in (done0, done1)]
        mine = jnp.where(sec == 0, done0, done1)
        other = px(jnp.where(sec == 0, done1, done0).astype(BF16))
        g_gain, g_bias, g_qkv, g_qv, g_out, g_up, g_up_bias, g_down = finish(scalars, mine, other, ff // 2)
    else:
        rows = placed([r1["keep"], low_got, b0["keep"], in_got])
        twin = pt(rows)

        def by_core(a, b):
            return jnp.where(ten == 0, jnp.stack([b, a]), jnp.stack([a, b]))

        g = jnp.stack([by_core(b0["g"][0], m0["g"][0]), by_core(r1["g"][0], m1["g"][0])])
        g = lax.psum_scatter(g.astype(F32), "section", scatter_dimension=0)
        g = lax.psum_scatter(g, "tensor", scatter_dimension=0)
        g = lax.psum_scatter(g, "dp", scatter_dimension=1, tiled=True)
        small = lax.psum(jnp.stack([b0["bsum"], r1["bsum"]]), ("section", "tensor", "dp"))
        small = lax.dynamic_index_in_dim(lax.dynamic_index_in_dim(small, sec, 0, False), ten, 0, False)
        g_gain, g_bias, g_qkv, _, g_out, g_up, _, g_down = parts(g[0], g[1], ff // 2)
        small = jnp.pad(small, ((0, 0), (MISC, HALF - MLP)))
        _, _, _, g_qv, _, _, g_up_bias, _ = parts(small, small, ff // 2)

    layer_outputs = ordered(rows[:2], twin[:2])
    input_grads = ordered(rows[2:], twin[2:]).astype(F32)

    return (
        layer_outputs,
        input_grads,
        g_gain[None],
        g_bias[None],
        g_qkv.transpose(1, 0, 2)[None],
        g_qv[None],
        g_out.T[None],
        g_up[None],
        g_up_bias,
        g_down.T[None],
    )


def solution(mesh):
    in_specs = (
        P(None, "dp", None),
        P(),
        P(None, "dp", None),
        P("section", None, "dp"),
        P("section", None, "dp"),
        P("section", "dp", None, "tensor"),
        P("section", None, "tensor"),
        P("section", "tensor", "dp"),
        P("section", "dp", "tensor"),
        P("section", "tensor"),
        P("section", "tensor", "dp"),
    )
    out_specs = (
        P("section", None, "dp", None),
        P("section", None, "dp", None),
        P("section", None, "dp"),
        P("section", None, "dp"),
        P("section", "dp", None, "tensor"),
        P("section", None, "tensor"),
        P("section", "tensor", "dp"),
        P("section", "dp", "tensor"),
        P("section", "tensor"),
        P("section", "tensor", "dp"),
    )
    return jax.shard_map(shards, mesh=mesh, in_specs=in_specs, out_specs=out_specs, check_vma=False)
```
